32 devices in a mesh: rep: 8 (over z, core), shard: 4 (over y, x).
Axes of the slice: x: 2, y: 2, z: 4, core: 2. Of those that a mesh axis runs over, the one named last changes fastest.
Arguments:
- inputs: bfloat16 [32, 1024, 1024], P(('rep', 'shard')), may hold values from -6 to 6
- lengths: int32 [32], P(('rep', 'shard')), may hold values from 256 to 1024, as said below
- gain_attn: bfloat16 [1024], P('shard'), may hold values from 0.099609375 to 1.8984375
- w_query: bfloat16 [1024, 1024], P('shard'), may hold values from -0.1875 to 0.1875
- w_key: bfloat16 [1024, 512], P('shard'), may hold values from -0.1875 to 0.1875
- w_value: bfloat16 [1024, 512], P('shard'), may hold values from -0.1875 to 0.1875
- gain_query: bfloat16 [64], P('shard'), may hold values from 0.099609375 to 1.8984375
- gain_key: bfloat16 [64], P('shard'), may hold values from 0.099609375 to 1.8984375
- w_out: bfloat16 [1024, 1024], P('shard'), may hold values from -3 to 3
- gain_mlp: bfloat16 [1024], P('shard'), may hold values from 0.099609375 to 1.8984375
- w_gate: bfloat16 [1024, 4608], P('shard'), may hold values from -0.1875 to 0.1875
- w_up: bfloat16 [1024, 4608], P('shard'), may hold values from -0.1875 to 0.1875
- w_down: bfloat16 [4608, 1024], P('shard'), may hold values from -0.09375 to 0.09375
- cotangent: bfloat16 [32, 1024, 1024], P(('rep', 'shard')), may hold values from -6 to 6
Outputs:
- output: bfloat16 [32, 1024, 1024], P(('rep', 'shard'))
- input_grad: bfloat16 [32, 1024, 1024], P(('rep', 'shard'))
- grad_gain_attn: float32 [1024], P('shard')
- grad_query: float32 [1024, 1024], P('shard')
- grad_key: float32 [1024, 512], P('shard')
- grad_value: float32 [1024, 512], P('shard')
- grad_gain_query: float32 [64], P('shard')
- grad_gain_key: float32 [64], P('shard')
- grad_out: float32 [1024, 1024], P('shard')
- grad_gain_mlp: float32 [1024], P('shard')
- grad_gate: float32 [1024, 4608], P('shard')
- grad_up: float32 [1024, 4608], P('shard')
- grad_down: float32 [4608, 1024], P('shard')
- statistics: float32 [3], replicated
The draws below stay inside these ranges and needn't reach their ends.
Inputs may be any that keep to these rules, and one draw needn't show every extreme that they name: lengths[s] counts the valid leading positions of slot s; some slot has exactly 1024 and some exactly 256.
All inputs are finite; a program needn't handle non-finite values.
Results may differ from the reference program's by a relative error of at most 0.013.
Values may be sent and summed in bfloat16 or wider, within the bound.
A program may use at most 320 MiB of HBM per device.

```python
import math
import jax
import jax.numpy as jnp
from jax import lax

D = 1024
HQ = 16
KV = 8
HD = 64
FF = 4608
SEQ = 1024
MIN_LEN = 256
SLOTS = 32


def draw_lengths(key, part):
    base_key = jax.random.fold_in(key, 11)
    first_key, second_key = jax.random.split(base_key)
    level = jax.random.randint(first_key, (SLOTS,), 0, 65)
    spread = MIN_LEN + (SEQ - MIN_LEN) * level * level // 4096
    order = jax.random.permutation(second_key, SLOTS)
    spread = spread.at[order[0]].set(SEQ)
    spread = spread.at[order[1]].set(MIN_LEN)
    return spread.astype(jnp.int32)


def with_spikes(values, stream_key, source, target, parts, factor):
    owner, partner = [(jnp.arange(values.shape[dim]) // (values.shape[dim] // parts)).reshape([-1 if axis == dim else 1 for axis in range(values.ndim)]) for dim in (source, target)]
    chosen = jax.random.permutation(stream_key, parts)[partner]
    strong = (owner == chosen) | (owner == (partner + parts // 2) % parts)
    return jnp.where(strong, factor * values, values)


def block_scale(rng, extent, cuts, low, largest):
    def one(position, shards_of):
        steps = jax.random.uniform(jax.random.fold_in(jax.random.fold_in(rng, 6), position), (shards_of,), jnp.float32, low / len(cuts), largest / len(cuts))
        return jnp.repeat(jnp.exp(steps), extent[position] // shards_of).reshape((-1,) + (1,) * (len(extent) - position - 1))

    level = one(*cuts[0])
    for cut in cuts[1:]:
        level = level * one(*cut)
    return level


def noise(key, extent, scale, reach, shards=(), kind=jnp.bfloat16):
    values = scale * jax.random.normal(key, extent, jnp.float32)
    if shards:
        values = values * block_scale(key, extent, shards, -0.22, 0.18)
    return jnp.clip(values, -reach, reach).astype(kind)


def heavy_noise(stream_key, dims, width, bound, cuts, heavy, kind=jnp.bfloat16):
    entries = width * jax.random.normal(stream_key, dims, jnp.float32)
    if cuts:
        entries = entries * block_scale(stream_key, dims, cuts, -0.22, 0.18)
    return jnp.clip(with_spikes(entries, jax.random.fold_in(stream_key, 3), *heavy), -bound, bound).astype(kind)


def setup_inputs(seed: int = 0) -> dict:
    splits = jax.random.split(jax.random.key(seed), 15)
    return {
        "inputs": heavy_noise(splits[0], (SLOTS, SEQ, D), 1.0, 6.0, ((0, 32),), (0, 2, 32, 2.75)),
        "lengths": draw_lengths(jax.random.fold_in(splits[14], 71), 0),
        "gain_attn": jnp.clip(1.0 + 0.18 * jax.random.normal(splits[2], (D,), jnp.float32), 0.099609375, 1.8984375).astype(jnp.bfloat16),
        "w_query": noise(splits[3], (D, HQ * HD), D ** -0.5, 0.1875, ((0, 4),)),
        "w_key": noise(splits[4], (D, KV * HD), D ** -0.5, 0.1875, ((0, 4),)),
        "w_value": noise(splits[5], (D, KV * HD), D ** -0.5, 0.1875, ((0, 4),)),
        "gain_query": jnp.clip(1.0 + 0.18 * jax.random.normal(splits[6], (HD,), jnp.float32), 0.099609375, 1.8984375).astype(jnp.bfloat16),
        "gain_key": jnp.clip(1.0 + 0.18 * jax.random.normal(splits[7], (HD,), jnp.float32), 0.099609375, 1.8984375).astype(jnp.bfloat16),
        "w_out": noise(splits[8], (HQ * HD, D), (max(4, HQ * HD // 256)) ** -0.5, 3.0, ((0, 4),)),
        "gain_mlp": jnp.clip(1.0 + 0.18 * jax.random.normal(splits[9], (D,), jnp.float32), 0.099609375, 1.8984375).astype(jnp.bfloat16),
        "w_gate": noise(splits[10], (D, FF), D ** -0.5, 0.1875, ((0, 4),)),
        "w_up": noise(splits[11], (D, FF), D ** -0.5, 0.1875, ((0, 4),)),
        "w_down": noise(splits[12], (FF, D), FF ** -0.5, 0.09375, ((0, 4),)),
        "cotangent": noise(splits[13], (SLOTS, SEQ, D), 1.0, 6.0, ((0, 32),)),
    }


EPS = 1e-05
NEG = -1e+30
ROPE_BASE = 1000000.0
HIGH = lax.Precision.HIGHEST

@jax.custom_vjp
def low(v):
    return lax.optimization_barrier(v.astype(jnp.bfloat16)).astype(jnp.float32)

@jax.custom_vjp
def low_back(v):
    return v

def low_keep(v):
    return (low(v), None)

def low_pass(kept, grad):
    return (grad,)

def back_keep(v):
    return (v, None)

def back_low(kept, grad):
    return (low(grad),)
low.defvjp(low_keep, low_pass)
low_back.defvjp(back_keep, back_low)

def rms_norm(values, norm_gain):
    return values * lax.rsqrt(lax.optimization_barrier(jnp.mean(values * values, axis=-1, keepdims=True)) + EPS) * norm_gain

def rope_tables(row_count, head_width):
    half_width = head_width // 2
    frequency = jnp.power(jnp.float32(ROPE_BASE), -jnp.arange(half_width, dtype=jnp.float32) * 2.0 / head_width)
    angles = jnp.arange(row_count, dtype=jnp.float32)[:, None] * frequency[None, :]
    cosine = jnp.concatenate([jnp.cos(angles), jnp.cos(angles)], axis=1)[:, None, :]
    sine_table = jnp.concatenate([jnp.sin(angles), jnp.sin(angles)], axis=1)[:, None, :]
    return (cosine, sine_table)

def rotate(values, cosine, sine_table):
    half_width = values.shape[-1] // 2
    turned = jnp.concatenate([-values[..., half_width:], values[..., :half_width]], axis=-1)
    return values * cosine + turned * sine_table

def head_parts(query_proj, key_proj, query_gain, key_gain, cosine, sine_table):
    row_count = query_proj.shape[0]
    head_width = query_gain.shape[0]
    query_rot = rotate(rms_norm(query_proj.reshape(row_count, -1, head_width), query_gain), cosine, sine_table)
    key_rot = rotate(rms_norm(key_proj.reshape(row_count, -1, head_width), key_gain), cosine, sine_table)
    return (query_rot.reshape(row_count, -1), key_rot.reshape(row_count, -1))

def matmul_high(left_side, right_side):
    return jnp.dot(left_side, right_side, precision=HIGH, preferred_element_type=jnp.float32)

def layer(layer_in, gain_attn, w_query, w_key, w_value, gain_query, gain_key, w_out, gain_mlp, w_gate, w_up, w_down, valid, cosine, sine_table):
    row_count = layer_in.shape[0]
    head_width = gain_query.shape[0]
    head_count = w_query.shape[1] // head_width
    group_count = w_key.shape[1] // head_width
    per_group = head_count // group_count
    normed_a = low(rms_norm(layer_in, gain_attn))
    query_proj = low_back(matmul_high(normed_a, w_query))
    key_proj = low_back(matmul_high(normed_a, w_key))
    value_low = low_back(low(matmul_high(normed_a, w_value)))
    query_rot, key_rot = head_parts(query_proj, key_proj, gain_query, gain_key, cosine, sine_table)
    query_low = low(query_rot).reshape(row_count, group_count, per_group, head_width)
    key_low = low(key_rot).reshape(row_count, group_count, head_width)
    value_grp = value_low.reshape(row_count, group_count, head_width)
    scale_factor = 1.0 / math.sqrt(head_width)
    scores = low_back(jnp.einsum('qgrd,kgd->grqk', query_low, key_low, precision=HIGH) * scale_factor)
    positions = jnp.arange(row_count)
    allowed = (positions[None, :] <= positions[:, None]) & (valid[None, :] > 0)
    scores = jnp.where(allowed, scores, NEG)
    top_score = lax.optimization_barrier(jnp.max(scores, axis=-1, keepdims=True))
    exp_scores = jnp.exp(scores - top_score)
    probs = low(exp_scores / lax.optimization_barrier(jnp.sum(exp_scores, axis=-1, keepdims=True)))
    attended = jnp.einsum('grqk,kgd->qgrd', probs, value_grp, precision=HIGH).reshape(row_count, head_count * head_width)
    attended = low_back(low(attended))
    attn_out = low_back(matmul_high(attended, w_out))
    resid = layer_in + attn_out
    normed_b = low(rms_norm(resid, gain_mlp))
    gate_pre = low_back(matmul_high(normed_b, w_gate))
    up_pre = low_back(matmul_high(normed_b, w_up))
    hidden = low(jax.nn.silu(gate_pre) * up_pre)
    mlp_out = low_back(matmul_high(hidden, w_down))
    valid_col = valid[:, None]
    result = valid_col * (resid + mlp_out)
    sums = jnp.stack([jnp.sum(valid_col * resid * resid), jnp.sum(valid_col * attn_out * attn_out), jnp.sum(valid_col * mlp_out * mlp_out)])
    return (result, sums)

def reference(inputs, lengths, gain_attn, w_query, w_key, w_value, gain_query, gain_key, w_out, gain_mlp, w_gate, w_up, w_down, cotangent):
    weights = tuple((weight.astype(jnp.float32) for weight in (gain_attn, w_query, w_key, w_value, gain_query, gain_key, w_out, gain_mlp, w_gate, w_up, w_down)))
    row_count = inputs.shape[1]
    cosine, sine_table = rope_tables(row_count, gain_query.shape[0])

    def one_slot(carry, slot):
        slot_in, slot_len, slot_cot = slot
        valid = (jnp.arange(row_count) < slot_len).astype(jnp.float32)

        def forward(layer_in, *params):
            return layer(layer_in, *params, valid, cosine, sine_table)
        result, backward, sums = jax.vjp(forward, slot_in.astype(jnp.float32), *weights, has_aux=True)
        grads = backward(slot_cot.astype(jnp.float32))
        new_grads = jax.tree.map(lambda total, piece: total + piece, carry[0], tuple(grads[1:]))
        return ((new_grads, carry[1] + sums), (result.astype(jnp.bfloat16), grads[0].astype(jnp.bfloat16)))
    init = (tuple((jnp.zeros_like(weight) for weight in weights)), jnp.zeros((3,), jnp.float32))
    (grads, totals), (output, input_grad) = lax.scan(one_slot, init, (inputs, lengths, cotangent))
    count = jnp.sum(lengths).astype(jnp.float32)
    statistics = jnp.sqrt(totals / (count * inputs.shape[2]))
    return (output, input_grad, grads[0], grads[1], grads[2], grads[3], grads[4], grads[5], grads[6], grads[7], grads[8], grads[9], grads[10], statistics)
```

```python
from functools import partial
import math

import jax
import jax.numpy as jnp
from jax import lax
from jax.experimental import pallas as pl
from jax.experimental.pallas import tpu as pltpu
from jax.sharding import PartitionSpec as P

EPS = 1e-05
ROPE_BASE = 1000000.0
F32 = jnp.float32
LOW = jnp.bfloat16
LANES = 128
MESH = pl.DeviceIdType.MESH


def rope_tables(row_count, head_width):
    half_width = head_width // 2
    frequency = jnp.power(
        jnp.float32(ROPE_BASE), -jnp.arange(half_width, dtype=jnp.float32) * 2.0 / head_width
    )
    angles = jnp.arange(row_count, dtype=jnp.float32)[:, None] * frequency[None, :]
    cosine, sine = jnp.cos(angles), jnp.sin(angles)
    repeats = LANES // head_width
    return jnp.tile(cosine, (1, 2 * repeats)), jnp.tile(
        jnp.concatenate([-sine, sine], axis=1), (1, repeats)
    )


def nn(left, right):
    return jnp.dot(left, right, preferred_element_type=F32)


def nt(left, right):
    return lax.dot_general(left, right, (((1,), (1,)), ((), ())), preferred_element_type=F32)


def tn(left, right):
    return lax.dot_general(left, right, (((0,), (0,)), ((), ())), preferred_element_type=F32)


def two_parts(column):
    high = column.astype(LOW)
    return high, (column - high.astype(F32)).astype(LOW)


def attend_kernel(block, width, lens_ref, q_ref, k_ref, v_ref, att_ref, qx_ref):
    rows = q_ref.shape[0]
    heads = q_ref.shape[1] // LANES
    length = lens_ref[pl.program_id(0)]
    lane = lax.broadcasted_iota(jnp.int32, (block, LANES), 1)
    keep = lax.broadcasted_iota(jnp.int32, (block, block), 1) <= lax.broadcasted_iota(
        jnp.int32, (block, block), 0
    )
    for step in range(rows // block):
        start = step * block
        here = pl.ds(start, block)

        @pl.when(start < length)
        def _():
            outs = []
            for head in range(heads):
                lanes = pl.ds(head * LANES, LANES)
                query = q_ref[here, lanes]
                probs = jnp.exp(nt(query, k_ref[here, :]))
                probs = jnp.where(keep, probs, 0.0).astype(LOW)
                total = nn(probs, v_ref[here, :])
                if step:
                    probs = jnp.exp(nt(query, k_ref[pl.ds(0, start), :])).astype(LOW)
                    total += nn(probs, v_ref[pl.ds(0, start), :])
                weight = total[:, width : width + 1]
                outs.append(total / weight)
                high, rest = two_parts(-jnp.log(weight))
                qx_ref[here, lanes] = jnp.where(
                    lane == width, high, jnp.where(lane == width + 1, rest, query)
                )
            for pair in range(heads // 2):
                att_ref[here, pl.ds(pair * LANES, LANES)] = jnp.where(
                    lane < width, outs[2 * pair], pltpu.roll(outs[2 * pair + 1], width, 1)
                ).astype(LOW)

        @pl.when(start >= length)
        def _():
            att_ref[here, :] = jnp.zeros((block, att_ref.shape[1]), LOW)
            qx_ref[here, :] = jnp.zeros((block, qx_ref.shape[1]), LOW)


def attend_back_kernel(block, width, lens_ref, q_ref, k_ref, v_ref, do_ref, dq_ref, dk_ref, dv_ref):
    rows = q_ref.shape[0]
    heads = q_ref.shape[1] // LANES
    length = lens_ref[pl.program_id(0)]
    lane = lax.broadcasted_iota(jnp.int32, (block, LANES), 1)
    keep = lax.broadcasted_iota(jnp.int32, (block, block), 0) <= lax.broadcasted_iota(
        jnp.int32, (block, block), 1
    )
    dk_ref[...] = jnp.zeros(dk_ref.shape, F32)
    dv_ref[...] = jnp.zeros(dv_ref.shape, F32)
    for step in range(rows // block):
        start = step * block
        here = pl.ds(start, block)

        @pl.when(start < length)
        def _():
            parts = []
            for head in range(heads):
                lanes = pl.ds(head * LANES, LANES)
                query = q_ref[here, lanes]
                dout = do_ref[here, lanes]

                def one(keys, masked):
                    key, value = k_ref[keys, :], v_ref[keys, :]
                    probs = jnp.exp(nt(key, query))
                    if masked:
                        probs = jnp.where(keep, probs, 0.0)
                    dscores = (probs * nt(value, dout)).astype(LOW)
                    dv_ref[keys, :] += nn(probs.astype(LOW), dout)
                    dk_ref[keys, :] += nn(dscores, query)
                    return tn(dscores, key)

                dquery = one(here, True)
                if step:
                    dquery += one(pl.ds(0, start), False)
                parts.append(dquery)
            for pair in range(heads // 2):
                dq_ref[here, pl.ds(pair * LANES, LANES)] = jnp.where(
                    lane < width, parts[2 * pair], pltpu.roll(parts[2 * pair + 1], width, 1)
                )

        @pl.when(start >= length)
        def _():
            dq_ref[here, :] = jnp.zeros((block, dq_ref.shape[1]), F32)


def attention_grid(slots, groups, per_group, rows):
    wide = pl.BlockSpec((rows, per_group * LANES), lambda s, g, lens: (s, g))
    dense = pl.BlockSpec((rows, per_group * LANES // 2), lambda s, g, lens: (s, g))
    narrow = pl.BlockSpec((rows, LANES), lambda s, g, lens: (s, g))
    return (slots, groups), wide, dense, narrow


def attend(lens, queries, keys, values, rows, width, block):
    slots, groups = queries.shape[0] // rows, keys.shape[1] // LANES
    per_group = queries.shape[1] // LANES // groups
    grid, wide, dense, narrow = attention_grid(slots, groups, per_group, rows)
    flops = 4 * slots * groups * per_group * rows * rows * LANES
    return pl.pallas_call(
        partial(attend_kernel, block, width),
        out_shape=(
            jax.ShapeDtypeStruct((queries.shape[0], queries.shape[1] // 2), LOW),
            jax.ShapeDtypeStruct(queries.shape, LOW),
        ),
        grid_spec=pltpu.PrefetchScalarGridSpec(
            num_scalar_prefetch=1,
            grid=grid,
            in_specs=[wide, narrow, narrow],
            out_specs=[dense, wide],
        ),
        cost_estimate=pl.CostEstimate(flops=flops, bytes_accessed=1 << 23, transcendentals=0),
        name="attend",
    )(lens, queries, keys, values)


def attend_back(lens, queries, keys, values, douts, rows, width, block):
    slots, groups = queries.shape[0] // rows, keys.shape[1] // LANES
    per_group = queries.shape[1] // LANES // groups
    grid, wide, dense, narrow = attention_grid(slots, groups, per_group, rows)
    flops = 10 * slots * groups * per_group * rows * rows * LANES
    return pl.pallas_call(
        partial(attend_back_kernel, block, width),
        out_shape=(
            jax.ShapeDtypeStruct((queries.shape[0], queries.shape[1] // 2), F32),
            jax.ShapeDtypeStruct(keys.shape, F32),
            jax.ShapeDtypeStruct(keys.shape, F32),
        ),
        grid_spec=pltpu.PrefetchScalarGridSpec(
            num_scalar_prefetch=1,
            grid=grid,
            in_specs=[wide, narrow, narrow, wide],
            out_specs=[dense, narrow, narrow],
        ),
        cost_estimate=pl.CostEstimate(flops=flops, bytes_accessed=1 << 24, transcendentals=0),
        name="attend_back",
    )(lens, queries, keys, values, douts)


def swap_halves(values, width):
    lane = lax.broadcasted_iota(jnp.int32, values.shape, 1)
    half = width // 2
    return jnp.where(
        lane % width < half, pltpu.roll(values, LANES - half, 1), pltpu.roll(values, half, 1)
    )


def head_sum(values, width):
    same = lax.broadcasted_iota(jnp.int32, (LANES, LANES), 0) // width
    same = (same == lax.broadcasted_iota(jnp.int32, (LANES, LANES), 1) // width).astype(LOW)
    high, rest = two_parts(values)
    return nn(high, same) + nn(rest, same)


def row_rsqrt(values):
    return lax.rsqrt(jnp.mean(values * values, axis=1, keepdims=True) + EPS)


def is_live(lens_ref, step, per_slot, block):
    return lax.rem(step, per_slot) * block < lens_ref[lax.div(step, per_slot)]


def qkv_kernel(
    per_slot, counts, width, scale, lens_ref, own_ref, other_ref, w_ref, ga_ref, gh_ref, cos_ref, sin_ref,
    normed_ref, raw_ref, q_ref, k_ref, v_ref,
):
    step = pl.program_id(0)
    block = own_ref.shape[0]
    q_tiles, kv_tiles = counts

    @pl.when(is_live(lens_ref, step, per_slot, block))
    def _():
        x = jnp.where(step < per_slot, own_ref[...], other_ref[...]).astype(F32)
        normed = (x * row_rsqrt(x) * ga_ref[...]).astype(LOW)
        normed_ref[...] = normed
        lane = lax.broadcasted_iota(jnp.int32, (block, LANES), 1)
        zero = jnp.zeros((block, LANES), F32)
        ones = jnp.where(lane < width + 2, 1.0, 0.0)
        cosine, sine = cos_ref[...], sin_ref[...]

        def put(ref, tile, values, rest):
            ref[:, pl.ds(2 * tile * LANES, LANES)] = jnp.where(lane < width, values, rest).astype(LOW)
            ref[:, pl.ds((2 * tile + 1) * LANES, LANES)] = jnp.where(
                lane < width, pltpu.roll(values, width, 1), rest
            ).astype(LOW)

        for tile in range(q_tiles + 2 * kv_tiles):
            lanes = pl.ds(tile * LANES, LANES)
            values = nn(normed, w_ref[:, lanes])
            if tile >= q_tiles + kv_tiles:
                put(v_ref, tile - q_tiles - kv_tiles, values, ones)
                continue
            raw_ref[:, lanes] = values
            is_query = tile < q_tiles
            gain = gh_ref[0:1, :] if is_query else gh_ref[1:2, :]
            values *= lax.rsqrt(head_sum(values * values, width) * (1.0 / width) + EPS) * gain
            values = values * cosine + swap_halves(values, width) * sine
            if is_query:
                put(q_ref, tile, values * scale, zero)
            else:
                put(k_ref, tile - q_tiles, values, ones)


def out_kernel(per_slot, lens_ref, att_ref, w_ref, own_ref, other_ref):
    step = pl.program_id(0)
    block = att_ref.shape[0]

    @pl.when(step < per_slot)
    def _():
        other_ref[...] = nn(att_ref[...], w_ref[...]).astype(LOW)

    @pl.when(step >= per_slot)
    def _():
        own_ref[...] = nn(att_ref[...], w_ref[...])


def resid_kernel(lens_ref, x_ref, part_ref, got_ref, gain_ref, resid_ref, normed_ref, sums_ref):
    step = pl.program_id(0)
    block = x_ref.shape[0]
    valid = lax.broadcasted_iota(jnp.int32, (block, 1), 0) + step * block < lens_ref[0]
    attn_out = part_ref[...] + got_ref[...].astype(F32)
    resid = x_ref[...].astype(F32) + attn_out
    resid_ref[...] = resid
    normed_ref[...] = (resid * row_rsqrt(resid) * gain_ref[...]).astype(LOW)

    @pl.when(step == 0)
    def _():
        sums_ref[...] = jnp.zeros(sums_ref.shape, F32)

    for row, values in ((0, resid), (1, attn_out)):
        sums_ref[row : row + 1, :] += jnp.sum(
            jnp.where(valid, values * values, 0.0), axis=0, keepdims=True
        )


def ffn_kernel(
    per_slot, chained, last, lens_ref, x_own, x_other, g_own, g_other, w_ref, wd_ref, *refs
):
    if chained:
        mlp_in, db_in, *refs = refs
    if last:
        mlp_own, db_own, mlp_other, db_other, grad_ref, gradd_ref, acc_ref, accd_ref = refs
    else:
        mlp_own, db_own, grad_ref, gradd_ref, acc_ref, accd_ref = refs
    step = pl.program_id(0)
    own = step < per_slot
    units = wd_ref.shape[0]
    block = x_own.shape[0]

    @pl.when(step == 0)
    def _():
        acc_ref[...] = jnp.zeros(acc_ref.shape, F32)
        accd_ref[...] = jnp.zeros(accd_ref.shape, F32)

    live = is_live(lens_ref, step, per_slot, block)

    def put(mlp, d_b):
        if not last:
            mlp_own[...] = mlp
            db_own[...] = d_b
            return

        @pl.when(own)
        def _():
            mlp_own[...] = mlp
            db_own[...] = d_b

        @pl.when(jnp.logical_not(own))
        def _():
            mlp_other[...] = mlp.astype(LOW)
            db_other[...] = d_b.astype(LOW)

    @pl.when(live)
    def _():
        x = jnp.where(own, x_own[...], x_other[...])
        g = jnp.where(own, g_own[...], g_other[...])
        gate = nn(x, w_ref[:, :units])
        up = nn(x, w_ref[:, units:])
        d_hidden = nt(g, wd_ref[...])
        sig = jax.nn.sigmoid(gate)
        silu = gate * sig
        hidden = (silu * up).astype(LOW)
        d_gate = (d_hidden * up * (sig * (1.0 + gate * (1.0 - sig)))).astype(LOW)
        d_up = (d_hidden * silu).astype(LOW)
        mlp = nn(hidden, wd_ref[...])
        d_b = nt(d_gate, w_ref[:, :units]) + nt(d_up, w_ref[:, units:])
        if chained:
            mlp += mlp_in[...]
            d_b += db_in[...]
        put(mlp, d_b)
        acc_ref[:, :units] += tn(x, d_gate)
        acc_ref[:, units:] += tn(x, d_up)
        accd_ref[...] += tn(hidden, g)

    @pl.when(jnp.logical_not(live))
    def _():
        zero = jnp.zeros(mlp_own.shape, F32)
        put(zero, zero)

    @pl.when(step == pl.num_programs(0) - 1)
    def _():
        grad_ref[...] = acc_ref[...].astype(LOW)
        gradd_ref[...] = accd_ref[...].astype(LOW)


def norm_back(values, dy, gain):
    inverse = row_rsqrt(values)
    scaled = dy * gain
    inner = jnp.mean(values * scaled, axis=1, keepdims=True)
    return inverse * scaled - values * (inverse * inverse * inverse * inner), dy * values * inverse


def resid_back_kernel(
    lens_ref, resid_ref, mlp_ref, mlp_got, db_ref, db_got, g_ref, gain_ref,
    out_ref, dresid_ref, dattn_ref, sums_ref,
):
    step = pl.program_id(0)
    block = resid_ref.shape[0]
    valid = lax.broadcasted_iota(jnp.int32, (block, 1), 0) + step * block < lens_ref[0]
    resid = resid_ref[...]
    mlp_out = mlp_ref[...] + mlp_got[...].astype(F32)
    out_ref[...] = jnp.where(valid, resid + mlp_out, 0.0).astype(LOW)
    d_norm, d_gain = norm_back(resid, db_ref[...] + db_got[...].astype(F32), gain_ref[...])
    d_resid = jnp.where(valid, g_ref[...].astype(F32) + d_norm, 0.0)
    dresid_ref[...] = d_resid
    dattn_ref[...] = d_resid.astype(LOW)

    @pl.when(step == 0)
    def _():
        sums_ref[...] = jnp.zeros(sums_ref.shape, F32)

    for row, values in ((0, mlp_out * mlp_out), (1, d_gain)):
        sums_ref[row : row + 1, :] += jnp.sum(
            jnp.where(valid, values, 0.0), axis=0, keepdims=True
        )


def dout_kernel(
    per_slot, width, lens_ref, own_ref, other_ref, att_ref, w_ref, do_ref, grad_ref, acc_ref
):
    step = pl.program_id(0)
    block = own_ref.shape[0]

    @pl.when(step == 0)
    def _():
        acc_ref[...] = jnp.zeros(acc_ref.shape, F32)

    @pl.when(is_live(lens_ref, step, per_slot, block))
    def _():
        d_attn = jnp.where(step < per_slot, own_ref[...], other_ref[...])
        lane = lax.broadcasted_iota(jnp.int32, (block, LANES), 1)
        att = att_ref[...]
        acc_ref[...] += tn(att, d_attn)
        for tile in range(att.shape[1] // LANES):
            lanes = slice(tile * LANES, (tile + 1) * LANES)
            dout = nt(d_attn, w_ref[lanes, :]).astype(LOW).astype(F32)
            delta = -head_sum(dout * att[:, lanes].astype(F32), width)
            for head, (values, column) in enumerate(
                ((dout, pltpu.roll(delta, width, 1)), (pltpu.roll(dout, width, 1), delta))
            ):
                high, rest = two_parts(column)
                column = jnp.where(
                    lane == width, high, jnp.where(lane == width + 1, rest, jnp.zeros_like(rest))
                )
                do_ref[:, pl.ds((2 * tile + head) * LANES, LANES)] = jnp.where(
                    lane < width, values.astype(LOW), column
                )

    @pl.when(step == pl.num_programs(0) - 1)
    def _():
        grad_ref[...] = acc_ref[...].astype(LOW)


def qkv_back_kernel(
    per_slot, counts, width, scale, lens_ref, dq_ref, dk_ref, dv_ref, raw_ref, normed_ref, w_ref, gh_ref,
    cos_ref, sin_ref, own_ref, other_ref, grad_ref, gain_ref, acc_ref, low_ref,
):
    step = pl.program_id(0)
    block = dq_ref.shape[0]
    q_tiles, kv_tiles = counts
    slot_step = lax.rem(step + per_slot, 2 * per_slot)

    @pl.when(step == 0)
    def _():
        acc_ref[...] = jnp.zeros(acc_ref.shape, F32)
        gain_ref[...] = jnp.zeros(gain_ref.shape, F32)

    live = is_live(lens_ref, slot_step, per_slot, block)

    def put(d_a):
        @pl.when(step < per_slot)
        def _():
            other_ref[...] = d_a.astype(LOW)

        @pl.when(step >= per_slot)
        def _():
            own_ref[...] = d_a

    @pl.when(live)
    def _():
        lane = lax.broadcasted_iota(jnp.int32, (block, LANES), 1)
        cosine, sine = cos_ref[...], sin_ref[...]

        def pair(ref, tile):
            return jnp.where(
                lane < width,
                ref[:, pl.ds(2 * tile * LANES, LANES)],
                pltpu.roll(ref[:, pl.ds((2 * tile + 1) * LANES, LANES)], width, 1),
            )

        for tile in range(q_tiles + 2 * kv_tiles):
            lanes = pl.ds(tile * LANES, LANES)
            if tile >= q_tiles + kv_tiles:
                low_ref[:, lanes] = pair(dv_ref, tile - q_tiles - kv_tiles).astype(LOW)
                continue
            is_query = tile < q_tiles
            if is_query:
                turned, row = dq_ref[:, lanes] * scale, 0
            else:
                turned, row = pair(dk_ref, tile - q_tiles), 1
            gain = gh_ref[row : row + 1, :]
            dy = turned * cosine + swap_halves(turned * sine, width)
            values = raw_ref[:, lanes]
            inverse = lax.rsqrt(head_sum(values * values, width) * (1.0 / width) + EPS)
            scaled = dy * gain
            inner = head_sum(values * scaled, width) * (1.0 / width)
            low_ref[:, lanes] = (
                inverse * scaled - values * (inverse * inverse * inverse * inner)
            ).astype(LOW)
            gain_ref[row : row + 1, :] += jnp.sum(dy * values * inverse, axis=0, keepdims=True)
        low = low_ref[...]
        acc_ref[...] += tn(normed_ref[...], low)
        put(nt(low, w_ref[...]))

    @pl.when(jnp.logical_not(live))
    def _():
        put(jnp.zeros(own_ref.shape, F32))

    @pl.when(step == pl.num_programs(0) - 1)
    def _():
        grad_ref[...] = acc_ref[...].astype(LOW)


def input_back_kernel(lens_ref, x_ref, part_ref, got_ref, dresid_ref, gain_ref, out_ref, sums_ref):
    step = pl.program_id(0)
    d_norm, d_gain = norm_back(
        x_ref[...].astype(F32), part_ref[...] + got_ref[...].astype(F32), gain_ref[...]
    )
    out_ref[...] = (dresid_ref[...] + d_norm).astype(LOW)

    @pl.when(step == 0)
    def _():
        sums_ref[...] = jnp.zeros(sums_ref.shape, F32)

    sums_ref[0:1, :] += jnp.sum(d_gain, axis=0, keepdims=True)


class Rows:
    def __init__(self, lens, rows, block):
        self.lens, self.block, self.per_slot = lens, block, rows // block

    def both(self, width):
        return pl.BlockSpec((self.block, width), lambda i, lens: (i, 0))

    def both_other_first(self, width):
        n = self.per_slot
        return pl.BlockSpec((self.block, width), lambda i, lens: (lax.rem(i + n, 2 * n), 0))

    def early(self, width):
        n = self.per_slot
        return pl.BlockSpec((self.block, width), lambda i, lens: (jnp.minimum(i, n - 1), 0))

    def late(self, width):
        n = self.per_slot
        return pl.BlockSpec((self.block, width), lambda i, lens: (jnp.maximum(i - n, 0), 0))

    def repeated(self, width):
        n = self.per_slot
        return pl.BlockSpec((self.block, width), lambda i, lens: (lax.rem(i, n), 0))

    def fixed(self, shape):
        return pl.BlockSpec(shape, lambda i, lens: (0, 0), pipeline_mode=pl.Buffered(1))

    def call(self, name, kernel, slots, in_specs, out_specs, outs, scratch, flops, *args):
        return pl.pallas_call(
            kernel,
            out_shape=[jax.ShapeDtypeStruct(shape, kind) for shape, kind in outs],
            grid_spec=pltpu.PrefetchScalarGridSpec(
                num_scalar_prefetch=1,
                grid=(slots * self.per_slot,),
                in_specs=in_specs,
                out_specs=out_specs,
                scratch_shapes=scratch,
            ),
            cost_estimate=pl.CostEstimate(
                flops=flops, bytes_accessed=1 << 24, transcendentals=0
            ),
            compiler_params=pltpu.CompilerParams(vmem_limit_bytes=60 << 20),
            name=name,
        )(self.lens, *args)


def core_swap(x):
    pairs = [(i, i ^ 1) for i in range(lax.axis_size("rep"))]
    return lax.ppermute(x, "rep", pairs)


def place():
    rep = lax.axis_index("rep")
    return lax.axis_index("shard"), lax.div(rep, 2), lax.rem(rep, 2)


def device(shard, group, core):
    return {"rep": 2 * group + core, "shard": shard}


def meet(devices):
    barrier = pltpu.get_barrier_semaphore()
    for where in devices:
        pl.semaphore_signal(barrier, inc=1, device_id=where, device_id_type=MESH)
    pl.semaphore_wait(barrier, len(devices))


def remote(source, target, send, recv, where):
    return pltpu.make_async_remote_copy(
        src_ref=source,
        dst_ref=target,
        send_sem=send,
        recv_sem=recv,
        device_id=where,
        device_id_type=MESH,
    )


def at_rows(ref, start, size):
    return ref.at[pl.ds(pl.multiple_of(start, 8), size), :]


def at(ref, row, rows, column, columns):
    return ref.at[
        pl.ds(pl.multiple_of(row, 8), rows), pl.ds(pl.multiple_of(column, LANES), columns)
    ]


class Copies:
    def __init__(self, send, recv):
        self.send, self.recv, self.used = send, recv, 0

    def __call__(self, source, target, where):
        slot = self.used
        self.used += 1
        return remote(source, target, self.send.at[slot], self.recv.at[slot], where)


def neighbours(me):
    return me + 1 - 2 * lax.rem(me, 2), me + 2 - 4 * lax.div(me, 2), 3 - me


def gather_kernel(shards, wide_parts, tall_parts, count, *refs):
    *refs, send, recv = refs
    sources, targets = refs[: count[0]], refs[count[0] :]
    me, group, core = place()
    half = shards // 2
    partner = device(me, group, 1 - core)
    meet(
        [device(lax.rem(me + k, shards), group, c) for k in range(1, shards) for c in range(2)]
        + [partner]
    )
    copies = Copies(send, recv)
    sent, due = [], []

    def go(source, target, where):
        copy = copies(source, target, where)
        copy.start()
        sent.append(copy.wait_send)
        return copy

    def passed_on(wide):
        fast, slow, _ = neighbours(me)
        later = []
        for block, first, second in wide:
            rows = block(me).shape[0] // 2
            first.wait_recv()
            later.append(go(block(fast).at[pl.ds(0, rows), :], block(fast).at[pl.ds(0, rows), :], device(slow, group, core)))
            second.wait_recv()
            later.append(go(block(slow).at[pl.ds(rows, rows), :], block(slow).at[pl.ds(rows, rows), :], device(fast, group, core)))
        return later

    wide = []
    for source, target, column, to, columns in wide_parts:
        source, target = sources[source], targets[target]
        rows = source.shape[0]
        mine = at(source, 0, rows, column(core), columns)

        def block(shard, target=target, rows=rows, to=to, columns=columns):
            return at(target, shard * rows, rows, to, columns)

        if shards == 4:
            fast, slow, _ = neighbours(me)
            wide.append(
                (
                    block,
                    go(mine, block(me), device(fast, group, core)),
                    go(mine, block(me), device(slow, group, core)),
                )
            )
        else:
            for k in range(1, shards):
                due.append(go(mine, block(me), device(lax.rem(me + k, shards), group, core)))
        due.append(go(at(source, 0, rows, column(1 - core), columns), block(me), partner))
    owner = lax.div(me, half)
    tall = []
    for source, target, row, rows in tall_parts:
        source, target = sources[source], targets[target]
        columns = source.shape[1] // 2

        def block(shard, target=target, rows=rows, columns=columns):
            return at(target, lax.rem(shard, half) * rows, rows, 0, 2 * columns)

        mine = at(source, row, rows, core * columns, columns)
        goal = at(target, lax.rem(me, half) * rows, rows, core * columns, columns)
        steps = [1, 2] if shards == 4 else list(range(1, shards))
        arrivals = []
        for k in steps:
            if shards == 4:
                to = origin = neighbours(me)[k - 1]
            else:
                to, origin = lax.rem(me + k, shards), lax.rem(me + shards - k, shards)
            pair = []
            for side in range(2):
                copy = copies(mine, goal, device(to, group, owner))
                pl.when(core == side)(copy.start)
                sent.append((core == side, copy.wait_send))
                pair.append(copy)
            arrivals.append((lax.div(origin, half) == core, pair))
        whole = copies(
            at(source, row, rows, 0, 2 * columns), block(me), partner
        )
        pl.when(owner != core)(whole.start)
        sent.append((owner != core, whole.wait_send))
        due.append((owner == core, whole))
        if shards == 4:
            tall.append((block, rows // 2, arrivals))
        else:
            for condition, pair in arrivals:
                due.extend((condition, copy) for copy in pair)
    gains, given = sources[-2:], targets[-2:]
    for k in range(1, shards):
        due.append(go(gains[0], given[0].at[me], device(lax.rem(me + k, shards), group, core)))
    due.append(go(gains[0], given[0].at[me], partner))
    due.append(go(gains[1], given[1], partner))
    if shards == 4:
        due.extend(passed_on(wide))
        fast, slow, _ = neighbours(me)
        for block, rows, arrivals in tall:
            for number, (condition, pair) in enumerate(arrivals):
                start = number * rows
                from_, to = (fast, slow) if number == 0 else (slow, fast)
                part = block(from_).at[pl.ds(start, rows), :]
                copy = copies(part, part, device(to, group, core))

                @pl.when(condition)
                def _(pair=pair, copy=copy):
                    for one in pair:
                        one.wait_recv()
                    copy.start()

                sent.append((condition, copy.wait_send))
                due.append((owner != core, copy))
    for item in sent:
        pl.when(item[0])(item[1]) if isinstance(item, tuple) else item()
    for item in due:
        pl.when(item[0])(item[1].wait_recv) if isinstance(item, tuple) else item.wait_recv()


def pack_kernel(shards, chunks, gate_ref, up_ref, down_ref, *refs):
    *packs, sems = refs
    core = lax.rem(lax.axis_index("rep"), 2)
    half = shards // 2
    total, rows = down_ref.shape[0], gate_ref.shape[0]
    piece = total // chunks
    columns = down_ref.shape[1] // 2
    copies = []
    for pack in packs:
        for row, chunk in pack[1]:
            for j, ref in enumerate((gate_ref, up_ref)):
                for i in range(half):
                    start = (core * half + i) * total + chunk * piece
                    copies.append(
                        (
                            at(ref, 0, rows, start, piece),
                            pack[0].at[pl.ds(row, rows), pl.ds((j * half + i) * piece, piece)],
                        )
                    )
            folds = 2 * half * piece // columns
            size = piece // folds
            for i in range(folds):
                copies.append(
                    (
                        at(down_ref, chunk * piece + i * size, size, core * columns, columns),
                        pack[0].at[pl.ds(row + rows, size), pl.ds(i * columns, columns)],
                    )
                )
    copies = [pltpu.make_async_copy(a, b, sems.at[k]) for k, (a, b) in enumerate(copies)]
    for copy in copies:
        copy.start()
    for copy in copies:
        copy.wait()


def add_up(parts, target, rows):
    def some(i, _):
        here = pl.ds(pl.multiple_of(i * rows, rows), rows)
        total = parts[0][here, :].astype(F32)
        for part in parts[1:]:
            total += part[here, :].astype(F32)
        target[here, :] = total.astype(target.dtype)
        return 0

    lax.fori_loop(0, target.shape[0] // rows, some, 0)


def reduce_over_plane(copies, load, shards, grad_ref, level, bufs):
    me, group, core = place()
    rows = level.shape[0]

    def block(shard, start=0, size=rows):
        return at_rows(grad_ref, shard * rows + start, size)

    own = bufs[0]
    local = pltpu.make_async_copy(block(me), own, load.at[0])
    if shards != 4:
        planes = bufs[1]
        out = [
            copies(block(lax.rem(me + k, shards)), planes.at[k - 1], device(lax.rem(me + k, shards), group, core))
            for k in range(1, shards)
        ]

        def start():
            local.start()
            for copy in out:
                copy.start()

        def end():
            local.wait()
            for copy in out:
                copy.wait_send()
                copy.wait_recv()
            add_up([own] + [planes.at[k] for k in range(shards - 1)], level, 16)

        return [start, end]
    fast, slow, across = neighbours(me)
    to_fast, to_slow = device(fast, group, core), device(slow, group, core)
    half = rows // 2
    planes, met_fast, met_slow, held_fast, held_slow = bufs[1:]
    upper, lower = pl.ds(0, half), pl.ds(half, half)
    loads = [
        local,
        pltpu.make_async_copy(block(fast, half, half), held_fast, load.at[1]),
        pltpu.make_async_copy(block(slow, 0, half), held_slow, load.at[2]),
    ]
    early = [
        copies(block(across, 0, half), met_fast, to_fast),
        copies(block(across, half, half), met_slow, to_slow),
        copies(block(fast, 0, half), planes.at[0, upper, :], to_fast),
        copies(block(slow, half, half), planes.at[1, lower, :], to_slow),
    ]
    late = [
        copies(held_fast, planes.at[0, lower, :], to_fast),
        copies(held_slow, planes.at[1, upper, :], to_slow),
    ]

    def start():
        for copy in early + loads:
            copy.start()

    def merge():
        for copy in loads:
            copy.wait()
        for copy, met, held, out in (
            (early[1], met_slow, held_fast, late[0]),
            (early[0], met_fast, held_slow, late[1]),
        ):
            copy.wait_recv()
            add_up([held, met], held, 16)
            out.start()

    def end():
        for copy in early[2:] + late:
            copy.wait_recv()
        for copy in early + late:
            copy.wait_send()
        add_up([own, planes.at[0], planes.at[1]], level, 16)

    return [start, merge, end]


def plane_buffers(shards, shape):
    half = (shape[0] // 2, shape[1])
    if shards != 4:
        return [pltpu.VMEM(shape, LOW), pltpu.VMEM((shards - 1,) + shape, LOW)]
    return [pltpu.VMEM(shape, LOW), pltpu.VMEM((2,) + shape, LOW)] + [pltpu.VMEM(half, LOW)] * 4


def reduce_over_line(copies, groups, part, total, bufs):
    me, group, core = place()
    if groups != 4:
        (slots,) = bufs
        out = [
            copies(part, slots.at[group], device(me, lax.rem(group + k, groups), core))
            for k in range(1, groups)
        ]

        def start():
            for copy in out:
                copy.start()

        def end():
            rows = part.shape[0]

            def some(i, _):
                here = pl.ds(pl.multiple_of(i * 8, 8), 8)
                slots[group, here, :] = part[here, :]
                return 0

            lax.fori_loop(0, rows // 8, some, 0)
            for copy in out:
                copy.wait_send()
                copy.wait_recv()
            add_up([slots.at[k] for k in range(groups)], total, 8)

        return [start, end]
    met, summed, other = bufs
    outer = jnp.logical_or(group == 0, group == groups - 1)
    inner = jnp.logical_not(outer)
    mate = device(me, group + 1 - 2 * lax.rem(group, 2), core)
    inward = copies(part, met, mate)
    between = copies(summed, other, device(me, groups - 1 - group, core))
    back = copies(total, total, mate)

    def start():
        pl.when(outer)(inward.start)

    def exchange():
        @pl.when(inner)
        def _():
            inward.wait_recv()
            add_up([part, met], summed, 16)
            between.start()

    def give():
        @pl.when(inner)
        def _():
            between.wait_recv()
            add_up([summed, other], total, 16)
            back.start()

    def end():
        @pl.when(outer)
        def _():
            inward.wait_send()
            back.wait_recv()

        @pl.when(inner)
        def _():
            between.wait_send()
            back.wait_send()

    return [start, exchange, give, end]


def line_buffers(groups, shape):
    if groups != 4:
        return [pltpu.VMEM((groups,) + shape, LOW)]
    return [pltpu.VMEM(shape, LOW)] * 3


def take(refs, count):
    return refs[:count], refs[count:]


def finish_kernel(shards, groups, counts, small_ref, *refs):
    grads, refs = take(refs, counts[0])
    pieces, refs = take(refs, counts[1])
    n = counts[0] + counts[1]
    mine, refs = take(refs, n)
    other, refs = take(refs, n)
    (total_ref,), refs = take(refs, 1)
    own, refs = take(refs, counts[1])
    levels, refs = take(refs, counts[0])
    per_plane, per_line = len(plane_buffers(shards, (16, LANES))), len(line_buffers(groups, (16, LANES)))
    plane_bufs, line_bufs = [], []
    for _ in range(counts[0]):
        some, refs = take(refs, per_plane)
        plane_bufs.append(some)
    for _ in range(n):
        some, refs = take(refs, per_line)
        line_bufs.append(some)
    small_a, small_b, small_c, send, recv, load = refs
    me, group, core = place()
    partner = device(me, group, 1 - core)
    plane = [device(lax.rem(me + k, shards), group, core) for k in range(1, shards)]
    line = [device(me, lax.rem(group + k, groups), core) for k in range(1, groups)]
    copies = Copies(send, recv)

    def go(source, target, where):
        copy = copies(source, target, where)
        copy.start()
        return copy

    def finish(some):
        for copy in some:
            copy.wait_send()
            copy.wait_recv()

    loads = [
        pltpu.make_async_copy(piece, own[i], load.at[3 * counts[0] + i])
        for i, piece in enumerate(pieces)
    ]
    for copy in loads:
        copy.start()
    small_a[me] = small_ref[...]
    meet(plane + line + [partner])
    small_copies = [go(small_ref, small_a.at[me], where) for where in plane]
    planes = [
        reduce_over_plane(
            copies, load.at[pl.ds(3 * i, 3)], shards, grad, levels[i], plane_bufs[i]
        )
        for i, grad in enumerate(grads)
    ]
    lines = [
        reduce_over_line(copies, groups, part, mine[i], line_bufs[i])
        for i, part in enumerate(list(levels) + list(own))
    ]
    swaps = [copies(mine[i], other[i], partner) for i in range(n)]

    def swap(i):
        swaps[i].start()

    for stages in planes:
        stages[0]()
    for copy in loads:
        copy.wait()
    ready = list(range(counts[0], n))
    for i in ready:
        lines[i][0]()
    finish(small_copies)
    small_b[group] = sum(small_a[k] for k in range(shards))
    small_copies = [go(small_b.at[group], small_b.at[group], where) for where in line]
    work = []
    for i in ready:
        work.append([(lines[i][k], i) for k in range(1, len(lines[i]))])
    for i in range(counts[0]):
        for stage in planes[i][1:-1]:
            stage()
    for some in work:
        some.pop(0)[0]()
    for i in range(counts[0]):
        planes[i][-1]()
        lines[i][0]()
        for some in work:
            if len(some) > 1:
                some.pop(0)[0]()
    work += [[(lines[i][k], i) for k in range(1, len(lines[i]))] for i in range(counts[0])]
    finish(small_copies)
    small_c[core] = sum(small_b[k] for k in range(groups))
    small_copies = [go(small_c.at[core], small_c.at[core], partner)]
    while any(work):
        for some in work:
            if some:
                stage, i = some.pop(0)
                stage()
                if not some:
                    swap(i)
    finish(small_copies)
    total_ref[...] = small_c[0] + small_c[1]
    finish(swaps)


def finish_sums(grads, small, pieces, shards, groups):
    n = len(pieces) + len(grads)
    levels = [(grad.shape[0] // shards, grad.shape[1]) for grad in grads]
    shapes = levels + [piece.shape for piece in pieces]
    vmem = pl.BlockSpec(memory_space=pltpu.VMEM)
    hbm = pl.BlockSpec(memory_space=pl.ANY)
    scratch = [pltpu.VMEM(shape, LOW) for shape in shapes[len(grads) :] + levels]
    for shape in levels:
        scratch += plane_buffers(shards, shape)
    for shape in shapes:
        scratch += line_buffers(groups, shape)
    count = len(grads) * max(6, shards - 1) + n * max(3, groups - 1) + n + shards + groups
    outs = pl.pallas_call(
        partial(finish_kernel, shards, groups, (len(grads), len(pieces))),
        out_shape=[jax.ShapeDtypeStruct(shape, LOW) for shape in shapes * 2]
        + [jax.ShapeDtypeStruct(small.shape, F32)],
        in_specs=[vmem] + [hbm] * n,
        out_specs=[vmem] * (2 * n + 1),
        scratch_shapes=scratch
        + [pltpu.VMEM((shards,) + small.shape, F32), pltpu.VMEM((groups,) + small.shape, F32)]
        + [pltpu.VMEM((2,) + small.shape, F32)]
        + [pltpu.SemaphoreType.DMA((count,)), pltpu.SemaphoreType.DMA((count,))]
        + [pltpu.SemaphoreType.DMA((3 * len(grads) + len(pieces),))],
        compiler_params=pltpu.CompilerParams(
            collective_id=1, has_side_effects=True, vmem_limit_bytes=62 << 20
        ),
        name="finish",
    )(small, *grads, *pieces)
    return outs[:n], outs[n : 2 * n], outs[2 * n]


def local(
    inputs,
    lengths,
    gain_attn,
    w_query,
    w_key,
    w_value,
    gain_query,
    gain_key,
    w_out,
    gain_mlp,
    w_gate,
    w_up,
    w_down,
    cotangent,
):
    shards = lax.axis_size("shard")
    core = lax.axis_index("rep") % 2
    first = core == 0
    rows, width_all = inputs.shape[1], inputs.shape[2]
    head_width = gain_query.shape[0] * shards
    q_half, kv_half = w_query.shape[1] // 2, w_key.shape[1] // 2
    d_half = width_all // 2
    d_rows, ff_rows = w_query.shape[0], w_down.shape[0]
    block = min(256, rows)
    scale = 1.0 / math.sqrt(head_width)
    counts = (q_half // LANES, kv_half // LANES)

    def ordered(mine, other, axis):
        return jnp.where(
            first,
            jnp.concatenate([mine, other], axis=axis),
            jnp.concatenate([other, mine], axis=axis),
        )

    half_shards = shards // 2
    groups = lax.axis_size("rep") // 2
    chunks = 3
    piece = ff_rows // chunks
    units = half_shards * piece
    folds = 2 * units // d_half
    head_rows = gain_query.shape[0]

    def fold(part):
        return jnp.concatenate(jnp.split(part, folds, axis=-2), axis=-1)

    def unfold(part):
        return jnp.concatenate(jnp.split(part, folds, axis=-1), axis=-2)

    packed_rows = d_rows + piece // folds
    hbm = pl.BlockSpec(memory_space=pl.ANY)
    vmem = pl.BlockSpec(memory_space=pltpu.VMEM)
    chunk_sets = [list(range(chunks - 1)), [chunks - 1]]

    def pack(*refs):
        *refs, pack_a, pack_b, sems = refs
        packs = [
            (ref, [(i * packed_rows, chunk) for i, chunk in enumerate(some)])
            for ref, some in zip((pack_a, pack_b), chunk_sets)
        ]
        pack_kernel(shards, chunks, *refs, *packs, sems)

    if piece % LANES == 0:
        packs = pl.pallas_call(
            pack,
            out_shape=[
                jax.ShapeDtypeStruct((len(some) * packed_rows, 2 * units), LOW) for some in chunk_sets
            ],
            in_specs=[hbm] * 3,
            out_specs=[vmem] * 2,
            scratch_shapes=[pltpu.SemaphoreType.DMA((chunks * (2 * half_shards + folds),))],
            compiler_params=pltpu.CompilerParams(vmem_limit_bytes=32 << 20),
            name="pack",
        )(w_gate, w_up, w_down)
    else:

        def my_half(weight):
            half = weight.shape[1] // 2
            return jnp.where(first, weight[:, :half], weight[:, half:])

        def chunk_of(weight, chunk):
            columns = weight.reshape(d_rows, shards, chunks, piece)[:, :, chunk]
            return my_half(columns.reshape(d_rows, shards * piece))

        def packed_chunk(chunk):
            tall = fold(my_half(w_down)[chunk * piece : (chunk + 1) * piece])
            wide = jnp.concatenate([chunk_of(w_gate, chunk), chunk_of(w_up, chunk)], axis=1)
            return jnp.concatenate([wide, tall])

        packs = [jnp.concatenate([packed_chunk(k) for k in some]) for some in chunk_sets]
    gathered = [lax.all_gather(part, "shard", axis=0) for part in packs]

    def gain_row(*gains):
        flat = jnp.concatenate(gains)
        return jnp.pad(flat, (0, max(d_rows, LANES) - flat.shape[0]))[None]

    gain_rows = jnp.pad(
        jnp.concatenate(
            [gain_row(gain_attn), gain_row(gain_mlp), gain_row(gain_query, gain_key)]
        ),
        ((0, 13), (0, 0)),
    )

    def half_of(width):
        return lambda core: core * width

    wide_parts = [
        (0, 0, half_of(q_half), 0, q_half),
        (1, 0, half_of(kv_half), q_half, kv_half),
        (2, 0, half_of(kv_half), q_half + kv_half, kv_half),
    ]
    tall_parts = [(3, 1, 0, w_out.shape[0])]
    copies = len(wide_parts) * (shards + 2) + len(tall_parts) * (2 * shards + 3) + shards + 1
    w_qkv, w_o, gains, x_other = pl.pallas_call(
        partial(gather_kernel, shards, wide_parts, tall_parts, (6, copies)),
        out_shape=[
            jax.ShapeDtypeStruct(shape, LOW)
            for shape in (
                (width_all, q_half + 2 * kv_half),
                (half_shards * w_out.shape[0], width_all),
                (shards,) + gain_rows.shape,
                inputs.shape[1:],
            )
        ],
        in_specs=[hbm] * 6,
        out_specs=[hbm] * 4,
        scratch_shapes=[pltpu.SemaphoreType.DMA((copies,)), pltpu.SemaphoreType.DMA((copies,))],
        compiler_params=pltpu.CompilerParams(collective_id=0, has_side_effects=True),
        name="gather",
    )(w_query, w_key, w_value, w_out, gain_rows, inputs[0])
    gain_a = gains[:, 0, :d_rows].reshape(1, -1).astype(F32)
    gain_m = gains[:, 1, :d_rows].reshape(1, -1).astype(F32)
    gain_q = gains[:, 2, :head_rows].reshape(1, -1).astype(F32)
    gain_k = gains[:, 2, head_rows : 2 * head_rows].reshape(1, -1).astype(F32)
    gain_h = jnp.tile(jnp.concatenate([gain_q, gain_k]), (4, LANES // head_width))

    def my_shards(columns):
        other = core_swap(
            lax.dynamic_slice_in_dim(columns, (1 - core) * half_shards, half_shards)
        )
        mine = lax.dynamic_slice_in_dim(columns, core * half_shards, half_shards)
        return ordered(mine, other, 2).reshape(-1, width_all)

    w_chunks = []
    for chunk in range(chunks):
        if chunk == chunks - 1:
            packed = gathered[1]
        else:
            packed = gathered[0][:, chunk * packed_rows : (chunk + 1) * packed_rows]
        w_chunks.append(
            (
                packed[:, :d_rows].reshape(width_all, 2 * units),
                my_shards(unfold(packed[:, d_rows:])),
            )
        )

    lens = jnp.concatenate([lengths, core_swap(lengths)])
    valid = (jnp.arange(rows) < lengths[0])[:, None]
    x_own = inputs[0]
    g_own = jnp.where(valid, cotangent[0], jnp.zeros((), LOW))
    g_other = core_swap(g_own)
    over = Rows(lens, rows, block)
    cosine, sine = rope_tables(rows, head_width)
    full, total = 2 * rows, w_qkv.shape[1]
    qk = q_half + kv_half

    normed_a, raw, queries, keys, values = over.call(
        "qkv",
        partial(qkv_kernel, over.per_slot, counts, head_width, scale),
        2,
        [over.early(width_all), over.late(width_all), over.fixed(w_qkv.shape)]
        + [over.fixed(gain_a.shape), over.fixed(gain_h.shape)]
        + [over.repeated(LANES), over.repeated(LANES)],
        [over.both(width_all), over.both(qk), over.both(2 * q_half), over.both(2 * kv_half)]
        + [over.both(2 * kv_half)],
        [((full, width_all), LOW), ((full, qk), F32), ((full, 2 * q_half), LOW)]
        + [((full, 2 * kv_half), LOW)] * 2,
        [],
        2 * full * width_all * total,
        x_own, x_other, w_qkv, gain_a, gain_h, cosine, sine,
    )
    attended, queries = attend(lens, queries, keys, values, rows, head_width, block)
    part, send = over.call(
        "out",
        partial(out_kernel, over.per_slot),
        2,
        [over.both_other_first(q_half), over.fixed(w_o.shape)],
        [over.late(width_all), over.early(width_all)],
        [((rows, width_all), F32), ((rows, width_all), LOW)],
        [],
        2 * full * q_half * width_all,
        attended, w_o,
    )
    wide, slim = over.both(width_all), over.fixed(gain_m.shape)
    eight = (8, width_all)
    resid, normed_b, sums_a = over.call(
        "resid",
        resid_kernel,
        1,
        [wide, wide, wide, slim],
        [wide, wide, pl.BlockSpec(eight, lambda i, lens: (0, 0))],
        [((rows, width_all), F32), ((rows, width_all), LOW), (eight, F32)],
        [],
        1 << 24,
        x_own, part, core_swap(send), gain_m,
    )
    normed_b_other = core_swap(normed_b)

    def across(grad_rows):
        half = grad_rows.shape[1] // 2
        mine = lax.dynamic_slice_in_dim(grad_rows, core * half, half, axis=1)
        other = core_swap(lax.dynamic_slice_in_dim(grad_rows, (1 - core) * half, half, axis=1))
        return ordered(mine, other, 0)

    def scatter(grad):
        return lax.psum_scatter(grad, "shard", scatter_dimension=0, tiled=True)

    sums = []
    ff_grads = []
    for chunk, (w_gu, w_d) in enumerate(w_chunks):
        last = chunk == chunks - 1
        ends = [over.early(width_all)] * 2 + [over.late(width_all)] * 2 if last else [wide] * 2
        end_shapes = [((full, width_all), F32)] * 2
        if last:
            end_shapes = [((rows, width_all), F32)] * 2 + [((rows, width_all), LOW)] * 2
        *sums, grad_gu, grad_d = over.call(
            "ffn",
            partial(ffn_kernel, over.per_slot, bool(sums), last),
            2,
            [over.early(width_all), over.late(width_all)] * 2
            + [over.fixed(w_gu.shape), over.fixed(w_d.shape)]
            + [wide] * len(sums),
            ends + [over.fixed(w_gu.shape), over.fixed(w_d.shape)],
            end_shapes + [(w_gu.shape, LOW), (w_d.shape, LOW)],
            [pltpu.VMEM(w_gu.shape, F32), pltpu.VMEM(w_d.shape, F32)],
            18 * full * width_all * units,
            normed_b, normed_b_other, g_own, g_other, w_gu, w_d, *sums,
        )
        grad_d = fold(across(grad_d).reshape(shards, piece, d_half))
        packed = jnp.concatenate([grad_gu.reshape(shards, d_rows, 2 * units), grad_d], axis=1)
        packed = packed.reshape(-1, 2 * units)
        ff_grads.append(packed if last else scatter(packed))
    mlp_part, db_part, mlp_send, db_send = sums
    db_got = core_swap(db_send)
    mlp_got = core_swap(mlp_send)
    output, d_resid, d_attn, sums_b = over.call(
        "resid_back",
        resid_back_kernel,
        1,
        [wide] * 6 + [slim],
        [wide, wide, wide, pl.BlockSpec(eight, lambda i, lens: (0, 0))],
        [((rows, width_all), LOW), ((rows, width_all), F32), ((rows, width_all), LOW)]
        + [(eight, F32)],
        [],
        1 << 24,
        resid, mlp_part, mlp_got, db_part, db_got, g_own, gain_m,
    )

    d_attn_other = core_swap(d_attn)
    d_heads, grad_out = over.call(
        "dout",
        partial(dout_kernel, over.per_slot, head_width),
        2,
        [over.early(width_all), over.late(width_all), over.both(q_half), over.fixed(w_o.shape)],
        [over.both(2 * q_half), over.fixed(w_o.shape)],
        [((full, 2 * q_half), LOW), (w_o.shape, LOW)],
        [pltpu.VMEM(w_o.shape, F32)],
        4 * full * q_half * width_all,
        d_attn, d_attn_other, attended, w_o,
    )
    grad_out = across(grad_out)
    d_query, d_key, d_value = attend_back(
        lens, queries, keys, values, d_heads, rows, head_width, block
    )
    n = over.per_slot
    turned = pl.BlockSpec((block, LANES), lambda i, lens: (lax.rem(i, n), 0))
    part, send, grad_qkv, gain_sums = over.call(
        "qkv_back",
        partial(qkv_back_kernel, over.per_slot, counts, head_width, scale),
        2,
        [over.both_other_first(q_half)]
        + [over.both_other_first(2 * kv_half)] * 2
        + [over.both_other_first(qk), over.both_other_first(width_all)]
        + [over.fixed(w_qkv.shape), over.fixed(gain_h.shape), turned, turned],
        [over.late(width_all), over.early(width_all), over.fixed(w_qkv.shape)]
        + [pl.BlockSpec((8, LANES), lambda i, lens: (0, 0))],
        [((rows, width_all), F32), ((rows, width_all), LOW), (w_qkv.shape, LOW)]
        + [((8, LANES), F32)],
        [pltpu.VMEM(w_qkv.shape, F32), pltpu.VMEM((block, total), LOW)],
        4 * full * width_all * total,
        d_query, d_key, d_value, raw, normed_a, w_qkv, gain_h, cosine, sine,
    )
    input_grad, sums_c = over.call(
        "input_back",
        input_back_kernel,
        1,
        [wide] * 4 + [slim],
        [wide, pl.BlockSpec(eight, lambda i, lens: (0, 0))],
        [((rows, width_all), LOW), (eight, F32)],
        [],
        1 << 24,
        x_own, part, core_swap(send), d_resid, gain_a,
    )
    grad_gm, grad_ga = sums_b[1:2], sums_c[0:1]
    grad_gh = gain_sums[:2].reshape(2, -1, head_width).sum(1)
    local_sums = jnp.stack(
        [jnp.sum(sums_a[0]), jnp.sum(sums_a[1]), jnp.sum(sums_b[0]), lengths[0].astype(F32)]
    )
    grad_attn = jnp.concatenate([grad_out, grad_qkv], axis=1)
    small = jnp.concatenate(
        [local_sums, grad_gh.reshape(-1), grad_ga.reshape(-1), grad_gm.reshape(-1)]
    )
    size = small.shape[0]
    small = jnp.pad(small, (0, -size % (8 * LANES))).reshape(-1, LANES)
    mine, other, small = finish_sums(
        [ff_grads[-1], grad_attn], small, ff_grads[:-1], shards, groups
    )
    edges = [4, 4 + head_width, 4 + 2 * head_width, 4 + 2 * head_width + width_all]
    totals, total_gq, total_gk, total_ga, total_gm = jnp.split(small.reshape(-1)[:size], edges)
    statistics = jnp.sqrt(totals[:3] / (totals[3] * width_all))
    me = lax.axis_index("shard")

    def own_piece(vector):
        size = vector.shape[0] // shards
        return lax.dynamic_slice_in_dim(vector, me * size, size)

    ff_last, attn_mine, *ff_mine = mine
    ff_mine.append(ff_last)
    ff_last, attn_other, *ff_other = other
    ff_other.append(ff_last)

    def columns_of(offset):
        def side(parts):
            return jnp.concatenate(
                [
                    part[:d_rows, offset + i * piece : offset + (i + 1) * piece]
                    for i in range(half_shards)
                    for part in parts
                ],
                axis=1,
            )

        return ordered(side(ff_mine), side(ff_other), 1).astype(F32)

    def down_side(parts):
        return jnp.concatenate([unfold(part[d_rows:]) for part in parts])

    grad_down = ordered(down_side(ff_mine), down_side(ff_other), 1).astype(F32)
    cuts = [d_half, d_half + q_half, d_half + q_half + kv_half]
    out_part, query_part, key_part, value_part = (
        ordered(mine, other, 1).astype(F32)
        for mine, other in zip(
            jnp.split(attn_mine, cuts, axis=1), jnp.split(attn_other, cuts, axis=1)
        )
    )
    return (
        output[None],
        input_grad[None],
        own_piece(total_ga),
        query_part,
        key_part,
        value_part,
        own_piece(total_gq),
        own_piece(total_gk),
        out_part,
        own_piece(total_gm),
        columns_of(0),
        columns_of(units),
        grad_down,
        statistics,
    )


def solution(mesh):
    in_specs = (
        P(("rep", "shard"), None, None),
        P(("rep", "shard")),
        P("shard"),
        P("shard", None),
        P("shard", None),
        P("shard", None),
        P("shard"),
        P("shard"),
        P("shard", None),
        P("shard"),
        P("shard", None),
        P("shard", None),
        P("shard", None),
        P(("rep", "shard"), None, None),
    )
    out_specs = (
        P(("rep", "shard"), None, None),
        P(("rep", "shard"), None, None),
        P("shard"),
        P("shard", None),
        P("shard", None),
        P("shard", None),
        P("shard"),
        P("shard"),
        P("shard", None),
        P("shard"),
        P("shard", None),
        P("shard", None),
        P("shard", None),
        P(),
    )
    return jax.shard_map(local, mesh=mesh, in_specs=in_specs, out_specs=out_specs, check_vma=False)
```

```python
from functools import partial
import math

import jax
import jax.numpy as jnp
from jax import lax
from jax.experimental import pallas as pl
from jax.experimental.pallas import tpu as pltpu
from jax.sharding import PartitionSpec as P

EPS = 1e-05
ROPE_BASE = 1000000.0
F32 = jnp.float32
LOW = jnp.bfloat16
LANES = 128
MESH = pl.DeviceIdType.MESH


def rope_tables(row_count, head_width):
    half_width = head_width // 2
    frequency = jnp.power(
        jnp.float32(ROPE_BASE), -jnp.arange(half_width, dtype=jnp.float32) * 2.0 / head_width
    )
    angles = jnp.arange(row_count, dtype=jnp.float32)[:, None] * frequency[None, :]
    cosine, sine = jnp.cos(angles), jnp.sin(angles)
    repeats = LANES // head_width
    return jnp.tile(cosine, (1, 2 * repeats)), jnp.tile(
        jnp.concatenate([-sine, sine], axis=1), (1, repeats)
    )


def nn(left, right):
    return jnp.dot(left, right, preferred_element_type=F32)


def nt(left, right):
    return lax.dot_general(left, right, (((1,), (1,)), ((), ())), preferred_element_type=F32)


def tn(left, right):
    return lax.dot_general(left, right, (((0,), (0,)), ((), ())), preferred_element_type=F32)


def core_swap(x):
    pairs = [(i, i ^ 1) for i in range(lax.axis_size("rep"))]
    return lax.ppermute(x, "rep", pairs)


def place():
    rep = lax.axis_index("rep")
    return lax.axis_index("shard"), lax.div(rep, 2), lax.rem(rep, 2)


def device(shard, group, core):
    return {"rep": 2 * group + core, "shard": shard}


def meet(devices):
    barrier = pltpu.get_barrier_semaphore()
    for where in devices:
        pl.semaphore_signal(barrier, inc=1, device_id=where, device_id_type=MESH)
    pl.semaphore_wait(barrier, len(devices))


def remote(source, target, send, recv, where):
    return pltpu.make_async_remote_copy(
        src_ref=source,
        dst_ref=target,
        send_sem=send,
        recv_sem=recv,
        device_id=where,
        device_id_type=MESH,
    )


def at_rows(ref, start, size):
    return ref.at[pl.ds(pl.multiple_of(start, 8), size), :]


def at(ref, row, rows, column, columns):
    return ref.at[
        pl.ds(pl.multiple_of(row, 8), rows), pl.ds(pl.multiple_of(column, LANES), columns)
    ]


class Copies:
    def __init__(self, send, recv):
        self.send, self.recv, self.used = send, recv, 0

    def __call__(self, source, target, where):
        slot = self.used
        self.used += 1
        return remote(source, target, self.send.at[slot], self.recv.at[slot], where)


def neighbours(me):
    return me + 1 - 2 * lax.rem(me, 2), me + 2 - 4 * lax.div(me, 2), 3 - me


def gather_kernel(shards, wide_parts, tall_parts, count, *refs):
    *refs, send, recv = refs
    sources, targets = refs[: count[0]], refs[count[0] :]
    me, group, core = place()
    half = shards // 2
    partner = device(me, group, 1 - core)
    meet(
        [device(lax.rem(me + k, shards), group, c) for k in range(1, shards) for c in range(2)]
        + [partner]
    )
    copies = Copies(send, recv)
    sent, due = [], []

    def go(source, target, where):
        copy = copies(source, target, where)
        copy.start()
        sent.append(copy.wait_send)
        return copy

    def passed_on(wide):
        fast, slow, _ = neighbours(me)
        later = []
        for block, first, second in wide:
            rows = block(me).shape[0] // 2
            first.wait_recv()
            later.append(go(block(fast).at[pl.ds(0, rows), :], block(fast).at[pl.ds(0, rows), :], device(slow, group, core)))
            second.wait_recv()
            later.append(go(block(slow).at[pl.ds(rows, rows), :], block(slow).at[pl.ds(rows, rows), :], device(fast, group, core)))
        return later

    wide = []
    for source, target, column, to, columns in wide_parts:
        source, target = sources[source], targets[target]
        rows = source.shape[0]
        mine = at(source, 0, rows, column(core), columns)

        def block(shard, target=target, rows=rows, to=to, columns=columns):
            return at(target, shard * rows, rows, to, columns)

        if shards == 4:
            fast, slow, _ = neighbours(me)
            wide.append(
                (
                    block,
                    go(mine, block(me), device(fast, group, core)),
                    go(mine, block(me), device(slow, group, core)),
                )
            )
        else:
            for k in range(1, shards):
                due.append(go(mine, block(me), device(lax.rem(me + k, shards), group, core)))
        due.append(go(at(source, 0, rows, column(1 - core), columns), block(me), partner))
    owner = lax.div(me, half)
    tall = []
    for source, target, row, rows in tall_parts:
        source, target = sources[source], targets[target]
        columns = source.shape[1] // 2

        def block(shard, target=target, rows=rows, columns=columns):
            return at(target, lax.rem(shard, half) * rows, rows, 0, 2 * columns)

        mine = at(source, row, rows, core * columns, columns)
        goal = at(target, lax.rem(me, half) * rows, rows, core * columns, columns)
        steps = [1, 2] if shards == 4 else list(range(1, shards))
        arrivals = []
        for k in steps:
            if shards == 4:
                to = origin = neighbours(me)[k - 1]
            else:
                to, origin = lax.rem(me + k, shards), lax.rem(me + shards - k, shards)
            pair = []
            for side in range(2):
                copy = copies(mine, goal, device(to, group, owner))
                pl.when(core == side)(copy.start)
                sent.append((core == side, copy.wait_send))
                pair.append(copy)
            arrivals.append((lax.div(origin, half) == core, pair))
        whole = copies(
            at(source, row, rows, 0, 2 * columns), block(me), partner
        )
        pl.when(owner != core)(whole.start)
        sent.append((owner != core, whole.wait_send))
        due.append((owner == core, whole))
        if shards == 4:
            tall.append((block, rows // 2, arrivals))
        else:
            for condition, pair in arrivals:
                due.extend((condition, copy) for copy in pair)
    gains, given = sources[-2:], targets[-2:]
    for k in range(1, shards):
        due.append(go(gains[0], given[0].at[me], device(lax.rem(me + k, shards), group, core)))
    due.append(go(gains[0], given[0].at[me], partner))
    due.append(go(gains[1], given[1], partner))
    if shards == 4:
        due.extend(passed_on(wide))
        fast, slow, _ = neighbours(me)
        for block, rows, arrivals in tall:
            for number, (condition, pair) in enumerate(arrivals):
                start = number * rows
                from_, to = (fast, slow) if number == 0 else (slow, fast)
                part = block(from_).at[pl.ds(start, rows), :]
                copy = copies(part, part, device(to, group, core))

                @pl.when(condition)
                def _(pair=pair, copy=copy):
                    for one in pair:
                        one.wait_recv()
                    copy.start()

                sent.append((condition, copy.wait_send))
                due.append((owner != core, copy))
    for item in sent:
        pl.when(item[0])(item[1]) if isinstance(item, tuple) else item()
    for item in due:
        pl.when(item[0])(item[1].wait_recv) if isinstance(item, tuple) else item.wait_recv()


def pack_kernel(shards, chunks, gate_ref, up_ref, down_ref, *refs):
    *packs, sems = refs
    core = lax.rem(lax.axis_index("rep"), 2)
    half = shards // 2
    total, rows = down_ref.shape[0], gate_ref.shape[0]
    piece = total // chunks
    columns = down_ref.shape[1] // 2
    copies = []
    for pack in packs:
        for row, chunk in pack[1]:
            for j, ref in enumerate((gate_ref, up_ref)):
                for i in range(half):
                    start = (core * half + i) * total + chunk * piece
                    copies.append(
                        (
                            at(ref, 0, rows, start, piece),
                            pack[0].at[pl.ds(row, rows), pl.ds((j * half + i) * piece, piece)],
                        )
                    )
            folds = 2 * half * piece // columns
            size = piece // folds
            for i in range(folds):
                copies.append(
                    (
                        at(down_ref, chunk * piece + i * size, size, core * columns, columns),
                        pack[0].at[pl.ds(row + rows, size), pl.ds(i * columns, columns)],
                    )
                )
    copies = [pltpu.make_async_copy(a, b, sems.at[k]) for k, (a, b) in enumerate(copies)]
    for copy in copies:
        copy.start()
    for copy in copies:
        copy.wait()


def add_up(parts, target, rows):
    def some(i, _):
        here = pl.ds(pl.multiple_of(i * rows, rows), rows)
        total = parts[0][here, :].astype(F32)
        for part in parts[1:]:
            total += part[here, :].astype(F32)
        target[here, :] = total.astype(target.dtype)
        return 0

    lax.fori_loop(0, target.shape[0] // rows, some, 0)


def reduce_over_plane(copies, load, shards, grad_ref, level, bufs):
    me, group, core = place()
    rows = level.shape[0]

    def block(shard, start=0, size=rows):
        return at_rows(grad_ref, shard * rows + start, size)

    own = bufs[0]
    local = pltpu.make_async_copy(block(me), own, load.at[0])
    if shards != 4:
        planes = bufs[1]
        out = [
            copies(block(lax.rem(me + k, shards)), planes.at[k - 1], device(lax.rem(me + k, shards), group, core))
            for k in range(1, shards)
        ]

        def start():
            local.start()
            for copy in out:
                copy.start()

        def end():
            local.wait()
            for copy in out:
                copy.wait_send()
                copy.wait_recv()
            add_up([own] + [planes.at[k] for k in range(shards - 1)], level, 16)

        return [start, idle, end]
    fast, slow, across = neighbours(me)
    to_fast, to_slow = device(fast, group, core), device(slow, group, core)
    half = rows // 2
    planes, met_fast, met_slow, held_fast, held_slow = bufs[1:]
    upper, lower = pl.ds(0, half), pl.ds(half, half)
    loads = [
        local,
        pltpu.make_async_copy(block(fast, half, half), held_fast, load.at[1]),
        pltpu.make_async_copy(block(slow, 0, half), held_slow, load.at[2]),
    ]
    early = [
        copies(block(across, 0, half), met_fast, to_fast),
        copies(block(across, half, half), met_slow, to_slow),
        copies(block(fast, 0, half), planes.at[0, upper, :], to_fast),
        copies(block(slow, half, half), planes.at[1, lower, :], to_slow),
    ]
    late = [
        copies(held_fast, planes.at[0, lower, :], to_fast),
        copies(held_slow, planes.at[1, upper, :], to_slow),
    ]

    def start():
        for copy in early + loads:
            copy.start()

    def merge():
        for copy in loads:
            copy.wait()
        for copy, met, held, out in (
            (early[1], met_slow, held_fast, late[0]),
            (early[0], met_fast, held_slow, late[1]),
        ):
            copy.wait_recv()
            add_up([held, met], held, 16)
            out.start()

    def end():
        for copy in early[2:] + late:
            copy.wait_recv()
        for copy in early + late:
            copy.wait_send()
        add_up([own, planes.at[0], planes.at[1]], level, 16)

    return [start, merge, end]


def plane_buffers(shards, shape):
    half = (shape[0] // 2, shape[1])
    if shards != 4:
        return [pltpu.VMEM(shape, LOW), pltpu.VMEM((shards - 1,) + shape, LOW)]
    return [pltpu.VMEM(shape, LOW), pltpu.VMEM((2,) + shape, LOW)] + [pltpu.VMEM(half, LOW)] * 4


def reduce_over_line(copies, groups, source, part, total, bufs):
    me, group, core = place()
    if groups != 4:
        (slots,) = bufs
        out = [
            copies(source, slots.at[group], device(me, lax.rem(group + k, groups), core))
            for k in range(1, groups)
        ]

        def start():
            for copy in out:
                copy.start()

        def end():
            rows = part.shape[0]

            def some(i, _):
                here = pl.ds(pl.multiple_of(i * 8, 8), 8)
                slots[group, here, :] = part[here, :]
                return 0

            lax.fori_loop(0, rows // 8, some, 0)
            for copy in out:
                copy.wait_send()
                copy.wait_recv()
            add_up([slots.at[k] for k in range(groups)], total, 8)

        return [start, idle, idle, end]
    met, summed, other = bufs
    outer = jnp.logical_or(group == 0, group == groups - 1)
    inner = jnp.logical_not(outer)
    mate = device(me, group + 1 - 2 * lax.rem(group, 2), core)
    inward = copies(source, met, mate)
    between = copies(summed, other, device(me, groups - 1 - group, core))
    back = copies(total, total, mate)

    def start():
        pl.when(outer)(inward.start)

    def exchange():
        @pl.when(inner)
        def _():
            inward.wait_recv()
            add_up([part, met], summed, 16)
            between.start()

    def give():
        @pl.when(inner)
        def _():
            between.wait_recv()
            add_up([summed, other], total, 16)
            back.start()

    def end():
        @pl.when(outer)
        def _():
            inward.wait_send()
            back.wait_recv()

        @pl.when(inner)
        def _():
            between.wait_send()
            back.wait_send()

    return [start, exchange, give, end]


def idle():
    pass


def line_buffers(groups, shape):
    if groups != 4:
        return [pltpu.VMEM((groups,) + shape, LOW)]
    return [pltpu.VMEM(shape, LOW)] * 3


PARTS = 4


class LineSum:
    def __init__(self, copies, groups, source, part, total, bufs):
        rows = part.shape[0] // PARTS
        each = len(bufs) // PARTS
        self.parts = [
            reduce_over_line(
                copies,
                groups,
                at_rows(source, i * rows, rows),
                at_rows(part, i * rows, rows),
                at_rows(total, i * rows, rows),
                bufs[i * each : (i + 1) * each],
            )
            for i in range(PARTS)
        ]

    def run(self, part, stage):
        self.parts[part][stage]()

    @staticmethod
    def buffers(groups, shape):
        return line_buffers(groups, (shape[0] // PARTS, shape[1])) * PARTS

    @staticmethod
    def copies(groups):
        return PARTS * max(3, groups - 1)


class Side:
    def __init__(self, shards, groups, plane_shapes, line_shapes, extra=0):
        self.shards, self.groups, self.extra = shards, groups, extra
        self.plane_shapes, self.line_shapes = plane_shapes, line_shapes

    def outs(self):
        return [jax.ShapeDtypeStruct(shape, LOW) for shape in self.plane_shapes + self.line_shapes]

    def scratch(self):
        groups, shards = self.groups, self.shards
        shapes = [pltpu.VMEM(shape, LOW) for shape in self.plane_shapes + self.line_shapes]
        for shape in self.plane_shapes:
            shapes += plane_buffers(shards, shape)
        for shape in self.line_shapes:
            shapes += [pltpu.VMEM(shape, LOW)] + LineSum.buffers(groups, shape)
        count = 2 * self.shards + len(self.plane_shapes) * max(6, shards - 1)
        count += len(self.line_shapes) * LineSum.copies(groups) + self.extra
        loads = 4 * len(self.plane_shapes) + 2 * len(self.line_shapes) + 1
        return shapes + [pltpu.SemaphoreType.DMA((count,))] * 2 + [pltpu.SemaphoreType.DMA((loads,))]

    def run(self, step, sources, outs, bufs):
        *bufs, send, recv, load = bufs
        totals, bufs = take(bufs, len(outs))
        me, group, core = place()
        copies = Copies(send, recv)
        shards, groups = self.shards, self.groups

        @pl.when(step == 0)
        def _():
            meet(everyone_near(shards, groups))

        planes, lines, loads = [], [], []
        for i, shape in enumerate(self.plane_shapes):
            some, bufs = take(bufs, len(plane_buffers(shards, shape)))
            planes.append(
                reduce_over_plane(
                    copies, load.at[pl.ds(3 * i, 3)], shards, sources[i], totals[i], some
                )
            )
        first = len(self.plane_shapes)
        for i, shape in enumerate(self.line_shapes):
            (own,), bufs = take(bufs, 1)
            some, bufs = take(bufs, len(LineSum.buffers(groups, shape)))
            loads.append(
                pltpu.make_async_copy(sources[first + i], own, load.at[3 * first + i])
            )
            lines.append(LineSum(copies, groups, sources[first + i], own, totals[first + i], some))

        def begin():
            for stages in planes:
                stages[0]()
            for part in range(PARTS):
                for line in lines:
                    line.run(part, 0)
            for one in loads:
                one.start()

        def load_done():
            for one in loads:
                one.wait()

        def of_lines(part, stage):
            def go():
                for line in lines:
                    line.run(part, stage)

            return go

        def merge():
            for stages in planes:
                stages[1]()

        plan = {
            0: [begin],
            2: [load_done, of_lines(0, 1)],
            3: [of_lines(1, 1), merge],
            4: [of_lines(2, 1), of_lines(0, 2)],
            5: [of_lines(3, 1), of_lines(1, 2)],
            6: [of_lines(2, 2)],
            7: [of_lines(3, 2)],
        }
        for when, stages in plan.items():

            @pl.when(step == when)
            def _(stages=stages):
                for stage in stages:
                    stage()

        count = len(outs)
        stores = [
            pltpu.make_async_copy(total, out, load.at[load.shape[0] - 1 - count + i])
            for i, (total, out) in enumerate(zip(totals, outs))
        ]

        def end():
            for stages, store in zip(planes, stores):
                stages[2]()
                store.start()
            for part in range(PARTS):
                for line in lines:
                    line.run(part, 3)
            for store in stores[len(planes) :]:
                store.start()
            for store in stores:
                store.wait()

        return copies, end


def everyone_near(shards, groups):
    me, group, core = place()
    return (
        [device(lax.rem(me + k, shards), group, core) for k in range(1, shards)]
        + [device(me, lax.rem(group + k, groups), core) for k in range(1, groups)]
        + [device(me, group, 1 - core)]
    )


def take(refs, count):
    return refs[:count], refs[count:]


def finish_kernel(shards, groups, counts, rows, length_ref, *refs):
    smalls, refs = take(refs, 1 + max(k for k, _ in rows))
    (grad_ref,), refs = take(refs, 1)
    lows, refs = take(refs, counts[0])
    ready, refs = take(refs, counts[1])
    n = counts[0] + 1
    mine, refs = take(refs, n)
    other, refs = take(refs, n + counts[1])
    (total_ref, level), refs = take(refs, 2)
    plane_bufs, refs = take(refs, len(plane_buffers(shards, (16, LANES))))
    own, refs = take(refs, counts[0])
    per_line = len(LineSum.buffers(groups, (32, LANES)))
    line_bufs = []
    for _ in range(n):
        some, refs = take(refs, per_line)
        line_bufs.append(some)
    small_a, small_b, small_c, send, recv, load = refs
    me, group, core = place()
    partner = device(me, group, 1 - core)
    plane = [device(lax.rem(me + k, shards), group, core) for k in range(1, shards)]
    line = [device(me, lax.rem(group + k, groups), core) for k in range(1, groups)]
    copies = Copies(send, recv)

    def go(source, target, where):
        copy = copies(source, target, where)
        copy.start()
        return copy

    def finish(some):
        for copy in some:
            copy.wait_send()
            copy.wait_recv()

    loads = [pltpu.make_async_copy(low, own[i], load.at[3 + i]) for i, low in enumerate(lows)]
    for copy in loads:
        copy.start()
    for i, (k, row) in enumerate(rows):
        values = smalls[k][row : row + 1, :]
        small_a[me, i : i + 1, : values.shape[1]] = values
        if values.shape[1] < small_a.shape[2]:
            rest = small_a.shape[2] - values.shape[1]
            small_a[me, i : i + 1, values.shape[1] :] = jnp.zeros((1, rest), F32)
    small_a[me, len(rows) :, :] = jnp.full(
        (small_a.shape[1] - len(rows), small_a.shape[2]), length_ref[0].astype(F32)
    )
    meet(everyone_near(shards, groups))
    stages = reduce_over_plane(copies, load.at[pl.ds(0, 3)], shards, grad_ref, level, plane_bufs)
    sums = [
        LineSum(copies, groups, low, own[i], mine[i], line_bufs[i]) for i, low in enumerate(lows)
    ]
    last = LineSum(copies, groups, level, level, mine[-1], line_bufs[-1])
    stages[0]()
    for part in range(PARTS):
        for one in sums:
            one.run(part, 0)
    swaps = [go(source, target, partner) for source, target in zip(ready, other[n:])]
    small_copies = [go(small_a.at[me], small_a.at[me], where) for where in plane]
    for copy in loads:
        copy.wait()
    finish(small_copies)
    small_b[group] = sum(small_a[k] for k in range(shards))
    small_copies = [go(small_b.at[group], small_b.at[group], where) for where in line]
    for part in range(2):
        for one in sums:
            one.run(part, 1)
    stages[1]()
    for part in range(2):
        for one in sums:
            one.run(part + 2, 1)
            one.run(part, 2)
    finish(small_copies)
    small_c[core] = sum(small_b[k] for k in range(groups))
    small_copies = [go(small_c.at[core], small_c.at[core], partner)]
    stages[2]()
    for part in range(PARTS):
        last.run(part, 0)
    for part in range(2, PARTS):
        for one in sums:
            one.run(part, 2)
        last.run(part - 2, 1)
    last.run(2, 1)
    last.run(0, 2)
    for part in range(PARTS):
        for one in sums:
            one.run(part, 3)
    swaps += [go(mine[i], other[i], partner) for i in range(counts[0])]
    last.run(3, 1)
    for part in range(1, PARTS):
        last.run(part, 2)
    for part in range(PARTS):
        last.run(part, 3)
    swaps.append(go(mine[-1], other[n - 1], partner))
    finish(small_copies)
    total_ref[...] = small_c[0] + small_c[1]
    finish(swaps)


def finish_sums(grad, length, smalls, rows, lows, ready, shards, groups):
    level = (grad.shape[0] // shards, grad.shape[1])
    shapes = [low.shape for low in lows] + [level]
    others = shapes + [one.shape for one in ready]
    vmem = pl.BlockSpec(memory_space=pltpu.VMEM)
    hbm = pl.BlockSpec(memory_space=pltpu.HBM)
    scratch = [pltpu.VMEM(level, LOW)] + plane_buffers(shards, level)
    scratch += [pltpu.VMEM(shape, LOW) for shape in shapes[:-1]]
    for shape in shapes:
        scratch += LineSum.buffers(groups, shape)
    count = 6 + 2 * shards + len(shapes) * LineSum.copies(groups) + len(others) + groups
    small = (8, max(one.shape[1] for one in smalls))
    outs = pl.pallas_call(
        partial(finish_kernel, shards, groups, (len(lows), len(ready)), rows),
        out_shape=[jax.ShapeDtypeStruct(shape, LOW) for shape in shapes + others]
        + [jax.ShapeDtypeStruct(small, F32)],
        in_specs=[pl.BlockSpec(memory_space=pltpu.SMEM)]
        + [vmem] * len(smalls)
        + [hbm] * (1 + len(lows) + len(ready)),
        out_specs=[vmem] * (len(shapes) + len(shapes)) + [hbm] * len(ready) + [vmem],
        scratch_shapes=scratch
        + [pltpu.VMEM((count,) + small, F32) for count in (shards, groups, 2)]
        + [pltpu.SemaphoreType.DMA((count,)), pltpu.SemaphoreType.DMA((count,))]
        + [pltpu.SemaphoreType.DMA((3 + len(lows),))],
        compiler_params=pltpu.CompilerParams(
            collective_id=1, has_side_effects=True, vmem_limit_bytes=56 << 20
        ),
        name="finish",
    )(length, *smalls, grad, *lows, *ready)
    n = len(shapes)
    return outs[:n], outs[n:-1], outs[-1]


def two_parts(column):
    high = column.astype(LOW)
    return high, (column - high.astype(F32)).astype(LOW)


def attend_kernel(block, width, lens_ref, q_ref, k_ref, v_ref, att_ref, qx_ref):
    rows = q_ref.shape[0]
    heads = q_ref.shape[1] // LANES
    length = lens_ref[pl.program_id(0)]
    lane = lax.broadcasted_iota(jnp.int32, (block, LANES), 1)
    keep = lax.broadcasted_iota(jnp.int32, (block, block), 1) <= lax.broadcasted_iota(
        jnp.int32, (block, block), 0
    )
    for step in range(rows // block):
        start = step * block
        here = pl.ds(start, block)

        @pl.when(start < length)
        def _():
            outs = []
            for head in range(heads):
                lanes = pl.ds(head * LANES, LANES)
                query = q_ref[here, lanes]
                probs = jnp.exp(nt(query, k_ref[here, :]))
                probs = jnp.where(keep, probs, 0.0).astype(LOW)
                total = nn(probs, v_ref[here, :])
                if step:
                    probs = jnp.exp(nt(query, k_ref[pl.ds(0, start), :])).astype(LOW)
                    total += nn(probs, v_ref[pl.ds(0, start), :])
                weight = total[:, width : width + 1]
                outs.append(total / weight)
                high, rest = two_parts(-jnp.log(weight))
                qx_ref[here, lanes] = jnp.where(
                    lane == width, high, jnp.where(lane == width + 1, rest, query)
                )
            for pair in range(heads // 2):
                att_ref[here, pl.ds(pair * LANES, LANES)] = jnp.where(
                    lane < width, outs[2 * pair], pltpu.roll(outs[2 * pair + 1], width, 1)
                ).astype(LOW)

        @pl.when(start >= length)
        def _():
            att_ref[here, :] = jnp.zeros((block, att_ref.shape[1]), LOW)
            qx_ref[here, :] = jnp.zeros((block, qx_ref.shape[1]), LOW)


def attend_back_kernel(block, width, side, q_ref, k_ref, v_ref, do_ref, *refs):
    count = len(side.plane_shapes) + len(side.line_shapes)
    sources, refs = take(refs, count)
    (dq_ref, dk_ref, dv_ref), refs = take(refs, 3)
    totals, bufs = take(refs, count)
    grid_step = pl.program_id(0) * pl.num_programs(1) + pl.program_id(1)
    _, end = side.run(grid_step, sources, totals, bufs)
    rows = q_ref.shape[0]
    heads = q_ref.shape[1] // LANES
    lane = lax.broadcasted_iota(jnp.int32, (block, LANES), 1)
    keep = lax.broadcasted_iota(jnp.int32, (block, block), 0) <= lax.broadcasted_iota(
        jnp.int32, (block, block), 1
    )
    dk_ref[...] = jnp.zeros(dk_ref.shape, F32)
    dv_ref[...] = jnp.zeros(dv_ref.shape, F32)
    for step in range(rows // block):
        start = step * block
        here = pl.ds(start, block)
        parts = []
        for head in range(heads):
            lanes = pl.ds(head * LANES, LANES)
            query = q_ref[here, lanes]
            dout = do_ref[here, lanes]

            def one(keys, masked):
                key, value = k_ref[keys, :], v_ref[keys, :]
                probs = jnp.exp(nt(key, query))
                if masked:
                    probs = jnp.where(keep, probs, 0.0)
                dscores = (probs * nt(value, dout)).astype(LOW)
                dv_ref[keys, :] += nn(probs.astype(LOW), dout)
                dk_ref[keys, :] += nn(dscores, query)
                return tn(dscores, key)

            dquery = one(here, True)
            if step:
                dquery += one(pl.ds(0, start), False)
            parts.append(dquery)
        for pair in range(heads // 2):
            dq_ref[here, pl.ds(pair * LANES, LANES)] = jnp.where(
                lane < width, parts[2 * pair], pltpu.roll(parts[2 * pair + 1], width, 1)
            )
    pl.when(grid_step == pl.num_programs(0) * pl.num_programs(1) - 1)(end)


def attention_grid(slots, groups, per_group, rows):
    wide = pl.BlockSpec((rows, per_group * LANES), lambda s, g, lens: (s, g))
    dense = pl.BlockSpec((rows, per_group * LANES // 2), lambda s, g, lens: (s, g))
    narrow = pl.BlockSpec((rows, LANES), lambda s, g, lens: (s, g))
    return (slots, groups), wide, dense, narrow


def attend(lens, queries, keys, values, rows, width, block):
    slots, groups = queries.shape[0] // rows, keys.shape[1] // LANES
    per_group = queries.shape[1] // LANES // groups
    grid, wide, dense, narrow = attention_grid(slots, groups, per_group, rows)
    flops = 4 * slots * groups * per_group * rows * rows * LANES
    return pl.pallas_call(
        partial(attend_kernel, block, width),
        out_shape=(
            jax.ShapeDtypeStruct((queries.shape[0], queries.shape[1] // 2), LOW),
            jax.ShapeDtypeStruct(queries.shape, LOW),
        ),
        grid_spec=pltpu.PrefetchScalarGridSpec(
            num_scalar_prefetch=1,
            grid=grid,
            in_specs=[wide, narrow, narrow],
            out_specs=[dense, wide],
        ),
        cost_estimate=pl.CostEstimate(flops=flops, bytes_accessed=1 << 23, transcendentals=0),
        name="attend",
    )(lens, queries, keys, values)


def attend_back(queries, keys, values, douts, rows, width, block, side, sources):
    slots, groups = queries.shape[0] // rows, keys.shape[1] // LANES
    per_group = queries.shape[1] // LANES // groups
    wide = pl.BlockSpec((rows, per_group * LANES), lambda s, g: (s, g))
    dense = pl.BlockSpec((rows, per_group * LANES // 2), lambda s, g: (s, g))
    narrow = pl.BlockSpec((rows, LANES), lambda s, g: (s, g))
    flops = 10 * slots * groups * per_group * rows * rows * LANES
    return pl.pallas_call(
        partial(attend_back_kernel, block, width, side),
        out_shape=[
            jax.ShapeDtypeStruct((queries.shape[0], queries.shape[1] // 2), F32),
            jax.ShapeDtypeStruct(keys.shape, F32),
            jax.ShapeDtypeStruct(keys.shape, F32),
        ]
        + side.outs(),
        grid=(slots, groups),
        in_specs=[wide, narrow, narrow, wide]
        + [pl.BlockSpec(memory_space=pltpu.HBM)] * len(sources),
        out_specs=[dense, narrow, narrow]
        + [pl.BlockSpec(memory_space=pltpu.HBM)] * len(side.outs()),
        scratch_shapes=side.scratch(),
        cost_estimate=pl.CostEstimate(flops=flops, bytes_accessed=1 << 24, transcendentals=0),
        compiler_params=pltpu.CompilerParams(
            collective_id=5, has_side_effects=True, vmem_limit_bytes=56 << 20
        ),
        name="attend_back",
    )(queries, keys, values, douts, *sources)


def swap_halves(values, width):
    lane = lax.broadcasted_iota(jnp.int32, values.shape, 1)
    half = width // 2
    return jnp.where(
        lane % width < half, pltpu.roll(values, LANES - half, 1), pltpu.roll(values, half, 1)
    )


def head_sum(values, width):
    same = lax.broadcasted_iota(jnp.int32, (LANES, LANES), 0) // width
    same = (same == lax.broadcasted_iota(jnp.int32, (LANES, LANES), 1) // width).astype(LOW)
    high, rest = two_parts(values)
    return nn(high, same) + nn(rest, same)


def row_rsqrt(values):
    return lax.rsqrt(jnp.mean(values * values, axis=1, keepdims=True) + EPS)


def is_live(lens_ref, step, per_slot, block):
    return lax.rem(step, per_slot) * block < lens_ref[lax.div(step, per_slot)]


def qkv_kernel(
    per_slot, counts, width, scale, lens_ref, own_ref, other_ref, w_ref, ga_ref, gh_ref, cos_ref, sin_ref,
    normed_ref, raw_ref, q_ref, k_ref, v_ref,
):
    step = pl.program_id(0)
    block = own_ref.shape[0]
    q_tiles, kv_tiles = counts

    @pl.when(is_live(lens_ref, step, per_slot, block))
    def _():
        x = jnp.where(step < per_slot, own_ref[...], other_ref[...]).astype(F32)
        normed = (x * row_rsqrt(x) * ga_ref[...]).astype(LOW)
        normed_ref[...] = normed
        lane = lax.broadcasted_iota(jnp.int32, (block, LANES), 1)
        zero = jnp.zeros((block, LANES), F32)
        ones = jnp.where(lane < width + 2, 1.0, 0.0)
        cosine, sine = cos_ref[...], sin_ref[...]

        def put(ref, tile, values, rest):
            ref[:, pl.ds(2 * tile * LANES, LANES)] = jnp.where(lane < width, values, rest).astype(LOW)
            ref[:, pl.ds((2 * tile + 1) * LANES, LANES)] = jnp.where(
                lane < width, pltpu.roll(values, width, 1), rest
            ).astype(LOW)

        for tile in range(q_tiles + 2 * kv_tiles):
            lanes = pl.ds(tile * LANES, LANES)
            if tile % 2 == 0:
                pair = nn(normed, w_ref[:, pl.ds(tile * LANES, 2 * LANES)])
            values = pair[:, (tile % 2) * LANES : (tile % 2 + 1) * LANES]
            if tile >= q_tiles + kv_tiles:
                put(v_ref, tile - q_tiles - kv_tiles, values, ones)
                continue
            raw_ref[:, lanes] = values
            is_query = tile < q_tiles
            gain = gh_ref[0:1, :] if is_query else gh_ref[1:2, :]
            values *= lax.rsqrt(head_sum(values * values, width) * (1.0 / width) + EPS) * gain
            values = values * cosine + swap_halves(values, width) * sine
            if is_query:
                put(q_ref, tile, values * scale, zero)
            else:
                put(k_ref, tile - q_tiles, values, ones)

    @pl.when(jnp.logical_not(is_live(lens_ref, step, per_slot, block)))
    def _():
        for ref in (normed_ref, raw_ref, q_ref, k_ref, v_ref):
            ref[...] = jnp.zeros(ref.shape, ref.dtype)


def out_kernel(per_slot, lens_ref, att_ref, w_ref, own_ref, other_ref):
    step = pl.program_id(0)
    block = att_ref.shape[0]

    @pl.when(step < per_slot)
    def _():
        other_ref[...] = nn(att_ref[...], w_ref[...]).astype(LOW)

    @pl.when(step >= per_slot)
    def _():
        own_ref[...] = nn(att_ref[...], w_ref[...])


def resid_kernel(lens_ref, x_ref, part_ref, got_ref, gain_ref, resid_ref, normed_ref, sums_ref):
    step = pl.program_id(0)
    block = x_ref.shape[0]
    valid = lax.broadcasted_iota(jnp.int32, (block, 1), 0) + step * block < lens_ref[0]
    attn_out = part_ref[...] + got_ref[...].astype(F32)
    resid = x_ref[...].astype(F32) + attn_out
    resid_ref[...] = resid
    normed_ref[...] = (resid * row_rsqrt(resid) * gain_ref[...]).astype(LOW)

    @pl.when(step == 0)
    def _():
        sums_ref[...] = jnp.zeros(sums_ref.shape, F32)

    for row, values in ((0, resid), (1, attn_out)):
        sums_ref[row : row + 1, :] += jnp.sum(
            jnp.where(valid, values * values, 0.0), axis=0, keepdims=True
        )


def ffn_kernel(
    per_slot, shards, chained, last, side, offset, x_own, x_other, g_own, g_other, gathered_ref, *refs
):
    if chained:
        (mlp_in, db_in), refs = take(refs, 2)
    count = len(side.plane_shapes) + len(side.line_shapes)
    sources, refs = take(refs, count)
    (mlp_own, db_own), refs = take(refs, 2)
    if last:
        (mlp_other, db_other), refs = take(refs, 2)
    (grad_out,), refs = take(refs, 1)
    totals, refs = take(refs, count)
    (acc_ref, accd_ref, given_ref, w_ref, wd_ref, grad_ref, load), bufs = take(refs, 7)
    step = pl.program_id(0)
    copies, end = side.run(step, sources, totals, bufs)
    own = step < per_slot
    units, depth = wd_ref.shape
    me, group, core = place()
    partner = device(me, group, 1 - core)
    half, columns, d_rows = shards // 2, depth // 2, depth // shards
    packed = grad_ref.shape[0] // shards
    size = packed - d_rows
    folds = grad_ref.shape[1] // columns

    def folded(ref, shard, fold):
        return ref.at[shard, pl.ds(offset + d_rows, size), pl.ds(fold * columns, columns)]

    def unfolded(i, fold):
        return at(wd_ref, (i * folds + fold) * size, size, core * columns, columns)

    tiles = [(i, fold) for i in range(half) for fold in range(folds)]
    given = [
        copies(folded(gathered_ref, (1 - core) * half + i, fold), unfolded(i, fold), partner)
        for i, fold in tiles
    ]
    loads = [
        pltpu.make_async_copy(
            gathered_ref.at[shard, pl.ds(offset, d_rows), :],
            w_ref.at[pl.ds(shard * d_rows, d_rows), :],
            load.at[shard],
        )
        for shard in range(shards)
    ] + [
        pltpu.make_async_copy(
            folded(gathered_ref, core * half + i, fold), unfolded(i, fold), load.at[shards + k]
        )
        for k, (i, fold) in enumerate(tiles)
    ]

    @pl.when(step == 0)
    def _():
        for copy in given + loads:
            copy.start()
        acc_ref[...] = jnp.zeros(acc_ref.shape, F32)
        accd_ref[...] = jnp.zeros(accd_ref.shape, F32)
        for copy in loads:
            copy.wait()
        for copy in given:
            copy.wait_send()
            copy.wait_recv()

    x = jnp.where(own, x_own[...], x_other[...])
    g = jnp.where(own, g_own[...], g_other[...])
    gate = nn(x, w_ref[:, :units])
    up = nn(x, w_ref[:, units:])
    d_hidden = nt(g, wd_ref[...])
    sig = jax.nn.sigmoid(gate)
    silu = gate * sig
    hidden = (silu * up).astype(LOW)
    d_gate = (d_hidden * up * (sig * (1.0 + gate * (1.0 - sig)))).astype(LOW)
    d_up = (d_hidden * silu).astype(LOW)
    mlp = nn(hidden, wd_ref[...])
    d_b = nt(d_gate, w_ref[:, :units]) + nt(d_up, w_ref[:, units:])
    if chained:
        mlp += mlp_in[...]
        d_b += db_in[...]
    if last:

        @pl.when(own)
        def _():
            mlp_own[...] = mlp
            db_own[...] = d_b

        @pl.when(jnp.logical_not(own))
        def _():
            mlp_other[...] = mlp.astype(LOW)
            db_other[...] = d_b.astype(LOW)

    else:
        mlp_own[...] = mlp
        db_own[...] = d_b
    acc_ref[:, :units] += tn(x, d_gate)
    acc_ref[:, units:] += tn(x, d_up)
    accd_ref[...] += tn(hidden, g)

    @pl.when(step == pl.num_programs(0) - 1)
    def _():
        mine = pl.ds(pl.multiple_of(core * columns, columns), columns)
        theirs = pl.ds(pl.multiple_of((1 - core) * columns, columns), columns)
        given_ref[...] = accd_ref[:, theirs].astype(LOW)
        for shard in range(shards):
            grad_ref[pl.ds(shard * packed, d_rows), :] = acc_ref[
                pl.ds(shard * d_rows, d_rows), :
            ].astype(LOW)
        out = []
        for i in range(half):
            for fold in range(folds):
                row = i * folds * size + fold * size
                to = pl.ds(
                    pl.multiple_of((core * half + i) * packed + d_rows, 8), size
                )
                lanes = pl.ds(fold * columns, columns)
                out.append(
                    copies(
                        given_ref.at[pl.ds(row, size), :],
                        grad_ref.at[to, lanes],
                        partner,
                    )
                )
                out[-1].start()
                grad_ref[to, lanes] = accd_ref[pl.ds(row, size), mine].astype(LOW)
        for copy in out:
            copy.wait_send()
            copy.wait_recv()
        store = pltpu.make_async_copy(grad_ref, grad_out, load.at[0])
        store.start()
        end()
        store.wait()


def norm_back(values, dy, gain):
    inverse = row_rsqrt(values)
    scaled = dy * gain
    inner = jnp.mean(values * scaled, axis=1, keepdims=True)
    return inverse * scaled - values * (inverse * inverse * inverse * inner), dy * values * inverse


def resid_back_kernel(
    lens_ref, resid_ref, mlp_ref, mlp_got, db_ref, db_got, g_ref, gain_ref,
    out_ref, dresid_ref, dattn_ref, sums_ref,
):
    step = pl.program_id(0)
    block = resid_ref.shape[0]
    valid = lax.broadcasted_iota(jnp.int32, (block, 1), 0) + step * block < lens_ref[0]
    resid = resid_ref[...]
    mlp_out = mlp_ref[...] + mlp_got[...].astype(F32)
    out_ref[...] = jnp.where(valid, resid + mlp_out, 0.0).astype(LOW)
    d_norm, d_gain = norm_back(resid, db_ref[...] + db_got[...].astype(F32), gain_ref[...])
    d_resid = jnp.where(valid, g_ref[...].astype(F32) + d_norm, 0.0)
    dresid_ref[...] = d_resid
    dattn_ref[...] = d_resid.astype(LOW)

    @pl.when(step == 0)
    def _():
        sums_ref[...] = jnp.zeros(sums_ref.shape, F32)

    for row, values in ((0, mlp_out * mlp_out), (1, d_gain)):
        sums_ref[row : row + 1, :] += jnp.sum(
            jnp.where(valid, values, 0.0), axis=0, keepdims=True
        )


def dout_kernel(
    per_slot, width, lens_ref, own_ref, other_ref, att_ref, w_ref, do_ref, grad_ref, acc_ref
):
    step = pl.program_id(0)
    block = own_ref.shape[0]

    @pl.when(step == 0)
    def _():
        acc_ref[...] = jnp.zeros(acc_ref.shape, F32)

    @pl.when(is_live(lens_ref, step, per_slot, block))
    def _():
        d_attn = jnp.where(step < per_slot, own_ref[...], other_ref[...])
        lane = lax.broadcasted_iota(jnp.int32, (block, LANES), 1)
        att = att_ref[...]
        acc_ref[...] += tn(att, d_attn)
        for tile in range(att.shape[1] // LANES):
            lanes = slice(tile * LANES, (tile + 1) * LANES)
            if tile % 2 == 0:
                pair = nt(d_attn, w_ref[tile * LANES : (tile + 2) * LANES, :])
            dout = pair[:, (tile % 2) * LANES : (tile % 2 + 1) * LANES].astype(LOW).astype(F32)
            delta = -head_sum(dout * att[:, lanes].astype(F32), width)
            for head, (values, column) in enumerate(
                ((dout, pltpu.roll(delta, width, 1)), (pltpu.roll(dout, width, 1), delta))
            ):
                high, rest = two_parts(column)
                column = jnp.where(
                    lane == width, high, jnp.where(lane == width + 1, rest, jnp.zeros_like(rest))
                )
                do_ref[:, pl.ds((2 * tile + head) * LANES, LANES)] = jnp.where(
                    lane < width, values.astype(LOW), column
                )

    @pl.when(jnp.logical_not(is_live(lens_ref, step, per_slot, block)))
    def _():
        do_ref[...] = jnp.zeros(do_ref.shape, LOW)

    @pl.when(step == pl.num_programs(0) - 1)
    def _():
        grad_ref[...] = acc_ref[...].astype(LOW)


def qkv_back_kernel(
    per_slot, counts, width, scale, lens_ref, dq_ref, dk_ref, dv_ref, raw_ref, normed_ref, w_ref, gh_ref,
    cos_ref, sin_ref, own_ref, other_ref, grad_ref, gain_ref, acc_ref, low_ref,
):
    step = pl.program_id(0)
    block = dq_ref.shape[0]
    q_tiles, kv_tiles = counts
    slot_step = lax.rem(step + per_slot, 2 * per_slot)

    @pl.when(step == 0)
    def _():
        acc_ref[...] = jnp.zeros(acc_ref.shape, F32)
        gain_ref[...] = jnp.zeros(gain_ref.shape, F32)

    live = is_live(lens_ref, slot_step, per_slot, block)

    def put(d_a):
        @pl.when(step < per_slot)
        def _():
            other_ref[...] = d_a.astype(LOW)

        @pl.when(step >= per_slot)
        def _():
            own_ref[...] = d_a

    @pl.when(live)
    def _():
        lane = lax.broadcasted_iota(jnp.int32, (block, LANES), 1)
        cosine, sine = cos_ref[...], sin_ref[...]

        def pair(ref, tile):
            return jnp.where(
                lane < width,
                ref[:, pl.ds(2 * tile * LANES, LANES)],
                pltpu.roll(ref[:, pl.ds((2 * tile + 1) * LANES, LANES)], width, 1),
            )

        for tile in range(q_tiles + 2 * kv_tiles):
            lanes = pl.ds(tile * LANES, LANES)
            if tile >= q_tiles + kv_tiles:
                low_ref[:, lanes] = pair(dv_ref, tile - q_tiles - kv_tiles).astype(LOW)
                continue
            is_query = tile < q_tiles
            if is_query:
                turned, row = dq_ref[:, lanes] * scale, 0
            else:
                turned, row = pair(dk_ref, tile - q_tiles), 1
            gain = gh_ref[row : row + 1, :]
            dy = turned * cosine + swap_halves(turned * sine, width)
            values = raw_ref[:, lanes]
            inverse = lax.rsqrt(head_sum(values * values, width) * (1.0 / width) + EPS)
            scaled = dy * gain
            inner = head_sum(values * scaled, width) * (1.0 / width)
            low_ref[:, lanes] = (
                inverse * scaled - values * (inverse * inverse * inverse * inner)
            ).astype(LOW)
            gain_ref[row : row + 1, :] += jnp.sum(dy * values * inverse, axis=0, keepdims=True)
        low = low_ref[...]
        acc_ref[...] += tn(normed_ref[...], low)
        put(nt(low, w_ref[...]))

    @pl.when(jnp.logical_not(live))
    def _():
        put(jnp.zeros(own_ref.shape, F32))

    @pl.when(step == pl.num_programs(0) - 1)
    def _():
        grad_ref[...] = acc_ref[...].astype(LOW)


def input_back_kernel(lens_ref, x_ref, part_ref, got_ref, dresid_ref, gain_ref, out_ref, sums_ref):
    step = pl.program_id(0)
    d_norm, d_gain = norm_back(
        x_ref[...].astype(F32), part_ref[...] + got_ref[...].astype(F32), gain_ref[...]
    )
    out_ref[...] = (dresid_ref[...] + d_norm).astype(LOW)

    @pl.when(step == 0)
    def _():
        sums_ref[...] = jnp.zeros(sums_ref.shape, F32)

    sums_ref[0:1, :] += jnp.sum(d_gain, axis=0, keepdims=True)


def assemble_kernel(chunks, half, folds, widths, *refs):
    parts, refs = take(refs, 4 * chunks)
    pairs, (gate_ref, up_ref, down_ref, *outs) = take(refs, 4)
    first = lax.rem(lax.axis_index("rep"), 2) == 0

    def sides(mine, other):
        return [jnp.where(first, mine, other), jnp.where(first, other, mine)]

    units = parts[0].shape[1] // 2
    piece = units // half
    for chunk in range(chunks):
        top, low, other_top, other_low = parts[4 * chunk : 4 * chunk + 4]
        for side, values in enumerate(sides(top[...], other_top[...])):
            for j, ref in enumerate((gate_ref, up_ref)):
                for i in range(half):
                    to = ((side * half + i) * chunks + chunk) * piece
                    start = j * units + i * piece
                    ref[:, to : to + piece] = values[:, start : start + piece].astype(F32)
        columns = down_ref.shape[2] // 2
        for side, values in enumerate(sides(low[...], other_low[...])):
            for fold in range(folds):
                down_ref[chunk * folds + fold, :, side * columns : (side + 1) * columns] = values[
                    :, fold * columns : (fold + 1) * columns
                ].astype(F32)
    columns = [pairs[0].shape[1], widths[0], widths[1], widths[1]]
    starts = [0, 0, widths[0], widths[0] + widths[1]]
    for ref, width, start, k in zip(outs, columns, starts, (0, 2, 2, 2)):
        mine, other = (one[:, start : start + width] for one in pairs[k : k + 2])
        for side, values in enumerate(sides(mine, other)):
            ref[:, side * width : (side + 1) * width] = values.astype(F32)


class Rows:
    def __init__(self, lens, rows, block):
        self.lens, self.block, self.per_slot = lens, block, rows // block

    def both(self, width):
        return pl.BlockSpec((self.block, width), lambda i, lens: (i, 0))

    def both_other_first(self, width):
        n = self.per_slot
        return pl.BlockSpec((self.block, width), lambda i, lens: (lax.rem(i + n, 2 * n), 0))

    def early(self, width):
        n = self.per_slot
        return pl.BlockSpec((self.block, width), lambda i, lens: (jnp.minimum(i, n - 1), 0))

    def late(self, width):
        n = self.per_slot
        return pl.BlockSpec((self.block, width), lambda i, lens: (jnp.maximum(i - n, 0), 0))

    def repeated(self, width):
        n = self.per_slot
        return pl.BlockSpec((self.block, width), lambda i, lens: (lax.rem(i, n), 0))

    def fixed(self, shape):
        return pl.BlockSpec(shape, lambda i, lens: (0, 0), pipeline_mode=pl.Buffered(1))

    def call(self, name, kernel, slots, in_specs, out_specs, outs, scratch, flops, *args):
        return pl.pallas_call(
            kernel,
            out_shape=[jax.ShapeDtypeStruct(shape, kind) for shape, kind in outs],
            grid_spec=pltpu.PrefetchScalarGridSpec(
                num_scalar_prefetch=1,
                grid=(slots * self.per_slot,),
                in_specs=in_specs,
                out_specs=out_specs,
                scratch_shapes=scratch,
            ),
            cost_estimate=pl.CostEstimate(
                flops=flops, bytes_accessed=1 << 24, transcendentals=0
            ),
            compiler_params=pltpu.CompilerParams(vmem_limit_bytes=60 << 20),
            name=name,
        )(self.lens, *args)


def local(
    inputs,
    lengths,
    gain_attn,
    w_query,
    w_key,
    w_value,
    gain_query,
    gain_key,
    w_out,
    gain_mlp,
    w_gate,
    w_up,
    w_down,
    cotangent,
):
    shards = lax.axis_size("shard")
    core = lax.axis_index("rep") % 2
    first = core == 0
    rows, width_all = inputs.shape[1], inputs.shape[2]
    head_width = gain_query.shape[0] * shards
    q_half, kv_half = w_query.shape[1] // 2, w_key.shape[1] // 2
    d_half = width_all // 2
    d_rows, ff_rows = w_query.shape[0], w_down.shape[0]
    block = min(256, rows)
    scale = 1.0 / math.sqrt(head_width)
    counts = (q_half // LANES, kv_half // LANES)

    def ordered(mine, other, axis):
        return jnp.where(
            first,
            jnp.concatenate([mine, other], axis=axis),
            jnp.concatenate([other, mine], axis=axis),
        )

    half_shards = shards // 2
    groups = lax.axis_size("rep") // 2
    chunks = 3
    piece = ff_rows // chunks
    units = half_shards * piece
    folds = 2 * units // d_half
    head_rows = gain_query.shape[0]

    def fold(part):
        return jnp.concatenate(jnp.split(part, folds, axis=-2), axis=-1)

    def unfold(part):
        return jnp.concatenate(jnp.split(part, folds, axis=-1), axis=-2)

    packed_rows = d_rows + piece // folds
    hbm = pl.BlockSpec(memory_space=pltpu.HBM)
    vmem = pl.BlockSpec(memory_space=pltpu.VMEM)
    chunk_sets = [list(range(chunks - 1)), [chunks - 1]]

    def pack(*refs):
        *refs, pack_a, pack_b, sems = refs
        packs = [
            (ref, [(i * packed_rows, chunk) for i, chunk in enumerate(some)])
            for ref, some in zip((pack_a, pack_b), chunk_sets)
        ]
        pack_kernel(shards, chunks, *refs, *packs, sems)

    if piece % LANES == 0:
        packs = pl.pallas_call(
            pack,
            out_shape=[
                jax.ShapeDtypeStruct((len(some) * packed_rows, 2 * units), LOW) for some in chunk_sets
            ],
            in_specs=[hbm] * 3,
            out_specs=[vmem] * 2,
            scratch_shapes=[pltpu.SemaphoreType.DMA((chunks * (2 * half_shards + folds),))],
            compiler_params=pltpu.CompilerParams(vmem_limit_bytes=32 << 20),
            name="pack",
        )(w_gate, w_up, w_down)
    else:

        def my_half(weight):
            half = weight.shape[1] // 2
            return jnp.where(first, weight[:, :half], weight[:, half:])

        def chunk_of(weight, chunk):
            columns = weight.reshape(d_rows, shards, chunks, piece)[:, :, chunk]
            return my_half(columns.reshape(d_rows, shards * piece))

        def packed_chunk(chunk):
            tall = fold(my_half(w_down)[chunk * piece : (chunk + 1) * piece])
            wide = jnp.concatenate([chunk_of(w_gate, chunk), chunk_of(w_up, chunk)], axis=1)
            return jnp.concatenate([wide, tall])

        packs = [jnp.concatenate([packed_chunk(k) for k in some]) for some in chunk_sets]
    gathered = [lax.all_gather(packs[0], "shard", axis=0)]
    later, _ = lax.optimization_barrier((packs[1], gathered[0]))
    gathered.append(lax.all_gather(later, "shard", axis=0))

    def gain_row(*gains):
        flat = jnp.concatenate(gains)
        return jnp.pad(flat, (0, max(d_rows, LANES) - flat.shape[0]))[None]

    gain_rows = jnp.pad(
        jnp.concatenate(
            [gain_row(gain_attn), gain_row(gain_mlp), gain_row(gain_query, gain_key)]
        ),
        ((0, 13), (0, 0)),
    )

    def half_of(width):
        return lambda core: core * width

    wide_parts = [
        (0, 0, half_of(q_half), 0, q_half),
        (1, 0, half_of(kv_half), q_half, kv_half),
        (2, 0, half_of(kv_half), q_half + kv_half, kv_half),
    ]
    tall_parts = [(3, 1, 0, w_out.shape[0])]
    copies = len(wide_parts) * (shards + 2) + len(tall_parts) * (2 * shards + 3) + shards + 1
    w_qkv, w_o, gains, x_other = pl.pallas_call(
        partial(gather_kernel, shards, wide_parts, tall_parts, (6, copies)),
        out_shape=[
            jax.ShapeDtypeStruct(shape, LOW)
            for shape in (
                (width_all, q_half + 2 * kv_half),
                (half_shards * w_out.shape[0], width_all),
                (shards,) + gain_rows.shape,
                inputs.shape[1:],
            )
        ],
        in_specs=[hbm] * 6,
        out_specs=[hbm] * 4,
        scratch_shapes=[pltpu.SemaphoreType.DMA((copies,)), pltpu.SemaphoreType.DMA((copies,))],
        compiler_params=pltpu.CompilerParams(collective_id=0, has_side_effects=True),
        name="gather",
    )(w_query, w_key, w_value, w_out, gain_rows, inputs[0])
    gain_a = gains[:, 0, :d_rows].reshape(1, -1).astype(F32)
    gain_m = gains[:, 1, :d_rows].reshape(1, -1).astype(F32)
    gain_q = gains[:, 2, :head_rows].reshape(1, -1).astype(F32)
    gain_k = gains[:, 2, head_rows : 2 * head_rows].reshape(1, -1).astype(F32)
    gain_h = jnp.tile(jnp.concatenate([gain_q, gain_k]), (4, LANES // head_width))

    lens = jnp.concatenate([lengths, core_swap(lengths)])
    valid = (jnp.arange(rows) < lengths[0])[:, None]
    x_own = inputs[0]
    g_own = jnp.where(valid, cotangent[0], jnp.zeros((), LOW))
    g_other = core_swap(g_own)
    over = Rows(lens, rows, block)
    cosine, sine = rope_tables(rows, head_width)
    full, total = 2 * rows, w_qkv.shape[1]
    qk = q_half + kv_half

    normed_a, raw, queries, keys, values = over.call(
        "qkv",
        partial(qkv_kernel, over.per_slot, counts, head_width, scale),
        2,
        [over.early(width_all), over.late(width_all), over.fixed(w_qkv.shape)]
        + [over.fixed(gain_a.shape), over.fixed(gain_h.shape)]
        + [over.repeated(LANES), over.repeated(LANES)],
        [over.both(width_all), over.both(qk), over.both(2 * q_half), over.both(2 * kv_half)]
        + [over.both(2 * kv_half)],
        [((full, width_all), LOW), ((full, qk), F32), ((full, 2 * q_half), LOW)]
        + [((full, 2 * kv_half), LOW)] * 2,
        [],
        2 * full * width_all * total,
        x_own, x_other, w_qkv, gain_a, gain_h, cosine, sine,
    )
    attended, queries = attend(lens, queries, keys, values, rows, head_width, block)
    part, send = over.call(
        "out",
        partial(out_kernel, over.per_slot),
        2,
        [over.both_other_first(q_half), over.fixed(w_o.shape)],
        [over.late(width_all), over.early(width_all)],
        [((rows, width_all), F32), ((rows, width_all), LOW)],
        [],
        2 * full * q_half * width_all,
        attended, w_o,
    )
    wide, slim = over.both(width_all), over.fixed(gain_m.shape)
    eight = (8, width_all)
    resid, normed_b, sums_a = over.call(
        "resid",
        resid_kernel,
        1,
        [wide, wide, wide, slim],
        [wide, wide, pl.BlockSpec(eight, lambda i, lens: (0, 0))],
        [((rows, width_all), F32), ((rows, width_all), LOW), (eight, F32)],
        [],
        1 << 24,
        x_own, part, core_swap(send), gain_m,
    )
    normed_b_other = core_swap(normed_b)

    def across(grad_rows):
        half = grad_rows.shape[1] // 2
        mine = lax.dynamic_slice_in_dim(grad_rows, core * half, half, axis=1)
        other = core_swap(lax.dynamic_slice_in_dim(grad_rows, (1 - core) * half, half, axis=1))
        return ordered(mine, other, 0)

    n = over.per_slot
    sums = []
    ff_grads, ff_levels, ff_totals = [], [], []
    packed_shape = (shards * packed_rows, 2 * units)
    level_shape = (packed_rows, 2 * units)
    first_rows = pl.BlockSpec((block, width_all), lambda i: (jnp.minimum(i, n - 1), 0))
    last_rows = pl.BlockSpec((block, width_all), lambda i: (jnp.maximum(i - n, 0), 0))
    all_rows = pl.BlockSpec((block, width_all), lambda i: (i, 0))

    wide_shape, tall_shape = (width_all, 2 * units), (units, width_all)
    for chunk in range(chunks):
        last = chunk == chunks - 1
        side = Side(
            shards,
            groups,
            [level_shape] if chunk >= 1 else [],
            [level_shape] if chunk >= 2 else [],
            2 * half_shards * folds,
        )
        late = chunk == chunks - 1
        sources = ff_grads[-1:] + ff_levels[-1:]
        ends = [first_rows] * 2 + [last_rows] * 2 if last else [all_rows] * 2
        end_shapes = [jax.ShapeDtypeStruct((full, width_all), F32)] * 2
        if last:
            end_shapes = [jax.ShapeDtypeStruct((rows, width_all), F32)] * 2 + [
                jax.ShapeDtypeStruct((rows, width_all), LOW)
            ] * 2
        outs = pl.pallas_call(
            partial(
                ffn_kernel, n, shards, bool(sums), last, side, 0 if late else chunk * packed_rows
            ),
            out_shape=end_shapes + [jax.ShapeDtypeStruct(packed_shape, LOW)] + side.outs(),
            grid=(2 * n,),
            in_specs=[first_rows, last_rows] * 2
            + [hbm]
            + [all_rows] * len(sums)
            + [hbm] * len(sources),
            out_specs=ends + [hbm] * (1 + len(side.outs())),
            scratch_shapes=[pltpu.VMEM(wide_shape, F32), pltpu.VMEM(tall_shape, F32)]
            + [pltpu.VMEM((units, d_half), LOW)]
            + [pltpu.VMEM(wide_shape, LOW), pltpu.VMEM(tall_shape, LOW)]
            + [pltpu.VMEM(packed_shape, LOW)]
            + [pltpu.SemaphoreType.DMA((shards + half_shards * folds,))]
            + side.scratch(),
            cost_estimate=pl.CostEstimate(
                flops=18 * full * width_all * units, bytes_accessed=1 << 25, transcendentals=0
            ),
            compiler_params=pltpu.CompilerParams(
                collective_id=2 + chunk, has_side_effects=True, vmem_limit_bytes=62 << 20
            ),
            name="ffn",
        )(normed_b, normed_b_other, g_own, g_other, gathered[late], *sums, *sources)
        sums = outs[: len(end_shapes)]
        ff_grads.append(outs[len(end_shapes)])
        rest = outs[len(end_shapes) + 1 :]
        ff_levels += rest[:1]
        ff_totals += rest[1:]
    mlp_part, db_part, mlp_send, db_send = sums
    db_got = core_swap(db_send)
    mlp_got = core_swap(mlp_send)
    output, d_resid, d_attn, sums_b = over.call(
        "resid_back",
        resid_back_kernel,
        1,
        [wide] * 6 + [slim],
        [wide, wide, wide, pl.BlockSpec(eight, lambda i, lens: (0, 0))],
        [((rows, width_all), LOW), ((rows, width_all), F32), ((rows, width_all), LOW)]
        + [(eight, F32)],
        [],
        1 << 24,
        resid, mlp_part, mlp_got, db_part, db_got, g_own, gain_m,
    )

    d_attn_other = core_swap(d_attn)
    d_heads, grad_out = over.call(
        "dout",
        partial(dout_kernel, over.per_slot, head_width),
        2,
        [over.early(width_all), over.late(width_all), over.both(q_half), over.fixed(w_o.shape)],
        [over.both(2 * q_half), over.fixed(w_o.shape)],
        [((full, 2 * q_half), LOW), (w_o.shape, LOW)],
        [pltpu.VMEM(w_o.shape, F32)],
        4 * full * q_half * width_all,
        d_attn, d_attn_other, attended, w_o,
    )
    grad_out = across(grad_out)
    o_level = (d_rows, d_half)
    d_query, d_key, d_value, ff_level, out_level, ff_total = attend_back(
        queries,
        keys,
        values,
        d_heads,
        rows,
        head_width,
        block,
        Side(shards, groups, [level_shape, o_level], [level_shape]),
        [ff_grads[-1], grad_out, ff_levels[-1]],
    )
    ff_totals.append(ff_total)
    turned = pl.BlockSpec((block, LANES), lambda i, lens: (lax.rem(i, n), 0))
    part, send, grad_qkv, gain_sums = over.call(
        "qkv_back",
        partial(qkv_back_kernel, over.per_slot, counts, head_width, scale),
        2,
        [over.both_other_first(q_half)]
        + [over.both_other_first(2 * kv_half)] * 2
        + [over.both_other_first(qk), over.both_other_first(width_all)]
        + [over.fixed(w_qkv.shape), over.fixed(gain_h.shape), turned, turned],
        [over.late(width_all), over.early(width_all), over.fixed(w_qkv.shape)]
        + [pl.BlockSpec((8, LANES), lambda i, lens: (0, 0))],
        [((rows, width_all), F32), ((rows, width_all), LOW), (w_qkv.shape, LOW)]
        + [((8, LANES), F32)],
        [pltpu.VMEM(w_qkv.shape, F32), pltpu.VMEM((block, total), LOW)],
        4 * full * width_all * total,
        d_query, d_key, d_value, raw, normed_a, w_qkv, gain_h, cosine, sine,
    )
    input_grad, sums_c = over.call(
        "input_back",
        input_back_kernel,
        1,
        [wide] * 4 + [slim],
        [wide, pl.BlockSpec(eight, lambda i, lens: (0, 0))],
        [((rows, width_all), LOW), (eight, F32)],
        [],
        1 << 24,
        x_own, part, core_swap(send), d_resid, gain_a,
    )
    mine, other, small = finish_sums(
        grad_qkv,
        lengths,
        [sums_a, sums_b, sums_c, gain_sums],
        [(2, 0), (1, 1), (0, 0), (0, 1), (1, 0), (3, 0), (3, 1)],
        [ff_level, out_level],
        ff_totals,
        shards,
        groups,
    )
    total_ga, total_gm = small[0], small[1]
    total_gh = small[5:7, :LANES].reshape(2, -1, head_width).sum(1)
    totals = jnp.concatenate([small[2:5].sum(1), small[7, :1]])
    statistics = jnp.sqrt(totals[:3] / (totals[3] * width_all))
    me = lax.axis_index("shard")

    def own_piece(vector):
        size = vector.shape[0] // shards
        return lax.dynamic_slice_in_dim(vector, me * size, size)

    ff_mine = ff_totals + [mine[0]]
    ff_other = list(other[3:]) + [other[0]]

    wide = (d_rows, shards * ff_rows)
    shapes = [wide, wide, (chunks * folds, piece // folds, width_all)]
    shapes += [w.shape for w in (w_out, w_query, w_key, w_value)]
    top = d_rows // 8
    low_rows = piece // folds // 8

    def blocks(part):
        return [
            pl.BlockSpec((top, part.shape[1]), lambda i: (i, 0)),
            pl.BlockSpec((low_rows, part.shape[1]), lambda i: (8 * top // low_rows + i, 0)),
        ]

    def whole(part):
        return pl.BlockSpec((top, part.shape[1]), lambda i: (i, 0))

    parts = [one for pair in zip(ff_mine, ff_other) for one in pair for _ in range(2)]
    specs = [one for pair in zip(ff_mine, ff_other) for part in pair for one in blocks(part)]
    pairs = [mine[1], other[1], mine[2], other[2]]
    grad_gate, grad_up, grad_down, grad_out, grad_query, grad_key, grad_value = pl.pallas_call(
        partial(assemble_kernel, chunks, half_shards, folds, (q_half, kv_half)),
        out_shape=[jax.ShapeDtypeStruct(shape, F32) for shape in shapes],
        grid=(8,),
        in_specs=specs + [whole(part) for part in pairs],
        out_specs=[pl.BlockSpec((top, shape[1]), lambda i: (i, 0)) for shape in shapes[:2]]
        + [pl.BlockSpec((shapes[2][0], low_rows, width_all), lambda i: (0, i, 0))]
        + [pl.BlockSpec((top, shape[1]), lambda i: (i, 0)) for shape in shapes[3:]],
        compiler_params=pltpu.CompilerParams(vmem_limit_bytes=48 << 20),
        name="assemble",
    )(*parts, *pairs)
    return (
        output[None],
        input_grad[None],
        own_piece(total_ga),
        grad_query,
        grad_key,
        grad_value,
        own_piece(total_gh[0]),
        own_piece(total_gh[1]),
        grad_out,
        own_piece(total_gm),
        grad_gate,
        grad_up,
        grad_down.reshape(w_down.shape),
        statistics,
    )


def solution(mesh):
    in_specs = (
        P(("rep", "shard"), None, None),
        P(("rep", "shard")),
        P("shard"),
        P("shard", None),
        P("shard", None),
        P("shard", None),
        P("shard"),
        P("shard"),
        P("shard", None),
        P("shard"),
        P("shard", None),
        P("shard", None),
        P("shard", None),
        P(("rep", "shard"), None, None),
    )
    out_specs = (
        P(("rep", "shard"), None, None),
        P(("rep", "shard"), None, None),
        P("shard"),
        P("shard", None),
        P("shard", None),
        P("shard", None),
        P("shard"),
        P("shard"),
        P("shard", None),
        P("shard"),
        P("shard", None),
        P("shard", None),
        P("shard", None),
        P(),
    )
    return jax.shard_map(local, mesh=mesh, in_specs=in_specs, out_specs=out_specs, check_vma=False)
```

```python
from functools import partial
import math

import jax
import jax.numpy as jnp
from jax import lax
from jax.experimental import pallas as pl
from jax.experimental.pallas import tpu as pltpu
from jax.sharding import PartitionSpec as P

EPS = 1e-05
ROPE_BASE = 1000000.0
F32 = jnp.float32
LOW = jnp.bfloat16
LANES = 128
MESH = pl.DeviceIdType.MESH


def rope_tables(row_count, head_width):
    half_width = head_width // 2
    frequency = jnp.power(
        jnp.float32(ROPE_BASE), -jnp.arange(half_width, dtype=jnp.float32) * 2.0 / head_width
    )
    angles = jnp.arange(row_count, dtype=jnp.float32)[:, None] * frequency[None, :]
    cosine, sine = jnp.cos(angles), jnp.sin(angles)
    repeats = LANES // head_width
    return jnp.tile(cosine, (1, 2 * repeats)), jnp.tile(
        jnp.concatenate([-sine, sine], axis=1), (1, repeats)
    )


def nn(left, right):
    return jnp.dot(left, right, preferred_element_type=F32)


def nt(left, right):
    return lax.dot_general(left, right, (((1,), (1,)), ((), ())), preferred_element_type=F32)


def tn(left, right):
    return lax.dot_general(left, right, (((0,), (0,)), ((), ())), preferred_element_type=F32)


def core_swap(x):
    pairs = [(i, i ^ 1) for i in range(lax.axis_size("rep"))]
    return lax.ppermute(x, "rep", pairs)


def place():
    rep = lax.axis_index("rep")
    return lax.axis_index("shard"), lax.div(rep, 2), lax.rem(rep, 2)


def device(shard, group, core):
    return {"rep": 2 * group + core, "shard": shard}


def meet(devices):
    barrier = pltpu.get_barrier_semaphore()
    for where in devices:
        pl.semaphore_signal(barrier, inc=1, device_id=where, device_id_type=MESH)
    pl.semaphore_wait(barrier, len(devices))


def remote(source, target, send, recv, where):
    return pltpu.make_async_remote_copy(
        src_ref=source,
        dst_ref=target,
        send_sem=send,
        recv_sem=recv,
        device_id=where,
        device_id_type=MESH,
    )


def at_rows(ref, start, size):
    return ref.at[pl.ds(pl.multiple_of(start, 8), size), :]


def at(ref, row, rows, column, columns):
    return ref.at[
        pl.ds(pl.multiple_of(row, 8), rows), pl.ds(pl.multiple_of(column, LANES), columns)
    ]


class Copies:
    def __init__(self, send, recv):
        self.send, self.recv, self.used = send, recv, 0

    def __call__(self, source, target, where):
        slot = self.used
        self.used += 1
        return remote(source, target, self.send.at[slot], self.recv.at[slot], where)


def neighbours(me):
    return me + 1 - 2 * lax.rem(me, 2), me + 2 - 4 * lax.div(me, 2), 3 - me


def gather_kernel(shards, wide_parts, tall_parts, count, *refs):
    *refs, send, recv = refs
    sources, targets = refs[: count[0]], refs[count[0] :]
    me, group, core = place()
    half = shards // 2
    partner = device(me, group, 1 - core)
    meet(
        [device(lax.rem(me + k, shards), group, c) for k in range(1, shards) for c in range(2)]
        + [partner]
    )
    copies = Copies(send, recv)
    sent, due = [], []

    def go(source, target, where):
        copy = copies(source, target, where)
        copy.start()
        sent.append(copy.wait_send)
        return copy

    def passed_on(wide):
        fast, slow, _ = neighbours(me)
        later = []
        for block, first, second in wide:
            rows = block(me).shape[0] // 2
            first.wait_recv()
            later.append(go(block(fast).at[pl.ds(0, rows), :], block(fast).at[pl.ds(0, rows), :], device(slow, group, core)))
            second.wait_recv()
            later.append(go(block(slow).at[pl.ds(rows, rows), :], block(slow).at[pl.ds(rows, rows), :], device(fast, group, core)))
        return later

    wide = []
    for source, target, column, to, columns in wide_parts:
        source, target = sources[source], targets[target]
        rows = source.shape[0]
        mine = at(source, 0, rows, column(core), columns)

        def block(shard, target=target, rows=rows, to=to, columns=columns):
            return at(target, shard * rows, rows, to, columns)

        if shards == 4:
            fast, slow, _ = neighbours(me)
            wide.append(
                (
                    block,
                    go(mine, block(me), device(fast, group, core)),
                    go(mine, block(me), device(slow, group, core)),
                )
            )
        else:
            for k in range(1, shards):
                due.append(go(mine, block(me), device(lax.rem(me + k, shards), group, core)))
        due.append(go(at(source, 0, rows, column(1 - core), columns), block(me), partner))
    owner = lax.div(me, half)
    tall = []
    for source, target, row, rows in tall_parts:
        source, target = sources[source], targets[target]
        columns = source.shape[1] // 2

        def block(shard, target=target, rows=rows, columns=columns):
            return at(target, lax.rem(shard, half) * rows, rows, 0, 2 * columns)

        mine = at(source, row, rows, core * columns, columns)
        goal = at(target, lax.rem(me, half) * rows, rows, core * columns, columns)
        steps = [1, 2] if shards == 4 else list(range(1, shards))
        arrivals = []
        for k in steps:
            if shards == 4:
                to = origin = neighbours(me)[k - 1]
            else:
                to, origin = lax.rem(me + k, shards), lax.rem(me + shards - k, shards)
            pair = []
            for side in range(2):
                copy = copies(mine, goal, device(to, group, owner))
                pl.when(core == side)(copy.start)
                sent.append((core == side, copy.wait_send))
                pair.append(copy)
            arrivals.append((lax.div(origin, half) == core, pair))
        whole = copies(
            at(source, row, rows, 0, 2 * columns), block(me), partner
        )
        pl.when(owner != core)(whole.start)
        sent.append((owner != core, whole.wait_send))
        due.append((owner == core, whole))
        if shards == 4:
            tall.append((block, rows // 2, arrivals))
        else:
            for condition, pair in arrivals:
                due.extend((condition, copy) for copy in pair)
    gains, given = sources[-2:], targets[-2:]
    for k in range(1, shards):
        due.append(go(gains[0], given[0].at[me], device(lax.rem(me + k, shards), group, core)))
    due.append(go(gains[0], given[0].at[me], partner))
    due.append(go(gains[1], given[1], partner))
    if shards == 4:
        due.extend(passed_on(wide))
        fast, slow, _ = neighbours(me)
        for block, rows, arrivals in tall:
            for number, (condition, pair) in enumerate(arrivals):
                start = number * rows
                from_, to = (fast, slow) if number == 0 else (slow, fast)
                part = block(from_).at[pl.ds(start, rows), :]
                copy = copies(part, part, device(to, group, core))

                @pl.when(condition)
                def _(pair=pair, copy=copy):
                    for one in pair:
                        one.wait_recv()
                    copy.start()

                sent.append((condition, copy.wait_send))
                due.append((owner != core, copy))
    for item in sent:
        pl.when(item[0])(item[1]) if isinstance(item, tuple) else item()
    for item in due:
        pl.when(item[0])(item[1].wait_recv) if isinstance(item, tuple) else item.wait_recv()


def pack_kernel(shards, chunks, gate_ref, up_ref, down_ref, *refs):
    *packs, sems = refs
    core = lax.rem(lax.axis_index("rep"), 2)
    half = shards // 2
    total, rows = down_ref.shape[0], gate_ref.shape[0]
    piece = total // chunks
    columns = down_ref.shape[1] // 2
    copies = []
    for pack in packs:
        for row, chunk in pack[1]:
            for j, ref in enumerate((gate_ref, up_ref)):
                for i in range(half):
                    start = (core * half + i) * total + chunk * piece
                    copies.append(
                        (
                            at(ref, 0, rows, start, piece),
                            pack[0].at[pl.ds(row, rows), pl.ds((j * half + i) * piece, piece)],
                        )
                    )
            folds = 2 * half * piece // columns
            size = piece // folds
            for i in range(folds):
                copies.append(
                    (
                        at(down_ref, chunk * piece + i * size, size, core * columns, columns),
                        pack[0].at[pl.ds(row + rows, size), pl.ds(i * columns, columns)],
                    )
                )
    copies = [pltpu.make_async_copy(a, b, sems.at[k]) for k, (a, b) in enumerate(copies)]
    for copy in copies:
        copy.start()
    for copy in copies:
        copy.wait()


def add_up(parts, target, least):
    total_rows = target.shape[0]
    rows = max(k for k in range(least, 97, least) if total_rows % k == 0)

    def some(i, _):
        here = pl.ds(pl.multiple_of(i * rows, rows), rows)
        total = parts[0][here, :].astype(F32)
        for part in parts[1:]:
            total += part[here, :].astype(F32)
        target[here, :] = total.astype(target.dtype)
        return 0

    lax.fori_loop(0, total_rows // rows, some, 0)


def reduce_over_plane(copies, load, shards, grad_ref, level, bufs):
    me, group, core = place()
    rows = level.shape[0]

    def block(shard, start=0, size=rows):
        return at_rows(grad_ref, shard * rows + start, size)

    own = bufs[0]
    local = pltpu.make_async_copy(block(me), own, load.at[0])
    if shards != 4:
        planes = bufs[1]
        out = [
            copies(block(lax.rem(me + k, shards)), planes.at[k - 1], device(lax.rem(me + k, shards), group, core))
            for k in range(1, shards)
        ]

        def start():
            local.start()
            for copy in out:
                copy.start()

        def end():
            local.wait()
            for copy in out:
                copy.wait_send()
                copy.wait_recv()
            add_up([own] + [planes.at[k] for k in range(shards - 1)], level, 16)

        return [start, idle, idle, end]
    fast, slow, across = neighbours(me)
    to_fast, to_slow = device(fast, group, core), device(slow, group, core)
    half = rows // 2
    planes, met_fast, met_slow, held_fast, held_slow = bufs[1:]
    upper, lower = pl.ds(0, half), pl.ds(half, half)
    loads = [
        local,
        pltpu.make_async_copy(block(fast, half, half), held_fast, load.at[1]),
        pltpu.make_async_copy(block(slow, 0, half), held_slow, load.at[2]),
    ]
    early = [
        copies(block(across, 0, half), met_fast, to_fast),
        copies(block(across, half, half), met_slow, to_slow),
        copies(block(fast, 0, half), planes.at[0, upper, :], to_fast),
        copies(block(slow, half, half), planes.at[1, lower, :], to_slow),
    ]
    late = [
        copies(held_fast, planes.at[0, lower, :], to_fast),
        copies(held_slow, planes.at[1, upper, :], to_slow),
    ]

    def start():
        for copy in early[:2] + loads:
            copy.start()

    def direct():
        for copy in early[2:]:
            copy.start()

    def merge():
        for copy in loads:
            copy.wait()
        for copy, met, held, out in (
            (early[1], met_slow, held_fast, late[0]),
            (early[0], met_fast, held_slow, late[1]),
        ):
            copy.wait_recv()
            add_up([held, met], held, 16)
            out.start()

    def end():
        for copy in early[2:] + late:
            copy.wait_recv()
        for copy in early + late:
            copy.wait_send()
        add_up([own, planes.at[0], planes.at[1]], level, 16)

    return [start, direct, merge, end]


def plane_buffers(shards, shape):
    half = (shape[0] // 2, shape[1])
    if shards != 4:
        return [pltpu.VMEM(shape, LOW), pltpu.VMEM((shards - 1,) + shape, LOW)]
    return [pltpu.VMEM(shape, LOW), pltpu.VMEM((2,) + shape, LOW)] + [pltpu.VMEM(half, LOW)] * 4


def reduce_over_line(copies, groups, source, part, total, bufs):
    me, group, core = place()
    if groups != 4:
        (slots,) = bufs
        out = [
            copies(source, slots.at[group], device(me, lax.rem(group + k, groups), core))
            for k in range(1, groups)
        ]

        def start():
            for copy in out:
                copy.start()

        def end():
            rows = part.shape[0]

            def some(i, _):
                here = pl.ds(pl.multiple_of(i * 8, 8), 8)
                slots[group, here, :] = part[here, :]
                return 0

            lax.fori_loop(0, rows // 8, some, 0)
            for copy in out:
                copy.wait_send()
                copy.wait_recv()
            add_up([slots.at[k] for k in range(groups)], total, 8)

        return [start, idle, idle, end]
    met, summed, other = bufs
    outer = jnp.logical_or(group == 0, group == groups - 1)
    inner = jnp.logical_not(outer)
    mate = device(me, group + 1 - 2 * lax.rem(group, 2), core)
    inward = copies(source, met, mate)
    between = copies(summed, other, device(me, groups - 1 - group, core))
    back = copies(total, total, mate)

    def start():
        pl.when(outer)(inward.start)

    def exchange():
        @pl.when(inner)
        def _():
            inward.wait_recv()
            add_up([part, met], summed, 16)
            between.start()

    def give():
        @pl.when(inner)
        def _():
            between.wait_recv()
            add_up([summed, other], total, 16)
            back.start()

    def end():
        @pl.when(outer)
        def _():
            inward.wait_send()
            back.wait_recv()

        @pl.when(inner)
        def _():
            between.wait_send()
            back.wait_send()

    return [start, exchange, give, end]


def idle():
    pass


def line_buffers(groups, shape):
    if groups != 4:
        return [pltpu.VMEM((groups,) + shape, LOW)]
    return [pltpu.VMEM(shape, LOW)] * 3


PARTS = 8


class LineSum:
    def __init__(self, copies, groups, source, part, total, bufs):
        rows = part.shape[0] // PARTS
        each = len(bufs) // PARTS
        self.parts = [
            reduce_over_line(
                copies,
                groups,
                at_rows(source, i * rows, rows),
                at_rows(part, i * rows, rows),
                at_rows(total, i * rows, rows),
                bufs[i * each : (i + 1) * each],
            )
            for i in range(PARTS)
        ]

    def run(self, part, stage):
        self.parts[part][stage]()

    @staticmethod
    def buffers(groups, shape):
        return line_buffers(groups, (shape[0] // PARTS, shape[1])) * PARTS

    @staticmethod
    def copies(groups):
        return PARTS * max(3, groups - 1)


class Side:
    def __init__(self, shards, groups, plane_shapes, line_shapes, extra=0):
        self.shards, self.groups, self.extra = shards, groups, extra
        self.plane_shapes, self.line_shapes = plane_shapes, line_shapes

    def outs(self):
        return [jax.ShapeDtypeStruct(shape, LOW) for shape in self.plane_shapes + self.line_shapes]

    def scratch(self):
        groups, shards = self.groups, self.shards
        shapes = [pltpu.VMEM(shape, LOW) for shape in self.plane_shapes + self.line_shapes]
        for shape in self.plane_shapes:
            shapes += plane_buffers(shards, shape)
        for shape in self.line_shapes:
            shapes += [pltpu.VMEM(shape, LOW)] + LineSum.buffers(groups, shape)
        count = 2 * self.shards + len(self.plane_shapes) * max(6, shards - 1)
        count += len(self.line_shapes) * LineSum.copies(groups) + self.extra
        loads = 4 * len(self.plane_shapes) + 2 * len(self.line_shapes) + 1
        return shapes + [pltpu.SemaphoreType.DMA((count,))] * 2 + [pltpu.SemaphoreType.DMA((loads,))]

    def run(self, step, sources, outs, bufs):
        *bufs, send, recv, load = bufs
        totals, bufs = take(bufs, len(outs))
        me, group, core = place()
        copies = Copies(send, recv)
        shards, groups = self.shards, self.groups

        @pl.when(step == 0)
        def _():
            meet(everyone_near(shards, groups))

        planes, lines, loads = [], [], []
        for i, shape in enumerate(self.plane_shapes):
            some, bufs = take(bufs, len(plane_buffers(shards, shape)))
            planes.append(
                reduce_over_plane(
                    copies, load.at[pl.ds(3 * i, 3)], shards, sources[i], totals[i], some
                )
            )
        first = len(self.plane_shapes)
        for i, shape in enumerate(self.line_shapes):
            (own,), bufs = take(bufs, 1)
            some, bufs = take(bufs, len(LineSum.buffers(groups, shape)))
            loads.append(
                pltpu.make_async_copy(sources[first + i], own, load.at[3 * first + i])
            )
            lines.append(LineSum(copies, groups, sources[first + i], own, totals[first + i], some))

        def begin():
            for stages in planes:
                stages[0]()
            for stages in planes:
                stages[1]()
            for part in range(PARTS):
                for line in lines:
                    line.run(part, 0)
            for one in loads:
                one.start()

        def load_done():
            for one in loads:
                one.wait()

        def of_lines(part, stage):
            def go():
                for line in lines:
                    line.run(part, stage)

            return go

        def merge():
            for stages in planes:
                stages[2]()

        plan = {
            0: [begin],
            1: [load_done, of_lines(0, 1)],
            2: [of_lines(1, 1)],
            3: [of_lines(2, 1), of_lines(3, 1), merge, of_lines(0, 2), of_lines(1, 2)],
            4: [of_lines(4, 1), of_lines(2, 2), of_lines(3, 2)],
            5: [of_lines(5, 1), of_lines(6, 1), of_lines(4, 2)],
            6: [of_lines(7, 1), of_lines(5, 2), of_lines(6, 2)],
            7: [of_lines(7, 2)],
        }
        for when, stages in plan.items():

            @pl.when(step == when)
            def _(stages=stages):
                for stage in stages:
                    stage()

        count = len(outs)
        stores = [
            pltpu.make_async_copy(total, out, load.at[load.shape[0] - 1 - count + i])
            for i, (total, out) in enumerate(zip(totals, outs))
        ]

        def end():
            for stages, store in zip(planes, stores):
                stages[3]()
                store.start()
            for part in range(PARTS):
                for line in lines:
                    line.run(part, 3)
            for store in stores[len(planes) :]:
                store.start()
            for store in stores:
                store.wait()

        return copies, end


class Blocks:
    def __init__(self, copies, partner, count, block, held, got):
        self.count, self.block = count, block
        self.copies = [
            copies(
                held.at[pl.ds(k % (held.shape[0] // block) * block, block), :],
                got.at[pl.ds(k * block, block), :],
                partner,
            )
            for k in range(count)
        ]
        self.slots = held.shape[0] // block
        self.held, self.got = held, got

    def begin(self, step, first):
        for k in range(self.count):

            @pl.when(step == first + k + 1)
            def _(k=k):
                self.copies[k].start()
                if k + 1 >= self.slots and k + 1 < self.count:
                    self.copies[k + 1 - self.slots].wait_send()

    def put(self, number, values):
        self.held[pl.ds(lax.rem(number, self.slots) * self.block, self.block), :] = values

    def take(self, step, first):
        for k in range(self.count):
            pl.when(step == first + k)(self.copies[k].wait_recv)
        start = jnp.clip(step - first, 0, self.count - 1) * self.block
        return self.got[pl.ds(pl.multiple_of(start, self.block), self.block), :]

    def end(self, sent_last, received):
        if sent_last:
            self.copies[-1].start()
        for k in range(max(0, self.count - self.slots), self.count):
            self.copies[k].wait_send()
        if received:
            for copy in self.copies:
                copy.wait_recv()


def everyone_near(shards, groups):
    me, group, core = place()
    return (
        [device(lax.rem(me + k, shards), group, core) for k in range(1, shards)]
        + [device(me, lax.rem(group + k, groups), core) for k in range(1, groups)]
        + [device(me, group, 1 - core)]
    )


def take(refs, count):
    return refs[:count], refs[count:]


def finish_kernel(shards, groups, counts, rows, length_ref, *refs):
    smalls, refs = take(refs, 1 + max(k for k, _ in rows))
    (grad_ref,), refs = take(refs, 1)
    lows, refs = take(refs, counts[0])
    ready, refs = take(refs, counts[1])
    n = counts[0] + 1
    mine, refs = take(refs, n)
    other, refs = take(refs, n + counts[1])
    (total_ref, level), refs = take(refs, 2)
    plane_bufs, refs = take(refs, len(plane_buffers(shards, (16, LANES))))
    own, refs = take(refs, counts[0])
    per_line = len(LineSum.buffers(groups, (32, LANES)))
    line_bufs = []
    for _ in range(n):
        some, refs = take(refs, per_line)
        line_bufs.append(some)
    small_a, small_b, small_c, send, recv, load = refs
    me, group, core = place()
    partner = device(me, group, 1 - core)
    plane = [device(lax.rem(me + k, shards), group, core) for k in range(1, shards)]
    line = [device(me, lax.rem(group + k, groups), core) for k in range(1, groups)]
    copies = Copies(send, recv)

    def go(source, target, where):
        copy = copies(source, target, where)
        copy.start()
        return copy

    def finish(some):
        for copy in some:
            copy.wait_send()
            copy.wait_recv()

    loads = [pltpu.make_async_copy(low, own[i], load.at[3 + i]) for i, low in enumerate(lows)]
    for copy in loads:
        copy.start()
    for i, (k, row) in enumerate(rows):
        values = smalls[k][row : row + 1, :]
        small_a[me, i : i + 1, : values.shape[1]] = values
        if values.shape[1] < small_a.shape[2]:
            rest = small_a.shape[2] - values.shape[1]
            small_a[me, i : i + 1, values.shape[1] :] = jnp.zeros((1, rest), F32)
    small_a[me, len(rows) :, :] = jnp.full(
        (small_a.shape[1] - len(rows), small_a.shape[2]), length_ref[0].astype(F32)
    )
    meet(everyone_near(shards, groups))
    stages = reduce_over_plane(copies, load.at[pl.ds(0, 3)], shards, grad_ref, level, plane_bufs)
    sums = [
        LineSum(copies, groups, low, own[i], mine[i], line_bufs[i]) for i, low in enumerate(lows)
    ]
    last = LineSum(copies, groups, level, level, mine[-1], line_bufs[-1])
    stages[0]()
    stages[1]()
    for part in range(PARTS):
        for one in sums:
            one.run(part, 0)
    swaps = [go(source, target, partner) for source, target in zip(ready, other[n:])]
    small_copies = [go(small_a.at[me], small_a.at[me], where) for where in plane]
    for copy in loads:
        copy.wait()
    finish(small_copies)
    small_b[group] = sum(small_a[k] for k in range(shards))
    small_copies = [go(small_b.at[group], small_b.at[group], where) for where in line]
    for part in range(PARTS // 2):
        for one in sums:
            one.run(part, 1)
    stages[2]()
    for part in range(PARTS // 2):
        for one in sums:
            one.run(part + PARTS // 2, 1)
            one.run(part, 2)
    finish(small_copies)
    small_c[core] = sum(small_b[k] for k in range(groups))
    small_copies = [go(small_c.at[core], small_c.at[core], partner)]
    stages[3]()
    for part in range(PARTS):
        last.run(part, 0)
    for part in range(PARTS // 2, PARTS):
        for one in sums:
            one.run(part, 2)
    for part in range(PARTS):
        last.run(part, 1)
        if part >= 2:
            last.run(part - 2, 2)
    for part in range(PARTS - 2, PARTS):
        last.run(part, 2)
    for part in range(PARTS):
        for one in sums:
            one.run(part, 3)
    swaps += [go(mine[i], other[i], partner) for i in range(counts[0])]
    for part in range(PARTS):
        last.run(part, 3)
    swaps.append(go(mine[-1], other[n - 1], partner))
    finish(small_copies)
    total_ref[...] = small_c[0] + small_c[1]
    finish(swaps)


def finish_sums(grad, length, smalls, rows, lows, ready, shards, groups):
    level = (grad.shape[0] // shards, grad.shape[1])
    shapes = [low.shape for low in lows] + [level]
    others = shapes + [one.shape for one in ready]
    vmem = pl.BlockSpec(memory_space=pltpu.VMEM)
    hbm = pl.BlockSpec(memory_space=pltpu.HBM)
    scratch = [pltpu.VMEM(level, LOW)] + plane_buffers(shards, level)
    scratch += [pltpu.VMEM(shape, LOW) for shape in shapes[:-1]]
    for shape in shapes:
        scratch += LineSum.buffers(groups, shape)
    count = 6 + 2 * shards + len(shapes) * LineSum.copies(groups) + len(others) + groups
    small = (8, max(one.shape[1] for one in smalls))
    outs = pl.pallas_call(
        partial(finish_kernel, shards, groups, (len(lows), len(ready)), rows),
        out_shape=[jax.ShapeDtypeStruct(shape, LOW) for shape in shapes + others]
        + [jax.ShapeDtypeStruct(small, F32)],
        in_specs=[pl.BlockSpec(memory_space=pltpu.SMEM)]
        + [vmem] * len(smalls)
        + [hbm] * (1 + len(lows) + len(ready)),
        out_specs=[vmem] * (len(shapes) + len(shapes)) + [hbm] * len(ready) + [vmem],
        scratch_shapes=scratch
        + [pltpu.VMEM((count,) + small, F32) for count in (shards, groups, 2)]
        + [pltpu.SemaphoreType.DMA((count,)), pltpu.SemaphoreType.DMA((count,))]
        + [pltpu.SemaphoreType.DMA((3 + len(lows),))],
        compiler_params=pltpu.CompilerParams(
            collective_id=1, has_side_effects=True, vmem_limit_bytes=56 << 20
        ),
        name="finish",
    )(length, *smalls, grad, *lows, *ready)
    n = len(shapes)
    return outs[:n], outs[n:-1], outs[-1]


def two_parts(column):
    high = column.astype(LOW)
    return high, (column - high.astype(F32)).astype(LOW)


def attend_kernel(block, width, lens_ref, q_ref, k_ref, v_ref, att_ref, qx_ref):
    rows = q_ref.shape[0]
    heads = q_ref.shape[1] // LANES
    length = lens_ref[pl.program_id(0)]
    lane = lax.broadcasted_iota(jnp.int32, (block, LANES), 1)
    keep = lax.broadcasted_iota(jnp.int32, (block, block), 1) <= lax.broadcasted_iota(
        jnp.int32, (block, block), 0
    )
    for step in range(rows // block):
        start = step * block
        here = pl.ds(start, block)

        @pl.when(start < length)
        def _():
            outs = []
            for head in range(heads):
                lanes = pl.ds(head * LANES, LANES)
                query = q_ref[here, lanes]
                probs = jnp.exp(nt(query, k_ref[here, :]))
                probs = jnp.where(keep, probs, 0.0).astype(LOW)
                total = nn(probs, v_ref[here, :])
                if step:
                    probs = jnp.exp(nt(query, k_ref[pl.ds(0, start), :])).astype(LOW)
                    total += nn(probs, v_ref[pl.ds(0, start), :])
                weight = total[:, width : width + 1]
                outs.append(total / weight)
                high, rest = two_parts(-jnp.log(weight))
                qx_ref[here, lanes] = jnp.where(
                    lane == width, high, jnp.where(lane == width + 1, rest, query)
                )
            for pair in range(heads // 2):
                att_ref[here, pl.ds(pair * LANES, LANES)] = jnp.where(
                    lane < width, outs[2 * pair], pltpu.roll(outs[2 * pair + 1], width, 1)
                ).astype(LOW)

        @pl.when(start >= length)
        def _():
            att_ref[here, :] = jnp.zeros((block, att_ref.shape[1]), LOW)
            qx_ref[here, :] = jnp.zeros((block, qx_ref.shape[1]), LOW)


def attend_back_kernel(block, width, side, q_ref, k_ref, v_ref, do_ref, *refs):
    count = len(side.plane_shapes) + len(side.line_shapes)
    sources, refs = take(refs, count)
    (dq_ref, dk_ref, dv_ref), refs = take(refs, 3)
    totals, bufs = take(refs, count)
    grid_step = pl.program_id(0) * pl.num_programs(1) + pl.program_id(1)
    _, end = side.run(grid_step, sources, totals, bufs)
    rows = q_ref.shape[0]
    heads = q_ref.shape[1] // LANES
    lane = lax.broadcasted_iota(jnp.int32, (block, LANES), 1)
    keep = lax.broadcasted_iota(jnp.int32, (block, block), 0) <= lax.broadcasted_iota(
        jnp.int32, (block, block), 1
    )
    dk_ref[...] = jnp.zeros(dk_ref.shape, F32)
    dv_ref[...] = jnp.zeros(dv_ref.shape, F32)
    for step in range(rows // block):
        start = step * block
        here = pl.ds(start, block)
        parts = []
        for head in range(heads):
            lanes = pl.ds(head * LANES, LANES)
            query = q_ref[here, lanes]
            dout = do_ref[here, lanes]

            def one(keys, masked):
                key, value = k_ref[keys, :], v_ref[keys, :]
                probs = jnp.exp(nt(key, query))
                if masked:
                    probs = jnp.where(keep, probs, 0.0)
                dscores = (probs * nt(value, dout)).astype(LOW)
                dv_ref[keys, :] += nn(probs.astype(LOW), dout)
                dk_ref[keys, :] += nn(dscores, query)
                return tn(dscores, key)

            dquery = one(here, True)
            if step:
                dquery += one(pl.ds(0, start), False)
            parts.append(dquery)
        for pair in range(heads // 2):
            dq_ref[here, pl.ds(pair * LANES, LANES)] = jnp.where(
                lane < width, parts[2 * pair], pltpu.roll(parts[2 * pair + 1], width, 1)
            )
    pl.when(grid_step == pl.num_programs(0) * pl.num_programs(1) - 1)(end)


def attention_grid(slots, groups, per_group, rows):
    wide = pl.BlockSpec((rows, per_group * LANES), lambda s, g, lens: (s, g))
    dense = pl.BlockSpec((rows, per_group * LANES // 2), lambda s, g, lens: (s, g))
    narrow = pl.BlockSpec((rows, LANES), lambda s, g, lens: (s, g))
    return (slots, groups), wide, dense, narrow


def attend(lens, queries, keys, values, rows, width, block):
    slots, groups = queries.shape[0] // rows, keys.shape[1] // LANES
    per_group = queries.shape[1] // LANES // groups
    grid, wide, dense, narrow = attention_grid(slots, groups, per_group, rows)
    flops = 4 * slots * groups * per_group * rows * rows * LANES
    return pl.pallas_call(
        partial(attend_kernel, block, width),
        out_shape=(
            jax.ShapeDtypeStruct((queries.shape[0], queries.shape[1] // 2), LOW),
            jax.ShapeDtypeStruct(queries.shape, LOW),
        ),
        grid_spec=pltpu.PrefetchScalarGridSpec(
            num_scalar_prefetch=1,
            grid=grid,
            in_specs=[wide, narrow, narrow],
            out_specs=[dense, wide],
        ),
        cost_estimate=pl.CostEstimate(flops=flops, bytes_accessed=1 << 23, transcendentals=0),
        name="attend",
    )(lens, queries, keys, values)


def attend_back(queries, keys, values, douts, rows, width, block, side, sources):
    slots, groups = queries.shape[0] // rows, keys.shape[1] // LANES
    per_group = queries.shape[1] // LANES // groups
    wide = pl.BlockSpec((rows, per_group * LANES), lambda s, g: (s, g))
    dense = pl.BlockSpec((rows, per_group * LANES // 2), lambda s, g: (s, g))
    narrow = pl.BlockSpec((rows, LANES), lambda s, g: (s, g))
    flops = 10 * slots * groups * per_group * rows * rows * LANES
    return pl.pallas_call(
        partial(attend_back_kernel, block, width, side),
        out_shape=[
            jax.ShapeDtypeStruct((queries.shape[0], queries.shape[1] // 2), F32),
            jax.ShapeDtypeStruct(keys.shape, F32),
            jax.ShapeDtypeStruct(keys.shape, F32),
        ]
        + side.outs(),
        grid=(slots, groups),
        in_specs=[wide, narrow, narrow, wide]
        + [pl.BlockSpec(memory_space=pltpu.HBM)] * len(sources),
        out_specs=[dense, narrow, narrow]
        + [pl.BlockSpec(memory_space=pltpu.HBM)] * len(side.outs()),
        scratch_shapes=side.scratch(),
        cost_estimate=pl.CostEstimate(flops=flops, bytes_accessed=1 << 24, transcendentals=0),
        compiler_params=pltpu.CompilerParams(
            collective_id=5, has_side_effects=True, vmem_limit_bytes=56 << 20
        ),
        name="attend_back",
    )(queries, keys, values, douts, *sources)


def swap_halves(values, width):
    lane = lax.broadcasted_iota(jnp.int32, values.shape, 1)
    half = width // 2
    return jnp.where(
        lane % width < half, pltpu.roll(values, LANES - half, 1), pltpu.roll(values, half, 1)
    )


def head_sum(values, width):
    same = lax.broadcasted_iota(jnp.int32, (LANES, LANES), 0) // width
    same = (same == lax.broadcasted_iota(jnp.int32, (LANES, LANES), 1) // width).astype(LOW)
    high, rest = two_parts(values)
    return nn(high, same) + nn(rest, same)


def row_rsqrt(values):
    return lax.rsqrt(jnp.mean(values * values, axis=1, keepdims=True) + EPS)


def is_live(lens_ref, step, per_slot, block):
    return lax.rem(step, per_slot) * block < lens_ref[lax.div(step, per_slot)]


def qkv_kernel(
    per_slot, counts, width, scale, lens_ref, own_ref, other_ref, w_ref, ga_ref, gh_ref, cos_ref, sin_ref,
    normed_ref, raw_ref, q_ref, k_ref, v_ref,
):
    step = pl.program_id(0)
    block = own_ref.shape[0]
    q_tiles, kv_tiles = counts

    @pl.when(is_live(lens_ref, step, per_slot, block))
    def _():
        x = jnp.where(step < per_slot, own_ref[...], other_ref[...]).astype(F32)
        normed = (x * row_rsqrt(x) * ga_ref[...]).astype(LOW)
        normed_ref[...] = normed
        lane = lax.broadcasted_iota(jnp.int32, (block, LANES), 1)
        zero = jnp.zeros((block, LANES), F32)
        ones = jnp.where(lane < width + 2, 1.0, 0.0)
        cosine, sine = cos_ref[...], sin_ref[...]

        def put(ref, tile, values, rest):
            ref[:, pl.ds(2 * tile * LANES, LANES)] = jnp.where(lane < width, values, rest).astype(LOW)
            ref[:, pl.ds((2 * tile + 1) * LANES, LANES)] = jnp.where(
                lane < width, pltpu.roll(values, width, 1), rest
            ).astype(LOW)

        for tile in range(q_tiles + 2 * kv_tiles):
            lanes = pl.ds(tile * LANES, LANES)
            if tile % 2 == 0:
                pair = nn(normed, w_ref[:, pl.ds(tile * LANES, 2 * LANES)])
            values = pair[:, (tile % 2) * LANES : (tile % 2 + 1) * LANES]
            if tile >= q_tiles + kv_tiles:
                put(v_ref, tile - q_tiles - kv_tiles, values, ones)
                continue
            raw_ref[:, lanes] = values
            is_query = tile < q_tiles
            gain = gh_ref[0:1, :] if is_query else gh_ref[1:2, :]
            values *= lax.rsqrt(head_sum(values * values, width) * (1.0 / width) + EPS) * gain
            values = values * cosine + swap_halves(values, width) * sine
            if is_query:
                put(q_ref, tile, values * scale, zero)
            else:
                put(k_ref, tile - q_tiles, values, ones)

    @pl.when(jnp.logical_not(is_live(lens_ref, step, per_slot, block)))
    def _():
        for ref in (normed_ref, raw_ref, q_ref, k_ref, v_ref):
            ref[...] = jnp.zeros(ref.shape, ref.dtype)


def out_kernel(
    per_slot, length_ref, att_ref, w_ref, x_ref, gain_ref, resid_ref, normed_ref, sums_ref,
    other_out, give, got, hold, other, send, recv, store,
):
    step = pl.program_id(0)
    block = att_ref.shape[0]
    me, group, core = place()
    partner = device(me, group, 1 - core)
    copies = Copies(send, recv)
    parts = Blocks(copies, partner, per_slot, block, give, got)
    normed_parts = Blocks(copies, partner, per_slot, block, hold, other)

    @pl.when(step == 0)
    def _():
        meet([partner])
        sums_ref[...] = jnp.zeros(sums_ref.shape, F32)

    parts.begin(step, 0)
    normed_parts.begin(step, per_slot)
    product = nn(att_ref[...], w_ref[...])

    @pl.when(step < per_slot)
    def _():
        parts.put(step, product.astype(LOW))

    @pl.when(step >= per_slot)
    def _():
        number = step - per_slot
        valid = lax.broadcasted_iota(jnp.int32, (block, 1), 0) + number * block < length_ref[0]
        attn_out = product + parts.take(step, per_slot).astype(F32)
        resid = x_ref[...].astype(F32) + attn_out
        resid_ref[...] = resid
        normed = (resid * row_rsqrt(resid) * gain_ref[...]).astype(LOW)
        normed_ref[...] = normed
        normed_parts.put(number, normed)
        for row, values in ((0, resid), (1, attn_out)):
            sums_ref[row : row + 1, :] += jnp.sum(
                jnp.where(valid, values * values, 0.0), axis=0, keepdims=True
            )

    @pl.when(step == 2 * per_slot - 1)
    def _():
        parts.end(False, False)
        normed_parts.end(True, True)
        copy = pltpu.make_async_copy(other, other_out, store.at[0])
        copy.start()
        copy.wait()


def ffn_kernel(
    per_slot, shards, chained, last, side, offset, x_own, x_other, g_own, g_other, gathered_ref, *refs
):
    if chained:
        (mlp_in, db_in), refs = take(refs, 2)
    if last:
        (length_ref, resid_ref, gain_ref), refs = take(refs, 3)
    count = len(side.plane_shapes) + len(side.line_shapes)
    sources, refs = take(refs, count)
    if last:
        (out_ref, dresid_ref, dattn_ref, sums_ref, dattn_out), refs = take(refs, 5)
    else:
        (mlp_ref, db_ref), refs = take(refs, 2)
    (grad_out,), refs = take(refs, 1)
    totals, refs = take(refs, count)
    (acc_ref, accd_ref, given_ref, w_ref, wd_ref, grad_ref, load), refs = take(refs, 7)
    exchange, bufs = take(refs, 6 if last else 0)
    step = pl.program_id(0)
    copies, end = side.run(step, sources, totals, bufs)
    own = step >= per_slot if last else step < per_slot
    units, depth = wd_ref.shape
    block = x_own.shape[0]
    me, group, core = place()
    partner = device(me, group, 1 - core)
    half, columns, d_rows = shards // 2, depth // 2, depth // shards
    packed = grad_ref.shape[0] // shards
    size = packed - d_rows
    folds = grad_ref.shape[1] // columns

    def folded(ref, shard, fold):
        return ref.at[shard, pl.ds(offset + d_rows, size), pl.ds(fold * columns, columns)]

    def unfolded(i, fold):
        return at(wd_ref, (i * folds + fold) * size, size, core * columns, columns)

    tiles = [(i, fold) for i in range(half) for fold in range(folds)]
    given = [
        copies(folded(gathered_ref, (1 - core) * half + i, fold), unfolded(i, fold), partner)
        for i, fold in tiles
    ]
    loads = [
        pltpu.make_async_copy(
            gathered_ref.at[shard, pl.ds(offset, d_rows), :],
            w_ref.at[pl.ds(shard * d_rows, d_rows), :],
            load.at[shard],
        )
        for shard in range(shards)
    ] + [
        pltpu.make_async_copy(
            folded(gathered_ref, core * half + i, fold), unfolded(i, fold), load.at[shards + k]
        )
        for k, (i, fold) in enumerate(tiles)
    ]

    if last:
        give_mlp, got_mlp, give_db, got_db, hold, other = exchange
        mlp_parts = Blocks(copies, partner, per_slot, block, give_mlp, got_mlp)
        db_parts = Blocks(copies, partner, per_slot, block, give_db, got_db)
        attn_parts = Blocks(copies, partner, per_slot, block, hold, other)
        mlp_parts.begin(step, 0)
        db_parts.begin(step, 0)
        attn_parts.begin(step, per_slot)

    @pl.when(step == 0)
    def _():
        if last:
            sums_ref[...] = jnp.zeros(sums_ref.shape, F32)
        for copy in given + loads:
            copy.start()
        acc_ref[...] = jnp.zeros(acc_ref.shape, F32)
        accd_ref[...] = jnp.zeros(accd_ref.shape, F32)
        for copy in loads:
            copy.wait()
        for copy in given:
            copy.wait_send()
            copy.wait_recv()

    x = jnp.where(own, x_own[...], x_other[...])
    g = jnp.where(own, g_own[...], g_other[...])
    gate = nn(x, w_ref[:, :units])
    up = nn(x, w_ref[:, units:])
    d_hidden = nt(g, wd_ref[...])
    sig = jax.nn.sigmoid(gate)
    silu = gate * sig
    hidden = (silu * up).astype(LOW)
    d_gate = (d_hidden * up * (sig * (1.0 + gate * (1.0 - sig)))).astype(LOW)
    d_up = (d_hidden * silu).astype(LOW)
    mlp = nn(hidden, wd_ref[...])
    d_b = nt(d_gate, w_ref[:, :units]) + nt(d_up, w_ref[:, units:])
    if chained:
        mlp += mlp_in[...]
        d_b += db_in[...]
    if last:

        @pl.when(step < per_slot)
        def _():
            mlp_parts.put(step, mlp.astype(LOW))
            db_parts.put(step, d_b.astype(LOW))

        @pl.when(step >= per_slot)
        def _():
            number = step - per_slot
            valid = lax.broadcasted_iota(jnp.int32, (block, 1), 0) + number * block < length_ref[0]
            resid = resid_ref[...]
            mlp_out = mlp + mlp_parts.take(step, per_slot).astype(F32)
            out_ref[...] = jnp.where(valid, resid + mlp_out, 0.0).astype(LOW)
            d_norm, d_gain = norm_back(
                resid, d_b + db_parts.take(step, per_slot).astype(F32), gain_ref[...]
            )
            d_resid = jnp.where(valid, g.astype(F32) + d_norm, 0.0)
            dresid_ref[...] = d_resid
            d_attn = d_resid.astype(LOW)
            dattn_ref[...] = d_attn
            attn_parts.put(number, d_attn)
            for row, values in ((0, mlp_out * mlp_out), (1, d_gain)):
                sums_ref[row : row + 1, :] += jnp.sum(
                    jnp.where(valid, values, 0.0), axis=0, keepdims=True
                )

    else:
        mlp_ref[...] = mlp
        db_ref[...] = d_b
    acc_ref[:, :units] += tn(x, d_gate)
    acc_ref[:, units:] += tn(x, d_up)
    accd_ref[...] += tn(hidden, g)

    @pl.when(step == pl.num_programs(0) - 1)
    def _():
        mine = pl.ds(pl.multiple_of(core * columns, columns), columns)
        theirs = pl.ds(pl.multiple_of((1 - core) * columns, columns), columns)
        given_ref[...] = accd_ref[:, theirs].astype(LOW)
        for shard in range(shards):
            grad_ref[pl.ds(shard * packed, d_rows), :] = acc_ref[
                pl.ds(shard * d_rows, d_rows), :
            ].astype(LOW)
        out = []
        for i in range(half):
            for fold in range(folds):
                row = i * folds * size + fold * size
                to = pl.ds(
                    pl.multiple_of((core * half + i) * packed + d_rows, 8), size
                )
                lanes = pl.ds(fold * columns, columns)
                out.append(
                    copies(
                        given_ref.at[pl.ds(row, size), :],
                        grad_ref.at[to, lanes],
                        partner,
                    )
                )
                out[-1].start()
                grad_ref[to, lanes] = accd_ref[pl.ds(row, size), mine].astype(LOW)
        for copy in out:
            copy.wait_send()
            copy.wait_recv()
        stores = [pltpu.make_async_copy(grad_ref, grad_out, load.at[0])]
        stores[0].start()
        if last:
            mlp_parts.end(False, False)
            db_parts.end(False, False)
            attn_parts.end(True, True)
            stores.append(pltpu.make_async_copy(other, dattn_out, load.at[1]))
            stores[1].start()
        end()
        for store in stores:
            store.wait()


def norm_back(values, dy, gain):
    inverse = row_rsqrt(values)
    scaled = dy * gain
    inner = jnp.mean(values * scaled, axis=1, keepdims=True)
    return inverse * scaled - values * (inverse * inverse * inverse * inner), dy * values * inverse


def dout_kernel(
    per_slot, width, lens_ref, own_ref, other_ref, att_ref, w_ref, do_ref, grad_ref, acc_ref
):
    step = pl.program_id(0)
    block = own_ref.shape[0]

    @pl.when(step == 0)
    def _():
        acc_ref[...] = jnp.zeros(acc_ref.shape, F32)

    @pl.when(is_live(lens_ref, step, per_slot, block))
    def _():
        d_attn = jnp.where(step < per_slot, own_ref[...], other_ref[...])
        lane = lax.broadcasted_iota(jnp.int32, (block, LANES), 1)
        att = att_ref[...]
        acc_ref[...] += tn(att, d_attn)
        for tile in range(att.shape[1] // LANES):
            lanes = slice(tile * LANES, (tile + 1) * LANES)
            if tile % 2 == 0:
                pair = nt(d_attn, w_ref[tile * LANES : (tile + 2) * LANES, :])
            dout = pair[:, (tile % 2) * LANES : (tile % 2 + 1) * LANES].astype(LOW).astype(F32)
            delta = -head_sum(dout * att[:, lanes].astype(F32), width)
            for head, (values, column) in enumerate(
                ((dout, pltpu.roll(delta, width, 1)), (pltpu.roll(dout, width, 1), delta))
            ):
                high, rest = two_parts(column)
                column = jnp.where(
                    lane == width, high, jnp.where(lane == width + 1, rest, jnp.zeros_like(rest))
                )
                do_ref[:, pl.ds((2 * tile + head) * LANES, LANES)] = jnp.where(
                    lane < width, values.astype(LOW), column
                )

    @pl.when(jnp.logical_not(is_live(lens_ref, step, per_slot, block)))
    def _():
        do_ref[...] = jnp.zeros(do_ref.shape, LOW)

    @pl.when(step == pl.num_programs(0) - 1)
    def _():
        grad_ref[...] = acc_ref[...].astype(LOW)


def qkv_back_kernel(
    per_slot, counts, width, scale, dq_ref, dk_ref, dv_ref, raw_ref, normed_ref, w_ref, gh_ref,
    cos_ref, sin_ref, x_ref, dresid_ref, ga_ref, out_ref, grad_ref, gain_ref, sums_ref,
    acc_ref, low_ref, give, got, send, recv,
):
    step = pl.program_id(0)
    block = dq_ref.shape[0]
    q_tiles, kv_tiles = counts
    me, group, core = place()
    partner = device(me, group, 1 - core)
    parts = Blocks(Copies(send, recv), partner, per_slot, block, give, got)

    @pl.when(step == 0)
    def _():
        meet([partner])
        acc_ref[...] = jnp.zeros(acc_ref.shape, F32)
        gain_ref[...] = jnp.zeros(gain_ref.shape, F32)
        sums_ref[...] = jnp.zeros(sums_ref.shape, F32)

    parts.begin(step, 0)
    lane = lax.broadcasted_iota(jnp.int32, (block, LANES), 1)
    cosine, sine = cos_ref[...], sin_ref[...]

    def pair(ref, tile):
        return jnp.where(
            lane < width,
            ref[:, pl.ds(2 * tile * LANES, LANES)],
            pltpu.roll(ref[:, pl.ds((2 * tile + 1) * LANES, LANES)], width, 1),
        )

    for tile in range(q_tiles + 2 * kv_tiles):
        lanes = pl.ds(tile * LANES, LANES)
        if tile >= q_tiles + kv_tiles:
            low_ref[:, lanes] = pair(dv_ref, tile - q_tiles - kv_tiles).astype(LOW)
            continue
        if tile < q_tiles:
            turned, row = dq_ref[:, lanes] * scale, 0
        else:
            turned, row = pair(dk_ref, tile - q_tiles), 1
        gain = gh_ref[row : row + 1, :]
        dy = turned * cosine + swap_halves(turned * sine, width)
        values = raw_ref[:, lanes]
        inverse = lax.rsqrt(head_sum(values * values, width) * (1.0 / width) + EPS)
        scaled = dy * gain
        inner = head_sum(values * scaled, width) * (1.0 / width)
        low_ref[:, lanes] = (
            inverse * scaled - values * (inverse * inverse * inverse * inner)
        ).astype(LOW)
        gain_ref[row : row + 1, :] += jnp.sum(dy * values * inverse, axis=0, keepdims=True)
    low = low_ref[...]
    acc_ref[...] += tn(normed_ref[...], low)
    d_a = nt(low, w_ref[...])

    @pl.when(step < per_slot)
    def _():
        parts.put(step, d_a.astype(LOW))

    @pl.when(step >= per_slot)
    def _():
        d_norm, d_gain = norm_back(
            x_ref[...].astype(F32), d_a + parts.take(step, per_slot).astype(F32), ga_ref[...]
        )
        out_ref[...] = (dresid_ref[...] + d_norm).astype(LOW)
        sums_ref[0:1, :] += jnp.sum(d_gain, axis=0, keepdims=True)

    @pl.when(step == 2 * per_slot - 1)
    def _():
        grad_ref[...] = acc_ref[...].astype(LOW)
        parts.end(False, False)


def assemble_kernel(chunks, half, folds, widths, *refs):
    parts, refs = take(refs, 4 * chunks)
    pairs, (gate_ref, up_ref, down_ref, *outs) = take(refs, 4)
    first = lax.rem(lax.axis_index("rep"), 2) == 0

    def sides(mine, other):
        return [jnp.where(first, mine, other), jnp.where(first, other, mine)]

    units = parts[0].shape[1] // 2
    piece = units // half
    for chunk in range(chunks):
        top, low, other_top, other_low = parts[4 * chunk : 4 * chunk + 4]
        for side, values in enumerate(sides(top[...], other_top[...])):
            for j, ref in enumerate((gate_ref, up_ref)):
                for i in range(half):
                    to = ((side * half + i) * chunks + chunk) * piece
                    start = j * units + i * piece
                    ref[:, to : to + piece] = values[:, start : start + piece].astype(F32)
        columns = down_ref.shape[2] // 2
        for side, values in enumerate(sides(low[...], other_low[...])):
            for fold in range(folds):
                down_ref[chunk * folds + fold, :, side * columns : (side + 1) * columns] = values[
                    :, fold * columns : (fold + 1) * columns
                ].astype(F32)
    columns = [pairs[0].shape[1], widths[0], widths[1], widths[1]]
    starts = [0, 0, widths[0], widths[0] + widths[1]]
    for ref, width, start, k in zip(outs, columns, starts, (0, 2, 2, 2)):
        mine, other = (one[:, start : start + width] for one in pairs[k : k + 2])
        for side, values in enumerate(sides(mine, other)):
            ref[:, side * width : (side + 1) * width] = values.astype(F32)


class Rows:
    def __init__(self, lens, rows, block):
        self.lens, self.block, self.per_slot = lens, block, rows // block

    def both(self, width):
        return pl.BlockSpec((self.block, width), lambda i, lens: (i, 0))

    def both_other_first(self, width):
        n = self.per_slot
        return pl.BlockSpec((self.block, width), lambda i, lens: (lax.rem(i + n, 2 * n), 0))

    def early(self, width):
        n = self.per_slot
        return pl.BlockSpec((self.block, width), lambda i, lens: (jnp.minimum(i, n - 1), 0))

    def late(self, width):
        n = self.per_slot
        return pl.BlockSpec((self.block, width), lambda i, lens: (jnp.maximum(i - n, 0), 0))

    def repeated(self, width):
        n = self.per_slot
        return pl.BlockSpec((self.block, width), lambda i, lens: (lax.rem(i, n), 0))

    def fixed(self, shape):
        return pl.BlockSpec(shape, lambda i, lens: (0, 0), pipeline_mode=pl.Buffered(1))

    def call(self, name, kernel, slots, in_specs, out_specs, outs, scratch, flops, *args):
        return pl.pallas_call(
            kernel,
            out_shape=[jax.ShapeDtypeStruct(shape, kind) for shape, kind in outs],
            grid_spec=pltpu.PrefetchScalarGridSpec(
                num_scalar_prefetch=1,
                grid=(slots * self.per_slot,),
                in_specs=in_specs,
                out_specs=out_specs,
                scratch_shapes=scratch,
            ),
            cost_estimate=pl.CostEstimate(
                flops=flops, bytes_accessed=1 << 24, transcendentals=0
            ),
            compiler_params=pltpu.CompilerParams(vmem_limit_bytes=60 << 20),
            name=name,
        )(self.lens, *args)


def local(
    inputs,
    lengths,
    gain_attn,
    w_query,
    w_key,
    w_value,
    gain_query,
    gain_key,
    w_out,
    gain_mlp,
    w_gate,
    w_up,
    w_down,
    cotangent,
):
    shards = lax.axis_size("shard")
    core = lax.axis_index("rep") % 2
    first = core == 0
    rows, width_all = inputs.shape[1], inputs.shape[2]
    head_width = gain_query.shape[0] * shards
    q_half, kv_half = w_query.shape[1] // 2, w_key.shape[1] // 2
    d_half = width_all // 2
    d_rows, ff_rows = w_query.shape[0], w_down.shape[0]
    block = min(256, rows)
    scale = 1.0 / math.sqrt(head_width)
    counts = (q_half // LANES, kv_half // LANES)

    def ordered(mine, other, axis):
        return jnp.where(
            first,
            jnp.concatenate([mine, other], axis=axis),
            jnp.concatenate([other, mine], axis=axis),
        )

    half_shards = shards // 2
    groups = lax.axis_size("rep") // 2
    chunks = 3
    piece = ff_rows // chunks
    units = half_shards * piece
    folds = 2 * units // d_half
    head_rows = gain_query.shape[0]

    def fold(part):
        return jnp.concatenate(jnp.split(part, folds, axis=-2), axis=-1)

    def unfold(part):
        return jnp.concatenate(jnp.split(part, folds, axis=-1), axis=-2)

    packed_rows = d_rows + piece // folds
    hbm = pl.BlockSpec(memory_space=pltpu.HBM)
    vmem = pl.BlockSpec(memory_space=pltpu.VMEM)
    chunk_sets = [list(range(chunks - 1)), [chunks - 1]]

    def pack(*refs):
        *refs, pack_a, pack_b, sems = refs
        packs = [
            (ref, [(i * packed_rows, chunk) for i, chunk in enumerate(some)])
            for ref, some in zip((pack_a, pack_b), chunk_sets)
        ]
        pack_kernel(shards, chunks, *refs, *packs, sems)

    if piece % LANES == 0:
        packs = pl.pallas_call(
            pack,
            out_shape=[
                jax.ShapeDtypeStruct((len(some) * packed_rows, 2 * units), LOW) for some in chunk_sets
            ],
            in_specs=[hbm] * 3,
            out_specs=[vmem] * 2,
            scratch_shapes=[pltpu.SemaphoreType.DMA((chunks * (2 * half_shards + folds),))],
            compiler_params=pltpu.CompilerParams(vmem_limit_bytes=32 << 20),
            name="pack",
        )(w_gate, w_up, w_down)
    else:

        def my_half(weight):
            half = weight.shape[1] // 2
            return jnp.where(first, weight[:, :half], weight[:, half:])

        def chunk_of(weight, chunk):
            columns = weight.reshape(d_rows, shards, chunks, piece)[:, :, chunk]
            return my_half(columns.reshape(d_rows, shards * piece))

        def packed_chunk(chunk):
            tall = fold(my_half(w_down)[chunk * piece : (chunk + 1) * piece])
            wide = jnp.concatenate([chunk_of(w_gate, chunk), chunk_of(w_up, chunk)], axis=1)
            return jnp.concatenate([wide, tall])

        packs = [jnp.concatenate([packed_chunk(k) for k in some]) for some in chunk_sets]
    gathered = [lax.all_gather(packs[0], "shard", axis=0)]

    def gain_row(*gains):
        flat = jnp.concatenate(gains)
        return jnp.pad(flat, (0, max(d_rows, LANES) - flat.shape[0]))[None]

    gain_rows = jnp.pad(
        jnp.concatenate(
            [gain_row(gain_attn), gain_row(gain_mlp), gain_row(gain_query, gain_key)]
        ),
        ((0, 13), (0, 0)),
    )

    def half_of(width):
        return lambda core: core * width

    wide_parts = [
        (0, 0, half_of(q_half), 0, q_half),
        (1, 0, half_of(kv_half), q_half, kv_half),
        (2, 0, half_of(kv_half), q_half + kv_half, kv_half),
    ]
    tall_parts = [(3, 1, 0, w_out.shape[0])]
    copies = len(wide_parts) * (shards + 2) + len(tall_parts) * (2 * shards + 3) + shards + 1
    w_qkv, w_o, gains, x_other = pl.pallas_call(
        partial(gather_kernel, shards, wide_parts, tall_parts, (6, copies)),
        out_shape=[
            jax.ShapeDtypeStruct(shape, LOW)
            for shape in (
                (width_all, q_half + 2 * kv_half),
                (half_shards * w_out.shape[0], width_all),
                (shards,) + gain_rows.shape,
                inputs.shape[1:],
            )
        ],
        in_specs=[hbm] * 6,
        out_specs=[hbm] * 4,
        scratch_shapes=[pltpu.SemaphoreType.DMA((copies,)), pltpu.SemaphoreType.DMA((copies,))],
        compiler_params=pltpu.CompilerParams(collective_id=0, has_side_effects=True),
        name="gather",
    )(w_query, w_key, w_value, w_out, gain_rows, inputs[0])
    gain_a = gains[:, 0, :d_rows].reshape(1, -1).astype(F32)
    gain_m = gains[:, 1, :d_rows].reshape(1, -1).astype(F32)
    gain_q = gains[:, 2, :head_rows].reshape(1, -1).astype(F32)
    gain_k = gains[:, 2, head_rows : 2 * head_rows].reshape(1, -1).astype(F32)
    gain_h = jnp.tile(jnp.concatenate([gain_q, gain_k]), (4, LANES // head_width))

    lens = jnp.concatenate([lengths, core_swap(lengths)])
    valid = (jnp.arange(rows) < lengths[0])[:, None]
    x_own = inputs[0]
    g_own = jnp.where(valid, cotangent[0], jnp.zeros((), LOW))
    g_other = core_swap(g_own)
    over = Rows(lens, rows, block)
    cosine, sine = rope_tables(rows, head_width)
    full, total = 2 * rows, w_qkv.shape[1]
    qk = q_half + kv_half

    normed_a, raw, queries, keys, values = over.call(
        "qkv",
        partial(qkv_kernel, over.per_slot, counts, head_width, scale),
        2,
        [over.early(width_all), over.late(width_all), over.fixed(w_qkv.shape)]
        + [over.fixed(gain_a.shape), over.fixed(gain_h.shape)]
        + [over.repeated(LANES), over.repeated(LANES)],
        [over.both(width_all), over.both(qk), over.both(2 * q_half), over.both(2 * kv_half)]
        + [over.both(2 * kv_half)],
        [((full, width_all), LOW), ((full, qk), F32), ((full, 2 * q_half), LOW)]
        + [((full, 2 * kv_half), LOW)] * 2,
        [],
        2 * full * width_all * total,
        x_own, x_other, w_qkv, gain_a, gain_h, cosine, sine,
    )
    attended, queries = attend(lens, queries, keys, values, rows, head_width, block)
    later, attended = lax.optimization_barrier((packs[1], attended))
    gathered.append(lax.all_gather(later, "shard", axis=0))
    n = over.per_slot
    eight = (8, width_all)
    first_rows = pl.BlockSpec((block, width_all), lambda i: (jnp.minimum(i, n - 1), 0))
    last_rows = pl.BlockSpec((block, width_all), lambda i: (jnp.maximum(i - n, 0), 0))
    all_rows = pl.BlockSpec((block, width_all), lambda i: (i, 0))
    smem = pl.BlockSpec(memory_space=pltpu.SMEM)

    def other_first(width):
        return pl.BlockSpec((block, width), lambda i: (lax.rem(i + n, 2 * n), 0))

    def held(shape):
        return pl.BlockSpec(shape, lambda i: (0, 0), pipeline_mode=pl.Buffered(1))

    sums_spec = pl.BlockSpec(eight, lambda i: (0, 0))
    slot_rows = pltpu.VMEM((rows, width_all), LOW)
    resid, normed_b, sums_a, normed_b_other = pl.pallas_call(
        partial(out_kernel, n),
        out_shape=[
            jax.ShapeDtypeStruct((rows, width_all), F32),
            jax.ShapeDtypeStruct((rows, width_all), LOW),
            jax.ShapeDtypeStruct(eight, F32),
            jax.ShapeDtypeStruct((rows, width_all), LOW),
        ],
        grid=(2 * n,),
        in_specs=[smem, other_first(q_half), held(w_o.shape), last_rows, held(gain_m.shape)],
        out_specs=[last_rows, last_rows, sums_spec, hbm],
        scratch_shapes=[pltpu.VMEM((2 * block, width_all), LOW), slot_rows, slot_rows, slot_rows]
        + [pltpu.SemaphoreType.DMA((2 * n,))] * 2
        + [pltpu.SemaphoreType.DMA((1,))],
        cost_estimate=pl.CostEstimate(
            flops=2 * full * q_half * width_all, bytes_accessed=1 << 24, transcendentals=0
        ),
        compiler_params=pltpu.CompilerParams(
            collective_id=6, has_side_effects=True, vmem_limit_bytes=40 << 20
        ),
        name="out",
    )(lengths, attended, w_o, x_own, gain_m)

    def across(grad_rows):
        half = grad_rows.shape[1] // 2
        mine = lax.dynamic_slice_in_dim(grad_rows, core * half, half, axis=1)
        other = core_swap(lax.dynamic_slice_in_dim(grad_rows, (1 - core) * half, half, axis=1))
        return ordered(mine, other, 0)

    sums = []
    ff_grads, ff_levels, ff_totals = [], [], []
    packed_shape = (shards * packed_rows, 2 * units)
    level_shape = (packed_rows, 2 * units)
    wide_shape, tall_shape = (width_all, 2 * units), (units, width_all)
    for chunk in range(chunks):
        last = chunk == chunks - 1
        side = Side(
            shards,
            groups,
            [level_shape] if chunk >= 1 else [],
            [level_shape] if chunk >= 2 else [],
            2 * half_shards * folds + 3 * n,
        )
        late = chunk == chunks - 1
        sources = ff_grads[-1:] + ff_levels[-1:]
        ends = [all_rows] * 2
        end_shapes = [jax.ShapeDtypeStruct((full, width_all), F32)] * 2
        own_rows, other_rows, sum_rows, more, more_specs, exchange = (
            first_rows, last_rows, all_rows, [], [], []
        )
        if last:
            own_rows, other_rows, sum_rows = last_rows, first_rows, other_first(width_all)
            more = [lengths, resid, gain_m]
            more_specs = [smem, last_rows, held(gain_m.shape)]
            ends = [last_rows] * 3 + [sums_spec, hbm]
            end_shapes = [
                jax.ShapeDtypeStruct((rows, width_all), LOW),
                jax.ShapeDtypeStruct((rows, width_all), F32),
                jax.ShapeDtypeStruct((rows, width_all), LOW),
                jax.ShapeDtypeStruct(eight, F32),
                jax.ShapeDtypeStruct((rows, width_all), LOW),
            ]
            exchange = [pltpu.VMEM((2 * block, width_all), LOW), slot_rows] * 3
        outs = pl.pallas_call(
            partial(
                ffn_kernel, n, shards, bool(sums), last, side, 0 if late else chunk * packed_rows
            ),
            out_shape=end_shapes + [jax.ShapeDtypeStruct(packed_shape, LOW)] + side.outs(),
            grid=(2 * n,),
            in_specs=[own_rows, other_rows] * 2
            + [hbm]
            + [sum_rows] * len(sums)
            + more_specs
            + [hbm] * len(sources),
            out_specs=ends + [hbm] * (1 + len(side.outs())),
            scratch_shapes=[pltpu.VMEM(wide_shape, F32), pltpu.VMEM(tall_shape, F32)]
            + [pltpu.VMEM((units, d_half), LOW)]
            + [pltpu.VMEM(wide_shape, LOW), pltpu.VMEM(tall_shape, LOW)]
            + [pltpu.VMEM(packed_shape, LOW)]
            + [pltpu.SemaphoreType.DMA((shards + half_shards * folds,))]
            + exchange
            + side.scratch(),
            cost_estimate=pl.CostEstimate(
                flops=18 * full * width_all * units, bytes_accessed=1 << 25, transcendentals=0
            ),
            compiler_params=pltpu.CompilerParams(
                collective_id=2 + chunk, has_side_effects=True, vmem_limit_bytes=67043328
            ),
            name="ffn",
        )(normed_b, normed_b_other, g_own, g_other, gathered[late], *sums, *more, *sources)
        sums = outs[: len(end_shapes)]
        ff_grads.append(outs[len(end_shapes)])
        rest = outs[len(end_shapes) + 1 :]
        ff_levels += rest[:1]
        ff_totals += rest[1:]
    output, d_resid, d_attn, sums_b, d_attn_other = sums

    d_heads, grad_out = over.call(
        "dout",
        partial(dout_kernel, over.per_slot, head_width),
        2,
        [over.early(width_all), over.late(width_all), over.both(q_half), over.fixed(w_o.shape)],
        [over.both(2 * q_half), over.fixed(w_o.shape)],
        [((full, 2 * q_half), LOW), (w_o.shape, LOW)],
        [pltpu.VMEM(w_o.shape, F32)],
        4 * full * q_half * width_all,
        d_attn, d_attn_other, attended, w_o,
    )
    grad_out = across(grad_out)
    o_level = (d_rows, d_half)
    d_query, d_key, d_value, ff_level, out_level, ff_total = attend_back(
        queries,
        keys,
        values,
        d_heads,
        rows,
        head_width,
        block,
        Side(shards, groups, [level_shape, o_level], [level_shape]),
        [ff_grads[-1], grad_out, ff_levels[-1]],
    )
    ff_totals.append(ff_total)
    turned = pl.BlockSpec((block, LANES), lambda i: (lax.rem(i, n), 0))
    input_grad, grad_qkv, gain_sums, sums_c = pl.pallas_call(
        partial(qkv_back_kernel, n, counts, head_width, scale),
        out_shape=[
            jax.ShapeDtypeStruct((rows, width_all), LOW),
            jax.ShapeDtypeStruct(w_qkv.shape, LOW),
            jax.ShapeDtypeStruct((8, LANES), F32),
            jax.ShapeDtypeStruct(eight, F32),
        ],
        grid=(2 * n,),
        in_specs=[other_first(q_half), other_first(2 * kv_half), other_first(2 * kv_half)]
        + [other_first(qk), other_first(width_all), held(w_qkv.shape), held(gain_h.shape)]
        + [turned, turned, last_rows, last_rows, held(gain_a.shape)],
        out_specs=[last_rows, held(w_qkv.shape)]
        + [pl.BlockSpec((8, LANES), lambda i: (0, 0)), sums_spec],
        scratch_shapes=[pltpu.VMEM(w_qkv.shape, F32), pltpu.VMEM((block, total), LOW)]
        + [pltpu.VMEM((2 * block, width_all), LOW), slot_rows]
        + [pltpu.SemaphoreType.DMA((n,))] * 2,
        cost_estimate=pl.CostEstimate(
            flops=4 * full * width_all * total, bytes_accessed=1 << 24, transcendentals=0
        ),
        compiler_params=pltpu.CompilerParams(
            collective_id=7, has_side_effects=True, vmem_limit_bytes=48 << 20
        ),
        name="qkv_back",
    )(
        d_query, d_key, d_value, raw, normed_a, w_qkv, gain_h, cosine, sine, x_own, d_resid, gain_a
    )
    mine, other, small = finish_sums(
        grad_qkv,
        lengths,
        [sums_a, sums_b, sums_c, gain_sums],
        [(2, 0), (1, 1), (0, 0), (0, 1), (1, 0), (3, 0), (3, 1)],
        [ff_level, out_level],
        ff_totals,
        shards,
        groups,
    )
    total_ga, total_gm = small[0], small[1]
    total_gh = small[5:7, :LANES].reshape(2, -1, head_width).sum(1)
    totals = jnp.concatenate([small[2:5].sum(1), small[7, :1]])
    statistics = jnp.sqrt(totals[:3] / (totals[3] * width_all))
    me = lax.axis_index("shard")

    def own_piece(vector):
        size = vector.shape[0] // shards
        return lax.dynamic_slice_in_dim(vector, me * size, size)

    ff_mine = ff_totals + [mine[0]]
    ff_other = list(other[3:]) + [other[0]]

    wide = (d_rows, shards * ff_rows)
    shapes = [wide, wide, (chunks * folds, piece // folds, width_all)]
    shapes += [w.shape for w in (w_out, w_query, w_key, w_value)]
    top = d_rows // 8
    low_rows = piece // folds // 8

    def blocks(part):
        return [
            pl.BlockSpec((top, part.shape[1]), lambda i: (i, 0)),
            pl.BlockSpec((low_rows, part.shape[1]), lambda i: (8 * top // low_rows + i, 0)),
        ]

    def whole(part):
        return pl.BlockSpec((top, part.shape[1]), lambda i: (i, 0))

    parts = [one for pair in zip(ff_mine, ff_other) for one in pair for _ in range(2)]
    specs = [one for pair in zip(ff_mine, ff_other) for part in pair for one in blocks(part)]
    pairs = [mine[1], other[1], mine[2], other[2]]
    grad_gate, grad_up, grad_down, grad_out, grad_query, grad_key, grad_value = pl.pallas_call(
        partial(assemble_kernel, chunks, half_shards, folds, (q_half, kv_half)),
        out_shape=[jax.ShapeDtypeStruct(shape, F32) for shape in shapes],
        grid=(8,),
        in_specs=specs + [whole(part) for part in pairs],
        out_specs=[pl.BlockSpec((top, shape[1]), lambda i: (i, 0)) for shape in shapes[:2]]
        + [pl.BlockSpec((shapes[2][0], low_rows, width_all), lambda i: (0, i, 0))]
        + [pl.BlockSpec((top, shape[1]), lambda i: (i, 0)) for shape in shapes[3:]],
        compiler_params=pltpu.CompilerParams(vmem_limit_bytes=48 << 20),
        name="assemble",
    )(*parts, *pairs)
    return (
        output[None],
        input_grad[None],
        own_piece(total_ga),
        grad_query,
        grad_key,
        grad_value,
        own_piece(total_gh[0]),
        own_piece(total_gh[1]),
        grad_out,
        own_piece(total_gm),
        grad_gate,
        grad_up,
        grad_down.reshape(w_down.shape),
        statistics,
    )


def solution(mesh):
    in_specs = (
        P(("rep", "shard"), None, None),
        P(("rep", "shard")),
        P("shard"),
        P("shard", None),
        P("shard", None),
        P("shard", None),
        P("shard"),
        P("shard"),
        P("shard", None),
        P("shard"),
        P("shard", None),
        P("shard", None),
        P("shard", None),
        P(("rep", "shard"), None, None),
    )
    out_specs = (
        P(("rep", "shard"), None, None),
        P(("rep", "shard"), None, None),
        P("shard"),
        P("shard", None),
        P("shard", None),
        P("shard", None),
        P("shard"),
        P("shard"),
        P("shard", None),
        P("shard"),
        P("shard", None),
        P("shard", None),
        P("shard", None),
        P(),
    )
    return jax.shard_map(local, mesh=mesh, in_specs=in_specs, out_specs=out_specs, check_vma=False)
```

```python
from functools import partial
import math

import jax
import jax.numpy as jnp
from jax import lax
from jax.experimental import pallas as pl
from jax.experimental.pallas import tpu as pltpu
from jax.sharding import PartitionSpec as P

EPS = 1e-05
ROPE_BASE = 1000000.0
F32 = jnp.float32
LOW = jnp.bfloat16
LANES = 128
MESH = pl.DeviceIdType.MESH


def rope_tables(row_count, head_width):
    half_width = head_width // 2
    frequency = jnp.power(
        jnp.float32(ROPE_BASE), -jnp.arange(half_width, dtype=jnp.float32) * 2.0 / head_width
    )
    angles = jnp.arange(row_count, dtype=jnp.float32)[:, None] * frequency[None, :]
    cosine, sine = jnp.cos(angles), jnp.sin(angles)
    repeats = LANES // head_width
    return jnp.tile(cosine, (1, 2 * repeats)), jnp.tile(
        jnp.concatenate([-sine, sine], axis=1), (1, repeats)
    )


def nn(left, right):
    return jnp.dot(left, right, preferred_element_type=F32)


def nt(left, right):
    return lax.dot_general(left, right, (((1,), (1,)), ((), ())), preferred_element_type=F32)


def tn(left, right):
    return lax.dot_general(left, right, (((0,), (0,)), ((), ())), preferred_element_type=F32)


def core_swap(x):
    pairs = [(i, i ^ 1) for i in range(lax.axis_size("rep"))]
    return lax.ppermute(x, "rep", pairs)


def place():
    rep = lax.axis_index("rep")
    return lax.axis_index("shard"), lax.div(rep, 2), lax.rem(rep, 2)


def device(shard, group, core):
    return {"rep": 2 * group + core, "shard": shard}


def meet(devices):
    barrier = pltpu.get_barrier_semaphore()
    for where in devices:
        pl.semaphore_signal(barrier, inc=1, device_id=where, device_id_type=MESH)
    pl.semaphore_wait(barrier, len(devices))


def remote(source, target, send, recv, where):
    return pltpu.make_async_remote_copy(
        src_ref=source,
        dst_ref=target,
        send_sem=send,
        recv_sem=recv,
        device_id=where,
        device_id_type=MESH,
    )


def at_rows(ref, start, size):
    return ref.at[pl.ds(pl.multiple_of(start, 8), size), :]


def at(ref, row, rows, column, columns):
    return ref.at[
        pl.ds(pl.multiple_of(row, 8), rows), pl.ds(pl.multiple_of(column, LANES), columns)
    ]


class Copies:
    def __init__(self, send, recv):
        self.send, self.recv, self.used = send, recv, 0

    def __call__(self, source, target, where):
        slot = self.used
        self.used += 1
        return remote(source, target, self.send.at[slot], self.recv.at[slot], where)


def neighbours(me):
    return me + 1 - 2 * lax.rem(me, 2), me + 2 - 4 * lax.div(me, 2), 3 - me


def gather_kernel(shards, wide_parts, tall_parts, count, *refs):
    *refs, send, recv = refs
    sources, targets = refs[: count[0]], refs[count[0] :]
    me, group, core = place()
    half = shards // 2
    partner = device(me, group, 1 - core)
    meet(
        [device(lax.rem(me + k, shards), group, c) for k in range(1, shards) for c in range(2)]
        + [partner]
    )
    copies = Copies(send, recv)
    sent, due = [], []

    def go(source, target, where):
        copy = copies(source, target, where)
        copy.start()
        sent.append(copy.wait_send)
        return copy

    def passed_on(wide):
        fast, slow, _ = neighbours(me)
        later = []
        for block, first, second in wide:
            rows = block(me).shape[0] // 2
            first.wait_recv()
            later.append(go(block(fast).at[pl.ds(0, rows), :], block(fast).at[pl.ds(0, rows), :], device(slow, group, core)))
            second.wait_recv()
            later.append(go(block(slow).at[pl.ds(rows, rows), :], block(slow).at[pl.ds(rows, rows), :], device(fast, group, core)))
        return later

    wide = []
    for source, target, column, to, columns in wide_parts:
        source, target = sources[source], targets[target]
        rows = source.shape[0]
        mine = at(source, 0, rows, column(core), columns)

        def block(shard, target=target, rows=rows, to=to, columns=columns):
            return at(target, shard * rows, rows, to, columns)

        if shards == 4:
            fast, slow, _ = neighbours(me)
            wide.append(
                (
                    block,
                    go(mine, block(me), device(fast, group, core)),
                    go(mine, block(me), device(slow, group, core)),
                )
            )
        else:
            for k in range(1, shards):
                due.append(go(mine, block(me), device(lax.rem(me + k, shards), group, core)))
        due.append(go(at(source, 0, rows, column(1 - core), columns), block(me), partner))
    owner = lax.div(me, half)
    tall = []
    for source, target, row, rows in tall_parts:
        source, target = sources[source], targets[target]
        columns = source.shape[1] // 2

        def block(shard, target=target, rows=rows, columns=columns):
            return at(target, lax.rem(shard, half) * rows, rows, 0, 2 * columns)

        mine = at(source, row, rows, core * columns, columns)
        goal = at(target, lax.rem(me, half) * rows, rows, core * columns, columns)
        steps = [1, 2] if shards == 4 else list(range(1, shards))
        arrivals = []
        for k in steps:
            if shards == 4:
                to = origin = neighbours(me)[k - 1]
            else:
                to, origin = lax.rem(me + k, shards), lax.rem(me + shards - k, shards)
            pair = []
            for side in range(2):
                copy = copies(mine, goal, device(to, group, owner))
                pl.when(core == side)(copy.start)
                sent.append((core == side, copy.wait_send))
                pair.append(copy)
            arrivals.append((lax.div(origin, half) == core, pair))
        whole = copies(
            at(source, row, rows, 0, 2 * columns), block(me), partner
        )
        pl.when(owner != core)(whole.start)
        sent.append((owner != core, whole.wait_send))
        due.append((owner == core, whole))
        if shards == 4:
            tall.append((block, rows // 2, arrivals))
        else:
            for condition, pair in arrivals:
                due.extend((condition, copy) for copy in pair)
    gains, given = sources[-2:], targets[-2:]
    for k in range(1, shards):
        due.append(go(gains[0], given[0].at[me], device(lax.rem(me + k, shards), group, core)))
    due.append(go(gains[0], given[0].at[me], partner))
    due.append(go(gains[1], given[1], partner))
    if shards == 4:
        due.extend(passed_on(wide))
        fast, slow, _ = neighbours(me)
        for block, rows, arrivals in tall:
            for number, (condition, pair) in enumerate(arrivals):
                start = number * rows
                from_, to = (fast, slow) if number == 0 else (slow, fast)
                part = block(from_).at[pl.ds(start, rows), :]
                copy = copies(part, part, device(to, group, core))

                @pl.when(condition)
                def _(pair=pair, copy=copy):
                    for one in pair:
                        one.wait_recv()
                    copy.start()

                sent.append((condition, copy.wait_send))
                due.append((owner != core, copy))
    for item in sent:
        pl.when(item[0])(item[1]) if isinstance(item, tuple) else item()
    for item in due:
        pl.when(item[0])(item[1].wait_recv) if isinstance(item, tuple) else item.wait_recv()


def pack_kernel(shards, chunks, gate_ref, up_ref, down_ref, *refs):
    *packs, sems = refs
    core = lax.rem(lax.axis_index("rep"), 2)
    half = shards // 2
    total, rows = down_ref.shape[0], gate_ref.shape[0]
    piece = total // chunks
    columns = down_ref.shape[1] // 2
    copies = []
    for pack in packs:
        for row, chunk in pack[1]:
            for j, ref in enumerate((gate_ref, up_ref)):
                for i in range(half):
                    start = (core * half + i) * total + chunk * piece
                    copies.append(
                        (
                            at(ref, 0, rows, start, piece),
                            pack[0].at[pl.ds(row, rows), pl.ds((j * half + i) * piece, piece)],
                        )
                    )
            folds = 2 * half * piece // columns
            size = piece // folds
            for i in range(folds):
                copies.append(
                    (
                        at(down_ref, chunk * piece + i * size, size, core * columns, columns),
                        pack[0].at[pl.ds(row + rows, size), pl.ds(i * columns, columns)],
                    )
                )
    copies = [pltpu.make_async_copy(a, b, sems.at[k]) for k, (a, b) in enumerate(copies)]
    for copy in copies:
        copy.start()
    for copy in copies:
        copy.wait()


def add_up(parts, target, least):
    total_rows = target.shape[0]
    rows = max(k for k in range(least, 97, least) if total_rows % k == 0)

    def some(i, _):
        here = pl.ds(pl.multiple_of(i * rows, rows), rows)
        total = parts[0][here, :].astype(F32)
        for part in parts[1:]:
            total += part[here, :].astype(F32)
        target[here, :] = total.astype(target.dtype)
        return 0

    lax.fori_loop(0, total_rows // rows, some, 0)


def reduce_over_plane(copies, load, shards, grad_ref, level, bufs):
    me, group, core = place()
    rows = level.shape[0]

    def block(shard, start=0, size=rows):
        return at_rows(grad_ref, shard * rows + start, size)

    own = bufs[0]
    local = pltpu.make_async_copy(block(me), own, load.at[0])
    if shards != 4:
        planes = bufs[1]
        out = [
            copies(block(lax.rem(me + k, shards)), planes.at[k - 1], device(lax.rem(me + k, shards), group, core))
            for k in range(1, shards)
        ]

        def start():
            local.start()
            for copy in out:
                copy.start()

        def end():
            local.wait()
            for copy in out:
                copy.wait_send()
                copy.wait_recv()
            add_up([own] + [planes.at[k] for k in range(shards - 1)], level, 16)

        return [start, idle, idle, end]
    fast, slow, across = neighbours(me)
    to_fast, to_slow = device(fast, group, core), device(slow, group, core)
    half = rows // 2
    planes, met_fast, met_slow, held_fast, held_slow = bufs[1:]
    upper, lower = pl.ds(0, half), pl.ds(half, half)
    loads = [
        local,
        pltpu.make_async_copy(block(fast, half, half), held_fast, load.at[1]),
        pltpu.make_async_copy(block(slow, 0, half), held_slow, load.at[2]),
    ]
    early = [
        copies(block(across, 0, half), met_fast, to_fast),
        copies(block(across, half, half), met_slow, to_slow),
        copies(block(fast, 0, half), planes.at[0, upper, :], to_fast),
        copies(block(slow, half, half), planes.at[1, lower, :], to_slow),
    ]
    late = [
        copies(held_fast, planes.at[0, lower, :], to_fast),
        copies(held_slow, planes.at[1, upper, :], to_slow),
    ]

    def start():
        for copy in early[:2] + loads:
            copy.start()

    def direct():
        for copy in early[2:]:
            copy.start()

    def merge():
        for copy in loads:
            copy.wait()
        for copy, met, held, out in (
            (early[1], met_slow, held_fast, late[0]),
            (early[0], met_fast, held_slow, late[1]),
        ):
            copy.wait_recv()
            add_up([held, met], held, 16)
            out.start()

    def end():
        for copy in early[2:] + late:
            copy.wait_recv()
        for copy in early + late:
            copy.wait_send()
        add_up([own, planes.at[0], planes.at[1]], level, 16)

    return [start, direct, merge, end]


def plane_buffers(shards, shape):
    half = (shape[0] // 2, shape[1])
    if shards != 4:
        return [pltpu.VMEM(shape, LOW), pltpu.VMEM((shards - 1,) + shape, LOW)]
    return [pltpu.VMEM(shape, LOW), pltpu.VMEM((2,) + shape, LOW)] + [pltpu.VMEM(half, LOW)] * 4


def reduce_over_line(copies, groups, source, part, total, bufs):
    me, group, core = place()
    if groups != 4:
        (slots,) = bufs
        out = [
            copies(source, slots.at[group], device(me, lax.rem(group + k, groups), core))
            for k in range(1, groups)
        ]

        def start():
            for copy in out:
                copy.start()

        def end():
            rows = part.shape[0]

            def some(i, _):
                here = pl.ds(pl.multiple_of(i * 8, 8), 8)
                slots[group, here, :] = part[here, :]
                return 0

            lax.fori_loop(0, rows // 8, some, 0)
            for copy in out:
                copy.wait_send()
                copy.wait_recv()
            add_up([slots.at[k] for k in range(groups)], total, 8)

        return [start, idle, idle, end]
    met, summed, other = bufs
    outer = jnp.logical_or(group == 0, group == groups - 1)
    inner = jnp.logical_not(outer)
    mate = device(me, group + 1 - 2 * lax.rem(group, 2), core)
    inward = copies(source, met, mate)
    between = copies(summed, other, device(me, groups - 1 - group, core))
    back = copies(total, total, mate)

    def start():
        pl.when(outer)(inward.start)

    def exchange():
        @pl.when(inner)
        def _():
            inward.wait_recv()
            add_up([part, met], summed, 16)
            between.start()

    def give():
        @pl.when(inner)
        def _():
            between.wait_recv()
            add_up([summed, other], total, 16)
            back.start()

    def end():
        @pl.when(outer)
        def _():
            inward.wait_send()
            back.wait_recv()

        @pl.when(inner)
        def _():
            between.wait_send()
            back.wait_send()

    return [start, exchange, give, end]


def idle():
    pass


def line_buffers(groups, shape):
    if groups != 4:
        return [pltpu.VMEM((groups,) + shape, LOW)]
    return [pltpu.VMEM(shape, LOW)] * 3


PARTS = 8


def parts_of(shape):
    return PARTS if shape[0] * shape[1] >= 1 << 18 else PARTS // 2


class LineSum:
    def __init__(self, copies, groups, source, part, total, bufs):
        self.count = parts_of(part.shape)
        rows = part.shape[0] // self.count
        each = len(bufs) // self.count
        self.parts = [
            reduce_over_line(
                copies,
                groups,
                at_rows(source, i * rows, rows),
                at_rows(part, i * rows, rows),
                at_rows(total, i * rows, rows),
                bufs[i * each : (i + 1) * each],
            )
            for i in range(self.count)
        ]

    def run(self, part, stage):
        if part < self.count:
            self.parts[part][stage]()

    def all(self, stage, first=0, last=None):
        for part in self.parts[first:last]:
            part[stage]()

    @staticmethod
    def buffers(groups, shape):
        count = parts_of(shape)
        return line_buffers(groups, (shape[0] // count, shape[1])) * count

    @staticmethod
    def copies(groups, shape):
        return parts_of(shape) * max(3, groups - 1)


class Side:
    def __init__(self, shards, groups, plane_shapes, line_shapes, extra=0):
        self.shards, self.groups, self.extra = shards, groups, extra
        self.plane_shapes, self.line_shapes = plane_shapes, line_shapes

    def outs(self):
        return [jax.ShapeDtypeStruct(shape, LOW) for shape in self.plane_shapes + self.line_shapes]

    def scratch(self):
        groups, shards = self.groups, self.shards
        shapes = [pltpu.VMEM(shape, LOW) for shape in self.plane_shapes + self.line_shapes]
        for shape in self.plane_shapes:
            shapes += plane_buffers(shards, shape)
        for shape in self.line_shapes:
            shapes += [pltpu.VMEM(shape, LOW)] + LineSum.buffers(groups, shape)
        count = 2 * self.shards + len(self.plane_shapes) * max(6, shards - 1)
        count += sum(LineSum.copies(groups, shape) for shape in self.line_shapes) + self.extra
        loads = 4 * len(self.plane_shapes) + 2 * len(self.line_shapes) + 1
        return shapes + [pltpu.SemaphoreType.DMA((count,))] * 2 + [pltpu.SemaphoreType.DMA((loads,))]

    def run(self, step, sources, outs, bufs):
        *bufs, send, recv, load = bufs
        totals, bufs = take(bufs, len(outs))
        me, group, core = place()
        copies = Copies(send, recv)
        shards, groups = self.shards, self.groups

        @pl.when(step == 0)
        def _():
            meet(everyone_near(shards, groups))

        planes, lines, loads = [], [], []
        for i, shape in enumerate(self.plane_shapes):
            some, bufs = take(bufs, len(plane_buffers(shards, shape)))
            planes.append(
                reduce_over_plane(
                    copies, load.at[pl.ds(3 * i, 3)], shards, sources[i], totals[i], some
                )
            )
        first = len(self.plane_shapes)
        for i, shape in enumerate(self.line_shapes):
            (own,), bufs = take(bufs, 1)
            some, bufs = take(bufs, len(LineSum.buffers(groups, shape)))
            source = at_rows(sources[first + i], 0, shape[0])
            loads.append(pltpu.make_async_copy(source, own, load.at[3 * first + i]))
            lines.append(LineSum(copies, groups, source, own, totals[first + i], some))

        def begin():
            for stages in planes:
                stages[0]()
            for stages in planes:
                stages[1]()
            for part in range(PARTS):
                for line in lines:
                    line.run(part, 0)
            for one in loads:
                one.start()

        def load_done():
            for one in loads:
                one.wait()

        def of_lines(part, stage):
            def go():
                for line in lines:
                    line.run(part, stage)

            return go

        def merge():
            for stages in planes:
                stages[2]()

        plan = {
            0: [begin],
            1: [load_done, of_lines(0, 1)],
            2: [of_lines(1, 1)],
            3: [of_lines(2, 1), of_lines(3, 1), merge, of_lines(0, 2), of_lines(1, 2)],
            4: [of_lines(4, 1), of_lines(2, 2), of_lines(3, 2)],
            5: [of_lines(5, 1), of_lines(6, 1), of_lines(4, 2)],
            6: [of_lines(7, 1), of_lines(5, 2), of_lines(6, 2)],
            7: [of_lines(7, 2)],
        }
        for when, stages in plan.items():

            @pl.when(step == when)
            def _(stages=stages):
                for stage in stages:
                    stage()

        count = len(outs)
        stores = [
            pltpu.make_async_copy(total, out, load.at[load.shape[0] - 1 - count + i])
            for i, (total, out) in enumerate(zip(totals, outs))
        ]

        def end():
            for stages, store in zip(planes, stores):
                stages[3]()
                store.start()
            for part in range(PARTS):
                for line in lines:
                    line.run(part, 3)
            for store in stores[len(planes) :]:
                store.start()
            for store in stores:
                store.wait()

        return copies, end


class Blocks:
    def __init__(self, copies, partner, count, block, held, got):
        self.count, self.block = count, block
        self.copies = [
            copies(
                held.at[pl.ds(k % (held.shape[0] // block) * block, block), :],
                got.at[pl.ds(k * block, block), :],
                partner,
            )
            for k in range(count)
        ]
        self.slots = held.shape[0] // block
        self.held, self.got = held, got

    def begin(self, step, first):
        for k in range(self.count):

            @pl.when(step == first + k + 1)
            def _(k=k):
                self.copies[k].start()
                if k + 1 >= self.slots and k + 1 < self.count:
                    self.copies[k + 1 - self.slots].wait_send()

    def put(self, number, values):
        self.held[pl.ds(lax.rem(number, self.slots) * self.block, self.block), :] = values

    def take(self, step, first):
        for k in range(self.count):
            pl.when(step == first + k)(self.copies[k].wait_recv)
        start = jnp.clip(step - first, 0, self.count - 1) * self.block
        return self.got[pl.ds(pl.multiple_of(start, self.block), self.block), :]

    def end(self, sent_last, received):
        if sent_last:
            self.copies[-1].start()
        for k in range(max(0, self.count - self.slots), self.count):
            self.copies[k].wait_send()
        if received:
            for copy in self.copies:
                copy.wait_recv()


def everyone_near(shards, groups):
    me, group, core = place()
    return (
        [device(lax.rem(me + k, shards), group, core) for k in range(1, shards)]
        + [device(me, lax.rem(group + k, groups), core) for k in range(1, groups)]
        + [device(me, group, 1 - core)]
    )


def take(refs, count):
    return refs[:count], refs[count:]


def finish_kernel(shards, groups, counts, rows, skip, length_ref, *refs):
    smalls, refs = take(refs, 1 + max(k for k, _ in rows))
    (grad_ref,), refs = take(refs, 1)
    lows, refs = take(refs, counts[0])
    ready, refs = take(refs, counts[1])
    n = counts[0] + 2
    mine_out, refs = take(refs, n)
    other, refs = take(refs, n + counts[1])
    (total_ref,), refs = take(refs, 1)
    mine, refs = take(refs, n)
    levels, refs = take(refs, 2)
    own, refs = take(refs, counts[0])
    plane_bufs = []
    for level in levels:
        some, refs = take(refs, len(plane_buffers(shards, level.shape)))
        plane_bufs.append(some)
    line_bufs = []
    for one in mine:
        some, refs = take(refs, len(LineSum.buffers(groups, one.shape)))
        line_bufs.append(some)
    small_a, small_b, small_c, send, recv, load = refs
    me, group, core = place()
    partner = device(me, group, 1 - core)
    plane = [device(lax.rem(me + k, shards), group, core) for k in range(1, shards)]
    line = [device(me, lax.rem(group + k, groups), core) for k in range(1, groups)]
    copies = Copies(send, recv)

    def go(source, target, where):
        copy = copies(source, target, where)
        copy.start()
        return copy

    def finish(some):
        for copy in some:
            copy.wait_send()
            copy.wait_recv()

    parts = [
        at_rows(low, 0 if i else skip, one.shape[0]) for i, (low, one) in enumerate(zip(lows, own))
    ]
    loads = [pltpu.make_async_copy(low, own[i], load.at[6 + i]) for i, low in enumerate(parts)]
    for copy in loads:
        copy.start()
    for i, (k, row) in enumerate(rows):
        values = smalls[k][row : row + 1, :]
        small_a[me, i : i + 1, : values.shape[1]] = values
        if values.shape[1] < small_a.shape[2]:
            rest = small_a.shape[2] - values.shape[1]
            small_a[me, i : i + 1, values.shape[1] :] = jnp.zeros((1, rest), F32)
    small_a[me, len(rows) :, :] = jnp.full(
        (small_a.shape[1] - len(rows), small_a.shape[2]), length_ref[0].astype(F32)
    )
    meet(everyone_near(shards, groups))
    columns = levels[0].shape[1]
    planes = [
        reduce_over_plane(
            copies,
            load.at[pl.ds(3 * i, 3)],
            shards,
            grad_ref.at[:, pl.ds(i * columns, columns)],
            level,
            plane_bufs[i],
        )
        for i, level in enumerate(levels)
    ]
    sums = [
        LineSum(copies, groups, source, part, mine[i], line_bufs[i])
        for i, (source, part) in enumerate(zip(parts + list(levels), list(own) + list(levels)))
    ]
    early, halves = sums[: counts[0]], sums[counts[0] :]
    for stages in planes:
        stages[0]()
        stages[1]()
    for one in early:
        one.all(0)
    small_copies = [go(small_a.at[me], small_a.at[me], where) for where in plane]
    swaps = [go(source, target, partner) for source, target in zip(ready, other[n:])]
    for copy in loads:
        copy.wait()
    planes[0][2]()
    planes[1][2]()
    for one in early:
        one.all(1, 0, one.count // 2)
    planes[0][3]()
    halves[0].all(0)
    finish(small_copies)
    small_b[group] = sum(small_a[k] for k in range(shards))
    small_copies = [go(small_b.at[group], small_b.at[group], where) for where in line]
    for one in early:
        one.all(1, one.count // 2)
        one.all(2, 0, one.count // 2)
    planes[1][3]()
    halves[1].all(0)
    for one in early:
        one.all(2, one.count // 2)
    finish(small_copies)
    small_c[core] = sum(small_b[k] for k in range(groups))
    small_copies = [go(small_c.at[core], small_c.at[core], partner)]
    halves[0].all(1)
    halves[1].all(1)
    halves[0].all(2)
    stores = []

    def hand(i):
        sums[i].all(3)
        swaps.append(go(mine[i], other[i], partner))
        stores.append(pltpu.make_async_copy(mine[i], mine_out[i], load.at[6 + counts[0] + i]))
        stores[-1].start()

    for i in range(counts[0]):
        hand(i)
    halves[1].all(2)
    hand(counts[0])
    hand(counts[0] + 1)
    finish(small_copies)
    total_ref[...] = small_c[0] + small_c[1]
    finish(swaps)
    for store in stores:
        store.wait()


def finish_sums(grad, length, smalls, rows, lows, skip, ready, shards, groups):
    level = (grad.shape[0] // shards, grad.shape[1] // 2)
    shapes = [(low.shape[0] - (0 if i else skip), low.shape[1]) for i, low in enumerate(lows)]
    shapes += [level] * 2
    others = shapes + [one.shape for one in ready]
    vmem = pl.BlockSpec(memory_space=pltpu.VMEM)
    hbm = pl.BlockSpec(memory_space=pltpu.HBM)
    scratch = [pltpu.VMEM(shape, LOW) for shape in shapes + [level] * 2 + shapes[: len(lows)]]
    for _ in range(2):
        scratch += plane_buffers(shards, level)
    for shape in shapes:
        scratch += LineSum.buffers(groups, shape)
    count = 2 * max(6, shards) + sum(LineSum.copies(groups, shape) for shape in shapes)
    count += len(others) + shards + groups
    small = (8, max(one.shape[1] for one in smalls))
    outs = pl.pallas_call(
        partial(finish_kernel, shards, groups, (len(lows), len(ready)), rows, skip),
        out_shape=[jax.ShapeDtypeStruct(shape, LOW) for shape in shapes + others]
        + [jax.ShapeDtypeStruct(small, F32)],
        in_specs=[pl.BlockSpec(memory_space=pltpu.SMEM)]
        + [vmem] * len(smalls)
        + [hbm] * (1 + len(lows) + len(ready)),
        out_specs=[hbm] * (len(shapes) + len(others)) + [vmem],
        scratch_shapes=scratch
        + [pltpu.VMEM((size,) + small, F32) for size in (shards, groups, 2)]
        + [pltpu.SemaphoreType.DMA((count,)), pltpu.SemaphoreType.DMA((count,))]
        + [pltpu.SemaphoreType.DMA((6 + len(lows) + len(shapes),))],
        compiler_params=pltpu.CompilerParams(
            collective_id=1, has_side_effects=True, vmem_limit_bytes=62 << 20
        ),
        name="finish",
    )(length, *smalls, grad, *lows, *ready)
    n = len(shapes)
    return outs[:n], outs[n:-1], outs[-1]


def two_parts(column):
    high = column.astype(LOW)
    return high, (column - high.astype(F32)).astype(LOW)


def attend_kernel(block, width, lens_ref, q_ref, k_ref, v_ref, att_ref, qx_ref):
    rows = q_ref.shape[0]
    heads = q_ref.shape[1] // LANES
    length = lens_ref[pl.program_id(0)]
    lane = lax.broadcasted_iota(jnp.int32, (block, LANES), 1)
    keep = lax.broadcasted_iota(jnp.int32, (block, block), 1) <= lax.broadcasted_iota(
        jnp.int32, (block, block), 0
    )
    for step in range(rows // block):
        start = step * block
        here = pl.ds(start, block)

        @pl.when(start < length)
        def _():
            outs = []
            for head in range(heads):
                lanes = pl.ds(head * LANES, LANES)
                query = q_ref[here, lanes]
                probs = jnp.exp(nt(query, k_ref[here, :]))
                probs = jnp.where(keep, probs, 0.0).astype(LOW)
                total = nn(probs, v_ref[here, :])
                if step:
                    probs = jnp.exp(nt(query, k_ref[pl.ds(0, start), :])).astype(LOW)
                    total += nn(probs, v_ref[pl.ds(0, start), :])
                weight = total[:, width : width + 1]
                outs.append(total / weight)
                high, rest = two_parts(-jnp.log(weight))
                qx_ref[here, lanes] = jnp.where(
                    lane == width, high, jnp.where(lane == width + 1, rest, query)
                )
            for pair in range(heads // 2):
                att_ref[here, pl.ds(pair * LANES, LANES)] = jnp.where(
                    lane < width, outs[2 * pair], pltpu.roll(outs[2 * pair + 1], width, 1)
                ).astype(LOW)

        @pl.when(start >= length)
        def _():
            att_ref[here, :] = jnp.zeros((block, att_ref.shape[1]), LOW)
            qx_ref[here, :] = jnp.zeros((block, qx_ref.shape[1]), LOW)


def attend_back_kernel(block, width, side, q_ref, k_ref, v_ref, do_ref, *refs):
    count = len(side.plane_shapes) + len(side.line_shapes)
    sources, refs = take(refs, count)
    (dq_ref, dk_ref, dv_ref), refs = take(refs, 3)
    totals, bufs = take(refs, count)
    grid_step = pl.program_id(0) * pl.num_programs(1) + pl.program_id(1)
    _, end = side.run(grid_step, sources, totals, bufs)
    rows = q_ref.shape[0]
    heads = q_ref.shape[1] // LANES
    lane = lax.broadcasted_iota(jnp.int32, (block, LANES), 1)
    keep = lax.broadcasted_iota(jnp.int32, (block, block), 0) <= lax.broadcasted_iota(
        jnp.int32, (block, block), 1
    )
    dk_ref[...] = jnp.zeros(dk_ref.shape, F32)
    dv_ref[...] = jnp.zeros(dv_ref.shape, F32)
    for step in range(rows // block):
        start = step * block
        here = pl.ds(start, block)
        parts = []
        for head in range(heads):
            lanes = pl.ds(head * LANES, LANES)
            query = q_ref[here, lanes]
            dout = do_ref[here, lanes]

            def one(keys, masked):
                key, value = k_ref[keys, :], v_ref[keys, :]
                probs = jnp.exp(nt(key, query))
                if masked:
                    probs = jnp.where(keep, probs, 0.0)
                dscores = (probs * nt(value, dout)).astype(LOW)
                dv_ref[keys, :] += nn(probs.astype(LOW), dout)
                dk_ref[keys, :] += nn(dscores, query)
                return tn(dscores, key)

            dquery = one(here, True)
            if step:
                dquery += one(pl.ds(0, start), False)
            parts.append(dquery)
        for pair in range(heads // 2):
            dq_ref[here, pl.ds(pair * LANES, LANES)] = jnp.where(
                lane < width, parts[2 * pair], pltpu.roll(parts[2 * pair + 1], width, 1)
            )
    pl.when(grid_step == pl.num_programs(0) * pl.num_programs(1) - 1)(end)


def attention_grid(slots, groups, per_group, rows):
    wide = pl.BlockSpec((rows, per_group * LANES), lambda s, g, lens: (s, g))
    dense = pl.BlockSpec((rows, per_group * LANES // 2), lambda s, g, lens: (s, g))
    narrow = pl.BlockSpec((rows, LANES), lambda s, g, lens: (s, g))
    return (slots, groups), wide, dense, narrow


def attend(lens, queries, keys, values, rows, width, block):
    slots, groups = queries.shape[0] // rows, keys.shape[1] // LANES
    per_group = queries.shape[1] // LANES // groups
    grid, wide, dense, narrow = attention_grid(slots, groups, per_group, rows)
    flops = 4 * slots * groups * per_group * rows * rows * LANES
    return pl.pallas_call(
        partial(attend_kernel, block, width),
        out_shape=(
            jax.ShapeDtypeStruct((queries.shape[0], queries.shape[1] // 2), LOW),
            jax.ShapeDtypeStruct(queries.shape, LOW),
        ),
        grid_spec=pltpu.PrefetchScalarGridSpec(
            num_scalar_prefetch=1,
            grid=grid,
            in_specs=[wide, narrow, narrow],
            out_specs=[dense, wide],
        ),
        cost_estimate=pl.CostEstimate(flops=flops, bytes_accessed=1 << 23, transcendentals=0),
        name="attend",
    )(lens, queries, keys, values)


def attend_back(queries, keys, values, douts, rows, width, block, side, sources):
    slots, groups = queries.shape[0] // rows, keys.shape[1] // LANES
    per_group = queries.shape[1] // LANES // groups
    wide = pl.BlockSpec((rows, per_group * LANES), lambda s, g: (s, g))
    dense = pl.BlockSpec((rows, per_group * LANES // 2), lambda s, g: (s, g))
    narrow = pl.BlockSpec((rows, LANES), lambda s, g: (s, g))
    flops = 10 * slots * groups * per_group * rows * rows * LANES
    return pl.pallas_call(
        partial(attend_back_kernel, block, width, side),
        out_shape=[
            jax.ShapeDtypeStruct((queries.shape[0], queries.shape[1] // 2), F32),
            jax.ShapeDtypeStruct(keys.shape, F32),
            jax.ShapeDtypeStruct(keys.shape, F32),
        ]
        + side.outs(),
        grid=(slots, groups),
        in_specs=[wide, narrow, narrow, wide]
        + [pl.BlockSpec(memory_space=pltpu.HBM)] * len(sources),
        out_specs=[dense, narrow, narrow]
        + [pl.BlockSpec(memory_space=pltpu.HBM)] * len(side.outs()),
        scratch_shapes=side.scratch(),
        cost_estimate=pl.CostEstimate(flops=flops, bytes_accessed=1 << 24, transcendentals=0),
        compiler_params=pltpu.CompilerParams(
            collective_id=5, has_side_effects=True, vmem_limit_bytes=62 << 20
        ),
        name="attend_back",
    )(queries, keys, values, douts, *sources)


def swap_halves(values, width):
    lane = lax.broadcasted_iota(jnp.int32, values.shape, 1)
    half = width // 2
    return jnp.where(
        lane % width < half, pltpu.roll(values, LANES - half, 1), pltpu.roll(values, half, 1)
    )


def head_sum(values, width):
    same = lax.broadcasted_iota(jnp.int32, (LANES, LANES), 0) // width
    same = (same == lax.broadcasted_iota(jnp.int32, (LANES, LANES), 1) // width).astype(LOW)
    high, rest = two_parts(values)
    return nn(high, same) + nn(rest, same)


def row_rsqrt(values):
    return lax.rsqrt(jnp.mean(values * values, axis=1, keepdims=True) + EPS)


def is_live(lens_ref, step, per_slot, block):
    return lax.rem(step, per_slot) * block < lens_ref[lax.div(step, per_slot)]


def qkv_kernel(
    per_slot, counts, width, scale, lens_ref, own_ref, other_ref, w_ref, ga_ref, gh_ref, cos_ref, sin_ref,
    normed_ref, raw_ref, q_ref, k_ref, v_ref,
):
    step = pl.program_id(0)
    block = own_ref.shape[0]
    q_tiles, kv_tiles = counts

    @pl.when(is_live(lens_ref, step, per_slot, block))
    def _():
        x = jnp.where(step < per_slot, own_ref[...], other_ref[...]).astype(F32)
        normed = (x * row_rsqrt(x) * ga_ref[...]).astype(LOW)
        normed_ref[...] = normed
        lane = lax.broadcasted_iota(jnp.int32, (block, LANES), 1)
        zero = jnp.zeros((block, LANES), F32)
        ones = jnp.where(lane < width + 2, 1.0, 0.0)
        cosine, sine = cos_ref[...], sin_ref[...]

        def put(ref, tile, values, rest):
            ref[:, pl.ds(2 * tile * LANES, LANES)] = jnp.where(lane < width, values, rest).astype(LOW)
            ref[:, pl.ds((2 * tile + 1) * LANES, LANES)] = jnp.where(
                lane < width, pltpu.roll(values, width, 1), rest
            ).astype(LOW)

        for tile in range(q_tiles + 2 * kv_tiles):
            lanes = pl.ds(tile * LANES, LANES)
            if tile % 2 == 0:
                pair = nn(normed, w_ref[:, pl.ds(tile * LANES, 2 * LANES)])
            values = pair[:, (tile % 2) * LANES : (tile % 2 + 1) * LANES]
            if tile >= q_tiles + kv_tiles:
                put(v_ref, tile - q_tiles - kv_tiles, values, ones)
                continue
            raw_ref[:, lanes] = values
            is_query = tile < q_tiles
            gain = gh_ref[0:1, :] if is_query else gh_ref[1:2, :]
            values *= lax.rsqrt(head_sum(values * values, width) * (1.0 / width) + EPS) * gain
            values = values * cosine + swap_halves(values, width) * sine
            if is_query:
                put(q_ref, tile, values * scale, zero)
            else:
                put(k_ref, tile - q_tiles, values, ones)

    @pl.when(jnp.logical_not(is_live(lens_ref, step, per_slot, block)))
    def _():
        for ref in (normed_ref, raw_ref, q_ref, k_ref, v_ref):
            ref[...] = jnp.zeros(ref.shape, ref.dtype)


def out_kernel(
    per_slot, length_ref, att_ref, w_ref, x_ref, gain_ref, resid_ref, normed_ref, sums_ref,
    other_out, give, got, hold, other, send, recv, store,
):
    step = pl.program_id(0)
    block = att_ref.shape[0]
    me, group, core = place()
    partner = device(me, group, 1 - core)
    copies = Copies(send, recv)
    parts = Blocks(copies, partner, per_slot, block, give, got)
    normed_parts = Blocks(copies, partner, per_slot, block, hold, other)

    @pl.when(step == 0)
    def _():
        meet([partner])
        sums_ref[...] = jnp.zeros(sums_ref.shape, F32)

    parts.begin(step, 0)
    normed_parts.begin(step, per_slot)
    product = nn(att_ref[...], w_ref[...])

    @pl.when(step < per_slot)
    def _():
        parts.put(step, product.astype(LOW))

    @pl.when(step >= per_slot)
    def _():
        number = step - per_slot
        valid = lax.broadcasted_iota(jnp.int32, (block, 1), 0) + number * block < length_ref[0]
        attn_out = product + parts.take(step, per_slot).astype(F32)
        resid = x_ref[...].astype(F32) + attn_out
        resid_ref[...] = resid
        normed = (resid * row_rsqrt(resid) * gain_ref[...]).astype(LOW)
        normed_ref[...] = normed
        normed_parts.put(number, normed)
        for row, values in ((0, resid), (1, attn_out)):
            sums_ref[row : row + 1, :] += jnp.sum(
                jnp.where(valid, values * values, 0.0), axis=0, keepdims=True
            )

    @pl.when(step == 2 * per_slot - 1)
    def _():
        parts.end(False, False)
        normed_parts.end(True, True)
        copy = pltpu.make_async_copy(other, other_out, store.at[0])
        copy.start()
        copy.wait()


def ffn_kernel(
    per_slot, shards, chained, last, side, offset, x_own, x_other, g_own, g_other, gathered_ref, *refs
):
    if chained:
        (mlp_in, db_in), refs = take(refs, 2)
    if last:
        (length_ref, resid_ref, gain_ref), refs = take(refs, 3)
    count = len(side.plane_shapes) + len(side.line_shapes)
    sources, refs = take(refs, count)
    if last:
        (out_ref, dresid_ref, dattn_ref, sums_ref, dattn_out), refs = take(refs, 5)
    else:
        (mlp_ref, db_ref), refs = take(refs, 2)
    (grad_out,), refs = take(refs, 1)
    totals, refs = take(refs, count)
    (acc_ref, accd_ref, given_ref, w_ref, wd_ref, grad_ref, load), refs = take(refs, 7)
    exchange, bufs = take(refs, 6 if last else 0)
    step = pl.program_id(0)
    copies, end = side.run(step, sources, totals, bufs)
    own = step >= per_slot if last else step < per_slot
    units, depth = wd_ref.shape
    block = x_own.shape[0]
    me, group, core = place()
    partner = device(me, group, 1 - core)
    half, columns, d_rows = shards // 2, depth // 2, depth // shards
    packed = grad_ref.shape[0] // shards
    size = packed - d_rows
    folds = grad_ref.shape[1] // columns

    def folded(ref, shard, fold):
        return ref.at[shard, pl.ds(offset + d_rows, size), pl.ds(fold * columns, columns)]

    def unfolded(i, fold):
        return at(wd_ref, (i * folds + fold) * size, size, core * columns, columns)

    tiles = [(i, fold) for i in range(half) for fold in range(folds)]
    given = [
        copies(folded(gathered_ref, (1 - core) * half + i, fold), unfolded(i, fold), partner)
        for i, fold in tiles
    ]
    loads = [
        pltpu.make_async_copy(
            gathered_ref.at[shard, pl.ds(offset, d_rows), :],
            w_ref.at[pl.ds(shard * d_rows, d_rows), :],
            load.at[shard],
        )
        for shard in range(shards)
    ] + [
        pltpu.make_async_copy(
            folded(gathered_ref, core * half + i, fold), unfolded(i, fold), load.at[shards + k]
        )
        for k, (i, fold) in enumerate(tiles)
    ]

    if last:
        give_mlp, got_mlp, give_db, got_db, hold, other = exchange
        mlp_parts = Blocks(copies, partner, per_slot, block, give_mlp, got_mlp)
        db_parts = Blocks(copies, partner, per_slot, block, give_db, got_db)
        attn_parts = Blocks(copies, partner, per_slot, block, hold, other)
        mlp_parts.begin(step, 0)
        db_parts.begin(step, 0)
        attn_parts.begin(step, per_slot)

    @pl.when(step == 0)
    def _():
        if last:
            sums_ref[...] = jnp.zeros(sums_ref.shape, F32)
        for copy in given + loads:
            copy.start()
        acc_ref[...] = jnp.zeros(acc_ref.shape, F32)
        accd_ref[...] = jnp.zeros(accd_ref.shape, F32)
        for copy in loads:
            copy.wait()
        for copy in given:
            copy.wait_send()
            copy.wait_recv()

    x = jnp.where(own, x_own[...], x_other[...])
    g = jnp.where(own, g_own[...], g_other[...])
    gate = nn(x, w_ref[:, :units])
    up = nn(x, w_ref[:, units:])
    d_hidden = nt(g, wd_ref[...])
    sig = jax.nn.sigmoid(gate)
    silu = gate * sig
    hidden = (silu * up).astype(LOW)
    d_gate = (d_hidden * up * (sig * (1.0 + gate * (1.0 - sig)))).astype(LOW)
    d_up = (d_hidden * silu).astype(LOW)
    mlp = nn(hidden, wd_ref[...])
    d_b = nt(d_gate, w_ref[:, :units]) + nt(d_up, w_ref[:, units:])
    if chained:
        mlp += mlp_in[...]
        d_b += db_in[...]
    if last:

        @pl.when(step < per_slot)
        def _():
            mlp_parts.put(step, mlp.astype(LOW))
            db_parts.put(step, d_b.astype(LOW))

        @pl.when(step >= per_slot)
        def _():
            number = step - per_slot
            valid = lax.broadcasted_iota(jnp.int32, (block, 1), 0) + number * block < length_ref[0]
            resid = resid_ref[...]
            mlp_out = mlp + mlp_parts.take(step, per_slot).astype(F32)
            out_ref[...] = jnp.where(valid, resid + mlp_out, 0.0).astype(LOW)
            d_norm, d_gain = norm_back(
                resid, d_b + db_parts.take(step, per_slot).astype(F32), gain_ref[...]
            )
            d_resid = jnp.where(valid, g.astype(F32) + d_norm, 0.0)
            dresid_ref[...] = d_resid
            d_attn = d_resid.astype(LOW)
            dattn_ref[...] = d_attn
            attn_parts.put(number, d_attn)
            for row, values in ((0, mlp_out * mlp_out), (1, d_gain)):
                sums_ref[row : row + 1, :] += jnp.sum(
                    jnp.where(valid, values, 0.0), axis=0, keepdims=True
                )

    else:
        mlp_ref[...] = mlp
        db_ref[...] = d_b
    acc_ref[:, :units] += tn(x, d_gate)
    acc_ref[:, units:] += tn(x, d_up)
    accd_ref[...] += tn(hidden, g)

    @pl.when(step == pl.num_programs(0) - 1)
    def _():
        mine = pl.ds(pl.multiple_of(core * columns, columns), columns)
        theirs = pl.ds(pl.multiple_of((1 - core) * columns, columns), columns)
        given_ref[...] = accd_ref[:, theirs].astype(LOW)
        for shard in range(shards):
            grad_ref[pl.ds(shard * packed, d_rows), :] = acc_ref[
                pl.ds(shard * d_rows, d_rows), :
            ].astype(LOW)
        out = []
        for i in range(half):
            for fold in range(folds):
                row = i * folds * size + fold * size
                to = pl.ds(
                    pl.multiple_of((core * half + i) * packed + d_rows, 8), size
                )
                lanes = pl.ds(fold * columns, columns)
                out.append(
                    copies(
                        given_ref.at[pl.ds(row, size), :],
                        grad_ref.at[to, lanes],
                        partner,
                    )
                )
                out[-1].start()
                grad_ref[to, lanes] = accd_ref[pl.ds(row, size), mine].astype(LOW)
        for copy in out:
            copy.wait_send()
            copy.wait_recv()
        stores = [pltpu.make_async_copy(grad_ref, grad_out, load.at[0])]
        stores[0].start()
        if last:
            mlp_parts.end(False, False)
            db_parts.end(False, False)
            attn_parts.end(True, True)
            stores.append(pltpu.make_async_copy(other, dattn_out, load.at[1]))
            stores[1].start()
        end()
        for store in stores:
            store.wait()


def norm_back(values, dy, gain):
    inverse = row_rsqrt(values)
    scaled = dy * gain
    inner = jnp.mean(values * scaled, axis=1, keepdims=True)
    return inverse * scaled - values * (inverse * inverse * inverse * inner), dy * values * inverse


def dout_kernel(
    per_slot, width, own_ref, other_ref, att_ref, w_ref, do_ref, grad_out,
    acc_ref, give, hold, send, recv, store,
):
    step = pl.program_id(0)
    block = own_ref.shape[0]
    me, group, core = place()

    @pl.when(step == 0)
    def _():
        meet([device(me, group, 1 - core)])
        acc_ref[...] = jnp.zeros(acc_ref.shape, F32)

    d_attn = jnp.where(step < per_slot, own_ref[...], other_ref[...])
    lane = lax.broadcasted_iota(jnp.int32, (block, LANES), 1)
    att = att_ref[...]
    acc_ref[...] += tn(att, d_attn)
    for tile in range(att.shape[1] // LANES):
        lanes = slice(tile * LANES, (tile + 1) * LANES)
        if tile % 2 == 0:
            pair = nt(d_attn, w_ref[tile * LANES : (tile + 2) * LANES, :])
        dout = pair[:, (tile % 2) * LANES : (tile % 2 + 1) * LANES].astype(LOW).astype(F32)
        delta = -head_sum(dout * att[:, lanes].astype(F32), width)
        for head, (values, column) in enumerate(
            ((dout, pltpu.roll(delta, width, 1)), (pltpu.roll(dout, width, 1), delta))
        ):
            high, rest = two_parts(column)
            column = jnp.where(
                lane == width, high, jnp.where(lane == width + 1, rest, jnp.zeros_like(rest))
            )
            do_ref[:, pl.ds((2 * tile + head) * LANES, LANES)] = jnp.where(
                lane < width, values.astype(LOW), column
            )

    @pl.when(step == pl.num_programs(0) - 1)
    def _():
        rows, columns = give.shape
        theirs = pl.ds(pl.multiple_of((1 - core) * columns, columns), columns)
        give[...] = acc_ref[:, theirs].astype(LOW)
        mine = pl.ds(pl.multiple_of(core * columns, columns), columns)
        goal = at_rows(hold, core * rows, rows)
        hold[pl.ds(pl.multiple_of(core * rows, rows), rows), :] = acc_ref[:, mine].astype(LOW)
        copy = Copies(send, recv)(give, goal, device(me, group, 1 - core))
        copy.start()
        copy.wait_send()
        copy.wait_recv()
        local = pltpu.make_async_copy(hold, grad_out, store.at[0])
        local.start()
        local.wait()


def qkv_back_kernel(
    per_slot, counts, width, scale, side, dq_ref, dk_ref, dv_ref, raw_ref, normed_ref, w_ref, gh_ref,
    cos_ref, sin_ref, x_ref, dresid_ref, ga_ref, *refs,
):
    step = pl.program_id(0)
    block = dq_ref.shape[0]
    q_tiles, kv_tiles = counts
    me, group, core = place()
    partner = device(me, group, 1 - core)
    count = len(side.plane_shapes) + len(side.line_shapes)
    sources, refs = take(refs, count)
    (out_ref, grad_ref, gain_ref, sums_ref), refs = take(refs, 4)
    totals, refs = take(refs, count)
    (acc_ref, low_ref, give, got), bufs = take(refs, 4)
    copies, end = side.run(step, sources, totals, bufs)
    parts = Blocks(copies, partner, per_slot, block, give, got)

    @pl.when(step == 0)
    def _():
        acc_ref[...] = jnp.zeros(acc_ref.shape, F32)
        gain_ref[...] = jnp.zeros(gain_ref.shape, F32)
        sums_ref[...] = jnp.zeros(sums_ref.shape, F32)

    parts.begin(step, 0)
    lane = lax.broadcasted_iota(jnp.int32, (block, LANES), 1)
    cosine, sine = cos_ref[...], sin_ref[...]

    def pair(ref, tile):
        return jnp.where(
            lane < width,
            ref[:, pl.ds(2 * tile * LANES, LANES)],
            pltpu.roll(ref[:, pl.ds((2 * tile + 1) * LANES, LANES)], width, 1),
        )

    for tile in range(q_tiles + 2 * kv_tiles):
        lanes = pl.ds(tile * LANES, LANES)
        if tile >= q_tiles + kv_tiles:
            low_ref[:, lanes] = pair(dv_ref, tile - q_tiles - kv_tiles).astype(LOW)
            continue
        if tile < q_tiles:
            turned, row = dq_ref[:, lanes] * scale, 0
        else:
            turned, row = pair(dk_ref, tile - q_tiles), 1
        gain = gh_ref[row : row + 1, :]
        dy = turned * cosine + swap_halves(turned * sine, width)
        values = raw_ref[:, lanes]
        inverse = lax.rsqrt(head_sum(values * values, width) * (1.0 / width) + EPS)
        scaled = dy * gain
        inner = head_sum(values * scaled, width) * (1.0 / width)
        low_ref[:, lanes] = (
            inverse * scaled - values * (inverse * inverse * inverse * inner)
        ).astype(LOW)
        gain_ref[row : row + 1, :] += jnp.sum(dy * values * inverse, axis=0, keepdims=True)
    low = low_ref[...]
    acc_ref[...] += tn(normed_ref[...], low)
    d_a = nt(low, w_ref[...])

    @pl.when(step < per_slot)
    def _():
        parts.put(step, d_a.astype(LOW))

    @pl.when(step >= per_slot)
    def _():
        d_norm, d_gain = norm_back(
            x_ref[...].astype(F32), d_a + parts.take(step, per_slot).astype(F32), ga_ref[...]
        )
        out_ref[...] = (dresid_ref[...] + d_norm).astype(LOW)
        sums_ref[0:1, :] += jnp.sum(d_gain, axis=0, keepdims=True)

    @pl.when(step == 2 * per_slot - 1)
    def _():
        grad_ref[...] = acc_ref[...].astype(LOW)
        parts.end(False, False)
        end()


def assemble_kernel(chunks, half, folds, head_width, model_width, *refs):
    parts, refs = take(refs, 4 * chunks)
    pairs, refs = take(refs, 6)
    small_ref, gate_ref, up_ref, down_ref, *outs, ga_ref, gm_ref, rest_ref = refs
    first = lax.rem(lax.axis_index("rep"), 2) == 0

    def sides(mine, other):
        return [jnp.where(first, mine, other), jnp.where(first, other, mine)]

    units = parts[0].shape[1] // 2
    piece = units // half
    for chunk in range(chunks):
        top, low, other_top, other_low = parts[4 * chunk : 4 * chunk + 4]
        for side, values in enumerate(sides(top[...], other_top[...])):
            for j, ref in enumerate((gate_ref, up_ref)):
                for i in range(half):
                    to = ((side * half + i) * chunks + chunk) * piece
                    start = j * units + i * piece
                    ref[:, to : to + piece] = values[:, start : start + piece].astype(F32)
        columns = down_ref.shape[2] // 2
        for side, values in enumerate(sides(low[...], other_low[...])):
            for fold in range(folds):
                down_ref[chunk * folds + fold, :, side * columns : (side + 1) * columns] = values[
                    :, fold * columns : (fold + 1) * columns
                ].astype(F32)
    starts = [0, 0, 0, outs[2].shape[1] // 2]
    for ref, k, start in zip(outs, (0, 2, 4, 4), starts):
        width = ref.shape[1] // 2
        mine, other = (one[:, start : start + width] for one in pairs[k : k + 2])
        for side, values in enumerate(sides(mine, other)):
            ref[:, side * width : (side + 1) * width] = values.astype(F32)

    @pl.when(pl.program_id(0) == 0)
    def _():
        me = lax.axis_index("shard")
        width = ga_ref.shape[1]
        here = pl.ds(pl.multiple_of(me * width, width), width)
        ga_ref[...] = small_ref[0:1, here]
        gm_ref[...] = small_ref[1:2, here]
        rest_ref[...] = jnp.zeros(rest_ref.shape, F32)
        lane = lax.broadcasted_iota(jnp.int32, (1, LANES), 1)
        count = small_ref[7:8, 0:1] * model_width
        roots = jnp.zeros((1, LANES), F32)
        for k in range(3):
            total = jnp.sum(small_ref[2 + k : 3 + k, :], axis=1, keepdims=True)
            roots = jnp.where(lane == k, jnp.sqrt(total / count), roots)
        rest_ref[0:1, :] = roots
        size = head_width * width // model_width
        for k in range(2):
            gains = jnp.broadcast_to(small_ref[5 + k : 6 + k, :LANES], (8, LANES))
            gains += pltpu.roll(gains, head_width, 1)
            gains = pltpu.roll(gains, lax.rem(LANES - me * size, LANES), 1)
            rest_ref[1 + k : 2 + k, :] = gains[0:1, :]


class Rows:
    def __init__(self, lens, rows, block):
        self.lens, self.block, self.per_slot = lens, block, rows // block

    def both(self, width):
        return pl.BlockSpec((self.block, width), lambda i, lens: (i, 0))

    def both_other_first(self, width):
        n = self.per_slot
        return pl.BlockSpec((self.block, width), lambda i, lens: (lax.rem(i + n, 2 * n), 0))

    def early(self, width):
        n = self.per_slot
        return pl.BlockSpec((self.block, width), lambda i, lens: (jnp.minimum(i, n - 1), 0))

    def late(self, width):
        n = self.per_slot
        return pl.BlockSpec((self.block, width), lambda i, lens: (jnp.maximum(i - n, 0), 0))

    def repeated(self, width):
        n = self.per_slot
        return pl.BlockSpec((self.block, width), lambda i, lens: (lax.rem(i, n), 0))

    def fixed(self, shape):
        return pl.BlockSpec(shape, lambda i, lens: (0, 0), pipeline_mode=pl.Buffered(1))

    def call(self, name, kernel, slots, in_specs, out_specs, outs, scratch, flops, *args):
        return pl.pallas_call(
            kernel,
            out_shape=[jax.ShapeDtypeStruct(shape, kind) for shape, kind in outs],
            grid_spec=pltpu.PrefetchScalarGridSpec(
                num_scalar_prefetch=1,
                grid=(slots * self.per_slot,),
                in_specs=in_specs,
                out_specs=out_specs,
                scratch_shapes=scratch,
            ),
            cost_estimate=pl.CostEstimate(
                flops=flops, bytes_accessed=1 << 24, transcendentals=0
            ),
            compiler_params=pltpu.CompilerParams(vmem_limit_bytes=62 << 20),
            name=name,
        )(self.lens, *args)


def local(
    inputs,
    lengths,
    gain_attn,
    w_query,
    w_key,
    w_value,
    gain_query,
    gain_key,
    w_out,
    gain_mlp,
    w_gate,
    w_up,
    w_down,
    cotangent,
):
    shards = lax.axis_size("shard")
    core = lax.axis_index("rep") % 2
    first = core == 0
    rows, width_all = inputs.shape[1], inputs.shape[2]
    head_width = gain_query.shape[0] * shards
    q_half, kv_half = w_query.shape[1] // 2, w_key.shape[1] // 2
    d_half = width_all // 2
    d_rows, ff_rows = w_query.shape[0], w_down.shape[0]
    block = min(256, rows)
    scale = 1.0 / math.sqrt(head_width)
    counts = (q_half // LANES, kv_half // LANES)

    def ordered(mine, other, axis):
        return jnp.where(
            first,
            jnp.concatenate([mine, other], axis=axis),
            jnp.concatenate([other, mine], axis=axis),
        )

    half_shards = shards // 2
    groups = lax.axis_size("rep") // 2
    chunks = 3
    piece = ff_rows // chunks
    units = half_shards * piece
    folds = 2 * units // d_half
    head_rows = gain_query.shape[0]

    def fold(part):
        return jnp.concatenate(jnp.split(part, folds, axis=-2), axis=-1)

    def unfold(part):
        return jnp.concatenate(jnp.split(part, folds, axis=-1), axis=-2)

    packed_rows = d_rows + piece // folds
    hbm = pl.BlockSpec(memory_space=pltpu.HBM)
    vmem = pl.BlockSpec(memory_space=pltpu.VMEM)
    chunk_sets = [list(range(chunks - 1)), [chunks - 1]]

    def pack(*refs):
        *refs, pack_a, pack_b, sems = refs
        packs = [
            (ref, [(i * packed_rows, chunk) for i, chunk in enumerate(some)])
            for ref, some in zip((pack_a, pack_b), chunk_sets)
        ]
        pack_kernel(shards, chunks, *refs, *packs, sems)

    if piece % LANES == 0:
        packs = pl.pallas_call(
            pack,
            out_shape=[
                jax.ShapeDtypeStruct((len(some) * packed_rows, 2 * units), LOW) for some in chunk_sets
            ],
            in_specs=[hbm] * 3,
            out_specs=[vmem] * 2,
            scratch_shapes=[pltpu.SemaphoreType.DMA((chunks * (2 * half_shards + folds),))],
            compiler_params=pltpu.CompilerParams(vmem_limit_bytes=62 << 20),
            name="pack",
        )(w_gate, w_up, w_down)
    else:

        def my_half(weight):
            half = weight.shape[1] // 2
            return jnp.where(first, weight[:, :half], weight[:, half:])

        def chunk_of(weight, chunk):
            columns = weight.reshape(d_rows, shards, chunks, piece)[:, :, chunk]
            return my_half(columns.reshape(d_rows, shards * piece))

        def packed_chunk(chunk):
            tall = fold(my_half(w_down)[chunk * piece : (chunk + 1) * piece])
            wide = jnp.concatenate([chunk_of(w_gate, chunk), chunk_of(w_up, chunk)], axis=1)
            return jnp.concatenate([wide, tall])

        packs = [jnp.concatenate([packed_chunk(k) for k in some]) for some in chunk_sets]
    gathered = [lax.all_gather(packs[0], "shard", axis=0)]

    def gain_row(*gains):
        flat = jnp.concatenate(gains)
        return jnp.pad(flat, (0, max(d_rows, LANES) - flat.shape[0]))[None]

    gain_rows = jnp.pad(
        jnp.concatenate(
            [gain_row(gain_attn), gain_row(gain_mlp), gain_row(gain_query, gain_key)]
        ),
        ((0, 13), (0, 0)),
    )

    def half_of(width):
        return lambda core: core * width

    wide_parts = [
        (0, 0, half_of(q_half), 0, q_half),
        (1, 0, half_of(kv_half), q_half, kv_half),
        (2, 0, half_of(kv_half), q_half + kv_half, kv_half),
    ]
    tall_parts = [(3, 1, 0, w_out.shape[0])]
    copies = len(wide_parts) * (shards + 2) + len(tall_parts) * (2 * shards + 3) + shards + 1
    w_qkv, w_o, gains, x_other = pl.pallas_call(
        partial(gather_kernel, shards, wide_parts, tall_parts, (6, copies)),
        out_shape=[
            jax.ShapeDtypeStruct(shape, LOW)
            for shape in (
                (width_all, q_half + 2 * kv_half),
                (half_shards * w_out.shape[0], width_all),
                (shards,) + gain_rows.shape,
                inputs.shape[1:],
            )
        ],
        in_specs=[hbm] * 6,
        out_specs=[hbm] * 4,
        scratch_shapes=[pltpu.SemaphoreType.DMA((copies,)), pltpu.SemaphoreType.DMA((copies,))],
        compiler_params=pltpu.CompilerParams(collective_id=0, has_side_effects=True),
        name="gather",
    )(w_query, w_key, w_value, w_out, gain_rows, inputs[0])
    gain_a = gains[:, 0, :d_rows].reshape(1, -1).astype(F32)
    gain_m = gains[:, 1, :d_rows].reshape(1, -1).astype(F32)
    gain_q = gains[:, 2, :head_rows].reshape(1, -1).astype(F32)
    gain_k = gains[:, 2, head_rows : 2 * head_rows].reshape(1, -1).astype(F32)
    gain_h = jnp.tile(jnp.concatenate([gain_q, gain_k]), (4, LANES // head_width))

    lens = jnp.concatenate([lengths, core_swap(lengths)])
    valid = (jnp.arange(rows) < lengths[0])[:, None]
    x_own = inputs[0]
    g_own = jnp.where(valid, cotangent[0], jnp.zeros((), LOW))
    g_other = core_swap(g_own)
    over = Rows(lens, rows, block)
    cosine, sine = rope_tables(rows, head_width)
    full, total = 2 * rows, w_qkv.shape[1]
    qk = q_half + kv_half

    normed_a, raw, queries, keys, values = over.call(
        "qkv",
        partial(qkv_kernel, over.per_slot, counts, head_width, scale),
        2,
        [over.early(width_all), over.late(width_all), over.fixed(w_qkv.shape)]
        + [over.fixed(gain_a.shape), over.fixed(gain_h.shape)]
        + [over.repeated(LANES), over.repeated(LANES)],
        [over.both(width_all), over.both(qk), over.both(2 * q_half), over.both(2 * kv_half)]
        + [over.both(2 * kv_half)],
        [((full, width_all), LOW), ((full, qk), F32), ((full, 2 * q_half), LOW)]
        + [((full, 2 * kv_half), LOW)] * 2,
        [],
        2 * full * width_all * total,
        x_own, x_other, w_qkv, gain_a, gain_h, cosine, sine,
    )
    attended, queries = attend(lens, queries, keys, values, rows, head_width, block)
    later, attended = lax.optimization_barrier((packs[1], attended))
    gathered.append(lax.all_gather(later, "shard", axis=0))
    n = over.per_slot
    eight = (8, width_all)
    first_rows = pl.BlockSpec((block, width_all), lambda i: (jnp.minimum(i, n - 1), 0))
    last_rows = pl.BlockSpec((block, width_all), lambda i: (jnp.maximum(i - n, 0), 0))
    all_rows = pl.BlockSpec((block, width_all), lambda i: (i, 0))
    smem = pl.BlockSpec(memory_space=pltpu.SMEM)

    def other_first(width):
        return pl.BlockSpec((block, width), lambda i: (lax.rem(i + n, 2 * n), 0))

    def held(shape):
        return pl.BlockSpec(shape, lambda i: (0, 0), pipeline_mode=pl.Buffered(1))

    sums_spec = pl.BlockSpec(eight, lambda i: (0, 0))
    slot_rows = pltpu.VMEM((rows, width_all), LOW)
    resid, normed_b, sums_a, normed_b_other = pl.pallas_call(
        partial(out_kernel, n),
        out_shape=[
            jax.ShapeDtypeStruct((rows, width_all), F32),
            jax.ShapeDtypeStruct((rows, width_all), LOW),
            jax.ShapeDtypeStruct(eight, F32),
            jax.ShapeDtypeStruct((rows, width_all), LOW),
        ],
        grid=(2 * n,),
        in_specs=[smem, other_first(q_half), held(w_o.shape), last_rows, held(gain_m.shape)],
        out_specs=[last_rows, last_rows, sums_spec, hbm],
        scratch_shapes=[pltpu.VMEM((2 * block, width_all), LOW), slot_rows, slot_rows, slot_rows]
        + [pltpu.SemaphoreType.DMA((2 * n,))] * 2
        + [pltpu.SemaphoreType.DMA((1,))],
        cost_estimate=pl.CostEstimate(
            flops=2 * full * q_half * width_all, bytes_accessed=1 << 24, transcendentals=0
        ),
        compiler_params=pltpu.CompilerParams(
            collective_id=6, has_side_effects=True, vmem_limit_bytes=62 << 20
        ),
        name="out",
    )(lengths, attended, w_o, x_own, gain_m)

    sums = []
    ff_grads, ff_levels, ff_totals = [], [], []
    packed_shape = (shards * packed_rows, 2 * units)
    level_shape = (packed_rows, 2 * units)
    wide_shape, tall_shape = (width_all, 2 * units), (units, width_all)
    for chunk in range(chunks):
        last = chunk == chunks - 1
        side = Side(
            shards,
            groups,
            [level_shape] if chunk >= 1 else [],
            [level_shape] if chunk >= 2 else [],
            2 * half_shards * folds + 3 * n,
        )
        late = chunk == chunks - 1
        sources = ff_grads[-1:] + ff_levels[-1:]
        ends = [all_rows] * 2
        end_shapes = [jax.ShapeDtypeStruct((full, width_all), F32)] * 2
        own_rows, other_rows, sum_rows, more, more_specs, exchange = (
            first_rows, last_rows, all_rows, [], [], []
        )
        if last:
            own_rows, other_rows, sum_rows = last_rows, first_rows, other_first(width_all)
            more = [lengths, resid, gain_m]
            more_specs = [smem, last_rows, held(gain_m.shape)]
            ends = [last_rows] * 3 + [sums_spec, hbm]
            end_shapes = [
                jax.ShapeDtypeStruct((rows, width_all), LOW),
                jax.ShapeDtypeStruct((rows, width_all), F32),
                jax.ShapeDtypeStruct((rows, width_all), LOW),
                jax.ShapeDtypeStruct(eight, F32),
                jax.ShapeDtypeStruct((rows, width_all), LOW),
            ]
            exchange = [pltpu.VMEM((2 * block, width_all), LOW), slot_rows] * 3
        outs = pl.pallas_call(
            partial(
                ffn_kernel, n, shards, bool(sums), last, side, 0 if late else chunk * packed_rows
            ),
            out_shape=end_shapes + [jax.ShapeDtypeStruct(packed_shape, LOW)] + side.outs(),
            grid=(2 * n,),
            in_specs=[own_rows, other_rows] * 2
            + [hbm]
            + [sum_rows] * len(sums)
            + more_specs
            + [hbm] * len(sources),
            out_specs=ends + [hbm] * (1 + len(side.outs())),
            scratch_shapes=[pltpu.VMEM(wide_shape, F32), pltpu.VMEM(tall_shape, F32)]
            + [pltpu.VMEM((units, d_half), LOW)]
            + [pltpu.VMEM(wide_shape, LOW), pltpu.VMEM(tall_shape, LOW)]
            + [pltpu.VMEM(packed_shape, LOW)]
            + [pltpu.SemaphoreType.DMA((shards + half_shards * folds,))]
            + exchange
            + side.scratch(),
            cost_estimate=pl.CostEstimate(
                flops=18 * full * width_all * units, bytes_accessed=1 << 25, transcendentals=0
            ),
            compiler_params=pltpu.CompilerParams(
                collective_id=2 + chunk, has_side_effects=True, vmem_limit_bytes=67043328
            ),
            name="ffn",
        )(normed_b, normed_b_other, g_own, g_other, gathered[late], *sums, *more, *sources)
        sums = outs[: len(end_shapes)]
        ff_grads.append(outs[len(end_shapes)])
        rest = outs[len(end_shapes) + 1 :]
        ff_levels += rest[:1]
        ff_totals += rest[1:]
    output, d_resid, d_attn, sums_b, d_attn_other = sums

    o_shape = w_o.shape
    d_heads, grad_out = pl.pallas_call(
        partial(dout_kernel, n, head_width),
        out_shape=[
            jax.ShapeDtypeStruct((full, 2 * q_half), LOW),
            jax.ShapeDtypeStruct((2 * o_shape[0], d_half), LOW),
        ],
        grid=(2 * n,),
        in_specs=[first_rows, last_rows, pl.BlockSpec((block, q_half), lambda i: (i, 0))]
        + [held(o_shape)],
        out_specs=[pl.BlockSpec((block, 2 * q_half), lambda i: (i, 0)), hbm],
        scratch_shapes=[pltpu.VMEM(o_shape, F32), pltpu.VMEM((o_shape[0], d_half), LOW)]
        + [pltpu.VMEM((2 * o_shape[0], d_half), LOW)]
        + [pltpu.SemaphoreType.DMA((1,))] * 3,
        cost_estimate=pl.CostEstimate(
            flops=4 * full * q_half * width_all, bytes_accessed=1 << 24, transcendentals=0
        ),
        compiler_params=pltpu.CompilerParams(
            collective_id=8, has_side_effects=True, vmem_limit_bytes=62 << 20
        ),
        name="dout",
    )(d_attn, d_attn_other, attended, w_o)
    o_level = (d_rows, d_half)
    d_query, d_key, d_value, ff_level, ff_total = attend_back(
        queries,
        keys,
        values,
        d_heads,
        rows,
        head_width,
        block,
        Side(shards, groups, [level_shape], [level_shape]),
        [ff_grads[-1], ff_levels[-1]],
    )
    ff_totals.append(ff_total)
    top_shape = (d_rows, 2 * units)
    side = Side(shards, groups, [o_level], [top_shape], n)
    turned = pl.BlockSpec((block, LANES), lambda i: (lax.rem(i, n), 0))
    input_grad, grad_qkv, gain_sums, sums_c, out_level, ff_top = pl.pallas_call(
        partial(qkv_back_kernel, n, counts, head_width, scale, side),
        out_shape=[
            jax.ShapeDtypeStruct((rows, width_all), LOW),
            jax.ShapeDtypeStruct(w_qkv.shape, LOW),
            jax.ShapeDtypeStruct((8, LANES), F32),
            jax.ShapeDtypeStruct(eight, F32),
        ]
        + side.outs(),
        grid=(2 * n,),
        in_specs=[other_first(q_half), other_first(2 * kv_half), other_first(2 * kv_half)]
        + [other_first(qk), other_first(width_all), held(w_qkv.shape), held(gain_h.shape)]
        + [turned, turned, last_rows, last_rows, held(gain_a.shape), hbm, hbm],
        out_specs=[last_rows, held(w_qkv.shape)]
        + [pl.BlockSpec((8, LANES), lambda i: (0, 0)), sums_spec, hbm, hbm],
        scratch_shapes=[pltpu.VMEM(w_qkv.shape, F32), pltpu.VMEM((block, total), LOW)]
        + [pltpu.VMEM((2 * block, width_all), LOW), slot_rows]
        + side.scratch(),
        cost_estimate=pl.CostEstimate(
            flops=4 * full * width_all * total, bytes_accessed=1 << 24, transcendentals=0
        ),
        compiler_params=pltpu.CompilerParams(
            collective_id=7, has_side_effects=True, vmem_limit_bytes=62 << 20
        ),
        name="qkv_back",
    )(
        d_query, d_key, d_value, raw, normed_a, w_qkv, gain_h, cosine, sine, x_own, d_resid, gain_a,
        grad_out, ff_level,
    )
    mine, other, small = finish_sums(
        grad_qkv,
        lengths,
        [sums_a, sums_b, sums_c, gain_sums],
        [(2, 0), (1, 1), (0, 0), (0, 1), (1, 0), (3, 0), (3, 1)],
        [ff_level, out_level],
        d_rows,
        ff_totals + [ff_top],
        shards,
        groups,
    )
    wide = (d_rows, shards * ff_rows)
    shapes = [wide, wide, (chunks * folds, piece // folds, width_all)]
    shapes += [w.shape for w in (w_out, w_query, w_key, w_value)]
    shapes += [(1, d_rows), (1, d_rows), (8, LANES)]
    top = d_rows // 8
    low_rows = piece // folds // 8

    def whole(part):
        return pl.BlockSpec((top, part.shape[1]), lambda i: (i, 0))

    def low(part, skip):
        return pl.BlockSpec((low_rows, part.shape[1]), lambda i: (skip // low_rows + i, 0))

    parts, specs = [], []
    for chunk in range(chunks):
        for total, rest in (
            (ff_totals[chunk], ff_totals[chunk]) if chunk < chunks - 1 else (ff_top, mine[0]),
            (other[4 + chunk], other[4 + chunk]) if chunk < chunks - 1 else (other[-1], other[0]),
        ):
            parts += [total, rest]
            specs += [whole(total), low(rest, d_rows if chunk < chunks - 1 else 0)]
    pairs = [one for pair in zip(mine[1:4], other[1:4]) for one in pair]
    small_specs = [pl.BlockSpec(shape, lambda i: (0, 0)) for shape in shapes[7:]]
    (
        grad_gate, grad_up, grad_down, grad_out, grad_query, grad_key, grad_value,
        grad_ga, grad_gm, rest,
    ) = pl.pallas_call(
        partial(assemble_kernel, chunks, half_shards, folds, head_width, width_all),
        out_shape=[jax.ShapeDtypeStruct(shape, F32) for shape in shapes],
        grid=(8,),
        in_specs=specs
        + [whole(part) for part in pairs]
        + [pl.BlockSpec(small.shape, lambda i: (0, 0))],
        out_specs=[pl.BlockSpec((top, shape[1]), lambda i: (i, 0)) for shape in shapes[:2]]
        + [pl.BlockSpec((shapes[2][0], low_rows, width_all), lambda i: (0, i, 0))]
        + [pl.BlockSpec((top, shape[1]), lambda i: (i, 0)) for shape in shapes[3:7]]
        + small_specs,
        compiler_params=pltpu.CompilerParams(vmem_limit_bytes=62 << 20),
        name="assemble",
    )(*parts, *pairs, small)
    return (
        output[None],
        input_grad[None],
        grad_ga.reshape(-1),
        grad_query,
        grad_key,
        grad_value,
        rest[1, :head_rows],
        rest[2, :head_rows],
        grad_out,
        grad_gm.reshape(-1),
        grad_gate,
        grad_up,
        grad_down.reshape(w_down.shape),
        rest[0, :3],
    )


def solution(mesh):
    in_specs = (
        P(("rep", "shard"), None, None),
        P(("rep", "shard")),
        P("shard"),
        P("shard", None),
        P("shard", None),
        P("shard", None),
        P("shard"),
        P("shard"),
        P("shard", None),
        P("shard"),
        P("shard", None),
        P("shard", None),
        P("shard", None),
        P(("rep", "shard"), None, None),
    )
    out_specs = (
        P(("rep", "shard"), None, None),
        P(("rep", "shard"), None, None),
        P("shard"),
        P("shard", None),
        P("shard", None),
        P("shard", None),
        P("shard"),
        P("shard"),
        P("shard", None),
        P("shard"),
        P("shard", None),
        P("shard", None),
        P("shard", None),
        P(),
    )
    return jax.shard_map(local, mesh=mesh, in_specs=in_specs, out_specs=out_specs, check_vma=False)
```

```python
from functools import partial
import math

import jax
import jax.numpy as jnp
from jax import lax
from jax.experimental import pallas as pl
from jax.experimental.pallas import tpu as pltpu
from jax.sharding import PartitionSpec as P

EPS = 1e-05
ROPE_BASE = 1000000.0
F32 = jnp.float32
LOW = jnp.bfloat16
LANES = 128
MESH = pl.DeviceIdType.MESH


def rope_tables(row_count, head_width):
    half_width = head_width // 2
    frequency = jnp.power(
        jnp.float32(ROPE_BASE), -jnp.arange(half_width, dtype=jnp.float32) * 2.0 / head_width
    )
    angles = jnp.arange(row_count, dtype=jnp.float32)[:, None] * frequency[None, :]
    cosine, sine = jnp.cos(angles), jnp.sin(angles)
    repeats = LANES // head_width
    return jnp.tile(cosine, (1, 2 * repeats)), jnp.tile(
        jnp.concatenate([-sine, sine], axis=1), (1, repeats)
    )


def nn(left, right):
    return jnp.dot(left, right, preferred_element_type=F32)


def nt(left, right):
    return lax.dot_general(left, right, (((1,), (1,)), ((), ())), preferred_element_type=F32)


def tn(left, right):
    return lax.dot_general(left, right, (((0,), (0,)), ((), ())), preferred_element_type=F32)


def core_swap(x):
    pairs = [(i, i ^ 1) for i in range(lax.axis_size("rep"))]
    return lax.ppermute(x, "rep", pairs)


def place():
    rep = lax.axis_index("rep")
    return lax.axis_index("shard"), lax.div(rep, 2), lax.rem(rep, 2)


def device(shard, group, core):
    return {"rep": 2 * group + core, "shard": shard}


def meet(devices):
    barrier = pltpu.get_barrier_semaphore()
    for where in devices:
        pl.semaphore_signal(barrier, inc=1, device_id=where, device_id_type=MESH)
    pl.semaphore_wait(barrier, len(devices))


def remote(source, target, send, recv, where):
    return pltpu.make_async_remote_copy(
        src_ref=source,
        dst_ref=target,
        send_sem=send,
        recv_sem=recv,
        device_id=where,
        device_id_type=MESH,
    )


def at_rows(ref, start, size):
    return ref.at[pl.ds(pl.multiple_of(start, 8), size), :]


def at(ref, row, rows, column, columns):
    return ref.at[
        pl.ds(pl.multiple_of(row, 8), rows), pl.ds(pl.multiple_of(column, LANES), columns)
    ]


class Copies:
    def __init__(self, send, recv):
        self.send, self.recv, self.used = send, recv, 0

    def __call__(self, source, target, where):
        slot = self.used
        self.used += 1
        return remote(source, target, self.send.at[slot], self.recv.at[slot], where)


def neighbours(me):
    return me + 1 - 2 * lax.rem(me, 2), me + 2 - 4 * lax.div(me, 2), 3 - me


def gather_kernel(shards, wide_parts, tall_parts, count, *refs):
    *refs, send, recv = refs
    sources, targets = refs[: count[0]], refs[count[0] :]
    me, group, core = place()
    half = shards // 2
    partner = device(me, group, 1 - core)
    meet(
        [device(lax.rem(me + k, shards), group, c) for k in range(1, shards) for c in range(2)]
        + [partner]
    )
    copies = Copies(send, recv)
    sent, due = [], []

    def go(source, target, where):
        copy = copies(source, target, where)
        copy.start()
        sent.append(copy.wait_send)
        return copy

    def passed_on(wide):
        fast, slow, _ = neighbours(me)
        later = []
        for block, first, second in wide:
            rows = block(me).shape[0] // 2
            first.wait_recv()
            later.append(go(block(fast).at[pl.ds(0, rows), :], block(fast).at[pl.ds(0, rows), :], device(slow, group, core)))
            second.wait_recv()
            later.append(go(block(slow).at[pl.ds(rows, rows), :], block(slow).at[pl.ds(rows, rows), :], device(fast, group, core)))
        return later

    wide = []
    for source, target, column, to, columns in wide_parts:
        source, target = sources[source], targets[target]
        rows = source.shape[0]
        mine = at(source, 0, rows, column(core), columns)

        def block(shard, target=target, rows=rows, to=to, columns=columns):
            return at(target, shard * rows, rows, to, columns)

        if shards == 4:
            fast, slow, _ = neighbours(me)
            wide.append(
                (
                    block,
                    go(mine, block(me), device(fast, group, core)),
                    go(mine, block(me), device(slow, group, core)),
                )
            )
        else:
            for k in range(1, shards):
                due.append(go(mine, block(me), device(lax.rem(me + k, shards), group, core)))
        due.append(go(at(source, 0, rows, column(1 - core), columns), block(me), partner))
    owner = lax.div(me, half)
    tall = []
    for source, target, row, rows in tall_parts:
        source, target = sources[source], targets[target]
        columns = source.shape[1] // 2

        def block(shard, target=target, rows=rows, columns=columns):
            return at(target, lax.rem(shard, half) * rows, rows, 0, 2 * columns)

        mine = at(source, row, rows, core * columns, columns)
        goal = at(target, lax.rem(me, half) * rows, rows, core * columns, columns)
        steps = [1, 2] if shards == 4 else list(range(1, shards))
        arrivals = []
        for k in steps:
            if shards == 4:
                to = origin = neighbours(me)[k - 1]
            else:
                to, origin = lax.rem(me + k, shards), lax.rem(me + shards - k, shards)
            pair = []
            for side in range(2):
                copy = copies(mine, goal, device(to, group, owner))
                pl.when(core == side)(copy.start)
                sent.append((core == side, copy.wait_send))
                pair.append(copy)
            arrivals.append((lax.div(origin, half) == core, pair))
        whole = copies(
            at(source, row, rows, 0, 2 * columns), block(me), partner
        )
        pl.when(owner != core)(whole.start)
        sent.append((owner != core, whole.wait_send))
        due.append((owner == core, whole))
        if shards == 4:
            tall.append((block, rows // 2, arrivals))
        else:
            for condition, pair in arrivals:
                due.extend((condition, copy) for copy in pair)
    gains, given = sources[-2:], targets[-2:]
    for k in range(1, shards):
        due.append(go(gains[0], given[0].at[me], device(lax.rem(me + k, shards), group, core)))
    due.append(go(gains[0], given[0].at[me], partner))
    due.append(go(gains[1], given[1], partner))
    if shards == 4:
        due.extend(passed_on(wide))
        fast, slow, _ = neighbours(me)
        for block, rows, arrivals in tall:
            for number, (condition, pair) in enumerate(arrivals):
                start = number * rows
                from_, to = (fast, slow) if number == 0 else (slow, fast)
                part = block(from_).at[pl.ds(start, rows), :]
                copy = copies(part, part, device(to, group, core))

                @pl.when(condition)
                def _(pair=pair, copy=copy):
                    for one in pair:
                        one.wait_recv()
                    copy.start()

                sent.append((condition, copy.wait_send))
                due.append((owner != core, copy))
    for item in sent:
        pl.when(item[0])(item[1]) if isinstance(item, tuple) else item()
    for item in due:
        pl.when(item[0])(item[1].wait_recv) if isinstance(item, tuple) else item.wait_recv()


def pack_kernel(shards, chunks, gate_ref, up_ref, down_ref, *refs):
    *packs, sems = refs
    core = lax.rem(lax.axis_index("rep"), 2)
    half = shards // 2
    total, rows = down_ref.shape[0], gate_ref.shape[0]
    piece = total // chunks
    columns = down_ref.shape[1] // 2
    copies = []
    for pack in packs:
        for row, chunk in pack[1]:
            for j, ref in enumerate((gate_ref, up_ref)):
                for i in range(half):
                    start = (core * half + i) * total + chunk * piece
                    copies.append(
                        (
                            at(ref, 0, rows, start, piece),
                            pack[0].at[pl.ds(row, rows), pl.ds((j * half + i) * piece, piece)],
                        )
                    )
            folds = 2 * half * piece // columns
            size = piece // folds
            for i in range(folds):
                copies.append(
                    (
                        at(down_ref, chunk * piece + i * size, size, core * columns, columns),
                        pack[0].at[pl.ds(row + rows, size), pl.ds(i * columns, columns)],
                    )
                )
    copies = [pltpu.make_async_copy(a, b, sems.at[k]) for k, (a, b) in enumerate(copies)]
    for copy in copies:
        copy.start()
    for copy in copies:
        copy.wait()


def add_up(parts, target, least):
    total_rows = target.shape[0]
    rows = max(k for k in range(least, 97, least) if total_rows % k == 0)

    def some(i, _):
        here = pl.ds(pl.multiple_of(i * rows, rows), rows)
        total = parts[0][here, :].astype(F32)
        for part in parts[1:]:
            total += part[here, :].astype(F32)
        target[here, :] = total.astype(target.dtype)
        return 0

    lax.fori_loop(0, total_rows // rows, some, 0)


def reduce_over_plane(copies, load, shards, grad_ref, level, bufs):
    me, group, core = place()
    rows = level.shape[0]

    def block(shard, start=0, size=rows):
        return at_rows(grad_ref, shard * rows + start, size)

    own = bufs[0]
    local = pltpu.make_async_copy(block(me), own, load.at[0])
    if shards != 4:
        planes = bufs[1]
        out = [
            copies(block(lax.rem(me + k, shards)), planes.at[k - 1], device(lax.rem(me + k, shards), group, core))
            for k in range(1, shards)
        ]

        def start():
            local.start()
            for copy in out:
                copy.start()

        def end():
            local.wait()
            for copy in out:
                copy.wait_send()
                copy.wait_recv()
            add_up([own] + [planes.at[k] for k in range(shards - 1)], level, 16)

        return [start, idle, idle, end]
    fast, slow, across = neighbours(me)
    to_fast, to_slow = device(fast, group, core), device(slow, group, core)
    half = rows // 2
    planes, met_fast, met_slow, held_fast, held_slow = bufs[1:]
    upper, lower = pl.ds(0, half), pl.ds(half, half)
    loads = [
        local,
        pltpu.make_async_copy(block(fast, half, half), held_fast, load.at[1]),
        pltpu.make_async_copy(block(slow, 0, half), held_slow, load.at[2]),
    ]
    early = [
        copies(block(across, 0, half), met_fast, to_fast),
        copies(block(across, half, half), met_slow, to_slow),
        copies(block(fast, 0, half), planes.at[0, upper, :], to_fast),
        copies(block(slow, half, half), planes.at[1, lower, :], to_slow),
    ]
    late = [
        copies(held_fast, planes.at[0, lower, :], to_fast),
        copies(held_slow, planes.at[1, upper, :], to_slow),
    ]

    def start():
        for copy in early[:2] + loads:
            copy.start()

    def direct():
        for copy in early[2:]:
            copy.start()

    def merge():
        for copy in loads:
            copy.wait()
        for copy, met, held, out in (
            (early[1], met_slow, held_fast, late[0]),
            (early[0], met_fast, held_slow, late[1]),
        ):
            copy.wait_recv()
            add_up([held, met], held, 16)
            out.start()

    def end():
        for copy in early[2:] + late:
            copy.wait_recv()
        for copy in early + late:
            copy.wait_send()
        add_up([own, planes.at[0], planes.at[1]], level, 16)

    return [start, direct, merge, end]


def plane_buffers(shards, shape):
    half = (shape[0] // 2, shape[1])
    if shards != 4:
        return [pltpu.VMEM(shape, LOW), pltpu.VMEM((shards - 1,) + shape, LOW)]
    return [pltpu.VMEM(shape, LOW), pltpu.VMEM((2,) + shape, LOW)] + [pltpu.VMEM(half, LOW)] * 4


def reduce_over_line(copies, groups, source, part, total, bufs):
    me, group, core = place()
    if groups != 4:
        (slots,) = bufs
        out = [
            copies(source, slots.at[group], device(me, lax.rem(group + k, groups), core))
            for k in range(1, groups)
        ]

        def start():
            for copy in out:
                copy.start()

        def end():
            rows = part.shape[0]

            def some(i, _):
                here = pl.ds(pl.multiple_of(i * 8, 8), 8)
                slots[group, here, :] = part[here, :]
                return 0

            lax.fori_loop(0, rows // 8, some, 0)
            for copy in out:
                copy.wait_send()
                copy.wait_recv()
            add_up([slots.at[k] for k in range(groups)], total, 8)

        return [start, idle, idle, end]
    met, summed, other = bufs
    outer = jnp.logical_or(group == 0, group == groups - 1)
    inner = jnp.logical_not(outer)
    mate = device(me, group + 1 - 2 * lax.rem(group, 2), core)
    inward = copies(source, met, mate)
    between = copies(summed, other, device(me, groups - 1 - group, core))
    back = copies(total, total, mate)

    def start():
        pl.when(outer)(inward.start)

    def exchange():
        @pl.when(inner)
        def _():
            inward.wait_recv()
            add_up([part, met], summed, 16)
            between.start()

    def give():
        @pl.when(inner)
        def _():
            between.wait_recv()
            add_up([summed, other], total, 16)
            back.start()

    def end():
        @pl.when(outer)
        def _():
            inward.wait_send()
            back.wait_recv()

        @pl.when(inner)
        def _():
            between.wait_send()
            back.wait_send()

    return [start, exchange, give, end]


def idle():
    pass


def line_buffers(groups, shape):
    if groups != 4:
        return [pltpu.VMEM((groups,) + shape, LOW)]
    return [pltpu.VMEM(shape, LOW)] * 3


PARTS = 8


def parts_of(shape):
    return PARTS if shape[0] * shape[1] >= 1 << 18 else PARTS // 2


class LineSum:
    def __init__(self, copies, groups, source, part, total, bufs):
        self.count = parts_of(part.shape)
        rows = part.shape[0] // self.count
        each = len(bufs) // self.count
        self.parts = [
            reduce_over_line(
                copies,
                groups,
                at_rows(source, i * rows, rows),
                at_rows(part, i * rows, rows),
                at_rows(total, i * rows, rows),
                bufs[i * each : (i + 1) * each],
            )
            for i in range(self.count)
        ]

    def run(self, part, stage):
        if part < self.count:
            self.parts[part][stage]()

    def all(self, stage, first=0, last=None):
        for part in self.parts[first:last]:
            part[stage]()

    @staticmethod
    def buffers(groups, shape):
        count = parts_of(shape)
        return line_buffers(groups, (shape[0] // count, shape[1])) * count

    @staticmethod
    def copies(groups, shape):
        return parts_of(shape) * max(3, groups - 1)


class Side:
    def __init__(self, shards, groups, plane_shapes, line_shapes, extra=0):
        self.shards, self.groups, self.extra = shards, groups, extra
        self.plane_shapes, self.line_shapes = plane_shapes, line_shapes

    def outs(self):
        return [jax.ShapeDtypeStruct(shape, LOW) for shape in self.plane_shapes + self.line_shapes]

    def scratch(self):
        groups, shards = self.groups, self.shards
        shapes = [pltpu.VMEM(shape, LOW) for shape in self.plane_shapes + self.line_shapes]
        for shape in self.plane_shapes:
            shapes += plane_buffers(shards, shape)
        for shape in self.line_shapes:
            shapes += [pltpu.VMEM(shape, LOW)] + LineSum.buffers(groups, shape)
        count = 2 * self.shards + len(self.plane_shapes) * max(6, shards - 1)
        count += sum(LineSum.copies(groups, shape) for shape in self.line_shapes) + self.extra
        loads = 4 * len(self.plane_shapes) + 2 * len(self.line_shapes) + 1
        return shapes + [pltpu.SemaphoreType.DMA((count,))] * 2 + [pltpu.SemaphoreType.DMA((loads,))]

    def run(self, step, sources, outs, bufs):
        *bufs, send, recv, load = bufs
        totals, bufs = take(bufs, len(outs))
        me, group, core = place()
        copies = Copies(send, recv)
        shards, groups = self.shards, self.groups

        @pl.when(step == 0)
        def _():
            meet(everyone_near(shards, groups))

        planes, lines, loads = [], [], []
        for i, shape in enumerate(self.plane_shapes):
            some, bufs = take(bufs, len(plane_buffers(shards, shape)))
            planes.append(
                reduce_over_plane(
                    copies, load.at[pl.ds(3 * i, 3)], shards, sources[i], totals[i], some
                )
            )
        first = len(self.plane_shapes)
        for i, shape in enumerate(self.line_shapes):
            (own,), bufs = take(bufs, 1)
            some, bufs = take(bufs, len(LineSum.buffers(groups, shape)))
            source = at_rows(sources[first + i], 0, shape[0])
            loads.append(pltpu.make_async_copy(source, own, load.at[3 * first + i]))
            lines.append(LineSum(copies, groups, source, own, totals[first + i], some))

        def begin():
            for stages in planes:
                stages[0]()
            for stages in planes:
                stages[1]()
            for part in range(PARTS):
                for line in lines:
                    line.run(part, 0)
            for one in loads:
                one.start()

        def load_done():
            for one in loads:
                one.wait()

        def of_lines(part, stage):
            def go():
                for line in lines:
                    line.run(part, stage)

            return go

        def merge():
            for stages in planes:
                stages[2]()

        received = {1: [0], 2: [1], 3: [2, 3], 4: [4], 5: [5, 6], 6: [7]}
        given = {3: [0, 1], 4: [2, 3], 5: [4], 6: [5, 6], 7: [7]}
        plan = {0: [begin]}
        for when in range(1, 8):
            plan[when] = [load_done] if when == 1 else []
            plan[when] += [of_lines(part, 1) for part in received.get(when, [])]
            plan[when] += [merge] if when == 3 else []
            plan[when] += [of_lines(part, 2) for part in given.get(when, [])]
        for when, stages in plan.items():

            @pl.when(step == when)
            def _(stages=stages):
                for stage in stages:
                    stage()

        count = len(outs)
        stores = [
            pltpu.make_async_copy(total, out, load.at[load.shape[0] - 1 - count + i])
            for i, (total, out) in enumerate(zip(totals, outs))
        ]

        def end():
            for stages, store in zip(planes, stores):
                stages[3]()
                store.start()
            for part in range(PARTS):
                for line in lines:
                    line.run(part, 3)
            for store in stores[len(planes) :]:
                store.start()
            for store in stores:
                store.wait()

        return copies, end


class Blocks:
    def __init__(self, copies, partner, count, block, held, got):
        self.count, self.block = count, block
        self.copies = [
            copies(
                held.at[pl.ds(k % (held.shape[0] // block) * block, block), :],
                got.at[pl.ds(k * block, block), :],
                partner,
            )
            for k in range(count)
        ]
        self.slots = held.shape[0] // block
        self.held, self.got = held, got

    def begin(self, step, first):
        for k in range(self.count):

            @pl.when(step == first + k + 1)
            def _(k=k):
                self.copies[k].start()
                if k + 1 >= self.slots and k + 1 < self.count:
                    self.copies[k + 1 - self.slots].wait_send()

    def put(self, number, values):
        self.held[pl.ds(lax.rem(number, self.slots) * self.block, self.block), :] = values

    def take(self, step, first):
        for k in range(self.count):
            pl.when(step == first + k)(self.copies[k].wait_recv)
        start = jnp.clip(step - first, 0, self.count - 1) * self.block
        return self.got[pl.ds(pl.multiple_of(start, self.block), self.block), :]

    def end(self, sent_last, received):
        if sent_last:
            self.copies[-1].start()
        for k in range(max(0, self.count - self.slots), self.count):
            self.copies[k].wait_send()
        if received:
            for copy in self.copies:
                copy.wait_recv()


def everyone_near(shards, groups):
    me, group, core = place()
    return (
        [device(lax.rem(me + k, shards), group, core) for k in range(1, shards)]
        + [device(me, lax.rem(group + k, groups), core) for k in range(1, groups)]
        + [device(me, group, 1 - core)]
    )


def take(refs, count):
    return refs[:count], refs[count:]


def finish_kernel(shards, groups, counts, rows, skip, length_ref, *refs):
    smalls, refs = take(refs, 1 + max(k for k, _ in rows))
    (grad_ref,), refs = take(refs, 1)
    lows, refs = take(refs, counts[0])
    ready, refs = take(refs, counts[1])
    n = counts[0] + 2
    mine_out, refs = take(refs, n)
    other, refs = take(refs, n + counts[1])
    (total_ref,), refs = take(refs, 1)
    mine, refs = take(refs, n)
    levels, refs = take(refs, 2)
    own, refs = take(refs, counts[0])
    plane_bufs = []
    for level in levels:
        some, refs = take(refs, len(plane_buffers(shards, level.shape)))
        plane_bufs.append(some)
    line_bufs = []
    for one in mine:
        some, refs = take(refs, len(LineSum.buffers(groups, one.shape)))
        line_bufs.append(some)
    small_a, small_b, small_c, send, recv, load = refs
    me, group, core = place()
    partner = device(me, group, 1 - core)
    plane = [device(lax.rem(me + k, shards), group, core) for k in range(1, shards)]
    line = [device(me, lax.rem(group + k, groups), core) for k in range(1, groups)]
    copies = Copies(send, recv)

    def go(source, target, where):
        copy = copies(source, target, where)
        copy.start()
        return copy

    def finish(some):
        for copy in some:
            copy.wait_send()
            copy.wait_recv()

    parts = [
        at_rows(low, 0 if i else skip, one.shape[0]) for i, (low, one) in enumerate(zip(lows, own))
    ]
    loads = [pltpu.make_async_copy(low, own[i], load.at[6 + i]) for i, low in enumerate(parts)]
    for copy in loads:
        copy.start()
    for i, (k, row) in enumerate(rows):
        values = smalls[k][row : row + 1, :]
        small_a[me, i : i + 1, : values.shape[1]] = values
        if values.shape[1] < small_a.shape[2]:
            rest = small_a.shape[2] - values.shape[1]
            small_a[me, i : i + 1, values.shape[1] :] = jnp.zeros((1, rest), F32)
    small_a[me, len(rows) :, :] = jnp.full(
        (small_a.shape[1] - len(rows), small_a.shape[2]), length_ref[0].astype(F32)
    )
    meet(everyone_near(shards, groups))
    columns = levels[0].shape[1]
    planes = [
        reduce_over_plane(
            copies,
            load.at[pl.ds(3 * i, 3)],
            shards,
            grad_ref.at[:, pl.ds(i * columns, columns)],
            level,
            plane_bufs[i],
        )
        for i, level in enumerate(levels)
    ]
    sums = [
        LineSum(copies, groups, source, part, mine[i], line_bufs[i])
        for i, (source, part) in enumerate(zip(parts + list(levels), list(own) + list(levels)))
    ]
    early, halves = sums[: counts[0]], sums[counts[0] :]
    for stages in planes:
        stages[0]()
        stages[1]()
    for one in early:
        one.all(0)
    small_copies = [go(small_a.at[me], small_a.at[me], where) for where in plane]
    swaps = [go(source, target, partner) for source, target in zip(ready, other[n:])]
    for copy in loads:
        copy.wait()
    planes[0][2]()
    planes[1][2]()
    for one in early:
        one.all(1, 0, one.count // 2)
    planes[0][3]()
    halves[0].all(0)
    finish(small_copies)
    small_b[group] = sum(small_a[k] for k in range(shards))
    small_copies = [go(small_b.at[group], small_b.at[group], where) for where in line]
    for one in early:
        one.all(1, one.count // 2)
        one.all(2, 0, one.count // 2)
    planes[1][3]()
    halves[1].all(0)
    for one in early:
        one.all(2, one.count // 2)
    finish(small_copies)
    small_c[core] = sum(small_b[k] for k in range(groups))
    small_copies = [go(small_c.at[core], small_c.at[core], partner)]
    halves[0].all(1)
    halves[1].all(1)
    halves[0].all(2)
    stores = []

    def hand(i):
        sums[i].all(3)
        swaps.append(go(mine[i], other[i], partner))
        stores.append(pltpu.make_async_copy(mine[i], mine_out[i], load.at[6 + counts[0] + i]))
        stores[-1].start()

    for i in range(counts[0]):
        hand(i)
    halves[1].all(2)
    hand(counts[0])
    hand(counts[0] + 1)
    finish(small_copies)
    total_ref[...] = small_c[0] + small_c[1]
    finish(swaps)
    for store in stores:
        store.wait()


def finish_sums(grad, length, smalls, rows, lows, skip, ready, shards, groups):
    level = (grad.shape[0] // shards, grad.shape[1] // 2)
    shapes = [(low.shape[0] - (0 if i else skip), low.shape[1]) for i, low in enumerate(lows)]
    shapes += [level] * 2
    others = shapes + [one.shape for one in ready]
    vmem = pl.BlockSpec(memory_space=pltpu.VMEM)
    hbm = pl.BlockSpec(memory_space=pltpu.HBM)
    scratch = [pltpu.VMEM(shape, LOW) for shape in shapes + [level] * 2 + shapes[: len(lows)]]
    for _ in range(2):
        scratch += plane_buffers(shards, level)
    for shape in shapes:
        scratch += LineSum.buffers(groups, shape)
    count = 2 * max(6, shards) + sum(LineSum.copies(groups, shape) for shape in shapes)
    count += len(others) + shards + groups
    small = (8, max(one.shape[1] for one in smalls))
    outs = pl.pallas_call(
        partial(finish_kernel, shards, groups, (len(lows), len(ready)), rows, skip),
        out_shape=[jax.ShapeDtypeStruct(shape, LOW) for shape in shapes + others]
        + [jax.ShapeDtypeStruct(small, F32)],
        in_specs=[pl.BlockSpec(memory_space=pltpu.SMEM)]
        + [vmem] * len(smalls)
        + [hbm] * (1 + len(lows) + len(ready)),
        out_specs=[hbm] * (len(shapes) + len(others)) + [vmem],
        scratch_shapes=scratch
        + [pltpu.VMEM((size,) + small, F32) for size in (shards, groups, 2)]
        + [pltpu.SemaphoreType.DMA((count,)), pltpu.SemaphoreType.DMA((count,))]
        + [pltpu.SemaphoreType.DMA((6 + len(lows) + len(shapes),))],
        compiler_params=pltpu.CompilerParams(
            collective_id=1, has_side_effects=True, vmem_limit_bytes=62 << 20
        ),
        name="finish",
    )(length, *smalls, grad, *lows, *ready)
    n = len(shapes)
    return outs[:n], outs[n:-1], outs[-1]


def two_parts(column):
    high = column.astype(LOW)
    return high, (column - high.astype(F32)).astype(LOW)


def below(ref, here, heads):
    return jnp.concatenate([ref[here, pl.ds(h * LANES, LANES)] for h in range(heads)], axis=0)


def attend_kernel(block, width, lens_ref, q_ref, k_ref, v_ref, att_ref, qx_ref):
    rows = q_ref.shape[0]
    heads = q_ref.shape[1] // LANES
    length = lens_ref[pl.program_id(0)]
    lane = lax.broadcasted_iota(jnp.int32, (block, LANES), 1)
    keep = lax.broadcasted_iota(jnp.int32, (block, block), 1) <= lax.broadcasted_iota(
        jnp.int32, (block, block), 0
    )
    for step in range(rows // block):
        start = step * block
        here = pl.ds(start, block)

        @pl.when(start < length)
        def _():
            outs = []
            for head in range(heads):
                lanes = pl.ds(head * LANES, LANES)
                query = q_ref[here, lanes]
                probs = jnp.exp(nt(query, k_ref[here, :]))
                probs = jnp.where(keep, probs, 0.0).astype(LOW)
                total = nn(probs, v_ref[here, :])
                if step:
                    probs = jnp.exp(nt(query, k_ref[pl.ds(0, start), :])).astype(LOW)
                    total += nn(probs, v_ref[pl.ds(0, start), :])
                weight = total[:, width : width + 1]
                outs.append(total / weight)
                high, rest = two_parts(-jnp.log(weight))
                qx_ref[here, lanes] = jnp.where(
                    lane == width, high, jnp.where(lane == width + 1, rest, query)
                )
            for pair in range(heads // 2):
                att_ref[here, pl.ds(pair * LANES, LANES)] = jnp.where(
                    lane < width, outs[2 * pair], pltpu.roll(outs[2 * pair + 1], width, 1)
                ).astype(LOW)

        @pl.when(start >= length)
        def _():
            att_ref[here, :] = jnp.zeros((block, att_ref.shape[1]), LOW)
            qx_ref[here, :] = jnp.zeros((block, qx_ref.shape[1]), LOW)


def attend_back_kernel(block, width, side, q_ref, k_ref, v_ref, do_ref, *refs):
    count = len(side.plane_shapes) + len(side.line_shapes)
    sources, refs = take(refs, count)
    (dq_ref, dk_ref, dv_ref), refs = take(refs, 3)
    totals, bufs = take(refs, count)
    grid_step = pl.program_id(0) * pl.num_programs(1) + pl.program_id(1)
    _, end = side.run(grid_step, sources, totals, bufs)
    rows = q_ref.shape[0]
    heads = q_ref.shape[1] // LANES
    lane = lax.broadcasted_iota(jnp.int32, (block, LANES), 1)
    shape = (block, heads * block)
    keep = lax.broadcasted_iota(jnp.int32, shape, 0) <= lax.rem(
        lax.broadcasted_iota(jnp.int32, shape, 1), block
    )
    dk_ref[...] = jnp.zeros(dk_ref.shape, F32)
    dv_ref[...] = jnp.zeros(dv_ref.shape, F32)
    for step in range(rows // block):
        start = step * block
        here = pl.ds(start, block)
        query, dout = below(q_ref, here, heads), below(do_ref, here, heads)

        def one(keys, masked):
            key, value = k_ref[keys, :], v_ref[keys, :]
            probs = jnp.exp(nt(key, query))
            if masked:
                probs = jnp.where(keep, probs, 0.0)
            dscores = (probs * nt(value, dout)).astype(LOW)
            dv_ref[keys, :] += nn(probs.astype(LOW), dout)
            dk_ref[keys, :] += nn(dscores, query)
            return tn(dscores, key)

        dquery = one(here, True)
        if step:
            dquery += one(pl.ds(0, start), False)
        for pair in range(heads // 2):
            first = dquery[2 * pair * block : (2 * pair + 1) * block]
            second = dquery[(2 * pair + 1) * block : (2 * pair + 2) * block]
            dq_ref[here, pl.ds(pair * LANES, LANES)] = jnp.where(
                lane < width, first, pltpu.roll(second, width, 1)
            )
    pl.when(grid_step == pl.num_programs(0) * pl.num_programs(1) - 1)(end)


def attention_grid(slots, groups, per_group, rows):
    wide = pl.BlockSpec((rows, per_group * LANES), lambda s, g, lens: (s, g))
    dense = pl.BlockSpec((rows, per_group * LANES // 2), lambda s, g, lens: (s, g))
    narrow = pl.BlockSpec((rows, LANES), lambda s, g, lens: (s, g))
    return (slots, groups), wide, dense, narrow


def attend(lens, queries, keys, values, rows, width, block):
    slots, groups = queries.shape[0] // rows, keys.shape[1] // LANES
    per_group = queries.shape[1] // LANES // groups
    grid, wide, dense, narrow = attention_grid(slots, groups, per_group, rows)
    flops = 4 * slots * groups * per_group * rows * rows * LANES
    return pl.pallas_call(
        partial(attend_kernel, block, width),
        out_shape=(
            jax.ShapeDtypeStruct((queries.shape[0], queries.shape[1] // 2), LOW),
            jax.ShapeDtypeStruct(queries.shape, LOW),
        ),
        grid_spec=pltpu.PrefetchScalarGridSpec(
            num_scalar_prefetch=1,
            grid=grid,
            in_specs=[wide, narrow, narrow],
            out_specs=[dense, wide],
        ),
        cost_estimate=pl.CostEstimate(flops=flops, bytes_accessed=1 << 23, transcendentals=0),
        name="attend",
    )(lens, queries, keys, values)


def attend_back(queries, keys, values, douts, rows, width, block, side, sources):
    slots, groups = queries.shape[0] // rows, keys.shape[1] // LANES
    per_group = queries.shape[1] // LANES // groups
    wide = pl.BlockSpec((rows, per_group * LANES), lambda s, g: (s, g))
    dense = pl.BlockSpec((rows, per_group * LANES // 2), lambda s, g: (s, g))
    narrow = pl.BlockSpec((rows, LANES), lambda s, g: (s, g))
    flops = 10 * slots * groups * per_group * rows * rows * LANES
    return pl.pallas_call(
        partial(attend_back_kernel, block, width, side),
        out_shape=[
            jax.ShapeDtypeStruct((queries.shape[0], queries.shape[1] // 2), F32),
            jax.ShapeDtypeStruct(keys.shape, F32),
            jax.ShapeDtypeStruct(keys.shape, F32),
        ]
        + side.outs(),
        grid=(slots, groups),
        in_specs=[wide, narrow, narrow, wide]
        + [pl.BlockSpec(memory_space=pltpu.HBM)] * len(sources),
        out_specs=[dense, narrow, narrow]
        + [pl.BlockSpec(memory_space=pltpu.HBM)] * len(side.outs()),
        scratch_shapes=side.scratch(),
        cost_estimate=pl.CostEstimate(flops=flops, bytes_accessed=1 << 24, transcendentals=0),
        compiler_params=pltpu.CompilerParams(
            collective_id=5, has_side_effects=True, vmem_limit_bytes=62 << 20
        ),
        name="attend_back",
    )(queries, keys, values, douts, *sources)


def swap_halves(values, width):
    lane = lax.broadcasted_iota(jnp.int32, values.shape, 1)
    half = width // 2
    return jnp.where(
        lane % width < half, pltpu.roll(values, LANES - half, 1), pltpu.roll(values, half, 1)
    )


def head_sum(values, width):
    same = lax.broadcasted_iota(jnp.int32, (LANES, LANES), 0) // width
    same = (same == lax.broadcasted_iota(jnp.int32, (LANES, LANES), 1) // width).astype(LOW)
    high, rest = two_parts(values)
    return nn(high, same) + nn(rest, same)


def row_rsqrt(values):
    return lax.rsqrt(jnp.mean(values * values, axis=1, keepdims=True) + EPS)


def is_live(lens_ref, step, per_slot, block):
    return lax.rem(step, per_slot) * block < lens_ref[lax.div(step, per_slot)]


def qkv_kernel(
    per_slot, counts, width, scale, lens_ref, own_ref, other_ref, w_ref, ga_ref, gh_ref, cos_ref, sin_ref,
    normed_ref, raw_ref, q_ref, k_ref, v_ref,
):
    step = pl.program_id(0)
    block = own_ref.shape[0]
    q_tiles, kv_tiles = counts

    @pl.when(is_live(lens_ref, step, per_slot, block))
    def _():
        x = jnp.where(step < per_slot, own_ref[...], other_ref[...]).astype(F32)
        normed = (x * row_rsqrt(x) * ga_ref[...]).astype(LOW)
        normed_ref[...] = normed
        lane = lax.broadcasted_iota(jnp.int32, (block, LANES), 1)
        zero = jnp.zeros((block, LANES), F32)
        ones = jnp.where(lane < width + 2, 1.0, 0.0)
        cosine, sine = cos_ref[...], sin_ref[...]

        def put(ref, tile, values, rest):
            ref[:, pl.ds(2 * tile * LANES, LANES)] = jnp.where(lane < width, values, rest).astype(LOW)
            ref[:, pl.ds((2 * tile + 1) * LANES, LANES)] = jnp.where(
                lane < width, pltpu.roll(values, width, 1), rest
            ).astype(LOW)

        for tile in range(q_tiles + 2 * kv_tiles):
            lanes = pl.ds(tile * LANES, LANES)
            if tile % 2 == 0:
                pair = nn(normed, w_ref[:, pl.ds(tile * LANES, 2 * LANES)])
            values = pair[:, (tile % 2) * LANES : (tile % 2 + 1) * LANES]
            if tile >= q_tiles + kv_tiles:
                put(v_ref, tile - q_tiles - kv_tiles, values, ones)
                continue
            raw_ref[:, lanes] = values
            is_query = tile < q_tiles
            gain = gh_ref[0:1, :] if is_query else gh_ref[1:2, :]
            values *= lax.rsqrt(head_sum(values * values, width) * (1.0 / width) + EPS) * gain
            values = values * cosine + swap_halves(values, width) * sine
            if is_query:
                put(q_ref, tile, values * scale, zero)
            else:
                put(k_ref, tile - q_tiles, values, ones)

    @pl.when(jnp.logical_not(is_live(lens_ref, step, per_slot, block)))
    def _():
        for ref in (normed_ref, raw_ref, q_ref, k_ref, v_ref):
            ref[...] = jnp.zeros(ref.shape, ref.dtype)


def out_kernel(
    per_slot, length_ref, att_ref, w_ref, x_ref, gain_ref, resid_ref, normed_ref, sums_ref,
    other_out, give, got, hold, other, send, recv, store,
):
    step = pl.program_id(0)
    block = att_ref.shape[0]
    me, group, core = place()
    partner = device(me, group, 1 - core)
    copies = Copies(send, recv)
    parts = Blocks(copies, partner, per_slot, block, give, got)
    normed_parts = Blocks(copies, partner, per_slot, block, hold, other)

    @pl.when(step == 0)
    def _():
        meet([partner])
        sums_ref[...] = jnp.zeros(sums_ref.shape, F32)

    parts.begin(step, 0)
    normed_parts.begin(step, per_slot)
    product = nn(att_ref[...], w_ref[...])

    @pl.when(step < per_slot)
    def _():
        parts.put(step, product.astype(LOW))

    @pl.when(step >= per_slot)
    def _():
        number = step - per_slot
        valid = lax.broadcasted_iota(jnp.int32, (block, 1), 0) + number * block < length_ref[0]
        attn_out = product + parts.take(step, per_slot).astype(F32)
        resid = x_ref[...].astype(F32) + attn_out
        resid_ref[...] = resid
        normed = (resid * row_rsqrt(resid) * gain_ref[...]).astype(LOW)
        normed_ref[...] = normed
        normed_parts.put(number, normed)
        for row, values in ((0, resid), (1, attn_out)):
            sums_ref[row : row + 1, :] += jnp.sum(
                jnp.where(valid, values * values, 0.0), axis=0, keepdims=True
            )

    @pl.when(step == 2 * per_slot - 1)
    def _():
        parts.end(False, False)
        normed_parts.end(True, True)
        copy = pltpu.make_async_copy(other, other_out, store.at[0])
        copy.start()
        copy.wait()


def ffn_kernel(
    per_slot, shards, chained, last, side, offset, x_own, x_other, g_own, g_other, gathered_ref, *refs
):
    if chained:
        (mlp_in, db_in), refs = take(refs, 2)
    if last:
        (length_ref, resid_ref, gain_ref), refs = take(refs, 3)
    count = len(side.plane_shapes) + len(side.line_shapes)
    sources, refs = take(refs, count)
    if last:
        (out_ref, dresid_ref, dattn_ref, sums_ref, dattn_out), refs = take(refs, 5)
    else:
        (mlp_ref, db_ref), refs = take(refs, 2)
    (grad_out,), refs = take(refs, 1)
    totals, refs = take(refs, count)
    (acc_ref, accd_ref, given_ref, w_ref, wd_ref, grad_ref, load), refs = take(refs, 7)
    exchange, bufs = take(refs, 6 if last else 0)
    step = pl.program_id(0)
    copies, end = side.run(step, sources, totals, bufs)
    own = step >= per_slot if last else step < per_slot
    units, depth = wd_ref.shape
    block = x_own.shape[0]
    me, group, core = place()
    partner = device(me, group, 1 - core)
    half, columns, d_rows = shards // 2, depth // 2, depth // shards
    packed = grad_ref.shape[0] // shards
    size = packed - d_rows
    folds = grad_ref.shape[1] // columns

    def folded(ref, shard, fold):
        return ref.at[shard, pl.ds(offset + d_rows, size), pl.ds(fold * columns, columns)]

    def unfolded(i, fold):
        return at(wd_ref, (i * folds + fold) * size, size, core * columns, columns)

    tiles = [(i, fold) for i in range(half) for fold in range(folds)]
    given = [
        copies(folded(gathered_ref, (1 - core) * half + i, fold), unfolded(i, fold), partner)
        for i, fold in tiles
    ]
    loads = [
        pltpu.make_async_copy(
            gathered_ref.at[shard, pl.ds(offset, d_rows), :],
            w_ref.at[pl.ds(shard * d_rows, d_rows), :],
            load.at[shard],
        )
        for shard in range(shards)
    ] + [
        pltpu.make_async_copy(
            folded(gathered_ref, core * half + i, fold), unfolded(i, fold), load.at[shards + k]
        )
        for k, (i, fold) in enumerate(tiles)
    ]

    if last:
        give_mlp, got_mlp, give_db, got_db, hold, other = exchange
        mlp_parts = Blocks(copies, partner, per_slot, block, give_mlp, got_mlp)
        db_parts = Blocks(copies, partner, per_slot, block, give_db, got_db)
        attn_parts = Blocks(copies, partner, per_slot, block, hold, other)
        mlp_parts.begin(step, 0)
        db_parts.begin(step, 0)
        attn_parts.begin(step, per_slot)

    @pl.when(step == 0)
    def _():
        if last:
            sums_ref[...] = jnp.zeros(sums_ref.shape, F32)
        for copy in given + loads:
            copy.start()
        acc_ref[...] = jnp.zeros(acc_ref.shape, F32)
        accd_ref[...] = jnp.zeros(accd_ref.shape, F32)
        for copy in loads:
            copy.wait()
        for copy in given:
            copy.wait_send()
            copy.wait_recv()

    x = jnp.where(own, x_own[...], x_other[...])
    g = jnp.where(own, g_own[...], g_other[...])
    gate = nn(x, w_ref[:, :units])
    up = nn(x, w_ref[:, units:])
    d_hidden = nt(g, wd_ref[...])
    sig = jax.nn.sigmoid(gate)
    silu = gate * sig
    hidden = (silu * up).astype(LOW)
    d_gate = (d_hidden * up * (sig * (1.0 + gate * (1.0 - sig)))).astype(LOW)
    d_up = (d_hidden * silu).astype(LOW)
    mlp = nn(hidden, wd_ref[...])
    d_b = nt(d_gate, w_ref[:, :units]) + nt(d_up, w_ref[:, units:])
    if chained:
        mlp += mlp_in[...]
        d_b += db_in[...]
    if last:

        @pl.when(step < per_slot)
        def _():
            mlp_parts.put(step, mlp.astype(LOW))
            db_parts.put(step, d_b.astype(LOW))

        @pl.when(step >= per_slot)
        def _():
            number = step - per_slot
            valid = lax.broadcasted_iota(jnp.int32, (block, 1), 0) + number * block < length_ref[0]
            resid = resid_ref[...]
            mlp_out = mlp + mlp_parts.take(step, per_slot).astype(F32)
            out_ref[...] = jnp.where(valid, resid + mlp_out, 0.0).astype(LOW)
            d_norm, d_gain = norm_back(
                resid, d_b + db_parts.take(step, per_slot).astype(F32), gain_ref[...]
            )
            d_resid = jnp.where(valid, g.astype(F32) + d_norm, 0.0)
            dresid_ref[...] = d_resid
            d_attn = d_resid.astype(LOW)
            dattn_ref[...] = d_attn
            attn_parts.put(number, d_attn)
            for row, values in ((0, mlp_out * mlp_out), (1, d_gain)):
                sums_ref[row : row + 1, :] += jnp.sum(
                    jnp.where(valid, values, 0.0), axis=0, keepdims=True
                )

    else:
        mlp_ref[...] = mlp
        db_ref[...] = d_b
    acc_ref[:, :units] += tn(x, d_gate)
    acc_ref[:, units:] += tn(x, d_up)
    accd_ref[...] += tn(hidden, g)

    @pl.when(step == pl.num_programs(0) - 1)
    def _():
        mine = pl.ds(pl.multiple_of(core * columns, columns), columns)
        theirs = pl.ds(pl.multiple_of((1 - core) * columns, columns), columns)
        given_ref[...] = accd_ref[:, theirs].astype(LOW)
        for shard in range(shards):
            grad_ref[pl.ds(shard * packed, d_rows), :] = acc_ref[
                pl.ds(shard * d_rows, d_rows), :
            ].astype(LOW)
        out = []
        for i in range(half):
            for fold in range(folds):
                row = i * folds * size + fold * size
                to = pl.ds(
                    pl.multiple_of((core * half + i) * packed + d_rows, 8), size
                )
                lanes = pl.ds(fold * columns, columns)
                out.append(
                    copies(
                        given_ref.at[pl.ds(row, size), :],
                        grad_ref.at[to, lanes],
                        partner,
                    )
                )
                out[-1].start()
                grad_ref[to, lanes] = accd_ref[pl.ds(row, size), mine].astype(LOW)
        for copy in out:
            copy.wait_send()
            copy.wait_recv()
        stores = [pltpu.make_async_copy(grad_ref, grad_out, load.at[0])]
        stores[0].start()
        if last:
            mlp_parts.end(False, False)
            db_parts.end(False, False)
            attn_parts.end(True, True)
            stores.append(pltpu.make_async_copy(other, dattn_out, load.at[1]))
            stores[1].start()
        end()
        for store in stores:
            store.wait()


def norm_back(values, dy, gain):
    inverse = row_rsqrt(values)
    scaled = dy * gain
    inner = jnp.mean(values * scaled, axis=1, keepdims=True)
    return inverse * scaled - values * (inverse * inverse * inverse * inner), dy * values * inverse


def dout_kernel(
    per_slot, width, own_ref, other_ref, att_ref, w_ref, do_ref, grad_out,
    acc_ref, give, hold, send, recv, store,
):
    step = pl.program_id(0)
    block = own_ref.shape[0]
    me, group, core = place()

    @pl.when(step == 0)
    def _():
        meet([device(me, group, 1 - core)])
        acc_ref[...] = jnp.zeros(acc_ref.shape, F32)

    d_attn = jnp.where(step < per_slot, own_ref[...], other_ref[...])
    lane = lax.broadcasted_iota(jnp.int32, (block, LANES), 1)
    att = att_ref[...]
    acc_ref[...] += tn(att, d_attn)
    for tile in range(att.shape[1] // LANES):
        lanes = slice(tile * LANES, (tile + 1) * LANES)
        if tile % 2 == 0:
            pair = nt(d_attn, w_ref[tile * LANES : (tile + 2) * LANES, :])
        dout = pair[:, (tile % 2) * LANES : (tile % 2 + 1) * LANES].astype(LOW).astype(F32)
        delta = -head_sum(dout * att[:, lanes].astype(F32), width)
        for head, (values, column) in enumerate(
            ((dout, pltpu.roll(delta, width, 1)), (pltpu.roll(dout, width, 1), delta))
        ):
            high, rest = two_parts(column)
            column = jnp.where(
                lane == width, high, jnp.where(lane == width + 1, rest, jnp.zeros_like(rest))
            )
            do_ref[:, pl.ds((2 * tile + head) * LANES, LANES)] = jnp.where(
                lane < width, values.astype(LOW), column
            )

    @pl.when(step == pl.num_programs(0) - 1)
    def _():
        rows, columns = give.shape
        theirs = pl.ds(pl.multiple_of((1 - core) * columns, columns), columns)
        give[...] = acc_ref[:, theirs].astype(LOW)
        mine = pl.ds(pl.multiple_of(core * columns, columns), columns)
        goal = at_rows(hold, core * rows, rows)
        hold[pl.ds(pl.multiple_of(core * rows, rows), rows), :] = acc_ref[:, mine].astype(LOW)
        copy = Copies(send, recv)(give, goal, device(me, group, 1 - core))
        copy.start()
        copy.wait_send()
        copy.wait_recv()
        local = pltpu.make_async_copy(hold, grad_out, store.at[0])
        local.start()
        local.wait()


def qkv_back_kernel(
    per_slot, counts, width, scale, side, dq_ref, dk_ref, dv_ref, raw_ref, normed_ref, w_ref, gh_ref,
    cos_ref, sin_ref, x_ref, dresid_ref, ga_ref, *refs,
):
    step = pl.program_id(0)
    block = dq_ref.shape[0]
    q_tiles, kv_tiles = counts
    me, group, core = place()
    partner = device(me, group, 1 - core)
    count = len(side.plane_shapes) + len(side.line_shapes)
    sources, refs = take(refs, count)
    (out_ref, grad_ref, gain_ref, sums_ref), refs = take(refs, 4)
    totals, refs = take(refs, count)
    (acc_ref, low_ref, give, got), bufs = take(refs, 4)
    copies, end = side.run(step, sources, totals, bufs)
    parts = Blocks(copies, partner, per_slot, block, give, got)

    @pl.when(step == 0)
    def _():
        acc_ref[...] = jnp.zeros(acc_ref.shape, F32)
        gain_ref[...] = jnp.zeros(gain_ref.shape, F32)
        sums_ref[...] = jnp.zeros(sums_ref.shape, F32)

    parts.begin(step, 0)
    lane = lax.broadcasted_iota(jnp.int32, (block, LANES), 1)
    cosine, sine = cos_ref[...], sin_ref[...]

    def pair(ref, tile):
        return jnp.where(
            lane < width,
            ref[:, pl.ds(2 * tile * LANES, LANES)],
            pltpu.roll(ref[:, pl.ds((2 * tile + 1) * LANES, LANES)], width, 1),
        )

    for tile in range(q_tiles + 2 * kv_tiles):
        lanes = pl.ds(tile * LANES, LANES)
        if tile >= q_tiles + kv_tiles:
            low_ref[:, lanes] = pair(dv_ref, tile - q_tiles - kv_tiles).astype(LOW)
            continue
        if tile < q_tiles:
            turned, row = dq_ref[:, lanes] * scale, 0
        else:
            turned, row = pair(dk_ref, tile - q_tiles), 1
        gain = gh_ref[row : row + 1, :]
        dy = turned * cosine + swap_halves(turned * sine, width)
        values = raw_ref[:, lanes]
        inverse = lax.rsqrt(head_sum(values * values, width) * (1.0 / width) + EPS)
        scaled = dy * gain
        inner = head_sum(values * scaled, width) * (1.0 / width)
        low_ref[:, lanes] = (
            inverse * scaled - values * (inverse * inverse * inverse * inner)
        ).astype(LOW)
        gain_ref[row : row + 1, :] += jnp.sum(dy * values * inverse, axis=0, keepdims=True)
    low = low_ref[...]
    acc_ref[...] += tn(normed_ref[...], low)
    d_a = nt(low, w_ref[...])

    @pl.when(step < per_slot)
    def _():
        parts.put(step, d_a.astype(LOW))

    @pl.when(step >= per_slot)
    def _():
        d_norm, d_gain = norm_back(
            x_ref[...].astype(F32), d_a + parts.take(step, per_slot).astype(F32), ga_ref[...]
        )
        out_ref[...] = (dresid_ref[...] + d_norm).astype(LOW)
        sums_ref[0:1, :] += jnp.sum(d_gain, axis=0, keepdims=True)

    @pl.when(step == 2 * per_slot - 1)
    def _():
        grad_ref[...] = acc_ref[...].astype(LOW)
        parts.end(False, False)
        end()


def assemble_kernel(chunks, half, folds, head_width, model_width, *refs):
    parts, refs = take(refs, 4 * chunks)
    pairs, refs = take(refs, 6)
    small_ref, gate_ref, up_ref, down_ref, *outs, ga_ref, gm_ref, stat_ref, gq_ref, gk_ref = refs
    first = lax.rem(lax.axis_index("rep"), 2) == 0

    def sides(mine, other):
        return [jnp.where(first, mine, other), jnp.where(first, other, mine)]

    units = parts[0].shape[1] // 2
    piece = units // half
    for chunk in range(chunks):
        top, low, other_top, other_low = parts[4 * chunk : 4 * chunk + 4]
        for side, values in enumerate(sides(top[...], other_top[...])):
            for j, ref in enumerate((gate_ref, up_ref)):
                for i in range(half):
                    to = ((side * half + i) * chunks + chunk) * piece
                    start = j * units + i * piece
                    ref[:, to : to + piece] = values[:, start : start + piece].astype(F32)
        columns = down_ref.shape[2] // 2
        for side, values in enumerate(sides(low[...], other_low[...])):
            for fold in range(folds):
                down_ref[chunk * folds + fold, :, side * columns : (side + 1) * columns] = values[
                    :, fold * columns : (fold + 1) * columns
                ].astype(F32)
    starts = [0, 0, 0, outs[2].shape[1] // 2]
    for ref, k, start in zip(outs, (0, 2, 4, 4), starts):
        width = ref.shape[1] // 2
        mine, other = (one[:, start : start + width] for one in pairs[k : k + 2])
        for side, values in enumerate(sides(mine, other)):
            ref[:, side * width : (side + 1) * width] = values.astype(F32)

    @pl.when(pl.program_id(0) == 0)
    def _():
        me = lax.axis_index("shard")
        width = ga_ref.shape[1]
        here = pl.ds(pl.multiple_of(me * width, width), width)
        ga_ref[...] = small_ref[0:1, here]
        gm_ref[...] = small_ref[1:2, here]
        lane = lax.broadcasted_iota(jnp.int32, (1, LANES), 1)
        count = small_ref[7:8, 0:1] * model_width
        roots = jnp.zeros((1, LANES), F32)
        for k in range(3):
            total = jnp.sum(small_ref[2 + k : 3 + k, :], axis=1, keepdims=True)
            roots = jnp.where(lane == k, jnp.sqrt(total / count), roots)
        stat_ref[...] = roots[:, : stat_ref.shape[1]]
        size = gq_ref.shape[1]
        for k, ref in enumerate((gq_ref, gk_ref)):
            gains = jnp.broadcast_to(small_ref[5 + k : 6 + k, :LANES], (8, LANES))
            gains += pltpu.roll(gains, head_width, 1)
            gains = pltpu.roll(gains, lax.rem(LANES - me * size, LANES), 1)
            ref[...] = gains[0:1, :size]


class Rows:
    def __init__(self, lens, rows, block):
        self.lens, self.block, self.per_slot = lens, block, rows // block

    def both(self, width):
        return pl.BlockSpec((self.block, width), lambda i, lens: (i, 0))

    def both_other_first(self, width):
        n = self.per_slot
        return pl.BlockSpec((self.block, width), lambda i, lens: (lax.rem(i + n, 2 * n), 0))

    def early(self, width):
        n = self.per_slot
        return pl.BlockSpec((self.block, width), lambda i, lens: (jnp.minimum(i, n - 1), 0))

    def late(self, width):
        n = self.per_slot
        return pl.BlockSpec((self.block, width), lambda i, lens: (jnp.maximum(i - n, 0), 0))

    def repeated(self, width):
        n = self.per_slot
        return pl.BlockSpec((self.block, width), lambda i, lens: (lax.rem(i, n), 0))

    def fixed(self, shape):
        return pl.BlockSpec(shape, lambda i, lens: (0, 0), pipeline_mode=pl.Buffered(1))

    def call(self, name, kernel, slots, in_specs, out_specs, outs, scratch, flops, *args):
        return pl.pallas_call(
            kernel,
            out_shape=[jax.ShapeDtypeStruct(shape, kind) for shape, kind in outs],
            grid_spec=pltpu.PrefetchScalarGridSpec(
                num_scalar_prefetch=1,
                grid=(slots * self.per_slot,),
                in_specs=in_specs,
                out_specs=out_specs,
                scratch_shapes=scratch,
            ),
            cost_estimate=pl.CostEstimate(
                flops=flops, bytes_accessed=1 << 24, transcendentals=0
            ),
            compiler_params=pltpu.CompilerParams(vmem_limit_bytes=62 << 20),
            name=name,
        )(self.lens, *args)


def local(
    inputs,
    lengths,
    gain_attn,
    w_query,
    w_key,
    w_value,
    gain_query,
    gain_key,
    w_out,
    gain_mlp,
    w_gate,
    w_up,
    w_down,
    cotangent,
):
    shards = lax.axis_size("shard")
    core = lax.axis_index("rep") % 2
    first = core == 0
    rows, width_all = inputs.shape[1], inputs.shape[2]
    head_width = gain_query.shape[0] * shards
    q_half, kv_half = w_query.shape[1] // 2, w_key.shape[1] // 2
    d_half = width_all // 2
    d_rows, ff_rows = w_query.shape[0], w_down.shape[0]
    block = min(256, rows)
    scale = 1.0 / math.sqrt(head_width)
    counts = (q_half // LANES, kv_half // LANES)

    def ordered(mine, other, axis):
        return jnp.where(
            first,
            jnp.concatenate([mine, other], axis=axis),
            jnp.concatenate([other, mine], axis=axis),
        )

    half_shards = shards // 2
    groups = lax.axis_size("rep") // 2
    chunks = 3
    piece = ff_rows // chunks
    units = half_shards * piece
    folds = 2 * units // d_half
    head_rows = gain_query.shape[0]

    def fold(part):
        return jnp.concatenate(jnp.split(part, folds, axis=-2), axis=-1)

    def unfold(part):
        return jnp.concatenate(jnp.split(part, folds, axis=-1), axis=-2)

    packed_rows = d_rows + piece // folds
    hbm = pl.BlockSpec(memory_space=pltpu.HBM)
    vmem = pl.BlockSpec(memory_space=pltpu.VMEM)
    chunk_sets = [list(range(chunks - 1)), [chunks - 1]]

    def pack(*refs):
        *refs, pack_a, pack_b, sems = refs
        packs = [
            (ref, [(i * packed_rows, chunk) for i, chunk in enumerate(some)])
            for ref, some in zip((pack_a, pack_b), chunk_sets)
        ]
        pack_kernel(shards, chunks, *refs, *packs, sems)

    if piece % LANES == 0:
        packs = pl.pallas_call(
            pack,
            out_shape=[
                jax.ShapeDtypeStruct((len(some) * packed_rows, 2 * units), LOW) for some in chunk_sets
            ],
            in_specs=[hbm] * 3,
            out_specs=[vmem] * 2,
            scratch_shapes=[pltpu.SemaphoreType.DMA((chunks * (2 * half_shards + folds),))],
            compiler_params=pltpu.CompilerParams(vmem_limit_bytes=62 << 20),
            name="pack",
        )(w_gate, w_up, w_down)
    else:

        def my_half(weight):
            half = weight.shape[1] // 2
            return jnp.where(first, weight[:, :half], weight[:, half:])

        def chunk_of(weight, chunk):
            columns = weight.reshape(d_rows, shards, chunks, piece)[:, :, chunk]
            return my_half(columns.reshape(d_rows, shards * piece))

        def packed_chunk(chunk):
            tall = fold(my_half(w_down)[chunk * piece : (chunk + 1) * piece])
            wide = jnp.concatenate([chunk_of(w_gate, chunk), chunk_of(w_up, chunk)], axis=1)
            return jnp.concatenate([wide, tall])

        packs = [jnp.concatenate([packed_chunk(k) for k in some]) for some in chunk_sets]
    gathered = [lax.all_gather(packs[0], "shard", axis=0)]

    def gain_row(*gains):
        flat = jnp.concatenate(gains)
        return jnp.pad(flat, (0, max(d_rows, LANES) - flat.shape[0]))[None]

    gain_rows = jnp.pad(
        jnp.concatenate(
            [gain_row(gain_attn), gain_row(gain_mlp), gain_row(gain_query, gain_key)]
        ),
        ((0, 13), (0, 0)),
    )

    def half_of(width):
        return lambda core: core * width

    wide_parts = [
        (0, 0, half_of(q_half), 0, q_half),
        (1, 0, half_of(kv_half), q_half, kv_half),
        (2, 0, half_of(kv_half), q_half + kv_half, kv_half),
    ]
    tall_parts = [(3, 1, 0, w_out.shape[0])]
    copies = len(wide_parts) * (shards + 2) + len(tall_parts) * (2 * shards + 3) + shards + 1
    w_qkv, w_o, gains, x_other = pl.pallas_call(
        partial(gather_kernel, shards, wide_parts, tall_parts, (6, copies)),
        out_shape=[
            jax.ShapeDtypeStruct(shape, LOW)
            for shape in (
                (width_all, q_half + 2 * kv_half),
                (half_shards * w_out.shape[0], width_all),
                (shards,) + gain_rows.shape,
                inputs.shape[1:],
            )
        ],
        in_specs=[hbm] * 6,
        out_specs=[hbm] * 4,
        scratch_shapes=[pltpu.SemaphoreType.DMA((copies,)), pltpu.SemaphoreType.DMA((copies,))],
        compiler_params=pltpu.CompilerParams(collective_id=0, has_side_effects=True),
        name="gather",
    )(w_query, w_key, w_value, w_out, gain_rows, inputs[0])
    gain_a = gains[:, 0, :d_rows].reshape(1, -1).astype(F32)
    gain_m = gains[:, 1, :d_rows].reshape(1, -1).astype(F32)
    gain_q = gains[:, 2, :head_rows].reshape(1, -1).astype(F32)
    gain_k = gains[:, 2, head_rows : 2 * head_rows].reshape(1, -1).astype(F32)
    gain_h = jnp.tile(jnp.concatenate([gain_q, gain_k]), (4, LANES // head_width))

    lens = jnp.concatenate([lengths, core_swap(lengths)])
    valid = (jnp.arange(rows) < lengths[0])[:, None]
    x_own = inputs[0]
    g_own = jnp.where(valid, cotangent[0], jnp.zeros((), LOW))
    g_other = core_swap(g_own)
    over = Rows(lens, rows, block)
    cosine, sine = rope_tables(rows, head_width)
    full, total = 2 * rows, w_qkv.shape[1]
    qk = q_half + kv_half

    normed_a, raw, queries, keys, values = over.call(
        "qkv",
        partial(qkv_kernel, over.per_slot, counts, head_width, scale),
        2,
        [over.early(width_all), over.late(width_all), over.fixed(w_qkv.shape)]
        + [over.fixed(gain_a.shape), over.fixed(gain_h.shape)]
        + [over.repeated(LANES), over.repeated(LANES)],
        [over.both(width_all), over.both(qk), over.both(2 * q_half), over.both(2 * kv_half)]
        + [over.both(2 * kv_half)],
        [((full, width_all), LOW), ((full, qk), F32), ((full, 2 * q_half), LOW)]
        + [((full, 2 * kv_half), LOW)] * 2,
        [],
        2 * full * width_all * total,
        x_own, x_other, w_qkv, gain_a, gain_h, cosine, sine,
    )
    attended, queries = attend(lens, queries, keys, values, rows, head_width, block)
    later, attended = lax.optimization_barrier((packs[1], attended))
    gathered.append(lax.all_gather(later, "shard", axis=0))
    n = over.per_slot
    eight = (8, width_all)
    first_rows = pl.BlockSpec((block, width_all), lambda i: (jnp.minimum(i, n - 1), 0))
    last_rows = pl.BlockSpec((block, width_all), lambda i: (jnp.maximum(i - n, 0), 0))
    all_rows = pl.BlockSpec((block, width_all), lambda i: (i, 0))
    smem = pl.BlockSpec(memory_space=pltpu.SMEM)

    def other_first(width):
        return pl.BlockSpec((block, width), lambda i: (lax.rem(i + n, 2 * n), 0))

    def held(shape):
        return pl.BlockSpec(shape, lambda i: (0, 0), pipeline_mode=pl.Buffered(1))

    sums_spec = pl.BlockSpec(eight, lambda i: (0, 0))
    slot_rows = pltpu.VMEM((rows, width_all), LOW)
    resid, normed_b, sums_a, normed_b_other = pl.pallas_call(
        partial(out_kernel, n),
        out_shape=[
            jax.ShapeDtypeStruct((rows, width_all), F32),
            jax.ShapeDtypeStruct((rows, width_all), LOW),
            jax.ShapeDtypeStruct(eight, F32),
            jax.ShapeDtypeStruct((rows, width_all), LOW),
        ],
        grid=(2 * n,),
        in_specs=[smem, other_first(q_half), held(w_o.shape), last_rows, held(gain_m.shape)],
        out_specs=[last_rows, last_rows, sums_spec, hbm],
        scratch_shapes=[pltpu.VMEM((2 * block, width_all), LOW), slot_rows, slot_rows, slot_rows]
        + [pltpu.SemaphoreType.DMA((2 * n,))] * 2
        + [pltpu.SemaphoreType.DMA((1,))],
        cost_estimate=pl.CostEstimate(
            flops=2 * full * q_half * width_all, bytes_accessed=1 << 24, transcendentals=0
        ),
        compiler_params=pltpu.CompilerParams(
            collective_id=6, has_side_effects=True, vmem_limit_bytes=62 << 20
        ),
        name="out",
    )(lengths, attended, w_o, x_own, gain_m)

    sums = []
    ff_grads, ff_levels, ff_totals = [], [], []
    packed_shape = (shards * packed_rows, 2 * units)
    level_shape = (packed_rows, 2 * units)
    wide_shape, tall_shape = (width_all, 2 * units), (units, width_all)
    for chunk in range(chunks):
        last = chunk == chunks - 1
        side = Side(
            shards,
            groups,
            [level_shape] if chunk >= 1 else [],
            [level_shape] if chunk >= 2 else [],
            2 * half_shards * folds + 3 * n,
        )
        late = chunk == chunks - 1
        sources = ff_grads[-1:] + ff_levels[-1:]
        ends = [all_rows] * 2
        end_shapes = [jax.ShapeDtypeStruct((full, width_all), F32)] * 2
        own_rows, other_rows, sum_rows, more, more_specs, exchange = (
            first_rows, last_rows, all_rows, [], [], []
        )
        if last:
            own_rows, other_rows, sum_rows = last_rows, first_rows, other_first(width_all)
            more = [lengths, resid, gain_m]
            more_specs = [smem, last_rows, held(gain_m.shape)]
            ends = [last_rows] * 3 + [sums_spec, hbm]
            end_shapes = [
                jax.ShapeDtypeStruct((rows, width_all), LOW),
                jax.ShapeDtypeStruct((rows, width_all), F32),
                jax.ShapeDtypeStruct((rows, width_all), LOW),
                jax.ShapeDtypeStruct(eight, F32),
                jax.ShapeDtypeStruct((rows, width_all), LOW),
            ]
            exchange = [pltpu.VMEM((2 * block, width_all), LOW), slot_rows] * 3
        outs = pl.pallas_call(
            partial(
                ffn_kernel, n, shards, bool(sums), last, side, 0 if late else chunk * packed_rows
            ),
            out_shape=end_shapes + [jax.ShapeDtypeStruct(packed_shape, LOW)] + side.outs(),
            grid=(2 * n,),
            in_specs=[own_rows, other_rows] * 2
            + [hbm]
            + [sum_rows] * len(sums)
            + more_specs
            + [hbm] * len(sources),
            out_specs=ends + [hbm] * (1 + len(side.outs())),
            scratch_shapes=[pltpu.VMEM(wide_shape, F32), pltpu.VMEM(tall_shape, F32)]
            + [pltpu.VMEM((units, d_half), LOW)]
            + [pltpu.VMEM(wide_shape, LOW), pltpu.VMEM(tall_shape, LOW)]
            + [pltpu.VMEM(packed_shape, LOW)]
            + [pltpu.SemaphoreType.DMA((shards + half_shards * folds,))]
            + exchange
            + side.scratch(),
            cost_estimate=pl.CostEstimate(
                flops=18 * full * width_all * units, bytes_accessed=1 << 25, transcendentals=0
            ),
            compiler_params=pltpu.CompilerParams(
                collective_id=2 + chunk, has_side_effects=True, vmem_limit_bytes=67043328
            ),
            name="ffn",
        )(normed_b, normed_b_other, g_own, g_other, gathered[late], *sums, *more, *sources)
        sums = outs[: len(end_shapes)]
        ff_grads.append(outs[len(end_shapes)])
        rest = outs[len(end_shapes) + 1 :]
        ff_levels += rest[:1]
        ff_totals += rest[1:]
    output, d_resid, d_attn, sums_b, d_attn_other = sums

    o_shape = w_o.shape
    d_heads, grad_out = pl.pallas_call(
        partial(dout_kernel, n, head_width),
        out_shape=[
            jax.ShapeDtypeStruct((full, 2 * q_half), LOW),
            jax.ShapeDtypeStruct((2 * o_shape[0], d_half), LOW),
        ],
        grid=(2 * n,),
        in_specs=[first_rows, last_rows, pl.BlockSpec((block, q_half), lambda i: (i, 0))]
        + [held(o_shape)],
        out_specs=[pl.BlockSpec((block, 2 * q_half), lambda i: (i, 0)), hbm],
        scratch_shapes=[pltpu.VMEM(o_shape, F32), pltpu.VMEM((o_shape[0], d_half), LOW)]
        + [pltpu.VMEM((2 * o_shape[0], d_half), LOW)]
        + [pltpu.SemaphoreType.DMA((1,))] * 3,
        cost_estimate=pl.CostEstimate(
            flops=4 * full * q_half * width_all, bytes_accessed=1 << 24, transcendentals=0
        ),
        compiler_params=pltpu.CompilerParams(
            collective_id=8, has_side_effects=True, vmem_limit_bytes=62 << 20
        ),
        name="dout",
    )(d_attn, d_attn_other, attended, w_o)
    o_level = (d_rows, d_half)
    d_query, d_key, d_value, ff_level, ff_total = attend_back(
        queries,
        keys,
        values,
        d_heads,
        rows,
        head_width,
        block,
        Side(shards, groups, [level_shape], [level_shape]),
        [ff_grads[-1], ff_levels[-1]],
    )
    ff_totals.append(ff_total)
    top_shape = (d_rows, 2 * units)
    side = Side(shards, groups, [o_level], [top_shape], n)
    turned = pl.BlockSpec((block, LANES), lambda i: (lax.rem(i, n), 0))
    input_grad, grad_qkv, gain_sums, sums_c, out_level, ff_top = pl.pallas_call(
        partial(qkv_back_kernel, n, counts, head_width, scale, side),
        out_shape=[
            jax.ShapeDtypeStruct((rows, width_all), LOW),
            jax.ShapeDtypeStruct(w_qkv.shape, LOW),
            jax.ShapeDtypeStruct((8, LANES), F32),
            jax.ShapeDtypeStruct(eight, F32),
        ]
        + side.outs(),
        grid=(2 * n,),
        in_specs=[other_first(q_half), other_first(2 * kv_half), other_first(2 * kv_half)]
        + [other_first(qk), other_first(width_all), held(w_qkv.shape), held(gain_h.shape)]
        + [turned, turned, last_rows, last_rows, held(gain_a.shape), hbm, hbm],
        out_specs=[last_rows, held(w_qkv.shape)]
        + [pl.BlockSpec((8, LANES), lambda i: (0, 0)), sums_spec, hbm, hbm],
        scratch_shapes=[pltpu.VMEM(w_qkv.shape, F32), pltpu.VMEM((block, total), LOW)]
        + [pltpu.VMEM((2 * block, width_all), LOW), slot_rows]
        + side.scratch(),
        cost_estimate=pl.CostEstimate(
            flops=4 * full * width_all * total, bytes_accessed=1 << 24, transcendentals=0
        ),
        compiler_params=pltpu.CompilerParams(
            collective_id=7, has_side_effects=True, vmem_limit_bytes=62 << 20
        ),
        name="qkv_back",
    )(
        d_query, d_key, d_value, raw, normed_a, w_qkv, gain_h, cosine, sine, x_own, d_resid, gain_a,
        grad_out, ff_level,
    )
    mine, other, small = finish_sums(
        grad_qkv,
        lengths,
        [sums_a, sums_b, sums_c, gain_sums],
        [(2, 0), (1, 1), (0, 0), (0, 1), (1, 0), (3, 0), (3, 1)],
        [ff_level, out_level],
        d_rows,
        ff_totals + [ff_top],
        shards,
        groups,
    )
    wide = (d_rows, shards * ff_rows)
    shapes = [wide, wide, (chunks * folds, piece // folds, width_all)]
    shapes += [w.shape for w in (w_out, w_query, w_key, w_value)]
    shapes += [(1, d_rows), (1, d_rows), (1, 3), (1, head_rows), (1, head_rows)]
    top = d_rows // 8
    low_rows = piece // folds // 8

    def whole(part):
        return pl.BlockSpec((top, part.shape[1]), lambda i: (i, 0))

    def low(part, skip):
        return pl.BlockSpec((low_rows, part.shape[1]), lambda i: (skip // low_rows + i, 0))

    parts, specs = [], []
    for chunk in range(chunks):
        for total, rest in (
            (ff_totals[chunk], ff_totals[chunk]) if chunk < chunks - 1 else (ff_top, mine[0]),
            (other[4 + chunk], other[4 + chunk]) if chunk < chunks - 1 else (other[-1], other[0]),
        ):
            parts += [total, rest]
            specs += [whole(total), low(rest, d_rows if chunk < chunks - 1 else 0)]
    pairs = [one for pair in zip(mine[1:4], other[1:4]) for one in pair]
    small_specs = [pl.BlockSpec(shape, lambda i: (0, 0)) for shape in shapes[7:]]
    (
        grad_gate, grad_up, grad_down, grad_out, grad_query, grad_key, grad_value,
        grad_ga, grad_gm, statistics, grad_gq, grad_gk,
    ) = pl.pallas_call(
        partial(assemble_kernel, chunks, half_shards, folds, head_width, width_all),
        out_shape=[jax.ShapeDtypeStruct(shape, F32) for shape in shapes],
        grid=(8,),
        in_specs=specs
        + [whole(part) for part in pairs]
        + [pl.BlockSpec(small.shape, lambda i: (0, 0))],
        out_specs=[pl.BlockSpec((top, shape[1]), lambda i: (i, 0)) for shape in shapes[:2]]
        + [pl.BlockSpec((shapes[2][0], low_rows, width_all), lambda i: (0, i, 0))]
        + [pl.BlockSpec((top, shape[1]), lambda i: (i, 0)) for shape in shapes[3:7]]
        + small_specs,
        compiler_params=pltpu.CompilerParams(vmem_limit_bytes=62 << 20),
        name="assemble",
    )(*parts, *pairs, small)
    return (
        output[None],
        input_grad[None],
        grad_ga.reshape(-1),
        grad_query,
        grad_key,
        grad_value,
        grad_gq.reshape(-1),
        grad_gk.reshape(-1),
        grad_out,
        grad_gm.reshape(-1),
        grad_gate,
        grad_up,
        grad_down.reshape(w_down.shape),
        statistics.reshape(-1),
    )


def solution(mesh):
    in_specs = (
        P(("rep", "shard"), None, None),
        P(("rep", "shard")),
        P("shard"),
        P("shard", None),
        P("shard", None),
        P("shard", None),
        P("shard"),
        P("shard"),
        P("shard", None),
        P("shard"),
        P("shard", None),
        P("shard", None),
        P("shard", None),
        P(("rep", "shard"), None, None),
    )
    out_specs = (
        P(("rep", "shard"), None, None),
        P(("rep", "shard"), None, None),
        P("shard"),
        P("shard", None),
        P("shard", None),
        P("shard", None),
        P("shard"),
        P("shard"),
        P("shard", None),
        P("shard"),
        P("shard", None),
        P("shard", None),
        P("shard", None),
        P(),
    )
    return jax.shard_map(local, mesh=mesh, in_specs=in_specs, out_specs=out_specs, check_vma=False)
```

```python
from functools import partial
import math

import jax
import jax.numpy as jnp
from jax import lax
from jax.experimental import pallas as pl
from jax.experimental.pallas import tpu as pltpu
from jax.sharding import PartitionSpec as P

EPS = 1e-05
ROPE_BASE = 1000000.0
F32 = jnp.float32
LOW = jnp.bfloat16
LANES = 128
MESH = pl.DeviceIdType.MESH


def rope_tables(row_count, head_width):
    half_width = head_width // 2
    lane = jnp.arange(LANES, dtype=jnp.int32)
    frequency = jnp.power(
        jnp.float32(ROPE_BASE), -(lane % half_width).astype(jnp.float32) * 2.0 / head_width
    )
    angles = jnp.arange(row_count, dtype=jnp.float32)[:, None] * frequency[None, :]
    sine = jnp.sin(angles)
    return jnp.cos(angles), jnp.where((lane % head_width < half_width)[None], -sine, sine)


def nn(left, right):
    return jnp.dot(left, right, preferred_element_type=F32)


def nt(left, right):
    return lax.dot_general(left, right, (((1,), (1,)), ((), ())), preferred_element_type=F32)


def tn(left, right):
    return lax.dot_general(left, right, (((0,), (0,)), ((), ())), preferred_element_type=F32)


def core_swap(x):
    pairs = [(i, i ^ 1) for i in range(lax.axis_size("rep"))]
    return lax.ppermute(x, "rep", pairs)


def place():
    rep = lax.axis_index("rep")
    return lax.axis_index("shard"), lax.div(rep, 2), lax.rem(rep, 2)


def device(shard, group, core):
    return {"rep": 2 * group + core, "shard": shard}


def meet(devices):
    barrier = pltpu.get_barrier_semaphore()
    for where in devices:
        pl.semaphore_signal(barrier, inc=1, device_id=where, device_id_type=MESH)
    pl.semaphore_wait(barrier, len(devices))


def remote(source, target, send, recv, where):
    return pltpu.make_async_remote_copy(
        src_ref=source,
        dst_ref=target,
        send_sem=send,
        recv_sem=recv,
        device_id=where,
        device_id_type=MESH,
    )


def at_rows(ref, start, size):
    return ref.at[pl.ds(pl.multiple_of(start, 8), size), :]


def at(ref, row, rows, column, columns):
    return ref.at[
        pl.ds(pl.multiple_of(row, 8), rows), pl.ds(pl.multiple_of(column, LANES), columns)
    ]


class Copies:
    def __init__(self, send, recv):
        self.send, self.recv, self.used = send, recv, 0

    def __call__(self, source, target, where):
        slot = self.used
        self.used += 1
        return remote(source, target, self.send.at[slot], self.recv.at[slot], where)


def neighbours(me):
    return me + 1 - 2 * lax.rem(me, 2), me + 2 - 4 * lax.div(me, 2), 3 - me


def gather_kernel(shards, wide_parts, tall_parts, count, *refs):
    *refs, send, recv = refs
    sources, targets = refs[: count[0]], refs[count[0] :]
    me, group, core = place()
    half = shards // 2
    partner = device(me, group, 1 - core)
    meet(
        [device(lax.rem(me + k, shards), group, c) for k in range(1, shards) for c in range(2)]
        + [partner]
    )
    copies = Copies(send, recv)
    sent, due = [], []

    def go(source, target, where):
        copy = copies(source, target, where)
        copy.start()
        sent.append(copy.wait_send)
        return copy

    def passed_on(wide):
        fast, slow, _ = neighbours(me)
        later = []
        for block, first, second in wide:
            rows = block(me).shape[0] // 2
            first.wait_recv()
            later.append(go(block(fast).at[pl.ds(0, rows), :], block(fast).at[pl.ds(0, rows), :], device(slow, group, core)))
            second.wait_recv()
            later.append(go(block(slow).at[pl.ds(rows, rows), :], block(slow).at[pl.ds(rows, rows), :], device(fast, group, core)))
        return later

    wide = []
    for source, target, column, to, columns in wide_parts:
        source, target = sources[source], targets[target]
        rows = source.shape[0]
        mine = at(source, 0, rows, column(core), columns)

        def block(shard, target=target, rows=rows, to=to, columns=columns):
            return at(target, shard * rows, rows, to, columns)

        if shards == 4:
            fast, slow, _ = neighbours(me)
            wide.append(
                (
                    block,
                    go(mine, block(me), device(fast, group, core)),
                    go(mine, block(me), device(slow, group, core)),
                )
            )
        else:
            for k in range(1, shards):
                due.append(go(mine, block(me), device(lax.rem(me + k, shards), group, core)))
        due.append(go(at(source, 0, rows, column(1 - core), columns), block(me), partner))
    owner = lax.div(me, half)
    tall = []
    for source, target, row, rows in tall_parts:
        source, target = sources[source], targets[target]
        columns = source.shape[1] // 2

        def block(shard, target=target, rows=rows, columns=columns):
            return at(target, lax.rem(shard, half) * rows, rows, 0, 2 * columns)

        mine = at(source, row, rows, core * columns, columns)
        goal = at(target, lax.rem(me, half) * rows, rows, core * columns, columns)
        steps = [1, 2] if shards == 4 else list(range(1, shards))
        arrivals = []
        for k in steps:
            if shards == 4:
                to = origin = neighbours(me)[k - 1]
            else:
                to, origin = lax.rem(me + k, shards), lax.rem(me + shards - k, shards)
            pair = []
            for side in range(2):
                copy = copies(mine, goal, device(to, group, owner))
                pl.when(core == side)(copy.start)
                sent.append((core == side, copy.wait_send))
                pair.append(copy)
            arrivals.append((lax.div(origin, half) == core, pair))
        whole = copies(
            at(source, row, rows, 0, 2 * columns), block(me), partner
        )
        pl.when(owner != core)(whole.start)
        sent.append((owner != core, whole.wait_send))
        due.append((owner == core, whole))
        if shards == 4:
            tall.append((block, rows // 2, arrivals))
        else:
            for condition, pair in arrivals:
                due.extend((condition, copy) for copy in pair)
    gains, given = sources[-2:], targets[-2:]
    for k in range(1, shards):
        due.append(go(gains[0], given[0].at[me], device(lax.rem(me + k, shards), group, core)))
    due.append(go(gains[0], given[0].at[me], partner))
    due.append(go(gains[1], given[1], partner))
    if shards == 4:
        due.extend(passed_on(wide))
        fast, slow, _ = neighbours(me)
        for block, rows, arrivals in tall:
            for number, (condition, pair) in enumerate(arrivals):
                start = number * rows
                from_, to = (fast, slow) if number == 0 else (slow, fast)
                part = block(from_).at[pl.ds(start, rows), :]
                copy = copies(part, part, device(to, group, core))

                @pl.when(condition)
                def _(pair=pair, copy=copy):
                    for one in pair:
                        one.wait_recv()
                    copy.start()

                sent.append((condition, copy.wait_send))
                due.append((owner != core, copy))
    for item in sent:
        pl.when(item[0])(item[1]) if isinstance(item, tuple) else item()
    for item in due:
        pl.when(item[0])(item[1].wait_recv) if isinstance(item, tuple) else item.wait_recv()


def pack_kernel(shards, chunks, gate_ref, up_ref, down_ref, *refs):
    *packs, sems = refs
    core = lax.rem(lax.axis_index("rep"), 2)
    half = shards // 2
    total, rows = down_ref.shape[0], gate_ref.shape[0]
    piece = total // chunks
    columns = down_ref.shape[1] // 2
    copies = []
    for pack in packs:
        for row, chunk in pack[1]:
            for j, ref in enumerate((gate_ref, up_ref)):
                for i in range(half):
                    start = (core * half + i) * total + chunk * piece
                    copies.append(
                        (
                            at(ref, 0, rows, start, piece),
                            pack[0].at[pl.ds(row, rows), pl.ds((j * half + i) * piece, piece)],
                        )
                    )
            folds = 2 * half * piece // columns
            size = piece // folds
            for i in range(folds):
                copies.append(
                    (
                        at(down_ref, chunk * piece + i * size, size, core * columns, columns),
                        pack[0].at[pl.ds(row + rows, size), pl.ds(i * columns, columns)],
                    )
                )
    copies = [pltpu.make_async_copy(a, b, sems.at[k]) for k, (a, b) in enumerate(copies)]
    for copy in copies:
        copy.start()
    for copy in copies:
        copy.wait()


def add_up(parts, target, least):
    total_rows = target.shape[0]
    rows = max(k for k in range(least, 97, least) if total_rows % k == 0)

    def some(i, _):
        here = pl.ds(pl.multiple_of(i * rows, rows), rows)
        total = parts[0][here, :].astype(F32)
        for part in parts[1:]:
            total += part[here, :].astype(F32)
        target[here, :] = total.astype(target.dtype)
        return 0

    lax.fori_loop(0, total_rows // rows, some, 0)


def reduce_over_plane(copies, load, shards, grad_ref, level, bufs):
    me, group, core = place()
    rows = level.shape[0]

    def block(shard, start=0, size=rows):
        return at_rows(grad_ref, shard * rows + start, size)

    own = bufs[0]
    local = pltpu.make_async_copy(block(me), own, load.at[0])
    if shards != 4:
        planes = bufs[1]
        out = [
            copies(block(lax.rem(me + k, shards)), planes.at[k - 1], device(lax.rem(me + k, shards), group, core))
            for k in range(1, shards)
        ]

        def start():
            local.start()
            for copy in out:
                copy.start()

        def end():
            local.wait()
            for copy in out:
                copy.wait_send()
                copy.wait_recv()
            add_up([own] + [planes.at[k] for k in range(shards - 1)], level, 16)

        return [start, idle, idle, end]
    fast, slow, across = neighbours(me)
    to_fast, to_slow = device(fast, group, core), device(slow, group, core)
    half = rows // 2
    planes, met_fast, met_slow, held_fast, held_slow = bufs[1:]
    upper, lower = pl.ds(0, half), pl.ds(half, half)
    loads = [
        local,
        pltpu.make_async_copy(block(fast, half, half), held_fast, load.at[1]),
        pltpu.make_async_copy(block(slow, 0, half), held_slow, load.at[2]),
    ]
    early = [
        copies(block(across, 0, half), met_fast, to_fast),
        copies(block(across, half, half), met_slow, to_slow),
        copies(block(fast, 0, half), planes.at[0, upper, :], to_fast),
        copies(block(slow, half, half), planes.at[1, lower, :], to_slow),
    ]
    late = [
        copies(held_fast, planes.at[0, lower, :], to_fast),
        copies(held_slow, planes.at[1, upper, :], to_slow),
    ]

    def start():
        for copy in early[:2] + loads:
            copy.start()

    def direct():
        for copy in early[2:]:
            copy.start()

    def merge():
        for copy in loads:
            copy.wait()
        for copy, met, held, out in (
            (early[1], met_slow, held_fast, late[0]),
            (early[0], met_fast, held_slow, late[1]),
        ):
            copy.wait_recv()
            add_up([held, met], held, 16)
            out.start()

    def end():
        for copy in early[2:] + late:
            copy.wait_recv()
        for copy in early + late:
            copy.wait_send()
        add_up([own, planes.at[0], planes.at[1]], level, 16)

    return [start, direct, merge, end]


def plane_buffers(shards, shape):
    half = (shape[0] // 2, shape[1])
    if shards != 4:
        return [pltpu.VMEM(shape, LOW), pltpu.VMEM((shards - 1,) + shape, LOW)]
    return [pltpu.VMEM(shape, LOW), pltpu.VMEM((2,) + shape, LOW)] + [pltpu.VMEM(half, LOW)] * 4


def reduce_over_line(copies, groups, source, part, total, bufs):
    me, group, core = place()
    if groups != 4:
        (slots,) = bufs
        out = [
            copies(source, slots.at[group], device(me, lax.rem(group + k, groups), core))
            for k in range(1, groups)
        ]

        def start():
            for copy in out:
                copy.start()

        def end():
            rows = part.shape[0]

            def some(i, _):
                here = pl.ds(pl.multiple_of(i * 8, 8), 8)
                slots[group, here, :] = part[here, :]
                return 0

            lax.fori_loop(0, rows // 8, some, 0)
            for copy in out:
                copy.wait_send()
                copy.wait_recv()
            add_up([slots.at[k] for k in range(groups)], total, 8)

        return [start, idle, idle, end]
    met, summed, other = bufs
    outer = jnp.logical_or(group == 0, group == groups - 1)
    inner = jnp.logical_not(outer)
    mate = device(me, group + 1 - 2 * lax.rem(group, 2), core)
    inward = copies(source, met, mate)
    between = copies(summed, other, device(me, groups - 1 - group, core))
    back = copies(total, total, mate)

    def start():
        pl.when(outer)(inward.start)

    def exchange():
        @pl.when(inner)
        def _():
            inward.wait_recv()
            add_up([part, met], summed, 16)
            between.start()

    def give():
        @pl.when(inner)
        def _():
            between.wait_recv()
            add_up([summed, other], total, 16)
            back.start()

    def end():
        @pl.when(outer)
        def _():
            inward.wait_send()
            back.wait_recv()

        @pl.when(inner)
        def _():
            between.wait_send()
            back.wait_send()

    return [start, exchange, give, end]


def idle():
    pass


def line_buffers(groups, shape):
    if groups != 4:
        return [pltpu.VMEM((groups,) + shape, LOW)]
    return [pltpu.VMEM(shape, LOW)] * 3


PARTS = 8


def parts_of(shape):
    return PARTS if shape[0] * shape[1] >= 1 << 18 else PARTS // 2


class LineSum:
    def __init__(self, copies, groups, source, part, total, bufs):
        self.count = parts_of(part.shape)
        rows = part.shape[0] // self.count
        each = len(bufs) // self.count
        self.parts = [
            reduce_over_line(
                copies,
                groups,
                at_rows(source, i * rows, rows),
                at_rows(part, i * rows, rows),
                at_rows(total, i * rows, rows),
                bufs[i * each : (i + 1) * each],
            )
            for i in range(self.count)
        ]

    def run(self, part, stage):
        if part < self.count:
            self.parts[part][stage]()

    def all(self, stage, first=0, last=None):
        for part in self.parts[first:last]:
            part[stage]()

    @staticmethod
    def buffers(groups, shape):
        count = parts_of(shape)
        return line_buffers(groups, (shape[0] // count, shape[1])) * count

    @staticmethod
    def copies(groups, shape):
        return parts_of(shape) * max(3, groups - 1)


class Side:
    def __init__(self, shards, groups, plane_shapes, line_shapes, extra=0):
        self.shards, self.groups, self.extra = shards, groups, extra
        self.plane_shapes, self.line_shapes = plane_shapes, line_shapes

    def outs(self):
        return [jax.ShapeDtypeStruct(shape, LOW) for shape in self.plane_shapes + self.line_shapes]

    def scratch(self):
        groups, shards = self.groups, self.shards
        shapes = [pltpu.VMEM(shape, LOW) for shape in self.plane_shapes + self.line_shapes]
        for shape in self.plane_shapes:
            shapes += plane_buffers(shards, shape)
        for shape in self.line_shapes:
            shapes += [pltpu.VMEM(shape, LOW)] + LineSum.buffers(groups, shape)
        count = 2 * self.shards + len(self.plane_shapes) * max(6, shards - 1)
        count += sum(LineSum.copies(groups, shape) for shape in self.line_shapes) + self.extra
        loads = 4 * len(self.plane_shapes) + 2 * len(self.line_shapes) + 1
        return shapes + [pltpu.SemaphoreType.DMA((count,))] * 2 + [pltpu.SemaphoreType.DMA((loads,))]

    def run(self, step, sources, outs, bufs):
        *bufs, send, recv, load = bufs
        totals, bufs = take(bufs, len(outs))
        me, group, core = place()
        copies = Copies(send, recv)
        shards, groups = self.shards, self.groups

        @pl.when(step == 0)
        def _():
            meet(everyone_near(shards, groups))

        planes, lines, loads = [], [], []
        for i, shape in enumerate(self.plane_shapes):
            some, bufs = take(bufs, len(plane_buffers(shards, shape)))
            planes.append(
                reduce_over_plane(
                    copies, load.at[pl.ds(3 * i, 3)], shards, sources[i], totals[i], some
                )
            )
        first = len(self.plane_shapes)
        for i, shape in enumerate(self.line_shapes):
            (own,), bufs = take(bufs, 1)
            some, bufs = take(bufs, len(LineSum.buffers(groups, shape)))
            source = at_rows(sources[first + i], 0, shape[0])
            loads.append(pltpu.make_async_copy(source, own, load.at[3 * first + i]))
            lines.append(LineSum(copies, groups, source, own, totals[first + i], some))

        def begin():
            for stages in planes:
                stages[0]()
            for stages in planes:
                stages[1]()
            for part in range(PARTS):
                for line in lines:
                    line.run(part, 0)
            for one in loads:
                one.start()

        def load_done():
            for one in loads:
                one.wait()

        def of_lines(part, stage):
            def go():
                for line in lines:
                    line.run(part, stage)

            return go

        def merge():
            for stages in planes:
                stages[2]()

        received = {1: [0], 2: [1], 3: [2, 3], 4: [4], 5: [5, 6], 6: [7]}
        given = {3: [0, 1], 4: [2, 3], 5: [4], 6: [5, 6], 7: [7]}
        plan = {0: [begin]}
        for when in range(1, 8):
            plan[when] = [load_done] if when == 1 else []
            plan[when] += [of_lines(part, 1) for part in received.get(when, [])]
            plan[when] += [merge] if when == 3 else []
            plan[when] += [of_lines(part, 2) for part in given.get(when, [])]
        for when, stages in plan.items():

            @pl.when(step == when)
            def _(stages=stages):
                for stage in stages:
                    stage()

        count = len(outs)
        stores = [
            pltpu.make_async_copy(total, out, load.at[load.shape[0] - 1 - count + i])
            for i, (total, out) in enumerate(zip(totals, outs))
        ]

        def end():
            for stages, store in zip(planes, stores):
                stages[3]()
                store.start()
            for part in range(PARTS):
                for line in lines:
                    line.run(part, 3)
            for store in stores[len(planes) :]:
                store.start()
            for store in stores:
                store.wait()

        return copies, end


class Blocks:
    def __init__(self, copies, partner, count, block, held, got):
        self.count, self.block = count, block
        self.copies = [
            copies(
                held.at[pl.ds(k % (held.shape[0] // block) * block, block), :],
                got.at[pl.ds(k * block, block), :],
                partner,
            )
            for k in range(count)
        ]
        self.slots = held.shape[0] // block
        self.held, self.got = held, got

    def begin(self, step, first):
        for k in range(self.count):

            @pl.when(step == first + k + 1)
            def _(k=k):
                self.copies[k].start()
                if k + 1 >= self.slots and k + 1 < self.count:
                    self.copies[k + 1 - self.slots].wait_send()

    def put(self, number, values):
        self.held[pl.ds(lax.rem(number, self.slots) * self.block, self.block), :] = values

    def take(self, step, first):
        for k in range(self.count):
            pl.when(step == first + k)(self.copies[k].wait_recv)
        start = jnp.clip(step - first, 0, self.count - 1) * self.block
        return self.got[pl.ds(pl.multiple_of(start, self.block), self.block), :]

    def end(self, sent_last, received):
        if sent_last:
            self.copies[-1].start()
        for k in range(max(0, self.count - self.slots), self.count):
            self.copies[k].wait_send()
        if received:
            for copy in self.copies:
                copy.wait_recv()


def everyone_near(shards, groups):
    me, group, core = place()
    return (
        [device(lax.rem(me + k, shards), group, core) for k in range(1, shards)]
        + [device(me, lax.rem(group + k, groups), core) for k in range(1, groups)]
        + [device(me, group, 1 - core)]
    )


def take(refs, count):
    return refs[:count], refs[count:]


def finish_kernel(shards, groups, counts, rows, skip, length_ref, *refs):
    smalls, refs = take(refs, 1 + max(k for k, _ in rows))
    (grad_ref,), refs = take(refs, 1)
    lows, refs = take(refs, counts[0])
    ready, refs = take(refs, counts[1])
    n = counts[0] + 2
    mine_out, refs = take(refs, n)
    other, refs = take(refs, n + counts[1])
    (total_ref,), refs = take(refs, 1)
    mine, refs = take(refs, n)
    levels, refs = take(refs, 2)
    own, refs = take(refs, counts[0])
    plane_bufs = []
    for level in levels:
        some, refs = take(refs, len(plane_buffers(shards, level.shape)))
        plane_bufs.append(some)
    line_bufs = []
    for one in mine:
        some, refs = take(refs, len(LineSum.buffers(groups, one.shape)))
        line_bufs.append(some)
    small_a, small_b, small_c, send, recv, load = refs
    me, group, core = place()
    partner = device(me, group, 1 - core)
    plane = [device(lax.rem(me + k, shards), group, core) for k in range(1, shards)]
    line = [device(me, lax.rem(group + k, groups), core) for k in range(1, groups)]
    copies = Copies(send, recv)

    def go(source, target, where):
        copy = copies(source, target, where)
        copy.start()
        return copy

    def finish(some):
        for copy in some:
            copy.wait_send()
            copy.wait_recv()

    parts = [
        at_rows(low, 0 if i else skip, one.shape[0]) for i, (low, one) in enumerate(zip(lows, own))
    ]
    loads = [pltpu.make_async_copy(low, own[i], load.at[6 + i]) for i, low in enumerate(parts)]
    for copy in loads:
        copy.start()
    for i, (k, row) in enumerate(rows):
        values = smalls[k][row : row + 1, :]
        small_a[me, i : i + 1, : values.shape[1]] = values
        if values.shape[1] < small_a.shape[2]:
            rest = small_a.shape[2] - values.shape[1]
            small_a[me, i : i + 1, values.shape[1] :] = jnp.zeros((1, rest), F32)
    small_a[me, len(rows) :, :] = jnp.full(
        (small_a.shape[1] - len(rows), small_a.shape[2]), length_ref[0].astype(F32)
    )
    meet(everyone_near(shards, groups))
    columns = levels[0].shape[1]
    planes = [
        reduce_over_plane(
            copies,
            load.at[pl.ds(3 * i, 3)],
            shards,
            grad_ref.at[:, pl.ds(i * columns, columns)],
            level,
            plane_bufs[i],
        )
        for i, level in enumerate(levels)
    ]
    sums = [
        LineSum(copies, groups, source, part, mine[i], line_bufs[i])
        for i, (source, part) in enumerate(zip(parts + list(levels), list(own) + list(levels)))
    ]
    early, halves = sums[: counts[0]], sums[counts[0] :]
    for stages in planes:
        stages[0]()
        stages[1]()
    for one in early:
        one.all(0)
    small_copies = [go(small_a.at[me], small_a.at[me], where) for where in plane]
    swaps = [go(source, target, partner) for source, target in zip(ready, other[n:])]
    for copy in loads:
        copy.wait()
    planes[0][2]()
    planes[1][2]()
    for one in early:
        one.all(1, 0, one.count // 2)
    planes[0][3]()
    halves[0].all(0)
    finish(small_copies)
    small_b[group] = sum(small_a[k] for k in range(shards))
    small_copies = [go(small_b.at[group], small_b.at[group], where) for where in line]
    for one in early:
        one.all(1, one.count // 2)
        one.all(2, 0, one.count // 2)
    planes[1][3]()
    halves[1].all(0)
    for one in early:
        one.all(2, one.count // 2)
    finish(small_copies)
    small_c[core] = sum(small_b[k] for k in range(groups))
    small_copies = [go(small_c.at[core], small_c.at[core], partner)]
    halves[0].all(1)
    halves[1].all(1)
    halves[0].all(2)
    stores = []

    def hand(i):
        sums[i].all(3)
        swaps.append(go(mine[i], other[i], partner))
        stores.append(pltpu.make_async_copy(mine[i], mine_out[i], load.at[6 + counts[0] + i]))
        stores[-1].start()

    for i in range(counts[0]):
        hand(i)
    halves[1].all(2)
    hand(counts[0])
    hand(counts[0] + 1)
    finish(small_copies)
    total_ref[...] = small_c[0] + small_c[1]
    finish(swaps)
    for store in stores:
        store.wait()


def finish_sums(grad, length, smalls, rows, lows, skip, ready, shards, groups):
    level = (grad.shape[0] // shards, grad.shape[1] // 2)
    shapes = [(low.shape[0] - (0 if i else skip), low.shape[1]) for i, low in enumerate(lows)]
    shapes += [level] * 2
    others = shapes + [one.shape for one in ready]
    vmem = pl.BlockSpec(memory_space=pltpu.VMEM)
    hbm = pl.BlockSpec(memory_space=pltpu.HBM)
    scratch = [pltpu.VMEM(shape, LOW) for shape in shapes + [level] * 2 + shapes[: len(lows)]]
    for _ in range(2):
        scratch += plane_buffers(shards, level)
    for shape in shapes:
        scratch += LineSum.buffers(groups, shape)
    count = 2 * max(6, shards) + sum(LineSum.copies(groups, shape) for shape in shapes)
    count += len(others) + shards + groups
    small = (8, max(one.shape[1] for one in smalls))
    outs = pl.pallas_call(
        partial(finish_kernel, shards, groups, (len(lows), len(ready)), rows, skip),
        out_shape=[jax.ShapeDtypeStruct(shape, LOW) for shape in shapes + others]
        + [jax.ShapeDtypeStruct(small, F32)],
        in_specs=[pl.BlockSpec(memory_space=pltpu.SMEM)]
        + [vmem] * len(smalls)
        + [hbm] * (1 + len(lows) + len(ready)),
        out_specs=[hbm] * (len(shapes) + len(others)) + [vmem],
        scratch_shapes=scratch
        + [pltpu.VMEM((size,) + small, F32) for size in (shards, groups, 2)]
        + [pltpu.SemaphoreType.DMA((count,)), pltpu.SemaphoreType.DMA((count,))]
        + [pltpu.SemaphoreType.DMA((6 + len(lows) + len(shapes),))],
        compiler_params=pltpu.CompilerParams(
            collective_id=1, has_side_effects=True, vmem_limit_bytes=62 << 20
        ),
        name="finish",
    )(length, *smalls, grad, *lows, *ready)
    n = len(shapes)
    return outs[:n], outs[n:-1], outs[-1]


def two_parts(column):
    high = column.astype(LOW)
    return high, (column - high.astype(F32)).astype(LOW)


def below(ref, here, heads):
    return jnp.concatenate([ref[here, pl.ds(h * LANES, LANES)] for h in range(heads)], axis=0)


def attend_kernel(block, width, lens_ref, q_ref, k_ref, v_ref, att_ref, qx_ref):
    rows = q_ref.shape[0]
    heads = q_ref.shape[1] // LANES
    length = lens_ref[pl.program_id(0)]
    lane = lax.broadcasted_iota(jnp.int32, (block, LANES), 1)
    keep = lax.broadcasted_iota(jnp.int32, (block, block), 1) <= lax.broadcasted_iota(
        jnp.int32, (block, block), 0
    )
    for step in range(rows // block):
        start = step * block
        here = pl.ds(start, block)

        @pl.when(start < length)
        def _():
            outs = []
            for head in range(heads):
                lanes = pl.ds(head * LANES, LANES)
                query = q_ref[here, lanes]
                probs = jnp.exp(nt(query, k_ref[here, :]))
                probs = jnp.where(keep, probs, 0.0).astype(LOW)
                total = nn(probs, v_ref[here, :])
                if step:
                    probs = jnp.exp(nt(query, k_ref[pl.ds(0, start), :])).astype(LOW)
                    total += nn(probs, v_ref[pl.ds(0, start), :])
                weight = total[:, width : width + 1]
                outs.append(total / weight)
                high, rest = two_parts(-jnp.log(weight))
                qx_ref[here, lanes] = jnp.where(
                    lane == width, high, jnp.where(lane == width + 1, rest, query)
                )
            for pair in range(heads // 2):
                att_ref[here, pl.ds(pair * LANES, LANES)] = jnp.where(
                    lane < width, outs[2 * pair], pltpu.roll(outs[2 * pair + 1], width, 1)
                ).astype(LOW)

        @pl.when(start >= length)
        def _():
            att_ref[here, :] = jnp.zeros((block, att_ref.shape[1]), LOW)
            qx_ref[here, :] = jnp.zeros((block, qx_ref.shape[1]), LOW)


def attend_back_kernel(block, width, side, q_ref, k_ref, v_ref, do_ref, *refs):
    count = len(side.plane_shapes) + len(side.line_shapes)
    sources, refs = take(refs, count)
    (dq_ref, dk_ref, dv_ref), refs = take(refs, 3)
    totals, bufs = take(refs, count)
    grid_step = pl.program_id(0) * pl.num_programs(1) + pl.program_id(1)
    _, end = side.run(grid_step, sources, totals, bufs)
    rows = q_ref.shape[0]
    heads = q_ref.shape[1] // LANES
    lane = lax.broadcasted_iota(jnp.int32, (block, LANES), 1)
    shape = (block, heads * block)
    keep = lax.broadcasted_iota(jnp.int32, shape, 0) <= lax.rem(
        lax.broadcasted_iota(jnp.int32, shape, 1), block
    )
    dk_ref[...] = jnp.zeros(dk_ref.shape, F32)
    dv_ref[...] = jnp.zeros(dv_ref.shape, F32)
    for step in range(rows // block):
        start = step * block
        here = pl.ds(start, block)
        query, dout = below(q_ref, here, heads), below(do_ref, here, heads)

        def one(keys, masked):
            key, value = k_ref[keys, :], v_ref[keys, :]
            probs = jnp.exp(nt(key, query))
            if masked:
                probs = jnp.where(keep, probs, 0.0)
            dscores = (probs * nt(value, dout)).astype(LOW)
            dv_ref[keys, :] += nn(probs.astype(LOW), dout)
            dk_ref[keys, :] += nn(dscores, query)
            return tn(dscores, key)

        dquery = one(here, True)
        if step:
            dquery += one(pl.ds(0, start), False)
        for pair in range(heads // 2):
            first = dquery[2 * pair * block : (2 * pair + 1) * block]
            second = dquery[(2 * pair + 1) * block : (2 * pair + 2) * block]
            dq_ref[here, pl.ds(pair * LANES, LANES)] = jnp.where(
                lane < width, first, pltpu.roll(second, width, 1)
            )
    pl.when(grid_step == pl.num_programs(0) * pl.num_programs(1) - 1)(end)


def attention_grid(slots, groups, per_group, rows):
    wide = pl.BlockSpec((rows, per_group * LANES), lambda s, g, lens: (s, g))
    dense = pl.BlockSpec((rows, per_group * LANES // 2), lambda s, g, lens: (s, g))
    narrow = pl.BlockSpec((rows, LANES), lambda s, g, lens: (s, g))
    return (slots, groups), wide, dense, narrow


def attend(lens, queries, keys, values, rows, width, block):
    slots, groups = queries.shape[0] // rows, keys.shape[1] // LANES
    per_group = queries.shape[1] // LANES // groups
    grid, wide, dense, narrow = attention_grid(slots, groups, per_group, rows)
    flops = 4 * slots * groups * per_group * rows * rows * LANES
    return pl.pallas_call(
        partial(attend_kernel, block, width),
        out_shape=(
            jax.ShapeDtypeStruct((queries.shape[0], queries.shape[1] // 2), LOW),
            jax.ShapeDtypeStruct(queries.shape, LOW),
        ),
        grid_spec=pltpu.PrefetchScalarGridSpec(
            num_scalar_prefetch=1,
            grid=grid,
            in_specs=[wide, narrow, narrow],
            out_specs=[dense, wide],
        ),
        cost_estimate=pl.CostEstimate(flops=flops, bytes_accessed=1 << 23, transcendentals=0),
        name="attend",
    )(lens, queries, keys, values)


def attend_back(queries, keys, values, douts, rows, width, block, side, sources):
    slots, groups = queries.shape[0] // rows, keys.shape[1] // LANES
    per_group = queries.shape[1] // LANES // groups
    wide = pl.BlockSpec((rows, per_group * LANES), lambda s, g: (s, g))
    dense = pl.BlockSpec((rows, per_group * LANES // 2), lambda s, g: (s, g))
    narrow = pl.BlockSpec((rows, LANES), lambda s, g: (s, g))
    flops = 10 * slots * groups * per_group * rows * rows * LANES
    return pl.pallas_call(
        partial(attend_back_kernel, block, width, side),
        out_shape=[
            jax.ShapeDtypeStruct((queries.shape[0], queries.shape[1] // 2), F32),
            jax.ShapeDtypeStruct(keys.shape, F32),
            jax.ShapeDtypeStruct(keys.shape, F32),
        ]
        + side.outs(),
        grid=(slots, groups),
        in_specs=[wide, narrow, narrow, wide]
        + [pl.BlockSpec(memory_space=pltpu.HBM)] * len(sources),
        out_specs=[dense, narrow, narrow]
        + [pl.BlockSpec(memory_space=pltpu.HBM)] * len(side.outs()),
        scratch_shapes=side.scratch(),
        cost_estimate=pl.CostEstimate(flops=flops, bytes_accessed=1 << 24, transcendentals=0),
        compiler_params=pltpu.CompilerParams(
            collective_id=5, has_side_effects=True, vmem_limit_bytes=62 << 20
        ),
        name="attend_back",
    )(queries, keys, values, douts, *sources)


def swap_halves(values, width):
    lane = lax.broadcasted_iota(jnp.int32, values.shape, 1)
    half = width // 2
    return jnp.where(
        lane % width < half, pltpu.roll(values, LANES - half, 1), pltpu.roll(values, half, 1)
    )


def head_sum(values, width):
    same = lax.broadcasted_iota(jnp.int32, (LANES, LANES), 0) // width
    same = (same == lax.broadcasted_iota(jnp.int32, (LANES, LANES), 1) // width).astype(LOW)
    high, rest = two_parts(values)
    return nn(high, same) + nn(rest, same)


def row_rsqrt(values):
    return lax.rsqrt(jnp.mean(values * values, axis=1, keepdims=True) + EPS)


def is_live(lens_ref, step, per_slot, block):
    return lax.rem(step, per_slot) * block < lens_ref[lax.div(step, per_slot)]


def qkv_kernel(
    per_slot, counts, width, scale, lens_ref, own_ref, other_ref, w_ref, ga_ref, gh_ref, cos_ref, sin_ref,
    normed_ref, raw_ref, q_ref, k_ref, v_ref,
):
    step = pl.program_id(0)
    block = own_ref.shape[0]
    q_tiles, kv_tiles = counts

    @pl.when(is_live(lens_ref, step, per_slot, block))
    def _():
        x = jnp.where(step < per_slot, own_ref[...], other_ref[...]).astype(F32)
        normed = (x * row_rsqrt(x) * ga_ref[...]).astype(LOW)
        normed_ref[...] = normed
        lane = lax.broadcasted_iota(jnp.int32, (block, LANES), 1)
        zero = jnp.zeros((block, LANES), F32)
        ones = jnp.where(lane < width + 2, 1.0, 0.0)
        cosine, sine = cos_ref[...], sin_ref[...]

        def put(ref, tile, values, rest):
            ref[:, pl.ds(2 * tile * LANES, LANES)] = jnp.where(lane < width, values, rest).astype(LOW)
            ref[:, pl.ds((2 * tile + 1) * LANES, LANES)] = jnp.where(
                lane < width, pltpu.roll(values, width, 1), rest
            ).astype(LOW)

        for tile in range(q_tiles + 2 * kv_tiles):
            lanes = pl.ds(tile * LANES, LANES)
            if tile % 2 == 0:
                pair = nn(normed, w_ref[:, pl.ds(tile * LANES, 2 * LANES)])
            values = pair[:, (tile % 2) * LANES : (tile % 2 + 1) * LANES]
            if tile >= q_tiles + kv_tiles:
                put(v_ref, tile - q_tiles - kv_tiles, values, ones)
                continue
            raw_ref[:, lanes] = values
            is_query = tile < q_tiles
            gain = gh_ref[0:1, :] if is_query else gh_ref[1:2, :]
            values *= lax.rsqrt(head_sum(values * values, width) * (1.0 / width) + EPS) * gain
            values = values * cosine + swap_halves(values, width) * sine
            if is_query:
                put(q_ref, tile, values * scale, zero)
            else:
                put(k_ref, tile - q_tiles, values, ones)

    @pl.when(jnp.logical_not(is_live(lens_ref, step, per_slot, block)))
    def _():
        for ref in (normed_ref, raw_ref, q_ref, k_ref, v_ref):
            ref[...] = jnp.zeros(ref.shape, ref.dtype)


def out_kernel(
    per_slot, length_ref, att_ref, w_ref, x_ref, gain_ref, resid_ref, normed_ref, sums_ref,
    other_out, give, got, hold, other, send, recv, store,
):
    step = pl.program_id(0)
    block = att_ref.shape[0]
    me, group, core = place()
    partner = device(me, group, 1 - core)
    copies = Copies(send, recv)
    parts = Blocks(copies, partner, per_slot, block, give, got)
    normed_parts = Blocks(copies, partner, per_slot, block, hold, other)

    @pl.when(step == 0)
    def _():
        meet([partner])
        sums_ref[...] = jnp.zeros(sums_ref.shape, F32)

    parts.begin(step, 0)
    normed_parts.begin(step, per_slot)
    product = nn(att_ref[...], w_ref[...])

    @pl.when(step < per_slot)
    def _():
        parts.put(step, product.astype(LOW))

    @pl.when(step >= per_slot)
    def _():
        number = step - per_slot
        valid = lax.broadcasted_iota(jnp.int32, (block, 1), 0) + number * block < length_ref[0]
        attn_out = product + parts.take(step, per_slot).astype(F32)
        resid = x_ref[...].astype(F32) + attn_out
        resid_ref[...] = resid
        normed = (resid * row_rsqrt(resid) * gain_ref[...]).astype(LOW)
        normed_ref[...] = normed
        normed_parts.put(number, normed)
        for row, values in ((0, resid), (1, attn_out)):
            sums_ref[row : row + 1, :] += jnp.sum(
                jnp.where(valid, values * values, 0.0), axis=0, keepdims=True
            )

    @pl.when(step == 2 * per_slot - 1)
    def _():
        parts.end(False, False)
        normed_parts.end(True, True)
        copy = pltpu.make_async_copy(other, other_out, store.at[0])
        copy.start()
        copy.wait()


def ffn_kernel(
    per_slot, shards, chained, last, side, offset, lens_ref, x_own, x_other, g_own, g_other,
    gathered_ref, *refs,
):
    if chained:
        (mlp_in, db_in), refs = take(refs, 2)
    if last:
        (resid_ref, gain_ref), refs = take(refs, 2)
    count = len(side.plane_shapes) + len(side.line_shapes)
    sources, refs = take(refs, count)
    if last:
        (out_ref, dresid_ref, dattn_ref, sums_ref, dattn_out), refs = take(refs, 5)
    else:
        (mlp_ref, db_ref), refs = take(refs, 2)
    (grad_out,), refs = take(refs, 1)
    totals, refs = take(refs, count)
    (acc_ref, accd_ref, given_ref, w_ref, wd_ref, grad_ref, load), refs = take(refs, 7)
    exchange, bufs = take(refs, 6 if last else 0)
    step = pl.program_id(0)
    copies, end = side.run(step, sources, totals, bufs)
    own = step >= per_slot if last else step < per_slot
    units, depth = wd_ref.shape
    block = x_own.shape[0]
    me, group, core = place()
    partner = device(me, group, 1 - core)
    half, columns, d_rows = shards // 2, depth // 2, depth // shards
    packed = grad_ref.shape[0] // shards
    size = packed - d_rows
    folds = grad_ref.shape[1] // columns

    def folded(ref, shard, fold):
        return ref.at[shard, pl.ds(offset + d_rows, size), pl.ds(fold * columns, columns)]

    def unfolded(i, fold):
        return at(wd_ref, (i * folds + fold) * size, size, core * columns, columns)

    tiles = [(i, fold) for i in range(half) for fold in range(folds)]
    given = [
        copies(folded(gathered_ref, (1 - core) * half + i, fold), unfolded(i, fold), partner)
        for i, fold in tiles
    ]
    loads = [
        pltpu.make_async_copy(
            gathered_ref.at[shard, pl.ds(offset, d_rows), :],
            w_ref.at[pl.ds(shard * d_rows, d_rows), :],
            load.at[shard],
        )
        for shard in range(shards)
    ] + [
        pltpu.make_async_copy(
            folded(gathered_ref, core * half + i, fold), unfolded(i, fold), load.at[shards + k]
        )
        for k, (i, fold) in enumerate(tiles)
    ]

    if last:
        give_mlp, got_mlp, give_db, got_db, hold, other = exchange
        mlp_parts = Blocks(copies, partner, per_slot, block, give_mlp, got_mlp)
        db_parts = Blocks(copies, partner, per_slot, block, give_db, got_db)
        attn_parts = Blocks(copies, partner, per_slot, block, hold, other)
        mlp_parts.begin(step, 0)
        db_parts.begin(step, 0)
        attn_parts.begin(step, per_slot)

    @pl.when(step == 0)
    def _():
        if last:
            sums_ref[...] = jnp.zeros(sums_ref.shape, F32)
        for copy in given + loads:
            copy.start()
        acc_ref[...] = jnp.zeros(acc_ref.shape, F32)
        accd_ref[...] = jnp.zeros(accd_ref.shape, F32)
        for copy in loads:
            copy.wait()
        for copy in given:
            copy.wait_send()
            copy.wait_recv()

    x = jnp.where(own, x_own[...], x_other[...])
    length = jnp.where(own, lens_ref[0], lens_ref[1])
    row = lax.broadcasted_iota(jnp.int32, (block, 1), 0) + lax.rem(step, per_slot) * block
    valid = row < length
    g = jnp.where(valid, jnp.where(own, g_own[...], g_other[...]), jnp.zeros((), LOW))
    gate = nn(x, w_ref[:, :units])
    up = nn(x, w_ref[:, units:])
    d_hidden = nt(g, wd_ref[...])
    sig = jax.nn.sigmoid(gate)
    silu = gate * sig
    hidden = (silu * up).astype(LOW)
    d_gate = (d_hidden * up * (sig * (1.0 + gate * (1.0 - sig)))).astype(LOW)
    d_up = (d_hidden * silu).astype(LOW)
    mlp = nn(hidden, wd_ref[...])
    d_b = nt(d_gate, w_ref[:, :units]) + nt(d_up, w_ref[:, units:])
    if chained:
        mlp += mlp_in[...]
        d_b += db_in[...]
    if last:

        @pl.when(step < per_slot)
        def _():
            mlp_parts.put(step, mlp.astype(LOW))
            db_parts.put(step, d_b.astype(LOW))

        @pl.when(step >= per_slot)
        def _():
            number = step - per_slot
            resid = resid_ref[...]
            mlp_out = mlp + mlp_parts.take(step, per_slot).astype(F32)
            out_ref[...] = jnp.where(valid, resid + mlp_out, 0.0).astype(LOW)
            d_norm, d_gain = norm_back(
                resid, d_b + db_parts.take(step, per_slot).astype(F32), gain_ref[...]
            )
            d_resid = jnp.where(valid, g.astype(F32) + d_norm, 0.0)
            dresid_ref[...] = d_resid
            d_attn = d_resid.astype(LOW)
            dattn_ref[...] = d_attn
            attn_parts.put(number, d_attn)
            for row, values in ((0, mlp_out * mlp_out), (1, d_gain)):
                sums_ref[row : row + 1, :] += jnp.sum(
                    jnp.where(valid, values, 0.0), axis=0, keepdims=True
                )

    else:
        mlp_ref[...] = mlp
        db_ref[...] = d_b
    acc_ref[:, :units] += tn(x, d_gate)
    acc_ref[:, units:] += tn(x, d_up)
    accd_ref[...] += tn(hidden, g)

    @pl.when(step == pl.num_programs(0) - 1)
    def _():
        mine = pl.ds(pl.multiple_of(core * columns, columns), columns)
        theirs = pl.ds(pl.multiple_of((1 - core) * columns, columns), columns)
        given_ref[...] = accd_ref[:, theirs].astype(LOW)
        for shard in range(shards):
            grad_ref[pl.ds(shard * packed, d_rows), :] = acc_ref[
                pl.ds(shard * d_rows, d_rows), :
            ].astype(LOW)
        out = []
        for i in range(half):
            for fold in range(folds):
                row = i * folds * size + fold * size
                to = pl.ds(
                    pl.multiple_of((core * half + i) * packed + d_rows, 8), size
                )
                lanes = pl.ds(fold * columns, columns)
                out.append(
                    copies(
                        given_ref.at[pl.ds(row, size), :],
                        grad_ref.at[to, lanes],
                        partner,
                    )
                )
                out[-1].start()
                grad_ref[to, lanes] = accd_ref[pl.ds(row, size), mine].astype(LOW)
        for copy in out:
            copy.wait_send()
            copy.wait_recv()
        stores = [pltpu.make_async_copy(grad_ref, grad_out, load.at[0])]
        stores[0].start()
        if last:
            mlp_parts.end(False, False)
            db_parts.end(False, False)
            attn_parts.end(True, True)
            stores.append(pltpu.make_async_copy(other, dattn_out, load.at[1]))
            stores[1].start()
        end()
        for store in stores:
            store.wait()


def norm_back(values, dy, gain):
    inverse = row_rsqrt(values)
    scaled = dy * gain
    inner = jnp.mean(values * scaled, axis=1, keepdims=True)
    return inverse * scaled - values * (inverse * inverse * inverse * inner), dy * values * inverse


def dout_kernel(
    per_slot, width, own_ref, other_ref, att_ref, w_ref, do_ref, grad_out,
    acc_ref, give, hold, send, recv, store,
):
    step = pl.program_id(0)
    block = own_ref.shape[0]
    me, group, core = place()

    @pl.when(step == 0)
    def _():
        meet([device(me, group, 1 - core)])
        acc_ref[...] = jnp.zeros(acc_ref.shape, F32)

    d_attn = jnp.where(step < per_slot, own_ref[...], other_ref[...])
    lane = lax.broadcasted_iota(jnp.int32, (block, LANES), 1)
    att = att_ref[...]
    acc_ref[...] += tn(att, d_attn)
    for tile in range(att.shape[1] // LANES):
        lanes = slice(tile * LANES, (tile + 1) * LANES)
        if tile % 2 == 0:
            pair = nt(d_attn, w_ref[tile * LANES : (tile + 2) * LANES, :])
        dout = pair[:, (tile % 2) * LANES : (tile % 2 + 1) * LANES].astype(LOW).astype(F32)
        delta = -head_sum(dout * att[:, lanes].astype(F32), width)
        for head, (values, column) in enumerate(
            ((dout, pltpu.roll(delta, width, 1)), (pltpu.roll(dout, width, 1), delta))
        ):
            high, rest = two_parts(column)
            column = jnp.where(
                lane == width, high, jnp.where(lane == width + 1, rest, jnp.zeros_like(rest))
            )
            do_ref[:, pl.ds((2 * tile + head) * LANES, LANES)] = jnp.where(
                lane < width, values.astype(LOW), column
            )

    @pl.when(step == pl.num_programs(0) - 1)
    def _():
        rows, columns = give.shape
        theirs = pl.ds(pl.multiple_of((1 - core) * columns, columns), columns)
        give[...] = acc_ref[:, theirs].astype(LOW)
        mine = pl.ds(pl.multiple_of(core * columns, columns), columns)
        goal = at_rows(hold, core * rows, rows)
        hold[pl.ds(pl.multiple_of(core * rows, rows), rows), :] = acc_ref[:, mine].astype(LOW)
        copy = Copies(send, recv)(give, goal, device(me, group, 1 - core))
        copy.start()
        copy.wait_send()
        copy.wait_recv()
        local = pltpu.make_async_copy(hold, grad_out, store.at[0])
        local.start()
        local.wait()


def qkv_back_kernel(
    per_slot, counts, width, scale, side, dq_ref, dk_ref, dv_ref, raw_ref, normed_ref, w_ref, gh_ref,
    cos_ref, sin_ref, x_ref, dresid_ref, ga_ref, *refs,
):
    step = pl.program_id(0)
    block = dq_ref.shape[0]
    q_tiles, kv_tiles = counts
    me, group, core = place()
    partner = device(me, group, 1 - core)
    count = len(side.plane_shapes) + len(side.line_shapes)
    sources, refs = take(refs, count)
    (out_ref, grad_ref, gain_ref, sums_ref), refs = take(refs, 4)
    totals, refs = take(refs, count)
    (acc_ref, low_ref, give, got), bufs = take(refs, 4)
    copies, end = side.run(step, sources, totals, bufs)
    parts = Blocks(copies, partner, per_slot, block, give, got)

    @pl.when(step == 0)
    def _():
        acc_ref[...] = jnp.zeros(acc_ref.shape, F32)
        gain_ref[...] = jnp.zeros(gain_ref.shape, F32)
        sums_ref[...] = jnp.zeros(sums_ref.shape, F32)

    parts.begin(step, 0)
    lane = lax.broadcasted_iota(jnp.int32, (block, LANES), 1)
    cosine, sine = cos_ref[...], sin_ref[...]

    def pair(ref, tile):
        return jnp.where(
            lane < width,
            ref[:, pl.ds(2 * tile * LANES, LANES)],
            pltpu.roll(ref[:, pl.ds((2 * tile + 1) * LANES, LANES)], width, 1),
        )

    for tile in range(q_tiles + 2 * kv_tiles):
        lanes = pl.ds(tile * LANES, LANES)
        if tile >= q_tiles + kv_tiles:
            low_ref[:, lanes] = pair(dv_ref, tile - q_tiles - kv_tiles).astype(LOW)
            continue
        if tile < q_tiles:
            turned, row = dq_ref[:, lanes] * scale, 0
        else:
            turned, row = pair(dk_ref, tile - q_tiles), 1
        gain = gh_ref[row : row + 1, :]
        dy = turned * cosine + swap_halves(turned * sine, width)
        values = raw_ref[:, lanes]
        inverse = lax.rsqrt(head_sum(values * values, width) * (1.0 / width) + EPS)
        scaled = dy * gain
        inner = head_sum(values * scaled, width) * (1.0 / width)
        low_ref[:, lanes] = (
            inverse * scaled - values * (inverse * inverse * inverse * inner)
        ).astype(LOW)
        gain_ref[row : row + 1, :] += jnp.sum(dy * values * inverse, axis=0, keepdims=True)
    low = low_ref[...]
    acc_ref[...] += tn(normed_ref[...], low)
    d_a = nt(low, w_ref[...])

    @pl.when(step < per_slot)
    def _():
        parts.put(step, d_a.astype(LOW))

    @pl.when(step >= per_slot)
    def _():
        d_norm, d_gain = norm_back(
            x_ref[...].astype(F32), d_a + parts.take(step, per_slot).astype(F32), ga_ref[...]
        )
        out_ref[...] = (dresid_ref[...] + d_norm).astype(LOW)
        sums_ref[0:1, :] += jnp.sum(d_gain, axis=0, keepdims=True)

    @pl.when(step == 2 * per_slot - 1)
    def _():
        grad_ref[...] = acc_ref[...].astype(LOW)
        parts.end(False, False)
        end()


def assemble_kernel(chunks, half, folds, head_width, model_width, *refs):
    parts, refs = take(refs, 4 * chunks)
    pairs, refs = take(refs, 6)
    small_ref, out_in, grad_in, gate_ref, up_ref, down_ref, *outs = refs
    *outs, ga_ref, gm_ref, stat_ref, gq_ref, gk_ref, out_ref, grad_ref = outs
    out_ref[...] = out_in[...]
    grad_ref[...] = grad_in[...]
    first = lax.rem(lax.axis_index("rep"), 2) == 0

    def sides(mine, other):
        return [jnp.where(first, mine, other), jnp.where(first, other, mine)]

    units = parts[0].shape[1] // 2
    piece = units // half
    for chunk in range(chunks):
        top, low, other_top, other_low = parts[4 * chunk : 4 * chunk + 4]
        for side, values in enumerate(sides(top[...], other_top[...])):
            for j, ref in enumerate((gate_ref, up_ref)):
                for i in range(half):
                    to = ((side * half + i) * chunks + chunk) * piece
                    start = j * units + i * piece
                    ref[:, to : to + piece] = values[:, start : start + piece].astype(F32)
        columns = down_ref.shape[2] // 2
        for side, values in enumerate(sides(low[...], other_low[...])):
            for fold in range(folds):
                down_ref[chunk * folds + fold, :, side * columns : (side + 1) * columns] = values[
                    :, fold * columns : (fold + 1) * columns
                ].astype(F32)
    starts = [0, 0, 0, outs[2].shape[1] // 2]
    for ref, k, start in zip(outs, (0, 2, 4, 4), starts):
        width = ref.shape[1] // 2
        mine, other = (one[:, start : start + width] for one in pairs[k : k + 2])
        for side, values in enumerate(sides(mine, other)):
            ref[:, side * width : (side + 1) * width] = values.astype(F32)

    @pl.when(pl.program_id(0) == 0)
    def _():
        me = lax.axis_index("shard")
        width = ga_ref.shape[1]
        here = pl.ds(pl.multiple_of(me * width, width), width)
        ga_ref[...] = small_ref[0:1, here]
        gm_ref[...] = small_ref[1:2, here]
        lane = lax.broadcasted_iota(jnp.int32, (1, LANES), 1)
        count = small_ref[7:8, 0:1] * model_width
        roots = jnp.zeros((1, LANES), F32)
        for k in range(3):
            total = jnp.sum(small_ref[2 + k : 3 + k, :], axis=1, keepdims=True)
            roots = jnp.where(lane == k, jnp.sqrt(total / count), roots)
        stat_ref[...] = roots[:, : stat_ref.shape[1]]
        size = gq_ref.shape[1]
        for k, ref in enumerate((gq_ref, gk_ref)):
            gains = jnp.broadcast_to(small_ref[5 + k : 6 + k, :LANES], (8, LANES))
            gains += pltpu.roll(gains, head_width, 1)
            gains = pltpu.roll(gains, lax.rem(LANES - me * size, LANES), 1)
            ref[...] = gains[0:1, :size]


class Rows:
    def __init__(self, lens, rows, block):
        self.lens, self.block, self.per_slot = lens, block, rows // block

    def both(self, width):
        return pl.BlockSpec((self.block, width), lambda i, lens: (i, 0))

    def both_other_first(self, width):
        n = self.per_slot
        return pl.BlockSpec((self.block, width), lambda i, lens: (lax.rem(i + n, 2 * n), 0))

    def early(self, width):
        n = self.per_slot
        return pl.BlockSpec((self.block, width), lambda i, lens: (jnp.minimum(i, n - 1), 0))

    def late(self, width):
        n = self.per_slot
        return pl.BlockSpec((self.block, width), lambda i, lens: (jnp.maximum(i - n, 0), 0))

    def repeated(self, width):
        n = self.per_slot
        return pl.BlockSpec((self.block, width), lambda i, lens: (lax.rem(i, n), 0))

    def fixed(self, shape):
        return pl.BlockSpec(shape, lambda i, lens: (0, 0), pipeline_mode=pl.Buffered(1))

    def call(self, name, kernel, slots, in_specs, out_specs, outs, scratch, flops, *args):
        return pl.pallas_call(
            kernel,
            out_shape=[jax.ShapeDtypeStruct(shape, kind) for shape, kind in outs],
            grid_spec=pltpu.PrefetchScalarGridSpec(
                num_scalar_prefetch=1,
                grid=(slots * self.per_slot,),
                in_specs=in_specs,
                out_specs=out_specs,
                scratch_shapes=scratch,
            ),
            cost_estimate=pl.CostEstimate(
                flops=flops, bytes_accessed=1 << 24, transcendentals=0
            ),
            compiler_params=pltpu.CompilerParams(vmem_limit_bytes=62 << 20),
            name=name,
        )(self.lens, *args)


def local(
    inputs,
    lengths,
    gain_attn,
    w_query,
    w_key,
    w_value,
    gain_query,
    gain_key,
    w_out,
    gain_mlp,
    w_gate,
    w_up,
    w_down,
    cotangent,
):
    shards = lax.axis_size("shard")
    core = lax.axis_index("rep") % 2
    first = core == 0
    rows, width_all = inputs.shape[1], inputs.shape[2]
    head_width = gain_query.shape[0] * shards
    q_half, kv_half = w_query.shape[1] // 2, w_key.shape[1] // 2
    d_half = width_all // 2
    d_rows, ff_rows = w_query.shape[0], w_down.shape[0]
    block = min(256, rows)
    scale = 1.0 / math.sqrt(head_width)
    counts = (q_half // LANES, kv_half // LANES)

    def ordered(mine, other, axis):
        return jnp.where(
            first,
            jnp.concatenate([mine, other], axis=axis),
            jnp.concatenate([other, mine], axis=axis),
        )

    half_shards = shards // 2
    groups = lax.axis_size("rep") // 2
    chunks = 3
    piece = ff_rows // chunks
    units = half_shards * piece
    folds = 2 * units // d_half
    head_rows = gain_query.shape[0]

    def fold(part):
        return jnp.concatenate(jnp.split(part, folds, axis=-2), axis=-1)

    def unfold(part):
        return jnp.concatenate(jnp.split(part, folds, axis=-1), axis=-2)

    packed_rows = d_rows + piece // folds
    hbm = pl.BlockSpec(memory_space=pltpu.HBM)
    vmem = pl.BlockSpec(memory_space=pltpu.VMEM)
    chunk_sets = [list(range(chunks - 1)), [chunks - 1]]

    def pack(*refs):
        *refs, pack_a, pack_b, sems = refs
        packs = [
            (ref, [(i * packed_rows, chunk) for i, chunk in enumerate(some)])
            for ref, some in zip((pack_a, pack_b), chunk_sets)
        ]
        pack_kernel(shards, chunks, *refs, *packs, sems)

    if piece % LANES == 0:
        packs = pl.pallas_call(
            pack,
            out_shape=[
                jax.ShapeDtypeStruct((len(some) * packed_rows, 2 * units), LOW) for some in chunk_sets
            ],
            in_specs=[hbm] * 3,
            out_specs=[vmem] * 2,
            scratch_shapes=[pltpu.SemaphoreType.DMA((chunks * (2 * half_shards + folds),))],
            compiler_params=pltpu.CompilerParams(vmem_limit_bytes=62 << 20),
            name="pack",
        )(w_gate, w_up, w_down)
    else:

        def my_half(weight):
            half = weight.shape[1] // 2
            return jnp.where(first, weight[:, :half], weight[:, half:])

        def chunk_of(weight, chunk):
            columns = weight.reshape(d_rows, shards, chunks, piece)[:, :, chunk]
            return my_half(columns.reshape(d_rows, shards * piece))

        def packed_chunk(chunk):
            tall = fold(my_half(w_down)[chunk * piece : (chunk + 1) * piece])
            wide = jnp.concatenate([chunk_of(w_gate, chunk), chunk_of(w_up, chunk)], axis=1)
            return jnp.concatenate([wide, tall])

        packs = [jnp.concatenate([packed_chunk(k) for k in some]) for some in chunk_sets]
    gathered = [lax.all_gather(packs[0], "shard", axis=0)]

    def gain_row(*gains):
        flat = jnp.concatenate(gains)
        return jnp.pad(flat, (0, max(d_rows, LANES) - flat.shape[0]))[None]

    gain_rows = jnp.pad(
        jnp.concatenate(
            [gain_row(gain_attn), gain_row(gain_mlp), gain_row(gain_query, gain_key)]
        ),
        ((0, 13), (0, 0)),
    )

    def half_of(width):
        return lambda core: core * width

    wide_parts = [
        (0, 0, half_of(q_half), 0, q_half),
        (1, 0, half_of(kv_half), q_half, kv_half),
        (2, 0, half_of(kv_half), q_half + kv_half, kv_half),
    ]
    tall_parts = [(3, 1, 0, w_out.shape[0])]
    copies = len(wide_parts) * (shards + 2) + len(tall_parts) * (2 * shards + 3) + shards + 1
    w_qkv, w_o, gains, x_other = pl.pallas_call(
        partial(gather_kernel, shards, wide_parts, tall_parts, (6, copies)),
        out_shape=[
            jax.ShapeDtypeStruct(shape, LOW)
            for shape in (
                (width_all, q_half + 2 * kv_half),
                (half_shards * w_out.shape[0], width_all),
                (shards,) + gain_rows.shape,
                inputs.shape[1:],
            )
        ],
        in_specs=[hbm] * 6,
        out_specs=[hbm] * 4,
        scratch_shapes=[pltpu.SemaphoreType.DMA((copies,)), pltpu.SemaphoreType.DMA((copies,))],
        compiler_params=pltpu.CompilerParams(collective_id=0, has_side_effects=True),
        name="gather",
    )(w_query, w_key, w_value, w_out, gain_rows, inputs[0])
    gain_a = gains[:, 0, :d_rows].reshape(1, -1).astype(F32)
    gain_m = gains[:, 1, :d_rows].reshape(1, -1).astype(F32)
    gain_q = gains[:, 2, :head_rows].reshape(1, -1).astype(F32)
    gain_k = gains[:, 2, head_rows : 2 * head_rows].reshape(1, -1).astype(F32)
    gain_h = jnp.tile(jnp.concatenate([gain_q, gain_k]), (4, LANES // head_width))

    lens = jnp.concatenate([lengths, core_swap(lengths)])
    x_own = inputs[0]
    g_own = cotangent[0]
    g_other = core_swap(g_own)
    over = Rows(lens, rows, block)
    cosine, sine = rope_tables(rows, head_width)
    full, total = 2 * rows, w_qkv.shape[1]
    qk = q_half + kv_half

    normed_a, raw, queries, keys, values = over.call(
        "qkv",
        partial(qkv_kernel, over.per_slot, counts, head_width, scale),
        2,
        [over.early(width_all), over.late(width_all), over.fixed(w_qkv.shape)]
        + [over.fixed(gain_a.shape), over.fixed(gain_h.shape)]
        + [over.repeated(LANES), over.repeated(LANES)],
        [over.both(width_all), over.both(qk), over.both(2 * q_half), over.both(2 * kv_half)]
        + [over.both(2 * kv_half)],
        [((full, width_all), LOW), ((full, qk), F32), ((full, 2 * q_half), LOW)]
        + [((full, 2 * kv_half), LOW)] * 2,
        [],
        2 * full * width_all * total,
        x_own, x_other, w_qkv, gain_a, gain_h, cosine, sine,
    )
    attended, queries = attend(lens, queries, keys, values, rows, head_width, block)
    later, attended = lax.optimization_barrier((packs[1], attended))
    gathered.append(lax.all_gather(later, "shard", axis=0))
    n = over.per_slot
    eight = (8, width_all)
    first_rows = pl.BlockSpec((block, width_all), lambda i: (jnp.minimum(i, n - 1), 0))
    last_rows = pl.BlockSpec((block, width_all), lambda i: (jnp.maximum(i - n, 0), 0))
    all_rows = pl.BlockSpec((block, width_all), lambda i: (i, 0))
    smem = pl.BlockSpec(memory_space=pltpu.SMEM)

    def other_first(width):
        return pl.BlockSpec((block, width), lambda i: (lax.rem(i + n, 2 * n), 0))

    def held(shape):
        return pl.BlockSpec(shape, lambda i: (0, 0), pipeline_mode=pl.Buffered(1))

    sums_spec = pl.BlockSpec(eight, lambda i: (0, 0))
    slot_rows = pltpu.VMEM((rows, width_all), LOW)
    resid, normed_b, sums_a, normed_b_other = pl.pallas_call(
        partial(out_kernel, n),
        out_shape=[
            jax.ShapeDtypeStruct((rows, width_all), F32),
            jax.ShapeDtypeStruct((rows, width_all), LOW),
            jax.ShapeDtypeStruct(eight, F32),
            jax.ShapeDtypeStruct((rows, width_all), LOW),
        ],
        grid=(2 * n,),
        in_specs=[smem, other_first(q_half), held(w_o.shape), last_rows, held(gain_m.shape)],
        out_specs=[last_rows, last_rows, sums_spec, hbm],
        scratch_shapes=[pltpu.VMEM((2 * block, width_all), LOW), slot_rows, slot_rows, slot_rows]
        + [pltpu.SemaphoreType.DMA((2 * n,))] * 2
        + [pltpu.SemaphoreType.DMA((1,))],
        cost_estimate=pl.CostEstimate(
            flops=2 * full * q_half * width_all, bytes_accessed=1 << 24, transcendentals=0
        ),
        compiler_params=pltpu.CompilerParams(
            collective_id=6, has_side_effects=True, vmem_limit_bytes=62 << 20
        ),
        name="out",
    )(lengths, attended, w_o, x_own, gain_m)

    sums = []
    ff_grads, ff_levels, ff_totals = [], [], []
    packed_shape = (shards * packed_rows, 2 * units)
    level_shape = (packed_rows, 2 * units)
    wide_shape, tall_shape = (width_all, 2 * units), (units, width_all)
    for chunk in range(chunks):
        last = chunk == chunks - 1
        side = Side(
            shards,
            groups,
            [level_shape] if chunk >= 1 else [],
            [level_shape] if chunk >= 2 else [],
            2 * half_shards * folds + 3 * n,
        )
        late = chunk == chunks - 1
        sources = ff_grads[-1:] + ff_levels[-1:]
        ends = [all_rows] * 2
        end_shapes = [jax.ShapeDtypeStruct((full, width_all), F32)] * 2
        own_rows, other_rows, sum_rows, more, more_specs, exchange = (
            first_rows, last_rows, all_rows, [], [], []
        )
        if last:
            own_rows, other_rows, sum_rows = last_rows, first_rows, other_first(width_all)
            more = [resid, gain_m]
            more_specs = [last_rows, held(gain_m.shape)]
            ends = [last_rows] * 3 + [sums_spec, hbm]
            end_shapes = [
                jax.ShapeDtypeStruct((rows, width_all), LOW),
                jax.ShapeDtypeStruct((rows, width_all), F32),
                jax.ShapeDtypeStruct((rows, width_all), LOW),
                jax.ShapeDtypeStruct(eight, F32),
                jax.ShapeDtypeStruct((rows, width_all), LOW),
            ]
            exchange = [pltpu.VMEM((2 * block, width_all), LOW), slot_rows] * 3
        outs = pl.pallas_call(
            partial(
                ffn_kernel, n, shards, bool(sums), last, side, 0 if late else chunk * packed_rows
            ),
            out_shape=end_shapes + [jax.ShapeDtypeStruct(packed_shape, LOW)] + side.outs(),
            grid=(2 * n,),
            in_specs=[smem]
            + [own_rows, other_rows] * 2
            + [hbm]
            + [sum_rows] * len(sums)
            + more_specs
            + [hbm] * len(sources),
            out_specs=ends + [hbm] * (1 + len(side.outs())),
            scratch_shapes=[pltpu.VMEM(wide_shape, F32), pltpu.VMEM(tall_shape, F32)]
            + [pltpu.VMEM((units, d_half), LOW)]
            + [pltpu.VMEM(wide_shape, LOW), pltpu.VMEM(tall_shape, LOW)]
            + [pltpu.VMEM(packed_shape, LOW)]
            + [pltpu.SemaphoreType.DMA((shards + half_shards * folds,))]
            + exchange
            + side.scratch(),
            cost_estimate=pl.CostEstimate(
                flops=18 * full * width_all * units, bytes_accessed=1 << 25, transcendentals=0
            ),
            compiler_params=pltpu.CompilerParams(
                collective_id=2 + chunk, has_side_effects=True, vmem_limit_bytes=67043328
            ),
            name="ffn",
        )(lens, normed_b, normed_b_other, g_own, g_other, gathered[late], *sums, *more, *sources)
        sums = outs[: len(end_shapes)]
        ff_grads.append(outs[len(end_shapes)])
        rest = outs[len(end_shapes) + 1 :]
        ff_levels += rest[:1]
        ff_totals += rest[1:]
    output, d_resid, d_attn, sums_b, d_attn_other = sums

    o_shape = w_o.shape
    d_heads, grad_out = pl.pallas_call(
        partial(dout_kernel, n, head_width),
        out_shape=[
            jax.ShapeDtypeStruct((full, 2 * q_half), LOW),
            jax.ShapeDtypeStruct((2 * o_shape[0], d_half), LOW),
        ],
        grid=(2 * n,),
        in_specs=[first_rows, last_rows, pl.BlockSpec((block, q_half), lambda i: (i, 0))]
        + [held(o_shape)],
        out_specs=[pl.BlockSpec((block, 2 * q_half), lambda i: (i, 0)), hbm],
        scratch_shapes=[pltpu.VMEM(o_shape, F32), pltpu.VMEM((o_shape[0], d_half), LOW)]
        + [pltpu.VMEM((2 * o_shape[0], d_half), LOW)]
        + [pltpu.SemaphoreType.DMA((1,))] * 3,
        cost_estimate=pl.CostEstimate(
            flops=4 * full * q_half * width_all, bytes_accessed=1 << 24, transcendentals=0
        ),
        compiler_params=pltpu.CompilerParams(
            collective_id=8, has_side_effects=True, vmem_limit_bytes=62 << 20
        ),
        name="dout",
    )(d_attn, d_attn_other, attended, w_o)
    o_level = (d_rows, d_half)
    d_query, d_key, d_value, ff_level, ff_total = attend_back(
        queries,
        keys,
        values,
        d_heads,
        rows,
        head_width,
        block,
        Side(shards, groups, [level_shape], [level_shape]),
        [ff_grads[-1], ff_levels[-1]],
    )
    ff_totals.append(ff_total)
    top_shape = (d_rows, 2 * units)
    side = Side(shards, groups, [o_level], [top_shape], n)
    turned = pl.BlockSpec((block, LANES), lambda i: (lax.rem(i, n), 0))
    input_grad, grad_qkv, gain_sums, sums_c, out_level, ff_top = pl.pallas_call(
        partial(qkv_back_kernel, n, counts, head_width, scale, side),
        out_shape=[
            jax.ShapeDtypeStruct((rows, width_all), LOW),
            jax.ShapeDtypeStruct(w_qkv.shape, LOW),
            jax.ShapeDtypeStruct((8, LANES), F32),
            jax.ShapeDtypeStruct(eight, F32),
        ]
        + side.outs(),
        grid=(2 * n,),
        in_specs=[other_first(q_half), other_first(2 * kv_half), other_first(2 * kv_half)]
        + [other_first(qk), other_first(width_all), held(w_qkv.shape), held(gain_h.shape)]
        + [turned, turned, last_rows, last_rows, held(gain_a.shape), hbm, hbm],
        out_specs=[last_rows, held(w_qkv.shape)]
        + [pl.BlockSpec((8, LANES), lambda i: (0, 0)), sums_spec, hbm, hbm],
        scratch_shapes=[pltpu.VMEM(w_qkv.shape, F32), pltpu.VMEM((block, total), LOW)]
        + [pltpu.VMEM((2 * block, width_all), LOW), slot_rows]
        + side.scratch(),
        cost_estimate=pl.CostEstimate(
            flops=4 * full * width_all * total, bytes_accessed=1 << 24, transcendentals=0
        ),
        compiler_params=pltpu.CompilerParams(
            collective_id=7, has_side_effects=True, vmem_limit_bytes=62 << 20
        ),
        name="qkv_back",
    )(
        d_query, d_key, d_value, raw, normed_a, w_qkv, gain_h, cosine, sine, x_own, d_resid, gain_a,
        grad_out, ff_level,
    )
    mine, other, small = finish_sums(
        grad_qkv,
        lengths,
        [sums_a, sums_b, sums_c, gain_sums],
        [(2, 0), (1, 1), (0, 0), (0, 1), (1, 0), (3, 0), (3, 1)],
        [ff_level, out_level],
        d_rows,
        ff_totals + [ff_top],
        shards,
        groups,
    )
    wide = (d_rows, shards * ff_rows)
    shapes = [wide, wide, (chunks * folds, piece // folds, width_all)]
    shapes += [w.shape for w in (w_out, w_query, w_key, w_value)]
    shapes += [(1, d_rows), (1, d_rows), (1, 3), (1, head_rows), (1, head_rows)]
    top = d_rows // 8
    low_rows = piece // folds // 8

    def whole(part):
        return pl.BlockSpec((top, part.shape[1]), lambda i: (i, 0))

    def low(part, skip):
        return pl.BlockSpec((low_rows, part.shape[1]), lambda i: (skip // low_rows + i, 0))

    parts, specs = [], []
    for chunk in range(chunks):
        for total, rest in (
            (ff_totals[chunk], ff_totals[chunk]) if chunk < chunks - 1 else (ff_top, mine[0]),
            (other[4 + chunk], other[4 + chunk]) if chunk < chunks - 1 else (other[-1], other[0]),
        ):
            parts += [total, rest]
            specs += [whole(total), low(rest, d_rows if chunk < chunks - 1 else 0)]
    pairs = [one for pair in zip(mine[1:4], other[1:4]) for one in pair]
    small_specs = [pl.BlockSpec(shape, lambda i: (0, 0)) for shape in shapes[7:]]
    eighth = pl.BlockSpec((rows // 8, width_all), lambda i: (i, 0))
    passed = [jax.ShapeDtypeStruct((rows, width_all), LOW)] * 2
    (
        grad_gate, grad_up, grad_down, grad_out, grad_query, grad_key, grad_value,
        grad_ga, grad_gm, statistics, grad_gq, grad_gk, output, input_grad,
    ) = pl.pallas_call(
        partial(assemble_kernel, chunks, half_shards, folds, head_width, width_all),
        out_shape=[jax.ShapeDtypeStruct(shape, F32) for shape in shapes] + passed,
        grid=(8,),
        in_specs=specs
        + [whole(part) for part in pairs]
        + [pl.BlockSpec(small.shape, lambda i: (0, 0)), eighth, eighth],
        out_specs=[pl.BlockSpec((top, shape[1]), lambda i: (i, 0)) for shape in shapes[:2]]
        + [pl.BlockSpec((shapes[2][0], low_rows, width_all), lambda i: (0, i, 0))]
        + [pl.BlockSpec((top, shape[1]), lambda i: (i, 0)) for shape in shapes[3:7]]
        + small_specs
        + [eighth, eighth],
        compiler_params=pltpu.CompilerParams(vmem_limit_bytes=62 << 20),
        name="assemble",
    )(*parts, *pairs, small, output, input_grad)
    return (
        output[None],
        input_grad[None],
        grad_ga.reshape(-1),
        grad_query,
        grad_key,
        grad_value,
        grad_gq.reshape(-1),
        grad_gk.reshape(-1),
        grad_out,
        grad_gm.reshape(-1),
        grad_gate,
        grad_up,
        grad_down.reshape(w_down.shape),
        statistics.reshape(-1),
    )


def solution(mesh):
    in_specs = (
        P(("rep", "shard"), None, None),
        P(("rep", "shard")),
        P("shard"),
        P("shard", None),
        P("shard", None),
        P("shard", None),
        P("shard"),
        P("shard"),
        P("shard", None),
        P("shard"),
        P("shard", None),
        P("shard", None),
        P("shard", None),
        P(("rep", "shard"), None, None),
    )
    out_specs = (
        P(("rep", "shard"), None, None),
        P(("rep", "shard"), None, None),
        P("shard"),
        P("shard", None),
        P("shard", None),
        P("shard", None),
        P("shard"),
        P("shard"),
        P("shard", None),
        P("shard"),
        P("shard", None),
        P("shard", None),
        P("shard", None),
        P(),
    )
    return jax.shard_map(local, mesh=mesh, in_specs=in_specs, out_specs=out_specs, check_vma=False)
```

```python
from functools import partial
import math

import jax
import jax.numpy as jnp
from jax import lax
from jax.experimental import pallas as pl
from jax.experimental.pallas import tpu as pltpu
from jax.sharding import PartitionSpec as P

EPS = 1e-05
ROPE_BASE = 1000000.0
F32 = jnp.float32
LOW = jnp.bfloat16
LANES = 128
MESH = pl.DeviceIdType.MESH


def rope_tables(row_count, head_width):
    half_width = head_width // 2
    lane = jnp.arange(LANES, dtype=jnp.int32)
    frequency = jnp.power(
        jnp.float32(ROPE_BASE), -(lane % half_width).astype(jnp.float32) * 2.0 / head_width
    )
    angles = jnp.arange(row_count, dtype=jnp.float32)[:, None] * frequency[None, :]
    sine = jnp.sin(angles)
    return jnp.cos(angles), jnp.where((lane % head_width < half_width)[None], -sine, sine)


def nn(left, right):
    return jnp.dot(left, right, preferred_element_type=F32)


def nt(left, right):
    return lax.dot_general(left, right, (((1,), (1,)), ((), ())), preferred_element_type=F32)


def tn(left, right):
    return lax.dot_general(left, right, (((0,), (0,)), ((), ())), preferred_element_type=F32)


def core_swap(x):
    pairs = [(i, i ^ 1) for i in range(lax.axis_size("rep"))]
    return lax.ppermute(x, "rep", pairs)


def place():
    rep = lax.axis_index("rep")
    return lax.axis_index("shard"), lax.div(rep, 2), lax.rem(rep, 2)


def device(shard, group, core):
    return {"rep": 2 * group + core, "shard": shard}


def meet(devices):
    barrier = pltpu.get_barrier_semaphore()
    for where in devices:
        pl.semaphore_signal(barrier, inc=1, device_id=where, device_id_type=MESH)
    pl.semaphore_wait(barrier, len(devices))


def remote(source, target, send, recv, where):
    return pltpu.make_async_remote_copy(
        src_ref=source,
        dst_ref=target,
        send_sem=send,
        recv_sem=recv,
        device_id=where,
        device_id_type=MESH,
    )


def at_rows(ref, start, size):
    return ref.at[pl.ds(pl.multiple_of(start, 8), size), :]


def at(ref, row, rows, column, columns):
    return ref.at[
        pl.ds(pl.multiple_of(row, 8), rows), pl.ds(pl.multiple_of(column, LANES), columns)
    ]


class Copies:
    def __init__(self, send, recv):
        self.send, self.recv, self.used = send, recv, 0

    def __call__(self, source, target, where):
        slot = self.used
        self.used += 1
        return remote(source, target, self.send.at[slot], self.recv.at[slot], where)


def neighbours(me):
    return me + 1 - 2 * lax.rem(me, 2), me + 2 - 4 * lax.div(me, 2), 3 - me


def gather_kernel(shards, wide_parts, tall_parts, count, *refs):
    *refs, send, recv = refs
    sources, targets = refs[: count[0]], refs[count[0] :]
    me, group, core = place()
    half = shards // 2
    partner = device(me, group, 1 - core)
    meet(
        [device(lax.rem(me + k, shards), group, c) for k in range(1, shards) for c in range(2)]
        + [partner]
    )
    copies = Copies(send, recv)
    sent, due = [], []

    def go(source, target, where):
        copy = copies(source, target, where)
        copy.start()
        sent.append(copy.wait_send)
        return copy

    def passed_on(wide):
        fast, slow, _ = neighbours(me)
        later = []
        for block, first, second in wide:
            rows = block(me).shape[0] // 2
            first.wait_recv()
            later.append(go(block(fast).at[pl.ds(0, rows), :], block(fast).at[pl.ds(0, rows), :], device(slow, group, core)))
            second.wait_recv()
            later.append(go(block(slow).at[pl.ds(rows, rows), :], block(slow).at[pl.ds(rows, rows), :], device(fast, group, core)))
        return later

    wide = []
    for source, target, column, to, columns in wide_parts:
        source, target = sources[source], targets[target]
        rows = source.shape[0]
        mine = at(source, 0, rows, column(core), columns)

        def block(shard, target=target, rows=rows, to=to, columns=columns):
            return at(target, shard * rows, rows, to, columns)

        if shards == 4:
            fast, slow, _ = neighbours(me)
            wide.append(
                (
                    block,
                    go(mine, block(me), device(fast, group, core)),
                    go(mine, block(me), device(slow, group, core)),
                )
            )
        else:
            for k in range(1, shards):
                due.append(go(mine, block(me), device(lax.rem(me + k, shards), group, core)))
        due.append(go(at(source, 0, rows, column(1 - core), columns), block(me), partner))
    owner = lax.div(me, half)
    tall = []
    for source, target, row, rows in tall_parts:
        source, target = sources[source], targets[target]
        columns = source.shape[1] // 2

        def block(shard, target=target, rows=rows, columns=columns):
            return at(target, lax.rem(shard, half) * rows, rows, 0, 2 * columns)

        mine = at(source, row, rows, core * columns, columns)
        goal = at(target, lax.rem(me, half) * rows, rows, core * columns, columns)
        steps = [1, 2] if shards == 4 else list(range(1, shards))
        arrivals = []
        for k in steps:
            if shards == 4:
                to = origin = neighbours(me)[k - 1]
            else:
                to, origin = lax.rem(me + k, shards), lax.rem(me + shards - k, shards)
            pair = []
            for side in range(2):
                copy = copies(mine, goal, device(to, group, owner))
                pl.when(core == side)(copy.start)
                sent.append((core == side, copy.wait_send))
                pair.append(copy)
            arrivals.append((lax.div(origin, half) == core, pair))
        whole = copies(
            at(source, row, rows, 0, 2 * columns), block(me), partner
        )
        pl.when(owner != core)(whole.start)
        sent.append((owner != core, whole.wait_send))
        due.append((owner == core, whole))
        if shards == 4:
            tall.append((block, rows // 2, arrivals))
        else:
            for condition, pair in arrivals:
                due.extend((condition, copy) for copy in pair)
    gains, given = sources[-2:], targets[-2:]
    for k in range(1, shards):
        due.append(go(gains[0], given[0].at[me], device(lax.rem(me + k, shards), group, core)))
    due.append(go(gains[0], given[0].at[me], partner))
    due.append(go(gains[1], given[1], partner))
    if shards == 4:
        due.extend(passed_on(wide))
        fast, slow, _ = neighbours(me)
        for block, rows, arrivals in tall:
            for number, (condition, pair) in enumerate(arrivals):
                start = number * rows
                from_, to = (fast, slow) if number == 0 else (slow, fast)
                part = block(from_).at[pl.ds(start, rows), :]
                copy = copies(part, part, device(to, group, core))

                @pl.when(condition)
                def _(pair=pair, copy=copy):
                    for one in pair:
                        one.wait_recv()
                    copy.start()

                sent.append((condition, copy.wait_send))
                due.append((owner != core, copy))
    for item in sent:
        pl.when(item[0])(item[1]) if isinstance(item, tuple) else item()
    for item in due:
        pl.when(item[0])(item[1].wait_recv) if isinstance(item, tuple) else item.wait_recv()


def pack_kernel(shards, chunks, gate_ref, up_ref, down_ref, *refs):
    *packs, sems = refs
    core = lax.rem(lax.axis_index("rep"), 2)
    half = shards // 2
    total, rows = down_ref.shape[0], gate_ref.shape[0]
    piece = total // chunks
    columns = down_ref.shape[1] // 2
    copies = []
    for pack in packs:
        for row, chunk in pack[1]:
            for j, ref in enumerate((gate_ref, up_ref)):
                for i in range(half):
                    start = (core * half + i) * total + chunk * piece
                    copies.append(
                        (
                            at(ref, 0, rows, start, piece),
                            pack[0].at[pl.ds(row, rows), pl.ds((j * half + i) * piece, piece)],
                        )
                    )
            folds = 2 * half * piece // columns
            size = piece // folds
            for i in range(folds):
                copies.append(
                    (
                        at(down_ref, chunk * piece + i * size, size, core * columns, columns),
                        pack[0].at[pl.ds(row + rows, size), pl.ds(i * columns, columns)],
                    )
                )
    copies = [pltpu.make_async_copy(a, b, sems.at[k]) for k, (a, b) in enumerate(copies)]
    for copy in copies:
        copy.start()
    for copy in copies:
        copy.wait()


def add_up(parts, target, least):
    total_rows = target.shape[0]
    rows = max(k for k in range(least, 97, least) if total_rows % k == 0)

    def some(i, _):
        here = pl.ds(pl.multiple_of(i * rows, rows), rows)
        total = parts[0][here, :].astype(F32)
        for part in parts[1:]:
            total += part[here, :].astype(F32)
        target[here, :] = total.astype(target.dtype)
        return 0

    lax.fori_loop(0, total_rows // rows, some, 0)


def reduce_over_plane(copies, load, shards, grad_ref, level, bufs):
    me, group, core = place()
    rows = level.shape[0]

    def block(shard, start=0, size=rows):
        return at_rows(grad_ref, shard * rows + start, size)

    own = bufs[0]
    local = pltpu.make_async_copy(block(me), own, load.at[0])
    if shards != 4:
        planes = bufs[1]
        out = [
            copies(block(lax.rem(me + k, shards)), planes.at[k - 1], device(lax.rem(me + k, shards), group, core))
            for k in range(1, shards)
        ]

        def start():
            local.start()
            for copy in out:
                copy.start()

        def end():
            local.wait()
            for copy in out:
                copy.wait_send()
                copy.wait_recv()
            add_up([own] + [planes.at[k] for k in range(shards - 1)], level, 16)

        return [start, idle, idle, end]
    fast, slow, across = neighbours(me)
    to_fast, to_slow = device(fast, group, core), device(slow, group, core)
    half = rows // 2
    planes, met_fast, met_slow, held_fast, held_slow = bufs[1:]
    upper, lower = pl.ds(0, half), pl.ds(half, half)
    loads = [
        local,
        pltpu.make_async_copy(block(fast, half, half), held_fast, load.at[1]),
        pltpu.make_async_copy(block(slow, 0, half), held_slow, load.at[2]),
    ]
    early = [
        copies(block(across, 0, half), met_fast, to_fast),
        copies(block(across, half, half), met_slow, to_slow),
        copies(block(fast, 0, half), planes.at[0, upper, :], to_fast),
        copies(block(slow, half, half), planes.at[1, lower, :], to_slow),
    ]
    late = [
        copies(held_fast, planes.at[0, lower, :], to_fast),
        copies(held_slow, planes.at[1, upper, :], to_slow),
    ]

    def start():
        for copy in early[:2] + loads:
            copy.start()

    def direct():
        for copy in early[2:]:
            copy.start()

    def merge():
        for copy in loads:
            copy.wait()
        for copy, met, held, out in (
            (early[1], met_slow, held_fast, late[0]),
            (early[0], met_fast, held_slow, late[1]),
        ):
            copy.wait_recv()
            add_up([held, met], held, 16)
            out.start()

    def end():
        for copy in early[2:] + late:
            copy.wait_recv()
        for copy in early + late:
            copy.wait_send()
        add_up([own, planes.at[0], planes.at[1]], level, 16)

    return [start, direct, merge, end]


def plane_buffers(shards, shape):
    half = (shape[0] // 2, shape[1])
    if shards != 4:
        return [pltpu.VMEM(shape, LOW), pltpu.VMEM((shards - 1,) + shape, LOW)]
    return [pltpu.VMEM(shape, LOW), pltpu.VMEM((2,) + shape, LOW)] + [pltpu.VMEM(half, LOW)] * 4


def reduce_over_line(copies, groups, source, part, total, bufs):
    me, group, core = place()
    if groups != 4:
        (slots,) = bufs
        out = [
            copies(source, slots.at[group], device(me, lax.rem(group + k, groups), core))
            for k in range(1, groups)
        ]

        def start():
            for copy in out:
                copy.start()

        def end():
            rows = part.shape[0]

            def some(i, _):
                here = pl.ds(pl.multiple_of(i * 8, 8), 8)
                slots[group, here, :] = part[here, :]
                return 0

            lax.fori_loop(0, rows // 8, some, 0)
            for copy in out:
                copy.wait_send()
                copy.wait_recv()
            add_up([slots.at[k] for k in range(groups)], total, 8)

        return [start, idle, idle, end]
    met, summed, other = bufs
    outer = jnp.logical_or(group == 0, group == groups - 1)
    inner = jnp.logical_not(outer)
    mate = device(me, group + 1 - 2 * lax.rem(group, 2), core)
    inward = copies(source, met, mate)
    between = copies(summed, other, device(me, groups - 1 - group, core))
    back = copies(total, total, mate)

    def start():
        pl.when(outer)(inward.start)

    def exchange():
        @pl.when(inner)
        def _():
            inward.wait_recv()
            add_up([part, met], summed, 16)
            between.start()

    def give():
        @pl.when(inner)
        def _():
            between.wait_recv()
            add_up([summed, other], total, 16)
            back.start()

    def end():
        @pl.when(outer)
        def _():
            inward.wait_send()
            back.wait_recv()

        @pl.when(inner)
        def _():
            between.wait_send()
            back.wait_send()

    return [start, exchange, give, end]


def idle():
    pass


def line_buffers(groups, shape):
    if groups != 4:
        return [pltpu.VMEM((groups,) + shape, LOW)]
    return [pltpu.VMEM(shape, LOW)] * 3


PARTS = 8


def parts_of(shape):
    return PARTS if shape[0] * shape[1] >= 1 << 18 else PARTS // 2


class LineSum:
    def __init__(self, copies, groups, source, part, total, bufs):
        self.count = parts_of(part.shape)
        rows = part.shape[0] // self.count
        each = len(bufs) // self.count
        self.parts = [
            reduce_over_line(
                copies,
                groups,
                at_rows(source, i * rows, rows),
                at_rows(part, i * rows, rows),
                at_rows(total, i * rows, rows),
                bufs[i * each : (i + 1) * each],
            )
            for i in range(self.count)
        ]

    def run(self, part, stage):
        if part < self.count:
            self.parts[part][stage]()

    def all(self, stage, first=0, last=None):
        for part in self.parts[first:last]:
            part[stage]()

    @staticmethod
    def buffers(groups, shape):
        count = parts_of(shape)
        return line_buffers(groups, (shape[0] // count, shape[1])) * count

    @staticmethod
    def copies(groups, shape):
        return parts_of(shape) * max(3, groups - 1)


class Side:
    def __init__(self, shards, groups, plane_shapes, line_shapes, extra=0):
        self.shards, self.groups, self.extra = shards, groups, extra
        self.plane_shapes, self.line_shapes = plane_shapes, line_shapes

    def outs(self):
        return [jax.ShapeDtypeStruct(shape, LOW) for shape in self.plane_shapes + self.line_shapes]

    def scratch(self):
        groups, shards = self.groups, self.shards
        shapes = [pltpu.VMEM(shape, LOW) for shape in self.plane_shapes + self.line_shapes]
        for shape in self.plane_shapes:
            shapes += plane_buffers(shards, shape)
        for shape in self.line_shapes:
            shapes += [pltpu.VMEM(shape, LOW)] + LineSum.buffers(groups, shape)
        count = 2 * self.shards + len(self.plane_shapes) * max(6, shards - 1)
        count += sum(LineSum.copies(groups, shape) for shape in self.line_shapes) + self.extra
        loads = 4 * len(self.plane_shapes) + 2 * len(self.line_shapes) + 1
        return shapes + [pltpu.SemaphoreType.DMA((count,))] * 2 + [pltpu.SemaphoreType.DMA((loads,))]

    def run(self, step, sources, outs, bufs):
        *bufs, send, recv, load = bufs
        totals, bufs = take(bufs, len(outs))
        me, group, core = place()
        copies = Copies(send, recv)
        shards, groups = self.shards, self.groups

        @pl.when(step == 0)
        def _():
            meet(everyone_near(shards, groups))

        planes, lines, loads = [], [], []
        for i, shape in enumerate(self.plane_shapes):
            some, bufs = take(bufs, len(plane_buffers(shards, shape)))
            planes.append(
                reduce_over_plane(
                    copies, load.at[pl.ds(3 * i, 3)], shards, sources[i], totals[i], some
                )
            )
        first = len(self.plane_shapes)
        for i, shape in enumerate(self.line_shapes):
            (own,), bufs = take(bufs, 1)
            some, bufs = take(bufs, len(LineSum.buffers(groups, shape)))
            source = at_rows(sources[first + i], 0, shape[0])
            loads.append(pltpu.make_async_copy(source, own, load.at[3 * first + i]))
            lines.append(LineSum(copies, groups, source, own, totals[first + i], some))

        def begin():
            for stages in planes:
                stages[0]()
            for stages in planes:
                stages[1]()
            for part in range(PARTS):
                for line in lines:
                    line.run(part, 0)
            for one in loads:
                one.start()

        def load_done():
            for one in loads:
                one.wait()

        def of_lines(part, stage):
            def go():
                for line in lines:
                    line.run(part, stage)

            return go

        def merge():
            for stages in planes:
                stages[2]()

        received = {1: [0], 2: [1], 3: [2, 3], 4: [4], 5: [5, 6], 6: [7]}
        given = {3: [0, 1], 4: [2, 3], 5: [4], 6: [5, 6], 7: [7]}
        plan = {0: [begin]}
        for when in range(1, 8):
            plan[when] = [load_done] if when == 1 else []
            plan[when] += [of_lines(part, 1) for part in received.get(when, [])]
            plan[when] += [merge] if when == 3 else []
            plan[when] += [of_lines(part, 2) for part in given.get(when, [])]
        for when, stages in plan.items():

            @pl.when(step == when)
            def _(stages=stages):
                for stage in stages:
                    stage()

        count = len(outs)
        stores = [
            pltpu.make_async_copy(total, out, load.at[load.shape[0] - 1 - count + i])
            for i, (total, out) in enumerate(zip(totals, outs))
        ]

        def end():
            for stages, store in zip(planes, stores):
                stages[3]()
                store.start()
            for part in range(PARTS):
                for line in lines:
                    line.run(part, 3)
            for store in stores[len(planes) :]:
                store.start()
            for store in stores:
                store.wait()

        return copies, end


class Blocks:
    def __init__(self, copies, partner, count, block, held, got):
        self.count, self.block = count, block
        self.copies = [
            copies(
                held.at[pl.ds(k % (held.shape[0] // block) * block, block), :],
                got.at[pl.ds(k * block, block), :],
                partner,
            )
            for k in range(count)
        ]
        self.slots = held.shape[0] // block
        self.held, self.got = held, got

    def begin(self, step, first):
        for k in range(self.count):

            @pl.when(step == first + k + 1)
            def _(k=k):
                self.copies[k].start()
                if k + 1 >= self.slots and k + 1 < self.count:
                    self.copies[k + 1 - self.slots].wait_send()

    def put(self, number, values):
        self.held[pl.ds(lax.rem(number, self.slots) * self.block, self.block), :] = values

    def take(self, step, first):
        for k in range(self.count):
            pl.when(step == first + k)(self.copies[k].wait_recv)
        start = jnp.clip(step - first, 0, self.count - 1) * self.block
        return self.got[pl.ds(pl.multiple_of(start, self.block), self.block), :]

    def end(self, sent_last, received):
        if sent_last:
            self.copies[-1].start()
        for k in range(max(0, self.count - self.slots), self.count):
            self.copies[k].wait_send()
        if received:
            for copy in self.copies:
                copy.wait_recv()


def everyone_near(shards, groups):
    me, group, core = place()
    return (
        [device(lax.rem(me + k, shards), group, core) for k in range(1, shards)]
        + [device(me, lax.rem(group + k, groups), core) for k in range(1, groups)]
        + [device(me, group, 1 - core)]
    )


def take(refs, count):
    return refs[:count], refs[count:]


def finish_kernel(shards, groups, counts, rows, skip, length_ref, *refs):
    smalls, refs = take(refs, 1 + max(k for k, _ in rows))
    (grad_ref,), refs = take(refs, 1)
    lows, refs = take(refs, counts[0])
    ready, refs = take(refs, counts[1])
    n = counts[0] + 2
    mine_out, refs = take(refs, n)
    other, refs = take(refs, n + counts[1])
    (total_ref,), refs = take(refs, 1)
    mine, refs = take(refs, n)
    levels, refs = take(refs, 2)
    own, refs = take(refs, counts[0])
    plane_bufs = []
    for level in levels:
        some, refs = take(refs, len(plane_buffers(shards, level.shape)))
        plane_bufs.append(some)
    line_bufs = []
    for one in mine:
        some, refs = take(refs, len(LineSum.buffers(groups, one.shape)))
        line_bufs.append(some)
    small_a, small_b, small_c, send, recv, load = refs
    me, group, core = place()
    partner = device(me, group, 1 - core)
    plane = [device(lax.rem(me + k, shards), group, core) for k in range(1, shards)]
    line = [device(me, lax.rem(group + k, groups), core) for k in range(1, groups)]
    copies = Copies(send, recv)

    def go(source, target, where):
        copy = copies(source, target, where)
        copy.start()
        return copy

    def finish(some):
        for copy in some:
            copy.wait_send()
            copy.wait_recv()

    parts = [
        at_rows(low, 0 if i else skip, one.shape[0]) for i, (low, one) in enumerate(zip(lows, own))
    ]
    loads = [pltpu.make_async_copy(low, own[i], load.at[6 + i]) for i, low in enumerate(parts)]
    for copy in loads:
        copy.start()
    for i, (k, row) in enumerate(rows):
        values = smalls[k][row : row + 1, :]
        small_a[me, i : i + 1, : values.shape[1]] = values
        if values.shape[1] < small_a.shape[2]:
            rest = small_a.shape[2] - values.shape[1]
            small_a[me, i : i + 1, values.shape[1] :] = jnp.zeros((1, rest), F32)
    small_a[me, len(rows) :, :] = jnp.full(
        (small_a.shape[1] - len(rows), small_a.shape[2]), length_ref[0].astype(F32)
    )
    meet(everyone_near(shards, groups))
    columns = levels[0].shape[1]
    planes = [
        reduce_over_plane(
            copies,
            load.at[pl.ds(3 * i, 3)],
            shards,
            grad_ref.at[:, pl.ds(i * columns, columns)],
            level,
            plane_bufs[i],
        )
        for i, level in enumerate(levels)
    ]
    sums = [
        LineSum(copies, groups, source, part, mine[i], line_bufs[i])
        for i, (source, part) in enumerate(zip(parts + list(levels), list(own) + list(levels)))
    ]
    early, halves = sums[: counts[0]], sums[counts[0] :]
    for stages in planes:
        stages[0]()
        stages[1]()
    for one in early:
        one.all(0)
    small_copies = [go(small_a.at[me], small_a.at[me], where) for where in plane]
    swaps = [go(source, target, partner) for source, target in zip(ready, other[n:])]
    for copy in loads:
        copy.wait()
    planes[0][2]()
    planes[1][2]()
    for one in early:
        one.all(1, 0, one.count // 2)
    planes[0][3]()
    halves[0].all(0)
    finish(small_copies)
    small_b[group] = sum(small_a[k] for k in range(shards))
    small_copies = [go(small_b.at[group], small_b.at[group], where) for where in line]
    for one in early:
        one.all(1, one.count // 2)
        one.all(2, 0, one.count // 2)
    planes[1][3]()
    halves[1].all(0)
    for one in early:
        one.all(2, one.count // 2)
    finish(small_copies)
    small_c[core] = sum(small_b[k] for k in range(groups))
    small_copies = [go(small_c.at[core], small_c.at[core], partner)]
    halves[0].all(1)
    halves[1].all(1)
    halves[0].all(2)
    stores = []

    def hand(i):
        sums[i].all(3)
        swaps.append(go(mine[i], other[i], partner))
        stores.append(pltpu.make_async_copy(mine[i], mine_out[i], load.at[6 + counts[0] + i]))
        stores[-1].start()

    for i in range(counts[0]):
        hand(i)
    halves[1].all(2)
    hand(counts[0])
    hand(counts[0] + 1)
    finish(small_copies)
    total_ref[...] = small_c[0] + small_c[1]
    finish(swaps)
    for store in stores:
        store.wait()


def finish_sums(grad, length, smalls, rows, lows, skip, ready, shards, groups):
    level = (grad.shape[0] // shards, grad.shape[1] // 2)
    shapes = [(low.shape[0] - (0 if i else skip), low.shape[1]) for i, low in enumerate(lows)]
    shapes += [level] * 2
    others = shapes + [one.shape for one in ready]
    vmem = pl.BlockSpec(memory_space=pltpu.VMEM)
    hbm = pl.BlockSpec(memory_space=pltpu.HBM)
    scratch = [pltpu.VMEM(shape, LOW) for shape in shapes + [level] * 2 + shapes[: len(lows)]]
    for _ in range(2):
        scratch += plane_buffers(shards, level)
    for shape in shapes:
        scratch += LineSum.buffers(groups, shape)
    count = 2 * max(6, shards) + sum(LineSum.copies(groups, shape) for shape in shapes)
    count += len(others) + shards + groups
    small = (8, max(one.shape[1] for one in smalls))
    outs = pl.pallas_call(
        partial(finish_kernel, shards, groups, (len(lows), len(ready)), rows, skip),
        out_shape=[jax.ShapeDtypeStruct(shape, LOW) for shape in shapes + others]
        + [jax.ShapeDtypeStruct(small, F32)],
        in_specs=[pl.BlockSpec(memory_space=pltpu.SMEM)]
        + [vmem] * len(smalls)
        + [hbm] * (1 + len(lows) + len(ready)),
        out_specs=[hbm] * (len(shapes) + len(others)) + [vmem],
        scratch_shapes=scratch
        + [pltpu.VMEM((size,) + small, F32) for size in (shards, groups, 2)]
        + [pltpu.SemaphoreType.DMA((count,)), pltpu.SemaphoreType.DMA((count,))]
        + [pltpu.SemaphoreType.DMA((6 + len(lows) + len(shapes),))],
        compiler_params=pltpu.CompilerParams(
            collective_id=1, has_side_effects=True, vmem_limit_bytes=62 << 20
        ),
        name="finish",
    )(length, *smalls, grad, *lows, *ready)
    n = len(shapes)
    return outs[:n], outs[n:-1], outs[-1]


def two_parts(column):
    high = column.astype(LOW)
    return high, (column - high.astype(F32)).astype(LOW)


def below(ref, here, heads):
    return jnp.concatenate([ref[here, pl.ds(h * LANES, LANES)] for h in range(heads)], axis=0)


def attend_kernel(block, width, lens_ref, q_ref, k_ref, v_ref, att_ref, qx_ref):
    rows = q_ref.shape[0]
    heads = q_ref.shape[1] // LANES
    length = lens_ref[pl.program_id(0)]
    lane = lax.broadcasted_iota(jnp.int32, (block, LANES), 1)
    keep = lax.broadcasted_iota(jnp.int32, (block, block), 1) <= lax.broadcasted_iota(
        jnp.int32, (block, block), 0
    )
    for step in range(rows // block):
        start = step * block
        here = pl.ds(start, block)

        @pl.when(start < length)
        def _():
            outs = []
            for head in range(heads):
                lanes = pl.ds(head * LANES, LANES)
                query = q_ref[here, lanes]
                probs = jnp.exp(nt(query, k_ref[here, :]))
                probs = jnp.where(keep, probs, 0.0).astype(LOW)
                total = nn(probs, v_ref[here, :])
                if step:
                    probs = jnp.exp(nt(query, k_ref[pl.ds(0, start), :])).astype(LOW)
                    total += nn(probs, v_ref[pl.ds(0, start), :])
                weight = total[:, width : width + 1]
                outs.append(total / weight)
                high, rest = two_parts(-jnp.log(weight))
                qx_ref[here, lanes] = jnp.where(
                    lane == width, high, jnp.where(lane == width + 1, rest, query)
                )
            for pair in range(heads // 2):
                att_ref[here, pl.ds(pair * LANES, LANES)] = jnp.where(
                    lane < width, outs[2 * pair], pltpu.roll(outs[2 * pair + 1], width, 1)
                ).astype(LOW)

        @pl.when(start >= length)
        def _():
            att_ref[here, :] = jnp.zeros((block, att_ref.shape[1]), LOW)
            qx_ref[here, :] = jnp.zeros((block, qx_ref.shape[1]), LOW)


def attend_back_kernel(block, width, side, q_ref, k_ref, v_ref, do_ref, *refs):
    count = len(side.plane_shapes) + len(side.line_shapes)
    sources, refs = take(refs, count)
    (dq_ref, dk_ref, dv_ref), refs = take(refs, 3)
    totals, bufs = take(refs, count)
    grid_step = pl.program_id(0) * pl.num_programs(1) + pl.program_id(1)
    _, end = side.run(grid_step, sources, totals, bufs)
    rows = q_ref.shape[0]
    heads = q_ref.shape[1] // LANES
    lane = lax.broadcasted_iota(jnp.int32, (block, LANES), 1)
    shape = (block, heads * block)
    keep = lax.broadcasted_iota(jnp.int32, shape, 0) <= lax.rem(
        lax.broadcasted_iota(jnp.int32, shape, 1), block
    )
    dk_ref[...] = jnp.zeros(dk_ref.shape, F32)
    dv_ref[...] = jnp.zeros(dv_ref.shape, F32)
    for step in range(rows // block):
        start = step * block
        here = pl.ds(start, block)
        query, dout = below(q_ref, here, heads), below(do_ref, here, heads)

        def one(keys, masked):
            key, value = k_ref[keys, :], v_ref[keys, :]
            probs = jnp.exp(nt(key, query))
            if masked:
                probs = jnp.where(keep, probs, 0.0)
            dscores = (probs * nt(value, dout)).astype(LOW)
            dv_ref[keys, :] += nn(probs.astype(LOW), dout)
            dk_ref[keys, :] += nn(dscores, query)
            return tn(dscores, key)

        dquery = one(here, True)
        if step:
            dquery += one(pl.ds(0, start), False)
        for pair in range(heads // 2):
            first = dquery[2 * pair * block : (2 * pair + 1) * block]
            second = dquery[(2 * pair + 1) * block : (2 * pair + 2) * block]
            dq_ref[here, pl.ds(pair * LANES, LANES)] = jnp.where(
                lane < width, first, pltpu.roll(second, width, 1)
            )
    pl.when(grid_step == pl.num_programs(0) * pl.num_programs(1) - 1)(end)


def attention_grid(slots, groups, per_group, rows):
    wide = pl.BlockSpec((rows, per_group * LANES), lambda s, g, lens: (s, g))
    dense = pl.BlockSpec((rows, per_group * LANES // 2), lambda s, g, lens: (s, g))
    narrow = pl.BlockSpec((rows, LANES), lambda s, g, lens: (s, g))
    return (slots, groups), wide, dense, narrow


def attend(lens, queries, keys, values, rows, width, block):
    slots, groups = queries.shape[0] // rows, keys.shape[1] // LANES
    per_group = queries.shape[1] // LANES // groups
    grid, wide, dense, narrow = attention_grid(slots, groups, per_group, rows)
    flops = 4 * slots * groups * per_group * rows * rows * LANES
    return pl.pallas_call(
        partial(attend_kernel, block, width),
        out_shape=(
            jax.ShapeDtypeStruct((queries.shape[0], queries.shape[1] // 2), LOW),
            jax.ShapeDtypeStruct(queries.shape, LOW),
        ),
        grid_spec=pltpu.PrefetchScalarGridSpec(
            num_scalar_prefetch=1,
            grid=grid,
            in_specs=[wide, narrow, narrow],
            out_specs=[dense, wide],
        ),
        cost_estimate=pl.CostEstimate(flops=flops, bytes_accessed=1 << 23, transcendentals=0),
        name="attend",
    )(lens, queries, keys, values)


def attend_back(queries, keys, values, douts, rows, width, block, side, sources):
    slots, groups = queries.shape[0] // rows, keys.shape[1] // LANES
    per_group = queries.shape[1] // LANES // groups
    wide = pl.BlockSpec((rows, per_group * LANES), lambda s, g: (s, g))
    dense = pl.BlockSpec((rows, per_group * LANES // 2), lambda s, g: (s, g))
    narrow = pl.BlockSpec((rows, LANES), lambda s, g: (s, g))
    flops = 10 * slots * groups * per_group * rows * rows * LANES
    return pl.pallas_call(
        partial(attend_back_kernel, block, width, side),
        out_shape=[
            jax.ShapeDtypeStruct((queries.shape[0], queries.shape[1] // 2), F32),
            jax.ShapeDtypeStruct(keys.shape, F32),
            jax.ShapeDtypeStruct(keys.shape, F32),
        ]
        + side.outs(),
        grid=(slots, groups),
        in_specs=[wide, narrow, narrow, wide]
        + [pl.BlockSpec(memory_space=pltpu.HBM)] * len(sources),
        out_specs=[dense, narrow, narrow]
        + [pl.BlockSpec(memory_space=pltpu.HBM)] * len(side.outs()),
        scratch_shapes=side.scratch(),
        cost_estimate=pl.CostEstimate(flops=flops, bytes_accessed=1 << 24, transcendentals=0),
        compiler_params=pltpu.CompilerParams(
            collective_id=5, has_side_effects=True, vmem_limit_bytes=62 << 20
        ),
        name="attend_back",
    )(queries, keys, values, douts, *sources)


def swap_halves(values, width):
    lane = lax.broadcasted_iota(jnp.int32, values.shape, 1)
    half = width // 2
    return jnp.where(
        lane % width < half, pltpu.roll(values, LANES - half, 1), pltpu.roll(values, half, 1)
    )


def head_sum(values, width):
    same = lax.broadcasted_iota(jnp.int32, (LANES, LANES), 0) // width
    same = (same == lax.broadcasted_iota(jnp.int32, (LANES, LANES), 1) // width).astype(LOW)
    high, rest = two_parts(values)
    return nn(high, same) + nn(rest, same)


def row_rsqrt(values):
    return lax.rsqrt(jnp.mean(values * values, axis=1, keepdims=True) + EPS)


def is_live(lens_ref, step, per_slot, block):
    return lax.rem(step, per_slot) * block < lens_ref[lax.div(step, per_slot)]


def qkv_kernel(
    per_slot, counts, width, scale, lens_ref, own_ref, other_ref, w_ref, ga_ref, gh_ref, cos_ref, sin_ref,
    normed_ref, raw_ref, q_ref, k_ref, v_ref,
):
    step = pl.program_id(0)
    block = own_ref.shape[0]
    q_tiles, kv_tiles = counts

    @pl.when(is_live(lens_ref, step, per_slot, block))
    def _():
        x = jnp.where(step < per_slot, own_ref[...], other_ref[...]).astype(F32)
        normed = (x * row_rsqrt(x) * ga_ref[...]).astype(LOW)
        normed_ref[...] = normed
        lane = lax.broadcasted_iota(jnp.int32, (block, LANES), 1)
        zero = jnp.zeros((block, LANES), F32)
        ones = jnp.where(lane < width + 2, 1.0, 0.0)
        cosine, sine = cos_ref[...], sin_ref[...]

        def put(ref, tile, values, rest):
            ref[:, pl.ds(2 * tile * LANES, LANES)] = jnp.where(lane < width, values, rest).astype(LOW)
            ref[:, pl.ds((2 * tile + 1) * LANES, LANES)] = jnp.where(
                lane < width, pltpu.roll(values, width, 1), rest
            ).astype(LOW)

        for tile in range(q_tiles + 2 * kv_tiles):
            lanes = pl.ds(tile * LANES, LANES)
            if tile % 2 == 0:
                pair = nn(normed, w_ref[:, pl.ds(tile * LANES, 2 * LANES)])
            values = pair[:, (tile % 2) * LANES : (tile % 2 + 1) * LANES]
            if tile >= q_tiles + kv_tiles:
                put(v_ref, tile - q_tiles - kv_tiles, values, ones)
                continue
            raw_ref[:, lanes] = values
            is_query = tile < q_tiles
            gain = gh_ref[0:1, :] if is_query else gh_ref[1:2, :]
            values *= lax.rsqrt(head_sum(values * values, width) * (1.0 / width) + EPS) * gain
            values = values * cosine + swap_halves(values, width) * sine
            if is_query:
                put(q_ref, tile, values * scale, zero)
            else:
                put(k_ref, tile - q_tiles, values, ones)

    @pl.when(jnp.logical_not(is_live(lens_ref, step, per_slot, block)))
    def _():
        for ref in (normed_ref, raw_ref, q_ref, k_ref, v_ref):
            ref[...] = jnp.zeros(ref.shape, ref.dtype)


def out_kernel(
    per_slot, length_ref, att_ref, w_ref, x_ref, gain_ref, resid_ref, normed_ref, sums_ref,
    other_out, give, got, hold, other, send, recv, store,
):
    step = pl.program_id(0)
    block = att_ref.shape[0]
    me, group, core = place()
    partner = device(me, group, 1 - core)
    copies = Copies(send, recv)
    parts = Blocks(copies, partner, per_slot, block, give, got)
    normed_parts = Blocks(copies, partner, per_slot, block, hold, other)

    @pl.when(step == 0)
    def _():
        meet([partner])
        sums_ref[...] = jnp.zeros(sums_ref.shape, F32)

    parts.begin(step, 0)
    normed_parts.begin(step, per_slot)
    product = nn(att_ref[...], w_ref[...])

    @pl.when(step < per_slot)
    def _():
        parts.put(step, product.astype(LOW))

    @pl.when(step >= per_slot)
    def _():
        number = step - per_slot
        valid = lax.broadcasted_iota(jnp.int32, (block, 1), 0) + number * block < length_ref[0]
        attn_out = product + parts.take(step, per_slot).astype(F32)
        resid = x_ref[...].astype(F32) + attn_out
        resid_ref[...] = resid
        normed = (resid * row_rsqrt(resid) * gain_ref[...]).astype(LOW)
        normed_ref[...] = normed
        normed_parts.put(number, normed)
        for row, values in ((0, resid), (1, attn_out)):
            sums_ref[row : row + 1, :] += jnp.sum(
                jnp.where(valid, values * values, 0.0), axis=0, keepdims=True
            )

    @pl.when(step == 2 * per_slot - 1)
    def _():
        parts.end(False, False)
        normed_parts.end(True, True)
        copy = pltpu.make_async_copy(other, other_out, store.at[0])
        copy.start()
        copy.wait()


def ffn_kernel(
    per_slot, shards, chained, last, side, offset, lens_ref, x_own, x_other, g_own, g_other,
    gathered_ref, *refs,
):
    if chained:
        (mlp_in, db_in), refs = take(refs, 2)
    if last:
        (resid_ref, gain_ref), refs = take(refs, 2)
    count = len(side.plane_shapes) + len(side.line_shapes)
    sources, refs = take(refs, count)
    if last:
        (out_ref, dresid_ref, dattn_ref, sums_ref, dattn_out), refs = take(refs, 5)
    else:
        (mlp_ref, db_ref), refs = take(refs, 2)
    (grad_out,), refs = take(refs, 1)
    totals, refs = take(refs, count)
    (acc_ref, accd_ref, given_ref, w_ref, wd_ref, grad_ref, load), refs = take(refs, 7)
    exchange, bufs = take(refs, 6 if last else 0)
    step = pl.program_id(0)
    copies, end = side.run(step, sources, totals, bufs)
    own = step >= per_slot if last else step < per_slot
    units, depth = wd_ref.shape
    block = x_own.shape[0]
    me, group, core = place()
    partner = device(me, group, 1 - core)
    half, columns, d_rows = shards // 2, depth // 2, depth // shards
    packed = grad_ref.shape[0] // shards
    size = packed - d_rows
    folds = grad_ref.shape[1] // columns

    def folded(ref, shard, fold):
        return ref.at[shard, pl.ds(offset + d_rows, size), pl.ds(fold * columns, columns)]

    def unfolded(i, fold):
        return at(wd_ref, (i * folds + fold) * size, size, core * columns, columns)

    tiles = [(i, fold) for i in range(half) for fold in range(folds)]
    given = [
        copies(folded(gathered_ref, (1 - core) * half + i, fold), unfolded(i, fold), partner)
        for i, fold in tiles
    ]
    loads = [
        pltpu.make_async_copy(
            gathered_ref.at[shard, pl.ds(offset, d_rows), :],
            w_ref.at[pl.ds(shard * d_rows, d_rows), :],
            load.at[shard],
        )
        for shard in range(shards)
    ] + [
        pltpu.make_async_copy(
            folded(gathered_ref, core * half + i, fold), unfolded(i, fold), load.at[shards + k]
        )
        for k, (i, fold) in enumerate(tiles)
    ]

    if last:
        give_mlp, got_mlp, give_db, got_db, hold, other = exchange
        mlp_parts = Blocks(copies, partner, per_slot, block, give_mlp, got_mlp)
        db_parts = Blocks(copies, partner, per_slot, block, give_db, got_db)
        attn_parts = Blocks(copies, partner, per_slot, block, hold, other)
        mlp_parts.begin(step, 0)
        db_parts.begin(step, 0)
        attn_parts.begin(step, per_slot)

    @pl.when(step == 0)
    def _():
        if last:
            sums_ref[...] = jnp.zeros(sums_ref.shape, F32)
        for copy in given + loads:
            copy.start()
        acc_ref[...] = jnp.zeros(acc_ref.shape, F32)
        accd_ref[...] = jnp.zeros(accd_ref.shape, F32)
        for copy in loads:
            copy.wait()
        for copy in given:
            copy.wait_send()
            copy.wait_recv()

    x = jnp.where(own, x_own[...], x_other[...])
    length = jnp.where(own, lens_ref[0], lens_ref[1])
    row = lax.broadcasted_iota(jnp.int32, (block, 1), 0) + lax.rem(step, per_slot) * block
    valid = row < length
    g = jnp.where(valid, jnp.where(own, g_own[...], g_other[...]), jnp.zeros((), LOW))
    gate = nn(x, w_ref[:, :units])
    up = nn(x, w_ref[:, units:])
    d_hidden = nt(g, wd_ref[...])
    sig = jax.nn.sigmoid(gate)
    silu = gate * sig
    hidden = (silu * up).astype(LOW)
    d_gate = (d_hidden * up * (sig * (1.0 + gate * (1.0 - sig)))).astype(LOW)
    d_up = (d_hidden * silu).astype(LOW)
    mlp = nn(hidden, wd_ref[...])
    d_b = nt(d_gate, w_ref[:, :units]) + nt(d_up, w_ref[:, units:])
    if chained:
        mlp += mlp_in[...]
        d_b += db_in[...]
    if last:

        @pl.when(step < per_slot)
        def _():
            mlp_parts.put(step, mlp.astype(LOW))
            db_parts.put(step, d_b.astype(LOW))

        @pl.when(step >= per_slot)
        def _():
            number = step - per_slot
            resid = resid_ref[...]
            mlp_out = mlp + mlp_parts.take(step, per_slot).astype(F32)
            out_ref[...] = jnp.where(valid, resid + mlp_out, 0.0).astype(LOW)
            d_norm, d_gain = norm_back(
                resid, d_b + db_parts.take(step, per_slot).astype(F32), gain_ref[...]
            )
            d_resid = jnp.where(valid, g.astype(F32) + d_norm, 0.0)
            dresid_ref[...] = d_resid
            d_attn = d_resid.astype(LOW)
            dattn_ref[...] = d_attn
            attn_parts.put(number, d_attn)
            for row, values in ((0, mlp_out * mlp_out), (1, d_gain)):
                sums_ref[row : row + 1, :] += jnp.sum(
                    jnp.where(valid, values, 0.0), axis=0, keepdims=True
                )

    else:
        mlp_ref[...] = mlp
        db_ref[...] = d_b
    acc_ref[:, :units] += tn(x, d_gate)
    acc_ref[:, units:] += tn(x, d_up)
    accd_ref[...] += tn(hidden, g)

    @pl.when(step == pl.num_programs(0) - 1)
    def _():
        mine = pl.ds(pl.multiple_of(core * columns, columns), columns)
        theirs = pl.ds(pl.multiple_of((1 - core) * columns, columns), columns)
        given_ref[...] = accd_ref[:, theirs].astype(LOW)
        for shard in range(shards):
            grad_ref[pl.ds(shard * packed, d_rows), :] = acc_ref[
                pl.ds(shard * d_rows, d_rows), :
            ].astype(LOW)
        out = []
        for i in range(half):
            for fold in range(folds):
                row = i * folds * size + fold * size
                to = pl.ds(
                    pl.multiple_of((core * half + i) * packed + d_rows, 8), size
                )
                lanes = pl.ds(fold * columns, columns)
                out.append(
                    copies(
                        given_ref.at[pl.ds(row, size), :],
                        grad_ref.at[to, lanes],
                        partner,
                    )
                )
                out[-1].start()
                grad_ref[to, lanes] = accd_ref[pl.ds(row, size), mine].astype(LOW)
        for copy in out:
            copy.wait_send()
            copy.wait_recv()
        stores = [pltpu.make_async_copy(grad_ref, grad_out, load.at[0])]
        stores[0].start()
        if last:
            mlp_parts.end(False, False)
            db_parts.end(False, False)
            attn_parts.end(True, True)
            stores.append(pltpu.make_async_copy(other, dattn_out, load.at[1]))
            stores[1].start()
        end()
        for store in stores:
            store.wait()


def norm_back(values, dy, gain):
    inverse = row_rsqrt(values)
    scaled = dy * gain
    inner = jnp.mean(values * scaled, axis=1, keepdims=True)
    return inverse * scaled - values * (inverse * inverse * inverse * inner), dy * values * inverse


def dout_kernel(
    per_slot, width, own_ref, other_ref, att_ref, w_ref, do_ref, grad_out,
    acc_ref, give, hold, send, recv, store,
):
    step = pl.program_id(0)
    block = own_ref.shape[0]
    me, group, core = place()

    @pl.when(step == 0)
    def _():
        meet([device(me, group, 1 - core)])
        acc_ref[...] = jnp.zeros(acc_ref.shape, F32)

    d_attn = jnp.where(step < per_slot, own_ref[...], other_ref[...])
    lane = lax.broadcasted_iota(jnp.int32, (block, LANES), 1)
    att = att_ref[...]
    acc_ref[...] += tn(att, d_attn)
    for tile in range(att.shape[1] // LANES):
        lanes = slice(tile * LANES, (tile + 1) * LANES)
        if tile % 2 == 0:
            pair = nt(d_attn, w_ref[tile * LANES : (tile + 2) * LANES, :])
        dout = pair[:, (tile % 2) * LANES : (tile % 2 + 1) * LANES].astype(LOW).astype(F32)
        delta = -head_sum(dout * att[:, lanes].astype(F32), width)
        for head, (values, column) in enumerate(
            ((dout, pltpu.roll(delta, width, 1)), (pltpu.roll(dout, width, 1), delta))
        ):
            high, rest = two_parts(column)
            column = jnp.where(
                lane == width, high, jnp.where(lane == width + 1, rest, jnp.zeros_like(rest))
            )
            do_ref[:, pl.ds((2 * tile + head) * LANES, LANES)] = jnp.where(
                lane < width, values.astype(LOW), column
            )

    @pl.when(step == pl.num_programs(0) - 1)
    def _():
        rows, columns = give.shape
        theirs = pl.ds(pl.multiple_of((1 - core) * columns, columns), columns)
        give[...] = acc_ref[:, theirs].astype(LOW)
        mine = pl.ds(pl.multiple_of(core * columns, columns), columns)
        goal = at_rows(hold, core * rows, rows)
        hold[pl.ds(pl.multiple_of(core * rows, rows), rows), :] = acc_ref[:, mine].astype(LOW)
        copy = Copies(send, recv)(give, goal, device(me, group, 1 - core))
        copy.start()
        copy.wait_send()
        copy.wait_recv()
        local = pltpu.make_async_copy(hold, grad_out, store.at[0])
        local.start()
        local.wait()


def qkv_back_kernel(
    per_slot, counts, width, scale, side, dq_ref, dk_ref, dv_ref, raw_ref, normed_ref, w_ref, gh_ref,
    cos_ref, sin_ref, x_ref, dresid_ref, ga_ref, *refs,
):
    step = pl.program_id(0)
    block = dq_ref.shape[0]
    q_tiles, kv_tiles = counts
    me, group, core = place()
    partner = device(me, group, 1 - core)
    count = len(side.plane_shapes) + len(side.line_shapes)
    sources, refs = take(refs, count)
    (out_ref, grad_ref, gain_ref, sums_ref), refs = take(refs, 4)
    totals, refs = take(refs, count)
    (acc_ref, low_ref, give, got), bufs = take(refs, 4)
    copies, end = side.run(step, sources, totals, bufs)
    parts = Blocks(copies, partner, per_slot, block, give, got)

    @pl.when(step == 0)
    def _():
        acc_ref[...] = jnp.zeros(acc_ref.shape, F32)
        gain_ref[...] = jnp.zeros(gain_ref.shape, F32)
        sums_ref[...] = jnp.zeros(sums_ref.shape, F32)

    parts.begin(step, 0)
    lane = lax.broadcasted_iota(jnp.int32, (block, LANES), 1)
    cosine, sine = cos_ref[...], sin_ref[...]

    def pair(ref, tile):
        return jnp.where(
            lane < width,
            ref[:, pl.ds(2 * tile * LANES, LANES)],
            pltpu.roll(ref[:, pl.ds((2 * tile + 1) * LANES, LANES)], width, 1),
        )

    for tile in range(q_tiles + 2 * kv_tiles):
        lanes = pl.ds(tile * LANES, LANES)
        if tile >= q_tiles + kv_tiles:
            low_ref[:, lanes] = pair(dv_ref, tile - q_tiles - kv_tiles).astype(LOW)
            continue
        if tile < q_tiles:
            turned, row = dq_ref[:, lanes] * scale, 0
        else:
            turned, row = pair(dk_ref, tile - q_tiles), 1
        gain = gh_ref[row : row + 1, :]
        dy = turned * cosine + swap_halves(turned * sine, width)
        values = raw_ref[:, lanes]
        inverse = lax.rsqrt(head_sum(values * values, width) * (1.0 / width) + EPS)
        scaled = dy * gain
        inner = head_sum(values * scaled, width) * (1.0 / width)
        low_ref[:, lanes] = (
            inverse * scaled - values * (inverse * inverse * inverse * inner)
        ).astype(LOW)
        gain_ref[row : row + 1, :] += jnp.sum(dy * values * inverse, axis=0, keepdims=True)
    low = low_ref[...]
    acc_ref[...] += tn(normed_ref[...], low)
    d_a = nt(low, w_ref[...])

    @pl.when(step < per_slot)
    def _():
        parts.put(step, d_a.astype(LOW))

    @pl.when(step >= per_slot)
    def _():
        d_norm, d_gain = norm_back(
            x_ref[...].astype(F32), d_a + parts.take(step, per_slot).astype(F32), ga_ref[...]
        )
        out_ref[...] = (dresid_ref[...] + d_norm).astype(LOW)
        sums_ref[0:1, :] += jnp.sum(d_gain, axis=0, keepdims=True)

    @pl.when(step == 2 * per_slot - 1)
    def _():
        grad_ref[...] = acc_ref[...].astype(LOW)
        parts.end(False, False)
        end()


def assemble_kernel(chunks, half, folds, head_width, model_width, *refs):
    parts, refs = take(refs, 4 * chunks)
    pairs, refs = take(refs, 6)
    small_ref, out_in, grad_in, gate_ref, up_ref, down_ref, *outs = refs
    *outs, ga_ref, gm_ref, stat_ref, gq_ref, gk_ref, out_ref, grad_ref = outs
    out_ref[...] = out_in[...]
    grad_ref[...] = grad_in[...]
    first = lax.rem(lax.axis_index("rep"), 2) == 0

    def sides(mine, other):
        return [jnp.where(first, mine, other), jnp.where(first, other, mine)]

    units = parts[0].shape[1] // 2
    piece = units // half
    for chunk in range(chunks):
        top, low, other_top, other_low = parts[4 * chunk : 4 * chunk + 4]
        for side, values in enumerate(sides(top[...], other_top[...])):
            for j, ref in enumerate((gate_ref, up_ref)):
                for i in range(half):
                    to = ((side * half + i) * chunks + chunk) * piece
                    start = j * units + i * piece
                    ref[:, to : to + piece] = values[:, start : start + piece].astype(F32)
        columns = down_ref.shape[2] // 2
        for side, values in enumerate(sides(low[...], other_low[...])):
            for fold in range(folds):
                down_ref[chunk * folds + fold, :, side * columns : (side + 1) * columns] = values[
                    :, fold * columns : (fold + 1) * columns
                ].astype(F32)
    starts = [0, 0, 0, outs[2].shape[1] // 2]
    for ref, k, start in zip(outs, (0, 2, 4, 4), starts):
        width = ref.shape[1] // 2
        mine, other = (one[:, start : start + width] for one in pairs[k : k + 2])
        for side, values in enumerate(sides(mine, other)):
            ref[:, side * width : (side + 1) * width] = values.astype(F32)

    @pl.when(pl.program_id(0) == 0)
    def _():
        me = lax.axis_index("shard")
        width = ga_ref.shape[1]
        here = pl.ds(pl.multiple_of(me * width, width), width)
        ga_ref[...] = small_ref[0:1, here]
        gm_ref[...] = small_ref[1:2, here]
        lane = lax.broadcasted_iota(jnp.int32, (1, LANES), 1)
        count = small_ref[7:8, 0:1] * model_width
        roots = jnp.zeros((1, LANES), F32)
        for k in range(3):
            total = jnp.sum(small_ref[2 + k : 3 + k, :], axis=1, keepdims=True)
            roots = jnp.where(lane == k, jnp.sqrt(total / count), roots)
        stat_ref[...] = roots[:, : stat_ref.shape[1]]
        size = gq_ref.shape[1]
        for k, ref in enumerate((gq_ref, gk_ref)):
            gains = jnp.broadcast_to(small_ref[5 + k : 6 + k, :LANES], (8, LANES))
            gains += pltpu.roll(gains, head_width, 1)
            gains = pltpu.roll(gains, lax.rem(LANES - me * size, LANES), 1)
            ref[...] = gains[0:1, :size]


class Rows:
    def __init__(self, lens, rows, block):
        self.lens, self.block, self.per_slot = lens, block, rows // block

    def both(self, width):
        return pl.BlockSpec((self.block, width), lambda i, lens: (i, 0))

    def both_other_first(self, width):
        n = self.per_slot
        return pl.BlockSpec((self.block, width), lambda i, lens: (lax.rem(i + n, 2 * n), 0))

    def early(self, width):
        n = self.per_slot
        return pl.BlockSpec((self.block, width), lambda i, lens: (jnp.minimum(i, n - 1), 0))

    def late(self, width):
        n = self.per_slot
        return pl.BlockSpec((self.block, width), lambda i, lens: (jnp.maximum(i - n, 0), 0))

    def repeated(self, width):
        n = self.per_slot
        return pl.BlockSpec((self.block, width), lambda i, lens: (lax.rem(i, n), 0))

    def fixed(self, shape):
        return pl.BlockSpec(shape, lambda i, lens: (0, 0), pipeline_mode=pl.Buffered(1))

    def call(self, name, kernel, slots, in_specs, out_specs, outs, scratch, flops, *args):
        return pl.pallas_call(
            kernel,
            out_shape=[jax.ShapeDtypeStruct(shape, kind) for shape, kind in outs],
            grid_spec=pltpu.PrefetchScalarGridSpec(
                num_scalar_prefetch=1,
                grid=(slots * self.per_slot,),
                in_specs=in_specs,
                out_specs=out_specs,
                scratch_shapes=scratch,
            ),
            cost_estimate=pl.CostEstimate(
                flops=flops, bytes_accessed=1 << 24, transcendentals=0
            ),
            compiler_params=pltpu.CompilerParams(vmem_limit_bytes=62 << 20),
            name=name,
        )(self.lens, *args)


def local(
    inputs,
    lengths,
    gain_attn,
    w_query,
    w_key,
    w_value,
    gain_query,
    gain_key,
    w_out,
    gain_mlp,
    w_gate,
    w_up,
    w_down,
    cotangent,
):
    shards = lax.axis_size("shard")
    core = lax.axis_index("rep") % 2
    first = core == 0
    rows, width_all = inputs.shape[1], inputs.shape[2]
    head_width = gain_query.shape[0] * shards
    q_half, kv_half = w_query.shape[1] // 2, w_key.shape[1] // 2
    d_half = width_all // 2
    d_rows, ff_rows = w_query.shape[0], w_down.shape[0]
    block = min(256, rows)
    scale = 1.0 / math.sqrt(head_width)
    counts = (q_half // LANES, kv_half // LANES)

    def ordered(mine, other, axis):
        return jnp.where(
            first,
            jnp.concatenate([mine, other], axis=axis),
            jnp.concatenate([other, mine], axis=axis),
        )

    half_shards = shards // 2
    groups = lax.axis_size("rep") // 2
    chunks = 3
    piece = ff_rows // chunks
    units = half_shards * piece
    folds = 2 * units // d_half
    head_rows = gain_query.shape[0]

    def fold(part):
        return jnp.concatenate(jnp.split(part, folds, axis=-2), axis=-1)

    def unfold(part):
        return jnp.concatenate(jnp.split(part, folds, axis=-1), axis=-2)

    packed_rows = d_rows + piece // folds
    hbm = pl.BlockSpec(memory_space=pltpu.HBM)
    vmem = pl.BlockSpec(memory_space=pltpu.VMEM)
    chunk_sets = [list(range(chunks - 1)), [chunks - 1]]

    def pack(*refs):
        *refs, pack_a, pack_b, sems = refs
        packs = [
            (ref, [(i * packed_rows, chunk) for i, chunk in enumerate(some)])
            for ref, some in zip((pack_a, pack_b), chunk_sets)
        ]
        pack_kernel(shards, chunks, *refs, *packs, sems)

    if piece % LANES == 0:
        packs = pl.pallas_call(
            pack,
            out_shape=[
                jax.ShapeDtypeStruct((len(some) * packed_rows, 2 * units), LOW) for some in chunk_sets
            ],
            in_specs=[hbm] * 3,
            out_specs=[vmem] * 2,
            scratch_shapes=[pltpu.SemaphoreType.DMA((chunks * (2 * half_shards + folds),))],
            compiler_params=pltpu.CompilerParams(vmem_limit_bytes=62 << 20),
            name="pack",
        )(w_gate, w_up, w_down)
    else:

        def my_half(weight):
            half = weight.shape[1] // 2
            return jnp.where(first, weight[:, :half], weight[:, half:])

        def chunk_of(weight, chunk):
            columns = weight.reshape(d_rows, shards, chunks, piece)[:, :, chunk]
            return my_half(columns.reshape(d_rows, shards * piece))

        def packed_chunk(chunk):
            tall = fold(my_half(w_down)[chunk * piece : (chunk + 1) * piece])
            wide = jnp.concatenate([chunk_of(w_gate, chunk), chunk_of(w_up, chunk)], axis=1)
            return jnp.concatenate([wide, tall])

        packs = [jnp.concatenate([packed_chunk(k) for k in some]) for some in chunk_sets]
    gathered = [lax.all_gather(packs[0], "shard", axis=0)]

    def gain_row(*gains):
        flat = jnp.concatenate(gains)
        return jnp.pad(flat, (0, max(d_rows, LANES) - flat.shape[0]))[None]

    gain_rows = jnp.pad(
        jnp.concatenate(
            [gain_row(gain_attn), gain_row(gain_mlp), gain_row(gain_query, gain_key)]
        ),
        ((0, 13), (0, 0)),
    )

    def half_of(width):
        return lambda core: core * width

    wide_parts = [
        (0, 0, half_of(q_half), 0, q_half),
        (1, 0, half_of(kv_half), q_half, kv_half),
        (2, 0, half_of(kv_half), q_half + kv_half, kv_half),
    ]
    tall_parts = [(3, 1, 0, w_out.shape[0])]
    copies = len(wide_parts) * (shards + 2) + len(tall_parts) * (2 * shards + 3) + shards + 1
    w_qkv, w_o, gains, x_other = pl.pallas_call(
        partial(gather_kernel, shards, wide_parts, tall_parts, (6, copies)),
        out_shape=[
            jax.ShapeDtypeStruct(shape, LOW)
            for shape in (
                (width_all, q_half + 2 * kv_half),
                (half_shards * w_out.shape[0], width_all),
                (shards,) + gain_rows.shape,
                inputs.shape[1:],
            )
        ],
        in_specs=[hbm] * 6,
        out_specs=[hbm] * 4,
        scratch_shapes=[pltpu.SemaphoreType.DMA((copies,)), pltpu.SemaphoreType.DMA((copies,))],
        compiler_params=pltpu.CompilerParams(collective_id=0, has_side_effects=True),
        name="gather",
    )(w_query, w_key, w_value, w_out, gain_rows, inputs[0])
    gain_a = gains[:, 0, :d_rows].reshape(1, -1).astype(F32)
    gain_m = gains[:, 1, :d_rows].reshape(1, -1).astype(F32)
    gain_q = gains[:, 2, :head_rows].reshape(1, -1).astype(F32)
    gain_k = gains[:, 2, head_rows : 2 * head_rows].reshape(1, -1).astype(F32)
    gain_h = jnp.tile(jnp.concatenate([gain_q, gain_k]), (4, LANES // head_width))

    lens = jnp.concatenate([lengths, core_swap(lengths)])
    x_own = inputs[0]
    g_own = cotangent[0]
    g_other = core_swap(g_own)
    over = Rows(lens, rows, block)
    cosine, sine = rope_tables(rows, head_width)
    full, total = 2 * rows, w_qkv.shape[1]
    qk = q_half + kv_half

    normed_a, raw, queries, keys, values = over.call(
        "qkv",
        partial(qkv_kernel, over.per_slot, counts, head_width, scale),
        2,
        [over.early(width_all), over.late(width_all), over.fixed(w_qkv.shape)]
        + [over.fixed(gain_a.shape), over.fixed(gain_h.shape)]
        + [over.repeated(LANES), over.repeated(LANES)],
        [over.both(width_all), over.both(qk), over.both(2 * q_half), over.both(2 * kv_half)]
        + [over.both(2 * kv_half)],
        [((full, width_all), LOW), ((full, qk), F32), ((full, 2 * q_half), LOW)]
        + [((full, 2 * kv_half), LOW)] * 2,
        [],
        2 * full * width_all * total,
        x_own, x_other, w_qkv, gain_a, gain_h, cosine, sine,
    )
    attended, queries = attend(
        lens, queries, keys, values, rows, head_width, min(512, rows)
    )
    later, attended = lax.optimization_barrier((packs[1], attended))
    gathered.append(lax.all_gather(later, "shard", axis=0))
    n = over.per_slot
    eight = (8, width_all)
    first_rows = pl.BlockSpec((block, width_all), lambda i: (jnp.minimum(i, n - 1), 0))
    last_rows = pl.BlockSpec((block, width_all), lambda i: (jnp.maximum(i - n, 0), 0))
    all_rows = pl.BlockSpec((block, width_all), lambda i: (i, 0))
    smem = pl.BlockSpec(memory_space=pltpu.SMEM)

    def other_first(width):
        return pl.BlockSpec((block, width), lambda i: (lax.rem(i + n, 2 * n), 0))

    def held(shape):
        return pl.BlockSpec(shape, lambda i: (0, 0), pipeline_mode=pl.Buffered(1))

    sums_spec = pl.BlockSpec(eight, lambda i: (0, 0))
    slot_rows = pltpu.VMEM((rows, width_all), LOW)
    resid, normed_b, sums_a, normed_b_other = pl.pallas_call(
        partial(out_kernel, n),
        out_shape=[
            jax.ShapeDtypeStruct((rows, width_all), F32),
            jax.ShapeDtypeStruct((rows, width_all), LOW),
            jax.ShapeDtypeStruct(eight, F32),
            jax.ShapeDtypeStruct((rows, width_all), LOW),
        ],
        grid=(2 * n,),
        in_specs=[smem, other_first(q_half), held(w_o.shape), last_rows, held(gain_m.shape)],
        out_specs=[last_rows, last_rows, sums_spec, hbm],
        scratch_shapes=[pltpu.VMEM((2 * block, width_all), LOW), slot_rows, slot_rows, slot_rows]
        + [pltpu.SemaphoreType.DMA((2 * n,))] * 2
        + [pltpu.SemaphoreType.DMA((1,))],
        cost_estimate=pl.CostEstimate(
            flops=2 * full * q_half * width_all, bytes_accessed=1 << 24, transcendentals=0
        ),
        compiler_params=pltpu.CompilerParams(
            collective_id=6, has_side_effects=True, vmem_limit_bytes=62 << 20
        ),
        name="out",
    )(lengths, attended, w_o, x_own, gain_m)

    sums = []
    ff_grads, ff_levels, ff_totals = [], [], []
    packed_shape = (shards * packed_rows, 2 * units)
    level_shape = (packed_rows, 2 * units)
    wide_shape, tall_shape = (width_all, 2 * units), (units, width_all)
    for chunk in range(chunks):
        last = chunk == chunks - 1
        side = Side(
            shards,
            groups,
            [level_shape] if chunk >= 1 else [],
            [level_shape] if chunk >= 2 else [],
            2 * half_shards * folds + 3 * n,
        )
        late = chunk == chunks - 1
        sources = ff_grads[-1:] + ff_levels[-1:]
        ends = [all_rows] * 2
        end_shapes = [jax.ShapeDtypeStruct((full, width_all), F32)] * 2
        own_rows, other_rows, sum_rows, more, more_specs, exchange = (
            first_rows, last_rows, all_rows, [], [], []
        )
        if last:
            own_rows, other_rows, sum_rows = last_rows, first_rows, other_first(width_all)
            more = [resid, gain_m]
            more_specs = [last_rows, held(gain_m.shape)]
            ends = [last_rows] * 3 + [sums_spec, hbm]
            end_shapes = [
                jax.ShapeDtypeStruct((rows, width_all), LOW),
                jax.ShapeDtypeStruct((rows, width_all), F32),
                jax.ShapeDtypeStruct((rows, width_all), LOW),
                jax.ShapeDtypeStruct(eight, F32),
                jax.ShapeDtypeStruct((rows, width_all), LOW),
            ]
            exchange = [pltpu.VMEM((2 * block, width_all), LOW), slot_rows] * 3
        outs = pl.pallas_call(
            partial(
                ffn_kernel, n, shards, bool(sums), last, side, 0 if late else chunk * packed_rows
            ),
            out_shape=end_shapes + [jax.ShapeDtypeStruct(packed_shape, LOW)] + side.outs(),
            grid=(2 * n,),
            in_specs=[smem]
            + [own_rows, other_rows] * 2
            + [hbm]
            + [sum_rows] * len(sums)
            + more_specs
            + [hbm] * len(sources),
            out_specs=ends + [hbm] * (1 + len(side.outs())),
            scratch_shapes=[pltpu.VMEM(wide_shape, F32), pltpu.VMEM(tall_shape, F32)]
            + [pltpu.VMEM((units, d_half), LOW)]
            + [pltpu.VMEM(wide_shape, LOW), pltpu.VMEM(tall_shape, LOW)]
            + [pltpu.VMEM(packed_shape, LOW)]
            + [pltpu.SemaphoreType.DMA((shards + half_shards * folds,))]
            + exchange
            + side.scratch(),
            cost_estimate=pl.CostEstimate(
                flops=18 * full * width_all * units, bytes_accessed=1 << 25, transcendentals=0
            ),
            compiler_params=pltpu.CompilerParams(
                collective_id=2 + chunk, has_side_effects=True, vmem_limit_bytes=67043328
            ),
            name="ffn",
        )(lens, normed_b, normed_b_other, g_own, g_other, gathered[late], *sums, *more, *sources)
        sums = outs[: len(end_shapes)]
        ff_grads.append(outs[len(end_shapes)])
        rest = outs[len(end_shapes) + 1 :]
        ff_levels += rest[:1]
        ff_totals += rest[1:]
    output, d_resid, d_attn, sums_b, d_attn_other = sums

    o_shape = w_o.shape
    d_heads, grad_out = pl.pallas_call(
        partial(dout_kernel, n, head_width),
        out_shape=[
            jax.ShapeDtypeStruct((full, 2 * q_half), LOW),
            jax.ShapeDtypeStruct((2 * o_shape[0], d_half), LOW),
        ],
        grid=(2 * n,),
        in_specs=[first_rows, last_rows, pl.BlockSpec((block, q_half), lambda i: (i, 0))]
        + [held(o_shape)],
        out_specs=[pl.BlockSpec((block, 2 * q_half), lambda i: (i, 0)), hbm],
        scratch_shapes=[pltpu.VMEM(o_shape, F32), pltpu.VMEM((o_shape[0], d_half), LOW)]
        + [pltpu.VMEM((2 * o_shape[0], d_half), LOW)]
        + [pltpu.SemaphoreType.DMA((1,))] * 3,
        cost_estimate=pl.CostEstimate(
            flops=4 * full * q_half * width_all, bytes_accessed=1 << 24, transcendentals=0
        ),
        compiler_params=pltpu.CompilerParams(
            collective_id=8, has_side_effects=True, vmem_limit_bytes=62 << 20
        ),
        name="dout",
    )(d_attn, d_attn_other, attended, w_o)
    o_level = (d_rows, d_half)
    d_query, d_key, d_value, ff_level, ff_total = attend_back(
        queries,
        keys,
        values,
        d_heads,
        rows,
        head_width,
        block,
        Side(shards, groups, [level_shape], [level_shape]),
        [ff_grads[-1], ff_levels[-1]],
    )
    ff_totals.append(ff_total)
    top_shape = (d_rows, 2 * units)
    side = Side(shards, groups, [o_level], [top_shape], n)
    turned = pl.BlockSpec((block, LANES), lambda i: (lax.rem(i, n), 0))
    input_grad, grad_qkv, gain_sums, sums_c, out_level, ff_top = pl.pallas_call(
        partial(qkv_back_kernel, n, counts, head_width, scale, side),
        out_shape=[
            jax.ShapeDtypeStruct((rows, width_all), LOW),
            jax.ShapeDtypeStruct(w_qkv.shape, LOW),
            jax.ShapeDtypeStruct((8, LANES), F32),
            jax.ShapeDtypeStruct(eight, F32),
        ]
        + side.outs(),
        grid=(2 * n,),
        in_specs=[other_first(q_half), other_first(2 * kv_half), other_first(2 * kv_half)]
        + [other_first(qk), other_first(width_all), held(w_qkv.shape), held(gain_h.shape)]
        + [turned, turned, last_rows, last_rows, held(gain_a.shape), hbm, hbm],
        out_specs=[last_rows, held(w_qkv.shape)]
        + [pl.BlockSpec((8, LANES), lambda i: (0, 0)), sums_spec, hbm, hbm],
        scratch_shapes=[pltpu.VMEM(w_qkv.shape, F32), pltpu.VMEM((block, total), LOW)]
        + [pltpu.VMEM((2 * block, width_all), LOW), slot_rows]
        + side.scratch(),
        cost_estimate=pl.CostEstimate(
            flops=4 * full * width_all * total, bytes_accessed=1 << 24, transcendentals=0
        ),
        compiler_params=pltpu.CompilerParams(
            collective_id=7, has_side_effects=True, vmem_limit_bytes=62 << 20
        ),
        name="qkv_back",
    )(
        d_query, d_key, d_value, raw, normed_a, w_qkv, gain_h, cosine, sine, x_own, d_resid, gain_a,
        grad_out, ff_level,
    )
    mine, other, small = finish_sums(
        grad_qkv,
        lengths,
        [sums_a, sums_b, sums_c, gain_sums],
        [(2, 0), (1, 1), (0, 0), (0, 1), (1, 0), (3, 0), (3, 1)],
        [ff_level, out_level],
        d_rows,
        ff_totals + [ff_top],
        shards,
        groups,
    )
    wide = (d_rows, shards * ff_rows)
    shapes = [wide, wide, (chunks * folds, piece // folds, width_all)]
    shapes += [w.shape for w in (w_out, w_query, w_key, w_value)]
    shapes += [(1, d_rows), (1, d_rows), (1, 3), (1, head_rows), (1, head_rows)]
    top = d_rows // 8
    low_rows = piece // folds // 8

    def whole(part):
        return pl.BlockSpec((top, part.shape[1]), lambda i: (i, 0))

    def low(part, skip):
        return pl.BlockSpec((low_rows, part.shape[1]), lambda i: (skip // low_rows + i, 0))

    parts, specs = [], []
    for chunk in range(chunks):
        for total, rest in (
            (ff_totals[chunk], ff_totals[chunk]) if chunk < chunks - 1 else (ff_top, mine[0]),
            (other[4 + chunk], other[4 + chunk]) if chunk < chunks - 1 else (other[-1], other[0]),
        ):
            parts += [total, rest]
            specs += [whole(total), low(rest, d_rows if chunk < chunks - 1 else 0)]
    pairs = [one for pair in zip(mine[1:4], other[1:4]) for one in pair]
    small_specs = [pl.BlockSpec(shape, lambda i: (0, 0)) for shape in shapes[7:]]
    eighth = pl.BlockSpec((rows // 8, width_all), lambda i: (i, 0))
    passed = [jax.ShapeDtypeStruct((rows, width_all), LOW)] * 2
    (
        grad_gate, grad_up, grad_down, grad_out, grad_query, grad_key, grad_value,
        grad_ga, grad_gm, statistics, grad_gq, grad_gk, output, input_grad,
    ) = pl.pallas_call(
        partial(assemble_kernel, chunks, half_shards, folds, head_width, width_all),
        out_shape=[jax.ShapeDtypeStruct(shape, F32) for shape in shapes] + passed,
        grid=(8,),
        in_specs=specs
        + [whole(part) for part in pairs]
        + [pl.BlockSpec(small.shape, lambda i: (0, 0)), eighth, eighth],
        out_specs=[pl.BlockSpec((top, shape[1]), lambda i: (i, 0)) for shape in shapes[:2]]
        + [pl.BlockSpec((shapes[2][0], low_rows, width_all), lambda i: (0, i, 0))]
        + [pl.BlockSpec((top, shape[1]), lambda i: (i, 0)) for shape in shapes[3:7]]
        + small_specs
        + [eighth, eighth],
        compiler_params=pltpu.CompilerParams(vmem_limit_bytes=62 << 20),
        name="assemble",
    )(*parts, *pairs, small, output, input_grad)
    return (
        output[None],
        input_grad[None],
        grad_ga.reshape(-1),
        grad_query,
        grad_key,
        grad_value,
        grad_gq.reshape(-1),
        grad_gk.reshape(-1),
        grad_out,
        grad_gm.reshape(-1),
        grad_gate,
        grad_up,
        grad_down.reshape(w_down.shape),
        statistics.reshape(-1),
    )


def solution(mesh):
    in_specs = (
        P(("rep", "shard"), None, None),
        P(("rep", "shard")),
        P("shard"),
        P("shard", None),
        P("shard", None),
        P("shard", None),
        P("shard"),
        P("shard"),
        P("shard", None),
        P("shard"),
        P("shard", None),
        P("shard", None),
        P("shard", None),
        P(("rep", "shard"), None, None),
    )
    out_specs = (
        P(("rep", "shard"), None, None),
        P(("rep", "shard"), None, None),
        P("shard"),
        P("shard", None),
        P("shard", None),
        P("shard", None),
        P("shard"),
        P("shard"),
        P("shard", None),
        P("shard"),
        P("shard", None),
        P("shard", None),
        P("shard", None),
        P(),
    )
    return jax.shard_map(local, mesh=mesh, in_specs=in_specs, out_specs=out_specs, check_vma=False)
```
